32 devices in a mesh: dp: 4 (over y, x), tensor: 8 (over z, core).
Axes of the slice: x: 2, y: 2, z: 4, core: 2. Of those that a mesh axis runs over, the one named last changes fastest.
Arguments:
- tokens: bfloat16 [8192, 1024], P(('dp', 'tensor')), may hold values from -6 to 6
- class_embed: float32 [4, 6, 1024], P('dp', None, 'tensor'), may hold values from -6 to 6
- item_lengths: int32 [4, 6], P('dp'), may hold values from 1 to 680, 2048 in all within a row
- token_codes: int32 [8192], P(('dp', 'tensor')), may hold values from 0 to 4095
- ada_weight: bfloat16 [1024, 6144], P('tensor'), may hold values from -0.375 to 0.375
- ada_bias: float32 [6144], replicated, may hold values from -4 to 4
- qkv_weight: bfloat16 [1024, 3, 1024], P(None, None, 'tensor'), may hold values from -0.1875 to 0.1875
- query_bias: float32 [1024], P('tensor'), may hold values from -6 to 6
- value_bias: float32 [1024], P('tensor'), may hold values from -6 to 6
- head_scale: float32 [16], P('tensor'), may hold values from 2 to 2.8
- proj_weight: bfloat16 [1024, 1024], P('tensor'), may hold values from -0.1875 to 0.1875
- proj_bias: float32 [1024], replicated, may hold values from -4 to 4
- up_weight: bfloat16 [1024, 4096], P(None, 'tensor'), may hold values from -0.1875 to 0.1875
- up_bias: float32 [4096], replicated, may hold values from -6 to 6
- down_weight: bfloat16 [4096, 1024], P('tensor'), may hold values from -0.09375 to 0.09375
- down_bias: float32 [1024], replicated, may hold values from -4 to 4
- out_grad: bfloat16 [8192, 1024], P(('dp', 'tensor')), may hold values from -6 to 6
Outputs:
- layer_out: bfloat16 [8192, 1024], P(('dp', 'tensor'))
- tokens_grad: float32 [8192, 1024], P(('dp', 'tensor'))
- embed_grad: float32 [4, 6, 1024], P('dp', None, 'tensor')
- adaw_grad: float32 [1024, 6144], P('tensor')
- adab_grad: float32 [6144], replicated
- qkvw_grad: float32 [1024, 3, 1024], P(None, None, 'tensor')
- qbias_grad: float32 [1024], P('tensor')
- vbias_grad: float32 [1024], P('tensor')
- hscale_grad: float32 [16], P('tensor')
- projw_grad: float32 [1024, 1024], P('tensor')
- projb_grad: float32 [1024], replicated
- upw_grad: float32 [1024, 4096], P(None, 'tensor')
- upb_grad: float32 [4096], P('tensor')
- downw_grad: float32 [4096, 1024], P('tensor')
- downb_grad: float32 [1024], replicated
- code_hist: float32 [4096], replicated
The draws below stay inside these ranges and needn't reach their ends.
Inputs may be any that keep to these rules, and one draw needn't show every extreme that they name: `item_lengths`: in each row the 6 lengths sum to 2048, and one of them is exactly 680.
All inputs are finite; a program needn't handle non-finite values.
Results may differ from the reference program's by a relative error of at most 0.028.
Values may be sent and summed in bfloat16 or wider, within the bound.
A program may use at most 128 MiB of HBM per device.

```python
import math
from functools import partial
import jax
import jax.numpy as jnp
import numpy as np
from jax import lax

D = 1024
HEADS = 16
HEAD = 64
FF = 4096
NBINS = 4096
ROW_LEN = 2048
ITEM_MAX = 680
SEGS = 6
BLOCK = 512
ROWS = 4
TOKENS = 8192


def set_ends(entries, stream_key, low, largest):
    extent = entries.shape
    place = [jax.random.randint(jax.random.fold_in(stream_key, axis), (), 0, extent[axis]) for axis in range(len(extent))]
    entries = entries.at[tuple(place)].set(low)
    longest = extent.index(max(extent))
    place[longest] = (place[longest] + 1) % extent[longest]
    return entries.at[tuple(place)].set(largest)


def shard_levels(rng, shape, cuts, least, largest):
    def one(dim, blocks):
        heights = jax.random.uniform(jax.random.fold_in(jax.random.fold_in(rng, 6), dim), (blocks,), jnp.float32, least / len(cuts), largest / len(cuts))
        return jnp.repeat(jnp.exp(heights), shape[dim] // blocks).reshape((-1,) + (1,) * (len(shape) - dim - 1))

    factor_of = one(*cuts[0])
    for cut in cuts[1:]:
        factor_of = factor_of * one(*cut)
    return factor_of


def rank_table(amount, slope):
    portions = [(1 << 20) // math.isqrt(standing ** slope) + 1 for standing in range(1, amount + 1)]
    scale = 1 + sum(portions) // (1 << 30)
    return np.cumsum(np.array([max(1, weight // scale) for weight in portions]))


def ranked(rng, extent, amount, lean):
    grid = rank_table(amount, lean)
    lot = jax.random.randint(jax.random.fold_in(rng, 1), extent, 0, int(grid[amount - 1]))
    rank = jnp.searchsorted(jnp.asarray(grid, jnp.int32), lot, side="right")
    return jax.random.permutation(jax.random.fold_in(rng, 2), amount)[rank].astype(jnp.int32)


def length_profile(count, total, most, slope):
    loads = [(1 << 20) // math.isqrt(standing ** slope) + 1 for standing in range(2, count + 1)]
    spare, given = total - most - (count - 1), [1] * (count - 1)
    while spare > 0:
        free = [i for i in range(count - 1) if given[i] < most]
        whole, left = sum([loads[i] for i in free]), spare
        for i in free:
            extra = min(most - given[i], max(1, left * loads[i] // whole), spare)
            given[i] = given[i] + extra
            spare = spare - extra
    return np.array([most] + given)


def ragged(key, amount, total, limit, skew):
    if amount == 2:
        one = jax.random.randint(key, (), max(1, total - limit), min(limit, total - 1) + 1)
        return jnp.stack([one, total - one])
    sizes = jnp.asarray(length_profile(amount, total, limit, skew), jnp.int32)
    twos = (amount - 1) // 2
    source_of, taker = sizes[1:1 + 2 * twos:2], sizes[2:2 + 2 * twos:2]
    margin = jnp.minimum(source_of - 1, limit - taker)
    moved = jax.random.randint(jax.random.fold_in(key, 1), (twos,), 0, 1 << 20) % (margin + 1)
    sizes = sizes.at[1:1 + 2 * twos:2].set(source_of - moved).at[2:2 + 2 * twos:2].set(taker + moved)
    return sizes[jax.random.permutation(jax.random.fold_in(key, 2), amount)]


def bell_draw(key, shape, scale, bound, cuts=(), kind=jnp.bfloat16):
    values = scale * jax.random.normal(key, shape, jnp.float32)
    if cuts:
        values = values * shard_levels(key, shape, cuts, -0.22, 0.18)
    return jnp.clip(values, -bound, bound).astype(kind)


def setup_inputs(seed: int = 0) -> dict:
    keys = jax.random.split(jax.random.key(seed), 18)
    tokens = bell_draw(keys[0], (TOKENS, D), 1.0, 6.0, ((0, 32),))
    class_embed = bell_draw(keys[1], (ROWS, SEGS, D), 1.0, 6.0, ((0, 4), (2, 8)), jnp.float32)
    item_lengths = jax.vmap(lambda own: ragged(own, SEGS, ROW_LEN, ITEM_MAX, 1))(jax.random.split(keys[2], ROWS)).reshape((ROWS, SEGS)).astype(jnp.int32)
    token_codes = set_ends(ranked(keys[3], (TOKENS,), NBINS, 2), jax.random.fold_in(keys[3], 3), 0, NBINS - 1).astype(jnp.int32)
    ada_weight = bell_draw(keys[4], (D, 6 * D), (D // 4) ** -0.5, 0.375, ((0, 8),))
    ada_bias = bell_draw(keys[5], (6 * D,), 0.3, 4.0, (), jnp.float32)
    qkv_weight = bell_draw(keys[6], (D, 3, D), D ** -0.5, 0.1875, ((2, 8),))
    query_bias = bell_draw(keys[7], (D,), 1.0, 6.0, ((0, 8),), jnp.float32)
    value_bias = bell_draw(keys[8], (D,), 1.0, 6.0, ((0, 8),), jnp.float32)
    head_scale = jnp.clip(2.0 + 0.79999995 * jax.random.uniform(keys[9], (HEADS,), jnp.float32) ** shard_levels(keys[9], (HEADS,), ((0, 8),), -0.2, 0.2), 2.0, 2.8)
    proj_weight = bell_draw(keys[10], (D, D), D ** -0.5, 0.1875, ((0, 8),))
    proj_bias = bell_draw(keys[11], (D,), 0.3, 4.0, (), jnp.float32)
    up_weight = bell_draw(keys[12], (D, FF), D ** -0.5, 0.1875, ((1, 8),))
    up_bias = bell_draw(keys[13], (FF,), 0.5, 6.0, (), jnp.float32)
    down_weight = bell_draw(keys[14], (FF, D), FF ** -0.5, 0.09375, ((0, 8),))
    down_bias = bell_draw(keys[15], (D,), 0.3, 4.0, (), jnp.float32)
    out_grad = bell_draw(keys[16], (TOKENS, D), 1.0, 6.0, ((0, 32),))
    return {"tokens": tokens, "class_embed": class_embed, "item_lengths": item_lengths, "token_codes": token_codes, "ada_weight": ada_weight, "ada_bias": ada_bias, "qkv_weight": qkv_weight, "query_bias": query_bias, "value_bias": value_bias, "head_scale": head_scale, "proj_weight": proj_weight, "proj_bias": proj_bias, "up_weight": up_weight, "up_bias": up_bias, "down_weight": down_weight, "down_bias": down_bias, "out_grad": out_grad}


@jax.custom_vjp
def low(v):
    return lax.optimization_barrier(v.astype(jnp.bfloat16)).astype(jnp.float32)

@jax.custom_vjp
def low_back(v):
    return v

def low_keep(v):
    return (low(v), None)

def low_pass(kept, grad):
    return (grad,)

def back_keep(v):
    return (v, None)

def back_low(kept, grad):
    return (low(grad),)
low.defvjp(low_keep, low_pass)
low_back.defvjp(back_keep, back_low)
epsilon = 1e-06
big_negative = -1e+30
scale_starts = (1, 5, 14, 30, 55, 91, 155, 255, 424)
highest = lax.Precision.HIGHEST

def item_layout(item_lengths):
    item_ends = jnp.cumsum(item_lengths, axis=1, dtype=jnp.int32)
    item_begin = item_ends - item_lengths
    position = jnp.arange(ROW_LEN, dtype=jnp.int32)
    segment = lax.optimization_barrier(jnp.sum((position[None, :, None] >= item_ends[:, None, :]).astype(jnp.int32), axis=2, dtype=jnp.int32))
    chosen = segment[:, :, None] == jnp.arange(SEGS, dtype=jnp.int32)[None, None, :]
    begin_tok = lax.optimization_barrier(jnp.sum(jnp.where(chosen, item_begin[:, None, :], 0), axis=2, dtype=jnp.int32))
    inside_pos = position[None, :] - begin_tok
    scale_ids = jnp.zeros_like(inside_pos)
    for threshold in scale_starts:
        scale_ids = scale_ids + (inside_pos >= threshold).astype(jnp.int32)
    return (segment, scale_ids)

def layer_norm(values):
    row_mean = lax.optimization_barrier(jnp.mean(values, axis=-1, keepdims=True))
    centred = values - row_mean
    row_var = lax.optimization_barrier(jnp.mean(centred * centred, axis=-1, keepdims=True))
    return centred * lax.rsqrt(row_var + epsilon)

def unit_rows(values):
    return values * lax.rsqrt(lax.optimization_barrier(jnp.sum(values * values, axis=-1, keepdims=True)) + epsilon)

def gelu_tanh(values):
    return 0.5 * values * (1.0 + jnp.tanh(0.7978845608028654 * (values + 0.044715 * values * values * values)))

def attend_row(query_unit, key_unit, value_in, segment, scale_ids):

    def one_block(block_index):
        offset = block_index * BLOCK
        query_block = lax.dynamic_slice_in_dim(query_unit, offset, BLOCK, 0)
        block_seg = lax.dynamic_slice_in_dim(segment, offset, BLOCK, 0)
        block_scale = lax.dynamic_slice_in_dim(scale_ids, offset, BLOCK, 0)
        allowed = (block_seg[:, None] == segment[None, :]) & (block_scale[:, None] >= scale_ids[None, :])
        scores = low_back(jnp.einsum('bhe,lhe->hbl', query_block, key_unit, precision=highest))
        scores = jnp.where(allowed[None], scores, big_negative)
        row_max = lax.optimization_barrier(jnp.max(scores, axis=2, keepdims=True))
        weights = jnp.exp(scores - row_max)
        attn_probs = low(weights / lax.optimization_barrier(jnp.sum(weights, axis=2, keepdims=True)))
        return jnp.einsum('hbl,lhe->bhe', attn_probs, value_in, precision=highest)
    blocks = lax.map(jax.checkpoint(one_block), jnp.arange(ROW_LEN // BLOCK, dtype=jnp.int32))
    return blocks.reshape(ROW_LEN, HEADS, HEAD)

def forward(tokens, class_embed, ada_weight, ada_bias, qkv_weight, query_bias, value_bias, head_scale, proj_weight, proj_bias, up_weight, up_bias, down_weight, down_bias, segment, scale_ids):
    cond_act = low(jax.nn.silu(class_embed)).reshape(ROWS * SEGS, D)
    modulation = (jnp.dot(cond_act, ada_weight, precision=highest) + ada_bias).reshape(ROWS, SEGS, 6 * D)

    def row_pass(packed):
        row_tokens, row_mod, row_segment, row_scale = packed
        per_token = jnp.take(row_mod, row_segment, axis=0)
        gamma_one, gamma_two, scale_one, scale_two, shift_one, shift_two = jnp.split(per_token, 6, axis=1)
        normed_one = low(layer_norm(row_tokens) * (1.0 + scale_one) + shift_one)
        projected = jnp.einsum('ld,dcf->lcf', normed_one, qkv_weight, precision=highest)
        query_raw = low_back(projected[:, 0] + query_bias).reshape(ROW_LEN, HEADS, HEAD)
        key_raw = low_back(projected[:, 1]).reshape(ROW_LEN, HEADS, HEAD)
        value_raw = low_back(projected[:, 2] + value_bias).reshape(ROW_LEN, HEADS, HEAD)
        query_unit = low(unit_rows(query_raw) * jnp.exp(head_scale)[:, None])
        key_unit = low(unit_rows(key_raw))
        value_in = low(value_raw)
        attended = attend_row(query_unit, key_unit, value_in, row_segment, row_scale)
        heads_out = low(low_back(attended)).reshape(ROW_LEN, D)
        attn_branch = low_back(jnp.dot(heads_out, proj_weight, precision=highest) + proj_bias)
        resid_mid = row_tokens + gamma_one * attn_branch
        normed_two = low(layer_norm(resid_mid) * (1.0 + scale_two) + shift_two)
        pre_act = low_back(jnp.dot(normed_two, up_weight, precision=highest) + up_bias)
        hidden = low(gelu_tanh(pre_act))
        mlp_branch = low_back(jnp.dot(hidden, down_weight, precision=highest) + down_bias)
        return resid_mid + gamma_two * mlp_branch
    outputs = lax.map(jax.checkpoint(row_pass), (tokens.reshape(ROWS, ROW_LEN, D), modulation, segment, scale_ids))
    return outputs.reshape(TOKENS, D)

def reference(tokens, class_embed, item_lengths, token_codes, ada_weight, ada_bias, qkv_weight, query_bias, value_bias, head_scale, proj_weight, proj_bias, up_weight, up_bias, down_weight, down_bias, out_grad):
    segment, scale_ids = item_layout(item_lengths)
    block_fn = partial(forward, segment=segment, scale_ids=scale_ids)
    result, pullback = jax.vjp(block_fn, tokens.astype(jnp.float32), class_embed, ada_weight.astype(jnp.float32), ada_bias, qkv_weight.astype(jnp.float32), query_bias, value_bias, head_scale, proj_weight.astype(jnp.float32), proj_bias, up_weight.astype(jnp.float32), up_bias, down_weight.astype(jnp.float32), down_bias)
    grads = pullback(out_grad.astype(jnp.float32))
    code_hist = jax.ops.segment_sum(jnp.ones((TOKENS,), jnp.float32), token_codes, num_segments=NBINS)
    return (result.astype(jnp.bfloat16), grads[0], grads[1], grads[2], grads[3], grads[4], grads[5], grads[6], grads[7], grads[8], grads[9], grads[10], grads[11], grads[12], grads[13], code_hist)
```

```python
import functools

import jax
import jax.numpy as jnp
from jax import lax
from jax.experimental import pallas as pl
from jax.experimental.pallas import tpu as pltpu
from jax.sharding import PartitionSpec as P

HEAD = 64
NBINS = 4096
ROW_LEN = 2048
SEGS = 6
D = 1024
ITEM_MAX = 680
CORES = 2
LANES = 128

epsilon = 1e-06
scale_starts = (1, 5, 14, 30, 55, 91, 155, 255, 424)
AHEAD = ITEM_MAX - scale_starts[-1] - 1
BEHIND = ITEM_MAX - 1
highest = lax.Precision.HIGHEST
f32 = jnp.float32
bf16 = jnp.bfloat16
MESH = pl.DeviceIdType.MESH
VMEM_LIMIT = 56 << 20


def dot(a, b, ca=1, cb=0, precision=None):
    return lax.dot_general(
        a, b, (((ca,), (cb,)), ((), ())), preferred_element_type=f32, precision=precision
    )


def item_layout(lengths):
    ends = jnp.cumsum(lengths, dtype=jnp.int32)
    begin = ends - lengths
    position = jnp.arange(ROW_LEN, dtype=jnp.int32)
    segment = jnp.sum((position[:, None] >= ends[None, :]).astype(jnp.int32), axis=1)
    chosen = segment[:, None] == jnp.arange(SEGS, dtype=jnp.int32)[None, :]
    inside = position - jnp.sum(jnp.where(chosen, begin[None, :], 0), axis=1)
    scale_ids = jnp.zeros_like(inside)
    for threshold in scale_starts:
        scale_ids = scale_ids + (inside >= threshold).astype(jnp.int32)
    return segment, scale_ids


def greet(peers):
    barrier = pltpu.get_barrier_semaphore()
    for p in peers:
        pl.semaphore_signal(barrier, inc=1, device_id=p, device_id_type=MESH)
    pl.semaphore_wait(barrier, len(peers))


def remote(src, dst, send, recv, to):
    return pltpu.make_async_remote_copy(
        src_ref=src,
        dst_ref=dst,
        send_sem=send,
        recv_sem=recv,
        device_id=to,
        device_id_type=MESH,
    )


class Place:
    def __init__(self, n, nd):
        self.n, self.nd, self.nz = n, nd, n // CORES
        self.dp, self.me = lax.axis_index("dp"), lax.axis_index("tensor")
        self.z, self.core = self.me // CORES, lax.rem(self.me, CORES)
        self.orders = orders_of(nd)
        self.far = sorted(range(1, self.nz), key=lambda o: min(o, self.nz - o))

    def chip(self, step):
        return lax.rem(self.z + step + self.nz, self.nz)

    def on_chip(self, step):
        return (self.dp, self.chip(step) * CORES + self.core)

    def twin(self):
        return (self.dp, self.z * CORES + 1 - self.core)

    def flip(self, bit):
        return (self.dp ^ (1 << bit), self.me)

    def line(self):
        return [(self.dp, lax.rem(self.me + o, self.n)) for o in range(1, self.n)]

    def greet_all(self):
        greet(self.line() + [self.flip(b) for b in range(bits_of(self.nd))])


def bits_of(nd):
    return nd.bit_length() - 1


def orders_of(nd):
    m = bits_of(nd)
    return [list(range(m)), [(m // 2 + i) % m for i in range(m)]]


def spread_plan(order):
    plan = [(0, list(order))]
    for i, bit in enumerate(order):
        plan += [(rel | (1 << bit), list(order[i + 1 :])) for rel, _ in list(plan)]
    return plan


class Spread:
    def __init__(self, place, ref_of, send, recv):
        self.place, self.ref_of, self.send, self.recv = place, ref_of, send, recv
        self.copies = {}

    def launch(self, part, rel, bits):
        p = self.place
        ref = self.ref_of(part, p.dp ^ rel)
        for bit in bits:
            to = rel | (1 << bit)
            c = remote(ref, ref, self.send.at[part, to], self.recv.at[part, to], p.flip(bit))
            c.start()
            self.copies[part, to] = c

    def begin(self):
        for part, order in enumerate(self.place.orders):
            self.launch(part, 0, order)

    def step(self, level):
        for part, order in enumerate(self.place.orders):
            for rel, bits in spread_plan(order):
                if rel and len(order) - 1 - len(bits) == level:
                    self.copies[part, rel].wait_recv()
                    self.launch(part, rel, bits)

    def end(self):
        for c in self.copies.values():
            c.wait_send()


def front_body(
    n, nd, steps, tok_ref, part_ref, extra_ref, apack_ref, mpack_ref,
    mod_ref, win_ref, wa_ref, wm_ref,
    zero, held, s1, r1, s2, r2, ts, tr, cs, cr, zs, zr, local_sem, das, dar, dms, dmr,
):
    p = Place(n, nd)
    tok = tok_ref.shape[0]
    half = apack_ref.shape[2] // 2
    zero[...] = jnp.zeros_like(zero)
    p.greet_all()
    line = p.line()
    sums = [
        remote(part_ref.at[q[1]], held.at[o], s1.at[o], r1.at[o], q) for o, q in enumerate(line)
    ]
    for c in sums:
        c.start()
    owns = [pltpu.make_async_copy(tok_ref, win_ref.at[0, 0], local_sem.at[0])]
    twins = [remote(tok_ref, win_ref.at[0, 1], cs.at[0], cr.at[0], p.twin())]
    owns[0].start()
    twins[0].start()
    moves = []
    for i, per_core in enumerate(steps):
        for c, step in enumerate(per_core):
            if step is None:
                continue
            go = (p.core == c) & (p.z + step >= 0) & (p.z + step < p.nz)
            got = (p.core == c) & (p.z - step >= 0) & (p.z - step < p.nz)
            copy = remote(
                tok_ref, win_ref.at[i + 1, 0], ts.at[i, c], tr.at[i, c], p.on_chip(step)
            )
            moves.append((i, c, go, got, copy))
            pl.when(go)(copy.start)
    zcopies = {}
    for w, (src, dst) in enumerate(
        ((apack_ref.at[p.dp], wa_ref.at[p.z, p.dp]), (mpack_ref.at[:, p.dp], wm_ref.at[p.z, :, p.dp]))
    ):
        for o in p.far:
            c = remote(src, dst, zs.at[w, o], zr.at[w, o], p.on_chip(o))
            c.start()
            zcopies[w, o] = c
    owns.append(pltpu.make_async_copy(apack_ref, wa_ref.at[p.z], local_sem.at[1]))
    owns.append(pltpu.make_async_copy(mpack_ref, wm_ref.at[p.z], local_sem.at[2]))
    owns[1].start()
    owns[2].start()

    for c in sums:
        c.wait()
    total = part_ref[p.me] + extra_ref[...]
    for o in range(n - 1):
        total = total + held[o]
    mod_ref[p.me] = total
    sums = [
        remote(mod_ref.at[p.me], mod_ref.at[p.me], s2.at[o], r2.at[o], q)
        for o, q in enumerate(line)
    ]
    for c in sums:
        c.start()

    def part_of(w, chip):
        if w == 0:
            return lambda part, d: wa_ref.at[chip, d, :, pl.ds(part * half, half)]
        return lambda part, d: wm_ref.at[chip, part, d]

    spreads = {}
    for w in range(2):
        for o in p.far:
            zcopies[w, o].wait_recv()
            sems = (das, dar) if w == 0 else (dms, dmr)
            s = Spread(p, part_of(w, p.chip(-o)), sems[0].at[o], sems[1].at[o])
            s.begin()
            spreads[w, o] = s
        if w == 0:
            for i in range(len(steps)):
                for j, c, go, got, copy in moves:
                    if j == i:
                        pl.when(got)(copy.wait_recv)
                none = p.core < 0
                any_got = none
                for j, c, go, got, copy in moves:
                    if j == i:
                        any_got = any_got | got
                fill = pltpu.make_async_copy(zero, win_ref.at[i + 1, 0], local_sem.at[3])

                @pl.when(jnp.logical_not(any_got))
                def _():
                    fill.start()
                    fill.wait()

                twins.append(
                    remote(
                        win_ref.at[i + 1, 0],
                        win_ref.at[i + 1, 1],
                        cs.at[i + 1],
                        cr.at[i + 1],
                        p.twin(),
                    )
                )
                twins[-1].start()
    for level in range(bits_of(nd)):
        for w in range(2):
            for o in p.far:
                spreads[w, o].step(level)
    for s in spreads.values():
        s.end()
    for c in zcopies.values():
        c.wait_send()
    for c in twins + sums:
        c.wait()
    for j, c, go, got, copy in moves:
        pl.when(go)(copy.wait_send)
    for c in owns:
        c.wait()


def front(tokens, part, extra, apack, mpack, steps, nd):
    n, rows, cols = part.shape
    nz = n // CORES
    rounds = len(steps)
    dma = pltpu.SemaphoreType.DMA
    vmem = pl.BlockSpec(memory_space=pltpu.VMEM)
    anywhere = pl.BlockSpec(memory_space=pl.ANY)
    return pl.pallas_call(
        functools.partial(front_body, n, nd, steps),
        out_shape=[
            jax.ShapeDtypeStruct(part.shape, f32),
            jax.ShapeDtypeStruct((rounds + 1, CORES) + tokens.shape, bf16),
            jax.ShapeDtypeStruct((nz,) + apack.shape, bf16),
            jax.ShapeDtypeStruct((nz,) + mpack.shape, bf16),
        ],
        in_specs=[anywhere, vmem, vmem, anywhere, anywhere],
        out_specs=[vmem, anywhere, anywhere, anywhere],
        scratch_shapes=[
            pltpu.VMEM(tokens.shape, bf16),
            pltpu.VMEM((n - 1, rows, cols), f32),
            dma((n - 1,)),
            dma((n - 1,)),
            dma((n - 1,)),
            dma((n - 1,)),
            dma((rounds, CORES)),
            dma((rounds, CORES)),
            dma((rounds + 1,)),
            dma((rounds + 1,)),
            dma((2, nz)),
            dma((2, nz)),
            dma((4,)),
            dma((nz, 2, nd)),
            dma((nz, 2, nd)),
            dma((nz, 2, nd)),
            dma((nz, 2, nd)),
        ],
        compiler_params=pltpu.CompilerParams(
            collective_id=0, has_side_effects=True, vmem_limit_bytes=24 << 20
        ),
        name="front",
    )(tokens, part, extra, apack, mpack)


def picks_of(seg):
    return (seg == lax.broadcasted_iota(jnp.int32, (seg.shape[0], 8), 1)).astype(bf16)


def two(x):
    high = x.astype(bf16)
    return high, (x - high.astype(f32)).astype(bf16)


def per_token(picks, table):
    high, low = two(table)
    return dot(picks, high) + dot(picks, low)


def per_item(picks, values):
    high, low = two(values)
    return dot(picks, high, 0, 0) + dot(picks, low, 0, 0)


def norm_parts(values):
    centred = values - jnp.mean(values, axis=-1, keepdims=True)
    rstd = lax.rsqrt(jnp.mean(centred * centred, axis=-1, keepdims=True) + epsilon)
    return centred * rstd, rstd


def norm_back(normal, rstd, scaled):
    return rstd * (
        scaled
        - jnp.mean(scaled, axis=-1, keepdims=True)
        - normal * jnp.mean(scaled * normal, axis=-1, keepdims=True)
    )


GAMMA_ONE, GAMMA_TWO, SCALE_ONE, SCALE_TWO, SHIFT_ONE, SHIFT_TWO = range(6)


def qkv_body(nq, x_ref, seg_ref, mod_ref, w_ref, qb_ref, vb_ref, n_ref, q_ref, k_ref, v_ref):
    normal, _ = norm_parts(x_ref[...].astype(f32))
    picks = picks_of(seg_ref[...])
    scale = per_token(picks, mod_ref[SCALE_ONE])
    shift = per_token(picks, mod_ref[SHIFT_ONE])
    normed = (normal * (1.0 + scale) + shift).astype(bf16)
    n_ref[...] = normed
    for s in range(w_ref.shape[0]):
        kv = dot(normed, w_ref[s, LANES : 3 * LANES, :], 1, 1)
        k_ref[s] = kv[:, :LANES]
        v_ref[s] = (kv[:, LANES:] + vb_ref[s]).astype(bf16)

    @pl.when(pl.program_id(0) < nq)
    def _():
        for s in range(w_ref.shape[0]):
            q_ref[s] = dot(normed, w_ref[s, :LANES, :], 1, 1) + qb_ref[s]


def norm_qkv(window, seg, mod, weights, qbias, vbias, block):
    rows, pairs = window.shape[0], weights.shape[0]
    steps, nq = rows // block, CORES
    whole = lambda *shape: pl.BlockSpec(shape, lambda i: (0,) * len(shape))
    tile = lambda cols: pl.BlockSpec((block, cols), lambda i: (i, 0))
    slots = pl.BlockSpec((pairs, block, LANES), lambda i: (0, i, 0))
    return pl.pallas_call(
        functools.partial(qkv_body, nq),
        grid=(steps,),
        in_specs=[
            tile(D),
            tile(1),
            whole(6, 8, D),
            whole(*weights.shape),
            whole(pairs, 1, LANES),
            whole(pairs, 1, LANES),
        ],
        out_specs=[
            tile(D),
            pl.BlockSpec((pairs, block, LANES), lambda i: (0, jnp.minimum(i, nq - 1), 0)),
            slots,
            slots,
        ],
        out_shape=[
            jax.ShapeDtypeStruct((rows, D), bf16),
            jax.ShapeDtypeStruct((pairs, nq * block, LANES), f32),
            jax.ShapeDtypeStruct((pairs, rows, LANES), f32),
            jax.ShapeDtypeStruct((pairs, rows, LANES), bf16),
        ],
        compiler_params=pltpu.CompilerParams(vmem_limit_bytes=VMEM_LIMIT),
        name="norm_qkv",
    )(window, seg, mod, weights, qbias, vbias)


def half_lanes(rows):
    return lax.broadcasted_iota(jnp.int32, (rows, LANES), 1) < HEAD


def half_sums(x):
    low = half_lanes(x.shape[0])
    a = jnp.sum(jnp.where(low, x, 0.0), axis=1, keepdims=True)
    b = jnp.sum(jnp.where(low, 0.0, x), axis=1, keepdims=True)
    return jnp.where(low, a, b)


def one_half(x, h):
    low = half_lanes(x.shape[0])
    return jnp.where(low if h == 0 else jnp.logical_not(low), x, jnp.zeros_like(x))


def attend_body(
    block, nq, nk, need_ref, q_ref, k_ref, v_ref, ehs_ref, lo_ref, hi_ref, e_ref, o_ref, l_ref,
    ku, v0, v1, acc,
):
    k = k_ref[0]
    ku[...] = (k * lax.rsqrt(half_sums(k * k) + epsilon)).astype(bf16)
    v = v_ref[0]
    low = half_lanes(v.shape[0])
    one = jnp.ones_like(v)
    v0[...] = jnp.where(low, v, one)
    v1[...] = jnp.where(low, one, v)
    for qi in range(nq):
        rows = pl.ds(qi * block, block)
        q = q_ref[0, rows, :]
        qu = (q * lax.rsqrt(half_sums(q * q) + epsilon) * ehs_ref[0]).astype(bf16)
        qs = [one_half(qu, h) for h in range(2)]
        lo, hi = lo_ref[rows, :], hi_ref[rows, :]
        acc[...] = jnp.zeros_like(acc)
        for ki in range(nk):

            @pl.when(need_ref[qi * nk + ki] > 0)
            def _():
                cols = pl.ds(ki * block, block)
                e = e_ref[:, cols]
                allowed = (e >= lo) & (e <= hi)
                for h in range(2):
                    s = dot(qs[h], ku[cols, :], 1, 1)
                    p = jnp.where(allowed, jnp.exp(s), 0.0).astype(bf16)
                    acc[h] += dot(p, (v0 if h == 0 else v1)[cols, :])

        a, b = acc[0], acc[1]
        low = half_lanes(block)
        other = jnp.where(low, pltpu.roll(a, HEAD, 1), pltpu.roll(b, HEAD, 1))
        o_ref[0, rows, :] = (jnp.where(low, a, b) / other).astype(bf16)
        turned = other.T
        l_ref[0, 0:1, rows] = turned[0:1, :]
        l_ref[0, 1:2, rows] = turned[HEAD : HEAD + 1, :]


def attend(need, q, k, v, ehs, lo, hi, e_row, block):
    pairs, t, _ = q.shape
    w = k.shape[1]
    nq, nk = t // block, w // block
    slot = lambda rows: pl.BlockSpec((1, rows, LANES), lambda i, *_: (i, 0, 0))
    whole = lambda *shape: pl.BlockSpec(shape, lambda i, *_: (0,) * len(shape))
    return pl.pallas_call(
        functools.partial(attend_body, block, nq, nk),
        grid_spec=pltpu.PrefetchScalarGridSpec(
            num_scalar_prefetch=1,
            grid=(pairs,),
            in_specs=[slot(t), slot(w), slot(w), slot(1), whole(t, 1), whole(t, 1), whole(1, w)],
            out_specs=[slot(t), pl.BlockSpec((1, 8, t), lambda i, *_: (i, 0, 0))],
            scratch_shapes=[
                pltpu.VMEM((w, LANES), bf16),
                pltpu.VMEM((w, LANES), bf16),
                pltpu.VMEM((w, LANES), bf16),
                pltpu.VMEM((2, block, LANES), f32),
            ],
        ),
        out_shape=[
            jax.ShapeDtypeStruct((pairs, t, LANES), bf16),
            jax.ShapeDtypeStruct((pairs, 8, t), f32),
        ],
        compiler_params=pltpu.CompilerParams(vmem_limit_bytes=VMEM_LIMIT),
        name="attend",
    )(need, q, k, v, ehs, lo, hi, e_row)


def back_body(
    block, nq, nk, need_ref, q_ref, k_ref, v_ref, g_ref, o_ref, l_ref, ehs_ref, lo_ref, hi_ref,
    e_ref, n_ref, a_ref, w_ref, dw_ref, gn_ref, sums_ref, ku, dk, dv, dq, gqs, gkv,
):
    t = nq * block
    k = k_ref[0]
    rk = lax.rsqrt(half_sums(k * k) + epsilon)
    ku[...] = (k * rk).astype(bf16)
    dk[...] = jnp.zeros_like(dk)
    dv[...] = jnp.zeros_like(dv)
    ehs = ehs_ref[0]
    qsum = jnp.zeros((1, LANES), f32)
    hsum = jnp.zeros((1, LANES), f32)
    for qi in range(nq):
        rows = pl.ds(qi * block, block)
        q = q_ref[0, rows, :]
        rq = lax.rsqrt(half_sums(q * q) + epsilon)
        qhat = q * rq
        qu = (qhat * ehs).astype(bf16)
        qs = [one_half(qu, h) for h in range(2)]
        g = g_ref[0, rows, :]
        gs = [one_half(g, h) for h in range(2)]
        turned = (g.astype(f32) * o_ref[0, rows, :].astype(f32)).T
        deltas = [
            jnp.sum(turned[:HEAD], axis=0, keepdims=True),
            jnp.sum(turned[HEAD:], axis=0, keepdims=True),
        ]
        invs = [1.0 / l_ref[0, h : h + 1, rows] for h in range(2)]
        lo, hi = lo_ref[:, rows], hi_ref[:, rows]
        dq[...] = jnp.zeros_like(dq)
        for ki in range(nk):

            @pl.when(need_ref[qi * nk + ki] > 0)
            def _():
                cols = pl.ds(ki * block, block)
                e = e_ref[cols, :]
                allowed = (e >= lo) & (e <= hi)
                kb, vb = ku[cols, :], v_ref[0, cols, :]
                for h in range(2):
                    s = dot(kb, qs[h], 1, 1)
                    p = jnp.where(allowed, jnp.exp(s) * invs[h], 0.0)
                    dp = dot(vb, gs[h], 1, 1)
                    ds = (p * (dp - deltas[h])).astype(bf16)
                    dv[cols, :] += dot(p.astype(bf16), gs[h])
                    dk[cols, :] += dot(ds, qs[h])
                    dq[...] += dot(ds, one_half(kb, h), 0, 0)

        d = dq[...]
        hsum = hsum + jnp.sum(d * qhat * ehs, axis=0, keepdims=True)
        gq = (ehs * rq * (d - qhat * half_sums(qhat * d))).astype(bf16)
        gqs[rows, :] = gq
        qsum = qsum + jnp.sum(gq.astype(f32), axis=0, keepdims=True)
    khat = k * rk
    d = dk[...]
    gkv[:, :LANES] = (rk * (d - khat * half_sums(khat * d))).astype(bf16)
    gv = dv[...].astype(bf16)
    gkv[:, LANES:] = gv
    sums_ref[...] = jnp.zeros_like(sums_ref)
    sums_ref[0, 0:1, :] = qsum
    sums_ref[0, 1:2, :] = jnp.sum(gv.astype(f32), axis=0, keepdims=True)
    sums_ref[0, 2:3, :] = hsum
    dw_ref[0, :LANES, :] = dot(gqs[...], n_ref[:t, :], 0, 0).astype(bf16)
    dw_ref[0, LANES : 3 * LANES, :] = dot(gkv[...], n_ref[...], 0, 0).astype(bf16)
    dw_ref[0, 3 * LANES :, :] = dot(o_ref[0], a_ref[...], 0, 0).astype(bf16)

    @pl.when(pl.program_id(0) == 0)
    def _():
        gn_ref[...] = jnp.zeros_like(gn_ref)

    gn_ref[...] += dot(gkv[...], w_ref[0, LANES : 3 * LANES, :])
    gn_ref[:t, :] += dot(gqs[...], w_ref[0, :LANES, :])


def attend_back(need, q, k, v, g, o, l, ehs, lo_row, hi_row, e_col, normed, wide, weights, block):
    pairs, t, _ = q.shape
    w = k.shape[1]
    nq, nk = t // block, w // block
    slot = lambda rows: pl.BlockSpec((1, rows, LANES), lambda i, *_: (i, 0, 0))
    whole = lambda *shape: pl.BlockSpec(shape, lambda i, *_: (0,) * len(shape))
    return pl.pallas_call(
        functools.partial(back_body, block, nq, nk),
        grid_spec=pltpu.PrefetchScalarGridSpec(
            num_scalar_prefetch=1,
            grid=(pairs,),
            in_specs=[
                slot(t),
                slot(w),
                slot(w),
                slot(t),
                slot(t),
                pl.BlockSpec((1, 8, t), lambda i, *_: (i, 0, 0)),
                slot(1),
                whole(1, t),
                whole(1, t),
                whole(w, 1),
                whole(w, D),
                whole(t, D),
                pl.BlockSpec((1, 4 * LANES, D), lambda i, *_: (i, 0, 0)),
            ],
            out_specs=[
                pl.BlockSpec((1, 4 * LANES, D), lambda i, *_: (i, 0, 0)),
                whole(w, D),
                slot(8),
            ],
            scratch_shapes=[
                pltpu.VMEM((w, LANES), bf16),
                pltpu.VMEM((w, LANES), f32),
                pltpu.VMEM((w, LANES), f32),
                pltpu.VMEM((block, LANES), f32),
                pltpu.VMEM((t, LANES), bf16),
                pltpu.VMEM((w, 2 * LANES), bf16),
            ],
        ),
        out_shape=[
            jax.ShapeDtypeStruct((pairs, 4 * LANES, D), bf16),
            jax.ShapeDtypeStruct((w, D), f32),
            jax.ShapeDtypeStruct((pairs, 8, LANES), f32),
        ],
        compiler_params=pltpu.CompilerParams(vmem_limit_bytes=VMEM_LIMIT),
        name="attend_back",
    )(need, q, k, v, g, o, l, ehs, lo_row, hi_row, e_col, normed, wide, weights)


def middle_body(
    n, nd, o_ref, w_ref, x_ref, g_ref, seg_ref, mod_ref, pb_ref,
    branch_ref, resid_ref, nwide_ref, gwide_ref, theirs, got, send, recv,
):
    p = Place(n, nd)
    tok = x_ref.shape[0]
    greet([p.twin()])
    picks = picks_of(seg_ref[...])
    gwide_ref[0] = (per_token(picks, mod_ref[GAMMA_TWO]) * g_ref[...].astype(f32)).astype(bf16)
    copies = [remote(gwide_ref.at[0], gwide_ref.at[1], send.at[0], recv.at[0], p.twin())]
    copies[0].start()

    def project(rows):
        total = dot(o_ref[0, rows, :], w_ref[0, 3 * LANES :, :])
        for s in range(1, o_ref.shape[0]):
            total += dot(o_ref[s, rows, :], w_ref[s, 3 * LANES :, :])
        return total

    theirs[...] = project(pl.ds(tok, tok)).astype(bf16)
    copies.append(remote(theirs, got, send.at[1], recv.at[1], p.twin()))
    copies[1].start()
    mine = project(pl.ds(0, tok)) + pb_ref[...]
    copies[1].wait()
    branch = mine + got[...].astype(f32)
    branch_ref[...] = branch
    resid = x_ref[...].astype(f32) + per_token(picks, mod_ref[GAMMA_ONE]) * branch
    resid_ref[...] = resid
    normal, _ = norm_parts(resid)
    scale = per_token(picks, mod_ref[SCALE_TWO])
    shift = per_token(picks, mod_ref[SHIFT_TWO])
    nwide_ref[0] = (normal * (1.0 + scale) + shift).astype(bf16)
    copies.append(remote(nwide_ref.at[0], nwide_ref.at[1], send.at[2], recv.at[2], p.twin()))
    copies[2].start()
    copies[0].wait()
    copies[2].wait()


def middle(heads_out, weights, tokens, out_grad, seg, mod, proj_bias, n, nd):
    tok = tokens.shape[0]
    dma = pltpu.SemaphoreType.DMA
    vmem = pl.BlockSpec(memory_space=pltpu.VMEM)
    return pl.pallas_call(
        functools.partial(middle_body, n, nd),
        out_shape=[
            jax.ShapeDtypeStruct((tok, D), f32),
            jax.ShapeDtypeStruct((tok, D), f32),
            jax.ShapeDtypeStruct((CORES, tok, D), bf16),
            jax.ShapeDtypeStruct((CORES, tok, D), bf16),
        ],
        in_specs=[vmem] * 7,
        out_specs=[vmem] * 4,
        scratch_shapes=[
            pltpu.VMEM((tok, D), bf16),
            pltpu.VMEM((tok, D), bf16),
            dma((3,)),
            dma((3,)),
        ],
        compiler_params=pltpu.CompilerParams(
            collective_id=1, has_side_effects=True, vmem_limit_bytes=40 << 20
        ),
        name="middle",
    )(heads_out, weights, tokens, out_grad, seg, mod, proj_bias)


def turn_body(
    n, nd, gx_ref, mlp_ref, resid_ref, branch_ref, g_ref, seg_ref, mod_ref, db_ref, w_ref, gw_ref,
    mid_ref, wide_ref, hg_ref, out_ref, items_ref, sums_ref, theirs, got, send, recv,
):
    p = Place(n, nd)
    tok = g_ref.shape[0]
    greet([p.twin()])
    theirs[0] = gx_ref[pl.ds(tok, tok), :].astype(bf16)
    theirs[1] = mlp_ref[pl.ds(tok, tok), :].astype(bf16)
    copies = [remote(theirs.at[i], got.at[i], send.at[i], recv.at[i], p.twin()) for i in range(2)]
    for c in copies:
        c.start()
    picks = picks_of(seg_ref[...])
    normal, rstd = norm_parts(resid_ref[...])
    scale = per_token(picks, mod_ref[SCALE_TWO])
    grad_final = g_ref[...].astype(f32)
    copies[0].wait()
    second = gx_ref[pl.ds(0, tok), :] + got[0].astype(f32)
    mid = grad_final + norm_back(normal, rstd, second * (1.0 + scale))
    mid_ref[...] = mid
    attn = (per_token(picks, mod_ref[GAMMA_ONE]) * mid).astype(bf16)
    wide_ref[0] = attn
    copies.append(remote(wide_ref.at[0], wide_ref.at[1], send.at[2], recv.at[2], p.twin()))
    copies[2].start()
    copies[1].wait()
    branch = mlp_ref[pl.ds(0, tok), :] + got[1].astype(f32) + db_ref[...]
    gamma = per_token(picks, mod_ref[GAMMA_TWO])
    out_ref[...] = (resid_ref[...] + gamma * branch).astype(bf16)
    items_ref[0] = per_item(picks, mid * branch_ref[...])
    items_ref[1] = per_item(picks, grad_final * branch)
    items_ref[2] = per_item(picks, second * normal)
    items_ref[3] = per_item(picks, second)
    sums_ref[...] = jnp.zeros_like(sums_ref)
    sums_ref[0:1, :] = jnp.sum(attn.astype(f32), axis=0, keepdims=True)
    sums_ref[1:2, :] = jnp.sum(gw_ref[0].astype(f32), axis=0, keepdims=True)
    copies[2].wait()
    for s in range(w_ref.shape[0]):
        for c in range(CORES):
            hg_ref[s, pl.ds(c * tok, tok), :] = dot(
                wide_ref[c], w_ref[s, 3 * LANES :, :], 1, 1
            ).astype(bf16)


def turn(gx, mlp_part, resid, branch, out_grad, seg, mod, down_bias, weights, gwide, n, nd):
    tok = out_grad.shape[0]
    pairs = weights.shape[0]
    dma = pltpu.SemaphoreType.DMA
    vmem = pl.BlockSpec(memory_space=pltpu.VMEM)
    return pl.pallas_call(
        functools.partial(turn_body, n, nd),
        out_shape=[
            jax.ShapeDtypeStruct((tok, D), f32),
            jax.ShapeDtypeStruct((CORES, tok, D), bf16),
            jax.ShapeDtypeStruct((pairs, CORES * tok, LANES), bf16),
            jax.ShapeDtypeStruct((tok, D), bf16),
            jax.ShapeDtypeStruct((4, 8, D), f32),
            jax.ShapeDtypeStruct((8, D), f32),
        ],
        in_specs=[vmem] * 10,
        out_specs=[vmem] * 6,
        scratch_shapes=[
            pltpu.VMEM((2, tok, D), bf16),
            pltpu.VMEM((2, tok, D), bf16),
            dma((3,)),
            dma((3,)),
        ],
        compiler_params=pltpu.CompilerParams(
            collective_id=2, has_side_effects=True, vmem_limit_bytes=48 << 20
        ),
        name="turn",
    )(gx, mlp_part, resid, branch, out_grad, seg, mod, down_bias, weights, gwide)


def mlp_body(x_ref, g_ref, w_ref, bias_ref, mlp_ref, gx_ref, dw_ref, dbias_ref):
    x, g = x_ref[...], g_ref[...]
    units = w_ref.shape[2] * w_ref.shape[3]
    up = w_ref[0, 0].reshape(units, D)
    down = w_ref[0, 1].reshape(units, D)
    pre = dot(x, up, 1, 1) + bias_ref[0]
    square = pre * pre
    th = jnp.tanh(0.7978845608028654 * pre * (1.0 + 0.044715 * square))
    half = 0.5 * (1.0 + th)
    hidden = (pre * half).astype(bf16)
    slope = half + 0.5 * pre * (1.0 - th * th) * (
        0.7978845608028654 * (1.0 + 3.0 * 0.044715 * square)
    )
    gp = (dot(g, down, 1, 1) * slope).astype(bf16)

    @pl.when(pl.program_id(0) == 0)
    def _():
        mlp_ref[...] = jnp.zeros_like(mlp_ref)
        gx_ref[...] = jnp.zeros_like(gx_ref)

    mlp_ref[...] += dot(hidden, down)
    gx_ref[...] += dot(gp, up)
    dw_ref[0, 0] = dot(gp, x, 0, 0).astype(bf16).reshape(dw_ref.shape[2:])
    dw_ref[0, 1] = dot(hidden, g, 0, 0).astype(bf16).reshape(dw_ref.shape[2:])
    dbias_ref[0] = jnp.sum(gp.astype(f32), axis=0, keepdims=True)


def mlp(x, g, weights, bias):
    t = x.shape[0]
    nz, _, nd, piece, _ = weights.shape
    count = min(nd, max(1, 256 // piece))
    per = nd // count
    steps, units = nz * per, count * piece
    whole = lambda *shape: pl.BlockSpec(shape, lambda i: (0,) * len(shape))
    block = pl.BlockSpec((1, 2, count, piece, D), lambda i: (i // per, 0, i % per, 0, 0))
    row = pl.BlockSpec((1, 1, units), lambda i: (i, 0, 0))
    return pl.pallas_call(
        mlp_body,
        grid=(steps,),
        in_specs=[whole(t, D), whole(t, D), block, row],
        out_specs=[whole(t, D), whole(t, D), block, row],
        out_shape=[
            jax.ShapeDtypeStruct((t, D), f32),
            jax.ShapeDtypeStruct((t, D), f32),
            jax.ShapeDtypeStruct(weights.shape, bf16),
            jax.ShapeDtypeStruct((steps, 1, units), f32),
        ],
        compiler_params=pltpu.CompilerParams(vmem_limit_bytes=VMEM_LIMIT),
        name="mlp",
    )(x, g, weights, bias.reshape(steps, 1, units))


class Reduce:
    def __init__(self, place, first, stage, zstage, out, sems):
        self.p, self.first, self.stage, self.zstage, self.out = place, first, stage, zstage, out
        self.ps, self.pr, self.zs, self.zr, self.os, self.or_ = sems
        self.copies, self.all = {}, []

    def held(self, part, level):
        rels = list(range(self.p.nd))
        for bit in self.p.orders[part][:level]:
            rels = [r for r in rels if not (r >> bit) & 1]
        return rels

    def current(self, part, level, chip, rel):
        if level == 0:
            return self.first(part, chip, self.p.dp ^ rel)
        return self.stage(part, level - 1, chip, self.held(part, level).index(rel))

    def send_plane(self, level, o):
        p = self.p
        chip = p.chip(o)
        for part, order in enumerate(p.orders):
            bit = order[level]
            for rel in self.held(part, level):
                if (rel >> bit) & 1:
                    slot = self.held(part, level + 1).index(rel ^ (1 << bit))
                    c = remote(
                        self.current(part, level, chip, rel),
                        self.stage(part, level, chip, slot),
                        self.ps.at[part, level, o, slot],
                        self.pr.at[part, level, o, slot],
                        p.flip(bit),
                    )
                    c.start()
                    self.copies[part, level, o, slot] = c
                    self.all.append(c)

    def add_plane(self, level, o):
        p = self.p
        chip = p.chip(o)
        for part in range(2):
            for slot, rel in enumerate(self.held(part, level + 1)):
                self.copies[part, level, o, slot].wait_recv()
                room = self.stage(part, level, chip, slot)
                mine = self.current(part, level, chip, rel)
                room[...] = (room[...].astype(f32) + mine[...].astype(f32)).astype(bf16)

    def send_line(self, o):
        p = self.p
        m = bits_of(p.nd)
        for part in range(2):
            c = remote(
                self.stage(part, m - 1, p.chip(o), 0),
                self.zstage(part, o),
                self.zs.at[part, o],
                self.zr.at[part, o],
                p.on_chip(o),
            )
            c.start()
            self.copies["z", part, o] = c
            self.all.append(c)

    def end_line(self):
        p = self.p
        m = bits_of(p.nd)
        for part in range(2):
            total = self.stage(part, m - 1, p.z, 0)[...].astype(f32)
            for o in p.far:
                self.copies["z", part, o].wait_recv()
                total = total + self.zstage(part, o)[...].astype(f32)
            self.out(part, p.dp)[...] = total.astype(bf16)
        self.back = Spread(p, self.out, self.os, self.or_)
        self.back.begin()

    def end(self):
        for c in self.all:
            c.wait_send()
        self.back.end()


def finish_body(
    n, nd, steps, dm_ref, da_ref, gn_ref, x_ref, mid_ref, seg_ref, mod_ref, part_ref, extra_ref,
    ym_ref, ya_ref, tg_ref, small_ref,
    mstage, astage, mz, az, gswap, gmine, ghalo, part, held,
    mps, mpr, mzs, mzr, mos, mor, aps, apr, azs, azr, aos, aor,
    gs, gr, hs, hr, s1, r1, s2, r2, s3, r3, s4, r4,
):
    p = Place(n, nd)
    nz, tok = p.nz, x_ref.shape[0]
    rounds = len(steps)
    half = D // 2
    m = bits_of(nd)
    p.greet_all()

    def room(buffer, narrow):
        def at(p_, level, chip, slot):
            base = sum(nd >> (i + 1) for i in range(level))
            return buffer.at[p_, base + slot, chip]

        return at

    cut = lambda part_: pl.ds(part_ * half, half)
    rm = Reduce(
        p,
        lambda q, chip, d: dm_ref.at[chip, q, d],
        room(mstage, False),
        lambda q, o: mz.at[q, o],
        lambda q, d: ym_ref.at[q, d],
        (mps, mpr, mzs, mzr, mos, mor),
    )
    ra = Reduce(
        p,
        lambda q, chip, d: da_ref.at[chip, d, :, cut(q)],
        room(astage, True),
        lambda q, o: az.at[q, o],
        lambda q, d: ya_ref.at[d, :, cut(q)],
        (aps, apr, azs, azr, aos, aor),
    )
    far = p.far + [0]
    gcopies = []
    for i in range(rounds + 1):
        gswap[i] = gn_ref[i, 1].astype(bf16)
        c = remote(gswap.at[i], gmine.at[i], gs.at[i], gr.at[i], p.twin())
        c.start()
        gcopies.append(c)
    for o in far:
        rm.send_plane(0, o)
    moves = []
    for i, per_core in enumerate(steps):
        gcopies[i + 1].wait()
        gmine[i + 1] = (gn_ref[i + 1, 0] + gmine[i + 1].astype(f32)).astype(bf16)
        for c, step in enumerate(per_core):
            if step is None:
                continue
            go = (p.core == c) & (p.z - step >= 0) & (p.z - step < nz)
            got = (p.core == c) & (p.z + step >= 0) & (p.z + step < nz)
            copy = remote(gmine.at[i + 1], ghalo.at[i], hs.at[i, c], hr.at[i, c], p.on_chip(-step))
            pl.when(go)(copy.start)
            moves.append((i, go, got, copy))
    gcopies[0].wait()
    first = gn_ref[0, 0] + gmine[0].astype(f32)
    tg_ref[...] = first
    for i, go, got, copy in moves:

        @pl.when(got)
        def _():
            copy.wait_recv()
            tg_ref[...] += ghalo[i].astype(f32)

    first = tg_ref[...]
    picks = picks_of(seg_ref[...])
    normal, rstd = norm_parts(x_ref[...].astype(f32))
    scale = per_token(picks, mod_ref[SCALE_ONE])
    tg_ref[...] = mid_ref[...] + norm_back(normal, rstd, first * (1.0 + scale))
    part[...] = part_ref[...]
    chunk = 6 * D // n
    for which, values in ((SCALE_ONE, first * normal), (SHIFT_ONE, first)):
        items = per_item(picks, values)
        begin, end = which * D, (which + 1) * D
        for j in range(n):
            a, b = max(begin, j * chunk), min(end, (j + 1) * chunk)
            if a < b:
                part[j, :, a - j * chunk : b - j * chunk] += items[:, a - begin : b - begin]
    line = p.line()
    sums = [remote(part.at[q[1]], held.at[o], s1.at[o], r1.at[o], q) for o, q in enumerate(line)]
    for c in sums:
        c.start()

    def advance(r, level):
        for o in far:
            r.add_plane(level, o)
            if level + 1 < m:
                r.send_plane(level + 1, o)
            elif o:
                r.send_line(o)

    advance(rm, 0)
    for o in far:
        ra.send_plane(0, o)
    for c in sums:
        c.wait()
    total = part[p.me] + extra_ref[...]
    for o in range(n - 1):
        total = total + held[o]
    small_ref[p.core, p.z, p.dp] = total
    mine = small_ref.at[p.core, p.z, p.dp]
    plane = [(lax.rem(p.dp + o, nd), p.me) for o in range(1, nd)]
    sums = [remote(mine, mine, s2.at[o], r2.at[o], q) for o, q in enumerate(plane)]
    for c in sums:
        c.start()
    for level in range(1, m):
        advance(rm, level)
    for c in sums:
        c.wait()
    mine = small_ref.at[p.core, p.z]
    sums = [remote(mine, mine, s3.at[o], r3.at[o], p.on_chip(o)) for o in p.far]
    for c in sums:
        c.start()
    advance(ra, 0)
    rm.end_line()
    for level in range(1, m):
        advance(ra, level)
    for c in sums:
        c.wait()
    mine = small_ref.at[p.core]
    last = remote(mine, mine, s4, r4, p.twin())
    last.start()
    ra.end_line()
    for level in range(m):
        rm.back.step(level)
        ra.back.step(level)
    last.wait()
    rm.end()
    ra.end()
    for i, go, got, copy in moves:
        pl.when(go)(copy.wait_send)


def finish(dm, da, gn, tokens, mid, seg, mod, part, extra, steps, nd):
    n, rows, cols = part.shape
    nz = n // CORES
    tok = tokens.shape[0]
    rounds = len(steps)
    piece, arows = dm.shape[3], da.shape[2]
    dma = pltpu.SemaphoreType.DMA
    vmem = pl.BlockSpec(memory_space=pltpu.VMEM)
    m = bits_of(nd)
    levels = max(1, nd // 2)
    plane = (2, m, nz, levels)
    wide = lambda: [
        dma(plane),
        dma(plane),
        dma((2, nz)),
        dma((2, nz)),
        dma((2, nd)),
        dma((2, nd)),
    ]
    return pl.pallas_call(
        functools.partial(finish_body, n, nd, steps),
        out_shape=[
            jax.ShapeDtypeStruct(dm.shape[1:], bf16),
            jax.ShapeDtypeStruct(da.shape[1:], bf16),
            jax.ShapeDtypeStruct((tok, D), f32),
            jax.ShapeDtypeStruct((CORES, nz, nd, rows, cols), f32),
        ],
        in_specs=[vmem] * 9,
        out_specs=[vmem] * 4,
        scratch_shapes=[
            pltpu.VMEM((2, nd - 1, nz, piece, D), bf16),
            pltpu.VMEM((2, nd - 1, nz, arows, D // 2), bf16),
            pltpu.VMEM((2, nz, piece, D), bf16),
            pltpu.VMEM((2, nz, arows, D // 2), bf16),
            pltpu.VMEM((rounds + 1, tok, D), bf16),
            pltpu.VMEM((rounds + 1, tok, D), bf16),
            pltpu.VMEM((rounds, tok, D), bf16),
            pltpu.VMEM((n, rows, cols), f32),
            pltpu.VMEM((n - 1, rows, cols), f32),
        ]
        + wide()
        + wide()
        + [
            dma((rounds + 1,)),
            dma((rounds + 1,)),
            dma((rounds, CORES)),
            dma((rounds, CORES)),
            dma((n - 1,)),
            dma((n - 1,)),
            dma((nd - 1,)),
            dma((nd - 1,)),
            dma((nz,)),
            dma((nz,)),
            dma,
            dma,
        ],
        compiler_params=pltpu.CompilerParams(
            collective_id=3, has_side_effects=True, vmem_limit_bytes=VMEM_LIMIT
        ),
        name="finish",
    )(dm, da, gn, tokens, mid, seg, mod, part, extra)


def local(
    nd,
    nt,
    tokens,
    class_embed,
    item_lengths,
    token_codes,
    ada_weight,
    ada_bias,
    qkv_weight,
    query_bias,
    value_bias,
    head_scale,
    proj_weight,
    proj_bias,
    up_weight,
    up_bias,
    down_weight,
    down_bias,
    out_grad,
):
    d, t = lax.axis_index("dp"), lax.axis_index("tensor")
    nz = nt // CORES
    z, core = t // CORES, t % CORES
    tok = tokens.shape[0]
    heads = head_scale.shape[0]
    width = heads * HEAD
    wide = nz * width
    pairs = wide // LANES
    units = up_weight.shape[1]
    feat = class_embed.shape[2]

    per_chip = CORES * tok
    seen = [[], []]
    for c in range(CORES):
        for step in range(1, nz):
            if step * per_chip - c * tok - tok < BEHIND:
                seen[c].append(step)
        for step in range(1, nz):
            if (step - 1) * per_chip + c * tok < AHEAD:
                seen[c].append(-step)
    rounds = max(len(s) for s in seen)
    steps = [
        tuple(s[len(s) - 1 - i] if i < len(s) else None for s in seen) for i in range(rounds)
    ]

    chunk = ada_weight.shape[1] // nt
    cond_act = jax.nn.silu(class_embed[0]).astype(bf16)
    ada_part = jnp.dot(cond_act, ada_weight, preferred_element_type=f32)
    part = jnp.pad(ada_part.reshape(SEGS, nt, chunk).transpose(1, 0, 2), ((0, 0), (0, 2), (0, 0)))
    bias_row = jnp.concatenate(
        [query_bias, value_bias, head_scale, jnp.zeros((chunk - 2 * width - heads,), f32)]
    )
    extra = jnp.pad(bias_row[None], ((SEGS, 7 - SEGS), (0, 0)))
    apack = jnp.concatenate(
        [qkv_weight.transpose(1, 2, 0).reshape(3 * width, D), proj_weight], axis=0
    ).reshape(nd, 4 * width // nd, D)
    mpack = jnp.stack([up_weight.T, down_weight]).reshape(2, nd, units // nd, D)
    summed, window, wattn, wmlp = front(tokens, part, extra, apack, mpack, steps, nd)

    segment, scale_ids = item_layout(item_lengths[0])
    rank = segment * 16 + scale_ids
    owners = []
    for s in [(0, 0)] + steps:
        for flip in range(CORES):
            c = core ^ flip
            step = jnp.where(c == 0, nz if s[0] is None else s[0], nz if s[1] is None else s[1])
            chip = z - step
            owners.append(jnp.where((chip >= 0) & (chip < nz), chip * CORES + c, -1))
    blocks = len(owners)
    seg_blocks, rank_blocks = segment.reshape(nt, tok), rank.reshape(nt, tok)
    take = lambda a, o: lax.dynamic_index_in_dim(a, jnp.maximum(o, 0), 0, keepdims=False)
    seg_win = jnp.concatenate([take(seg_blocks, o) for o in owners])
    e_win = jnp.concatenate([jnp.where(o >= 0, take(rank_blocks, o), -1) for o in owners])
    lo = seg_win[: CORES * tok] * 16
    hi = e_win[: CORES * tok]
    e_blocks = e_win.reshape(blocks, tok)
    e_max, e_min = jnp.max(e_blocks, axis=1), jnp.min(e_blocks, axis=1)
    need = (
        (e_max[None, :] >= jnp.min(lo.reshape(CORES, tok), axis=1)[:, None])
        & (e_min[None, :] <= jnp.max(hi.reshape(CORES, tok), axis=1)[:, None])
        & (e_max[None, :] >= 0)
    ).astype(jnp.int32).reshape(CORES * blocks)
    seg_own = seg_win[:tok, None]

    modulation = summed[:, :SEGS].transpose(1, 0, 2).reshape(SEGS, 6, D) + ada_bias.reshape(6, D)
    mod = jnp.pad(modulation.transpose(1, 0, 2), ((0, 0), (0, 2), (0, 0)))
    biases = lax.dynamic_index_in_dim(
        summed[:, SEGS].reshape(nz, CORES, chunk), core, 1, keepdims=False
    )
    qbias = biases[:, :width].reshape(pairs, 1, LANES)
    vbias = biases[:, width : 2 * width].reshape(pairs, 1, LANES)
    exp_scale = jnp.exp(biases[:, 2 * width : 2 * width + heads]).reshape(nz * heads, 1)
    ehs = jnp.broadcast_to(exp_scale, (nz * heads, HEAD)).reshape(pairs, 1, LANES)
    merge = nz // pairs
    weights = (
        wattn.reshape(pairs, merge, 4, width, D)
        .transpose(0, 2, 1, 3, 4)
        .reshape(pairs, 4 * LANES, D)
    )

    window = window.reshape(blocks * tok, D)
    normed, q_raw, k_raw, v_in = norm_qkv(
        window, seg_win[:, None], mod, weights, qbias, vbias, tok
    )
    heads_out, weight_sums = attend(
        need, q_raw, k_raw, v_in, ehs, lo[:, None], hi[:, None], e_win[None, :], tok
    )
    branch, resid, nwide, gwide = middle(
        heads_out, weights, tokens, out_grad, seg_own, mod, proj_bias[None], nt, nd
    )
    up_own = lax.dynamic_index_in_dim(
        up_bias.reshape(nz, CORES, units), core, 1, keepdims=False
    )
    mlp_part, gx_part, dmlp, dbias = mlp(
        nwide.reshape(CORES * tok, D), gwide.reshape(CORES * tok, D), wmlp, up_own
    )
    mid, awide, heads_grad, layer_out, items, sums = turn(
        gx_part, mlp_part, resid, branch, out_grad, seg_own, mod, down_bias[None], weights,
        gwide, nt, nd,
    )
    dattn, gn, head_sums = attend_back(
        need, q_raw, k_raw, v_in, heads_grad, heads_out, weight_sums, ehs, lo[None, :],
        hi[None, :], e_win[:, None], normed, awide.reshape(CORES * tok, D), weights, tok,
    )

    low_codes = 64
    hot = lambda v, k: (v[:, None] == jnp.arange(k, dtype=jnp.int32)[None, :]).astype(bf16)
    hist = dot(
        hot(token_codes // low_codes, NBINS // low_codes),
        hot(token_codes % low_codes, low_codes),
        0,
        0,
    ).reshape(NBINS)
    row_six = jnp.concatenate([sums[0], sums[1], hist])
    to_all = lambda v: jnp.where(
        (jnp.arange(CORES) == core)[None, :, None], v[:, None, :], 0.0
    ).reshape(-1)
    row_seven = jnp.concatenate(
        [
            to_all(dbias.reshape(nz, units)),
            to_all(head_sums[:, 0].reshape(nz, width)),
            to_all(head_sums[:, 1].reshape(nz, width)),
        ]
    )
    hs_part = to_all(jnp.sum(head_sums[:, 2].reshape(nz, heads, HEAD), axis=2)).reshape(nt, heads)
    none = jnp.zeros((SEGS, D), f32)
    mod_part = jnp.concatenate(
        [items[0, :SEGS], items[1, :SEGS], none, items[2, :SEGS], none, items[3, :SEGS]], axis=1
    )
    payload = jnp.concatenate([mod_part, row_six[None], row_seven[None]], axis=0)
    payload = payload.reshape(8, nt, chunk).transpose(1, 0, 2)
    tail = jnp.pad(hs_part[:, None, :], ((0, 0), (7, 0), (0, LANES - heads)))
    own_tail = jnp.pad(
        cond_act.astype(f32), ((0, 8 - SEGS), (chunk, LANES - feat))
    )
    dattn = (
        dattn.reshape(pairs, 4, merge, width, D)
        .transpose(0, 2, 1, 3, 4)
        .reshape(nz, nd, 4 * width // nd, D)
    )
    ymlp, yattn, tokens_grad, small = finish(
        dmlp,
        dattn,
        gn.reshape(rounds + 1, CORES, tok, D),
        tokens,
        mid,
        seg_own,
        mod,
        jnp.concatenate([payload, tail], axis=2),
        own_tail,
        steps,
        nd,
    )

    rows_all = small[..., :chunk].transpose(2, 3, 1, 0, 4).reshape(nd, 8, 6 * D)
    mod_all = rows_all[:, :SEGS].reshape(nd * SEGS, 6 * D)
    mod_own = lax.dynamic_index_in_dim(rows_all, d, 0, keepdims=False)[:SEGS]
    bias_sums = jnp.sum(rows_all[:, SEGS:], axis=0)
    own_small = lax.dynamic_index_in_dim(small, core, 0, keepdims=False)
    own_small = lax.dynamic_index_in_dim(own_small, z, 0, keepdims=False)
    cond_all = own_small[:, :SEGS, chunk : chunk + feat].reshape(nd * SEGS, feat)
    hscale_grad = jnp.sum(own_small[:, 7, chunk : chunk + heads], axis=0)
    adaw_grad = dot(cond_all, mod_all, 0, 0, highest)
    adab_grad = jnp.sum(mod_all, axis=0)
    cond_grad = dot(mod_own, ada_weight.astype(f32), 1, 1, highest)
    embed_grad = jax.vjp(jax.nn.silu, class_embed)[1](cond_grad[None])[0]
    projb_grad, downb_grad = bias_sums[0, :D], bias_sums[0, D : 2 * D]
    code_hist = bias_sums[0, 2 * D :]
    at = lambda base, k: lax.dynamic_slice_in_dim(bias_sums[1], base + t * k, k, 0)
    upb_grad = at(0, units)
    qbias_grad = at(nt * units, width)
    vbias_grad = at(nt * (units + width), width)
    yattn = yattn.reshape(4 * width, D)
    qkvw_grad = yattn[: 3 * width].astype(f32).reshape(3, width, D).transpose(2, 0, 1)
    projw_grad = yattn[3 * width :].astype(f32)
    upw_grad = ymlp[0].reshape(units, D).astype(f32).T
    downw_grad = ymlp[1].reshape(units, D).astype(f32)
    return (
        layer_out,
        tokens_grad,
        embed_grad,
        adaw_grad,
        adab_grad,
        qkvw_grad,
        qbias_grad,
        vbias_grad,
        hscale_grad,
        projw_grad,
        projb_grad,
        upw_grad,
        upb_grad,
        downw_grad,
        downb_grad,
        code_hist,
    )


def solution(mesh):
    placed = (
        P(("dp", "tensor"), None),
        P("dp", None, "tensor"),
        P("dp", None),
        P(("dp", "tensor")),
        P("tensor", None),
        P(),
        P(None, None, "tensor"),
        P("tensor"),
        P("tensor"),
        P("tensor"),
        P("tensor", None),
        P(),
        P(None, "tensor"),
        P(),
        P("tensor", None),
        P(),
        P(("dp", "tensor"), None),
    )
    return jax.shard_map(
        functools.partial(local, mesh.shape["dp"], mesh.shape["tensor"]),
        mesh=mesh,
        in_specs=placed,
        out_specs=(
            P(("dp", "tensor"), None),
            P(("dp", "tensor"), None),
            P("dp", None, "tensor"),
            P("tensor", None),
            P(),
            P(None, None, "tensor"),
            P("tensor"),
            P("tensor"),
            P("tensor"),
            P("tensor", None),
            P(),
            P(None, "tensor"),
            P("tensor"),
            P("tensor", None),
            P(),
            P(),
        ),
        check_vma=False,
    )
```

```python
import functools

import jax
import jax.numpy as jnp
from jax import lax
from jax.experimental import pallas as pl
from jax.experimental.pallas import tpu as pltpu
from jax.sharding import PartitionSpec as P

HEAD = 64
NBINS = 4096
ROW_LEN = 2048
SEGS = 6
D = 1024
ITEM_MAX = 680
CORES = 2
LANES = 128

epsilon = 1e-06
scale_starts = (1, 5, 14, 30, 55, 91, 155, 255, 424)
AHEAD = ITEM_MAX - scale_starts[-1] - 1
BEHIND = ITEM_MAX - 1
highest = lax.Precision.HIGHEST
f32 = jnp.float32
bf16 = jnp.bfloat16
MESH = pl.DeviceIdType.MESH
VMEM_LIMIT = 56 << 20


def dot(a, b, ca=1, cb=0, precision=None):
    return lax.dot_general(
        a, b, (((ca,), (cb,)), ((), ())), preferred_element_type=f32, precision=precision
    )


def item_layout(lengths):
    ends = jnp.cumsum(lengths, dtype=jnp.int32)
    begin = ends - lengths
    position = jnp.arange(ROW_LEN, dtype=jnp.int32)
    segment = jnp.sum((position[:, None] >= ends[None, :]).astype(jnp.int32), axis=1)
    chosen = segment[:, None] == jnp.arange(SEGS, dtype=jnp.int32)[None, :]
    inside = position - jnp.sum(jnp.where(chosen, begin[None, :], 0), axis=1)
    scale_ids = jnp.zeros_like(inside)
    for threshold in scale_starts:
        scale_ids = scale_ids + (inside >= threshold).astype(jnp.int32)
    return segment, scale_ids


def greet(peers):
    barrier = pltpu.get_barrier_semaphore()
    for p in peers:
        pl.semaphore_signal(barrier, inc=1, device_id=p, device_id_type=MESH)
    pl.semaphore_wait(barrier, len(peers))


def remote(src, dst, send, recv, to):
    return pltpu.make_async_remote_copy(
        src_ref=src,
        dst_ref=dst,
        send_sem=send,
        recv_sem=recv,
        device_id=to,
        device_id_type=MESH,
    )


class Place:
    def __init__(self, n, nd):
        self.n, self.nd, self.nz = n, nd, n // CORES
        self.dp, self.me = lax.axis_index("dp"), lax.axis_index("tensor")
        self.z, self.core = self.me // CORES, lax.rem(self.me, CORES)
        self.orders = orders_of(nd)
        self.far = sorted(range(1, self.nz), key=lambda o: min(o, self.nz - o))

    def chip(self, step):
        return lax.rem(self.z + step + self.nz, self.nz)

    def on_chip(self, step):
        return (self.dp, self.chip(step) * CORES + self.core)

    def twin(self):
        return (self.dp, self.z * CORES + 1 - self.core)

    def flip(self, bit):
        return (self.dp ^ (1 << bit), self.me)

    def line(self):
        return [(self.dp, lax.rem(self.me + o, self.n)) for o in range(1, self.n)]

    def greet_all(self):
        greet(self.line() + [self.flip(b) for b in range(bits_of(self.nd))])


def bits_of(nd):
    return nd.bit_length() - 1


def orders_of(nd):
    m = bits_of(nd)
    return [list(range(m)), [(m // 2 + i) % m for i in range(m)]]


def spread_plan(order):
    plan = [(0, list(order))]
    for i, bit in enumerate(order):
        plan += [(rel | (1 << bit), list(order[i + 1 :])) for rel, _ in list(plan)]
    return plan


class Spread:
    def __init__(self, place, ref_of, send, recv):
        self.place, self.ref_of, self.send, self.recv = place, ref_of, send, recv
        self.levels = bits_of(place.nd)

    def sends(self, part, rel, bits):
        p = self.place
        ref = self.ref_of(part, p.dp ^ rel)
        for bit in bits:
            to = rel | (1 << bit)
            yield remote(ref, ref, self.send.at[part, to], self.recv.at[part, to], p.flip(bit))

    def arrived(self, level):
        for part, order in enumerate(self.place.orders):
            for rel, bits in spread_plan(order):
                if rel and len(order) - 1 - len(bits) == level:
                    yield part, rel, bits

    def begin(self):
        for part, order in enumerate(self.place.orders):
            for c in self.sends(part, 0, order):
                c.start()

    def step(self, level):
        p = self.place
        for part, rel, bits in self.arrived(level):
            ref = self.ref_of(part, p.dp ^ rel)
            remote(
                ref, ref, self.send.at[part, rel], self.recv.at[part, rel], p.flip(0)
            ).wait_recv()
            for c in self.sends(part, rel, bits):
                c.start()

    def end(self):
        for part, order in enumerate(self.place.orders):
            for rel, bits in spread_plan(order):
                for c in self.sends(part, rel, bits):
                    c.wait_send()


class Line:
    def __init__(self, place, own, ref_of, send, recv):
        self.p, self.own, self.ref_of, self.send, self.recv = place, own, ref_of, send, recv
        self.ways = (1, -1)

    def inside(self, z):
        return (z >= 0) & (z < self.p.nz)

    def source(self, w, step):
        z = self.p.z - self.ways[w] * step
        return jnp.clip(z, 0, self.p.nz - 1), self.inside(z)

    def copy(self, w, step):
        p = self.p
        to = p.z + self.ways[w]
        chip, have = self.source(w, step - 1)
        src = self.own if step == 1 else self.ref_of(chip)
        c = remote(
            src,
            self.ref_of(chip),
            self.send.at[w, step],
            self.recv.at[w, step],
            (p.dp, jnp.clip(to, 0, p.nz - 1) * CORES + p.core),
        )
        return c, have & self.inside(to)

    def start(self, step=1):
        for w in range(2):
            c, do = self.copy(w, step)
            pl.when(do)(c.start)

    def got(self, step, then):
        for w in range(2):
            chip, have = self.source(w, step)
            to = self.p.z + self.ways[w]
            ref = self.ref_of(chip)
            wait = remote(
                ref, ref, self.send.at[w, step], self.recv.at[w, step], self.p.twin()
            )
            on, more = None, None
            if step + 1 < self.p.nz:
                on, more = self.copy(w, step + 1)

            @pl.when(have)
            def _():
                wait.wait_recv()
                if on is not None:
                    pl.when(more)(on.start)
                then(w, chip)

    def each(self, step, do):
        for w in range(2):
            chip, have = self.source(w, step)
            pl.when(have)(functools.partial(do, w, chip))

    def end(self):
        for step in range(1, self.p.nz):
            for w in range(2):
                c, do = self.copy(w, step)
                pl.when(do)(c.wait_send)


def picks_of(seg):
    return (seg == lax.broadcasted_iota(jnp.int32, (seg.shape[0], 8), 1)).astype(bf16)


def two(x):
    high = x.astype(bf16)
    return high, (x - high.astype(f32)).astype(bf16)


def per_token(picks, table):
    high, low = two(table)
    return dot(picks, high) + dot(picks, low)


def per_item(picks, values):
    high, low = two(values)
    return dot(picks, high, 0, 0) + dot(picks, low, 0, 0)


def norm_parts(values):
    centred = values - jnp.mean(values, axis=-1, keepdims=True)
    rstd = lax.rsqrt(jnp.mean(centred * centred, axis=-1, keepdims=True) + epsilon)
    return centred * rstd, rstd


def norm_back(normal, rstd, scaled):
    return rstd * (
        scaled
        - jnp.mean(scaled, axis=-1, keepdims=True)
        - normal * jnp.mean(scaled * normal, axis=-1, keepdims=True)
    )


GAMMA_ONE, GAMMA_TWO, SCALE_ONE, SCALE_TWO, SHIFT_ONE, SHIFT_TWO = range(6)


def half_lanes(rows):
    return lax.broadcasted_iota(jnp.int32, (rows, LANES), 1) < HEAD


def half_sums(x):
    low = half_lanes(x.shape[0])
    a = jnp.sum(jnp.where(low, x, 0.0), axis=1, keepdims=True)
    b = jnp.sum(jnp.where(low, 0.0, x), axis=1, keepdims=True)
    return jnp.where(low, a, b)


def one_half(x, h):
    low = half_lanes(x.shape[0])
    return jnp.where(low if h == 0 else jnp.logical_not(low), x, jnp.zeros_like(x))


def back_body(
    block, nq, nk, need_ref, q_ref, k_ref, v_ref, g_ref, o_ref, l_ref, ehs_ref, lo_ref, hi_ref,
    e_ref, n_ref, a_ref, w_ref, dw_ref, gn_ref, sums_ref, ku, dk, dv, dq, gqs, gkv,
):
    t = nq * block
    k = k_ref[0]
    rk = lax.rsqrt(half_sums(k * k) + epsilon)
    ku[...] = (k * rk).astype(bf16)
    dk[...] = jnp.zeros_like(dk)
    dv[...] = jnp.zeros_like(dv)
    ehs = ehs_ref[0]
    qsum = jnp.zeros((1, LANES), f32)
    hsum = jnp.zeros((1, LANES), f32)
    for qi in range(nq):
        rows = pl.ds(qi * block, block)
        q = q_ref[0, rows, :]
        rq = lax.rsqrt(half_sums(q * q) + epsilon)
        qhat = q * rq
        qu = (qhat * ehs).astype(bf16)
        qs = [one_half(qu, h) for h in range(2)]
        g = g_ref[0, rows, :]
        gs = [one_half(g, h) for h in range(2)]
        turned = (g.astype(f32) * o_ref[0, rows, :].astype(f32)).T
        deltas = [
            jnp.sum(turned[:HEAD], axis=0, keepdims=True),
            jnp.sum(turned[HEAD:], axis=0, keepdims=True),
        ]
        invs = [1.0 / l_ref[0, h : h + 1, rows] for h in range(2)]
        lo, hi = lo_ref[:, rows], hi_ref[:, rows]
        dq[...] = jnp.zeros_like(dq)
        for ki in range(nk):

            @pl.when(need_ref[qi * nk + ki] > 0)
            def _():
                cols = pl.ds(ki * block, block)
                e = e_ref[cols, :]
                allowed = (e >= lo) & (e <= hi)
                kb, vb = ku[cols, :], v_ref[0, cols, :]
                for h in range(2):
                    s = dot(kb, qs[h], 1, 1)
                    p = jnp.where(allowed, jnp.exp(s) * invs[h], 0.0)
                    dp = dot(vb, gs[h], 1, 1)
                    ds = (p * (dp - deltas[h])).astype(bf16)
                    dv[cols, :] += dot(p.astype(bf16), gs[h])
                    dk[cols, :] += dot(ds, qs[h])
                    dq[...] += dot(ds, one_half(kb, h), 0, 0)

        d = dq[...]
        hsum = hsum + jnp.sum(d * qhat * ehs, axis=0, keepdims=True)
        gq = (ehs * rq * (d - qhat * half_sums(qhat * d))).astype(bf16)
        gqs[rows, :] = gq
        qsum = qsum + jnp.sum(gq.astype(f32), axis=0, keepdims=True)
    khat = k * rk
    d = dk[...]
    gkv[:, :LANES] = (rk * (d - khat * half_sums(khat * d))).astype(bf16)
    gv = dv[...].astype(bf16)
    gkv[:, LANES:] = gv
    sums_ref[...] = jnp.zeros_like(sums_ref)
    sums_ref[0, 0:1, :] = qsum
    sums_ref[0, 1:2, :] = jnp.sum(gv.astype(f32), axis=0, keepdims=True)
    sums_ref[0, 2:3, :] = hsum
    dw_ref[0, :LANES, :] = dot(gqs[...], n_ref[:t, :], 0, 0).astype(bf16)
    dw_ref[0, LANES : 3 * LANES, :] = dot(gkv[...], n_ref[...], 0, 0).astype(bf16)
    dw_ref[0, 3 * LANES :, :] = dot(o_ref[0], a_ref[...], 0, 0).astype(bf16)

    @pl.when(pl.program_id(0) == 0)
    def _():
        gn_ref[...] = jnp.zeros_like(gn_ref)

    gn_ref[...] += dot(gkv[...], w_ref[0, LANES : 3 * LANES, :])
    gn_ref[:t, :] += dot(gqs[...], w_ref[0, :LANES, :])


def attend_back(need, q, k, v, g, o, l, ehs, lo_row, hi_row, e_col, normed, wide, weights, block):
    pairs, t, _ = q.shape
    w = k.shape[1]
    nq, nk = t // block, w // block
    slot = lambda rows: pl.BlockSpec((1, rows, LANES), lambda i, *_: (i, 0, 0))
    whole = lambda *shape: pl.BlockSpec(shape, lambda i, *_: (0,) * len(shape))
    return pl.pallas_call(
        functools.partial(back_body, block, nq, nk),
        grid_spec=pltpu.PrefetchScalarGridSpec(
            num_scalar_prefetch=1,
            grid=(pairs,),
            in_specs=[
                slot(t),
                slot(w),
                slot(w),
                slot(t),
                slot(t),
                pl.BlockSpec((1, 8, t), lambda i, *_: (i, 0, 0)),
                slot(1),
                whole(1, t),
                whole(1, t),
                whole(w, 1),
                whole(w, D),
                whole(t, D),
                pl.BlockSpec((1, 4 * LANES, D), lambda i, *_: (i, 0, 0)),
            ],
            out_specs=[
                pl.BlockSpec((1, 4 * LANES, D), lambda i, *_: (i, 0, 0)),
                whole(w, D),
                slot(8),
            ],
            scratch_shapes=[
                pltpu.VMEM((w, LANES), bf16),
                pltpu.VMEM((w, LANES), f32),
                pltpu.VMEM((w, LANES), f32),
                pltpu.VMEM((block, LANES), f32),
                pltpu.VMEM((t, LANES), bf16),
                pltpu.VMEM((w, 2 * LANES), bf16),
            ],
        ),
        out_shape=[
            jax.ShapeDtypeStruct((pairs, 4 * LANES, D), bf16),
            jax.ShapeDtypeStruct((w, D), f32),
            jax.ShapeDtypeStruct((pairs, 8, LANES), f32),
        ],
        compiler_params=pltpu.CompilerParams(vmem_limit_bytes=VMEM_LIMIT),
        name="attend_back",
    )(need, q, k, v, g, o, l, ehs, lo_row, hi_row, e_col, normed, wide, weights)


def ranks_at(lengths_ref, owner, tok, shape, axis):
    place = jnp.maximum(owner, 0) * tok + lax.broadcasted_iota(jnp.int32, shape, axis)
    item = jnp.zeros(shape, jnp.int32)
    begin = jnp.zeros(shape, jnp.int32)
    end = jnp.int32(0)
    for i in range(SEGS):
        end = end + lengths_ref[i]
        past = place >= end
        item = item + past.astype(jnp.int32)
        begin = jnp.where(past, end, begin)
    rank = item * 16
    for threshold in scale_starts:
        rank = rank + (place - begin >= threshold).astype(jnp.int32)
    there = owner >= 0
    return item, jnp.where(there, rank, -1)


def owners_of(p, steps):
    owners = []
    for s in [(0, 0)] + list(steps):
        for flip in range(CORES):
            c = p.core ^ flip
            far = [p.nz if v is None else v for v in s]
            chip = p.z - jnp.where(c == 0, far[0], far[1])
            owners.append(jnp.where((chip >= 0) & (chip < p.nz), chip * CORES + c, -1))
    return owners


def seen_lists(steps, tok):
    lists = []
    for qi in range(CORES):
        seen = set()
        for c in range(CORES):
            query = c ^ qi
            for i, s in enumerate([(0, 0)] + list(steps)):
                for flip in range(CORES):
                    owner = c ^ flip
                    if s[owner] is None:
                        continue
                    off = owner - s[owner] * CORES - query
                    near = off == 0
                    behind = off < 0 and (-off - 1) * tok + 1 <= BEHIND
                    ahead = off > 0 and (off - 1) * tok + 1 <= AHEAD
                    if near or behind or ahead:
                        seen.add(2 * i + flip)
        lists.append(seen)
    both = sorted(lists[0] & lists[1])
    rest = [sorted(v - set(both)) for v in lists]
    size = max(len(r) for r in rest)
    for r in rest:
        spare = [b for b in range(2 * len(steps) + 2) if b not in both and b not in r]
        r += spare[: size - len(r)]
    return [both + rest[0], both + rest[1]]


def block_at(lists, qi, j):
    a, b = lists[0][j], lists[1][j]
    return a if a == b else jnp.where(qi == 0, a, b)


def forward_body(
    n, nd, steps, width, len_ref, tok_ref, grad_ref, part_ref, extra_ref, abias_ref, pb_ref,
    apack_ref, mpack_ref,
    n_out, q_out, k_out, v_out, o_ref, l_ref, wa_out, wm_ref, branch_ref, resid_ref, nwide_ref,
    gwide_ref, mod_ref, ehs_ref,
    win, wa, modc, held, normed, qv, kv, vv, qb, vb, masks, ku, v0, v1, theirs, got,
    s1, r1, s2, r2, ts, tr, cs, cr, azs, azr, mzs, mzr, local_sem, out_sem, das, dar, dms, dmr,
    ms, mr,
):
    p = Place(n, nd)
    nz, tok = p.nz, grad_ref.shape[0]
    rounds = len(steps)
    blocks = 2 * rounds + 2
    pairs = qv.shape[0]
    merge = LANES // width
    rows = 4 * width // nd
    half = D // 2
    chunk = modc.shape[2]
    owners = owners_of(p, steps)
    p.greet_all()
    line = p.line()

    a_at = lambda chip, d: wa.at[chip, pl.ds(d * rows, rows)]
    mine = pl.ds(p.dp * rows, rows)
    al = Line(p, apack_ref.at[mine], lambda chip: wa.at[chip, mine], azs, azr)
    ml = Line(p, mpack_ref.at[:, p.dp], lambda chip: wm_ref.at[chip, :, p.dp], mzs, mzr)

    def a_spread(w, step, chip):
        return Spread(
            p,
            lambda part, d: wa.at[chip, pl.ds(d * rows, rows), pl.ds(part * half, half)],
            das.at[w, step],
            dar.at[w, step],
        )

    def m_spread(w, step, chip):
        return Spread(
            p, lambda part, d: wm_ref.at[chip, part, d], dms.at[w, step], dmr.at[w, step]
        )

    al.start()
    owns = [
        pltpu.make_async_copy(tok_ref, win.at[0], local_sem.at[0]),
        pltpu.make_async_copy(apack_ref, wa.at[p.z], local_sem.at[1]),
        pltpu.make_async_copy(mpack_ref, wm_ref.at[p.z], local_sem.at[2]),
    ]
    for c in owns:
        c.start()
    sums = [
        remote(part_ref.at[q[1]], held.at[o], s1.at[o], r1.at[o], q) for o, q in enumerate(line)
    ]
    for c in sums:
        c.start()
    twins = [
        remote(tok_ref if i == 0 else win.at[2 * i], win.at[2 * i + 1], cs.at[i], cr.at[i], p.twin())
        for i in range(rounds + 1)
    ]
    twins[0].start()
    for c in sums:
        c.wait()
    total = part_ref[p.me] + extra_ref[...] + abias_ref[p.me]
    for o in range(n - 1):
        total = total + held[o]
    modc[p.me] = total
    sums = [
        remote(modc.at[p.me], modc.at[p.me], s2.at[o], r2.at[o], q) for o, q in enumerate(line)
    ]
    for c in sums:
        c.start()
    moves = []
    for i, per_core in enumerate(steps):
        for c, step in enumerate(per_core):
            if step is None:
                continue
            go = (p.core == c) & (p.z + step >= 0) & (p.z + step < nz)
            have = (p.core == c) & (p.z - step >= 0) & (p.z - step < nz)
            to = (p.dp, jnp.clip(p.z + step, 0, nz - 1) * CORES + p.core)
            moves.append((i, go, have, remote(tok_ref, win.at[2 * i + 2], ts.at[i, c], tr.at[i, c], to)))
    al.got(1, lambda w, chip: a_spread(w, 1, chip).begin())
    for i, go, have, copy in moves:
        pl.when(go)(copy.start)
    for step in range(2, nz):
        al.got(step, lambda w, chip: a_spread(w, step, chip).begin())
    ml.start()

    for c in sums:
        c.wait()
    for j in range(n):
        mod_ref[:, j * chunk : (j + 1) * chunk] = modc[j]
    table = lambda which: mod_ref[:, which * D : (which + 1) * D]
    for s in range(pairs):
        parts = []
        for i in range(merge):
            r = modc[(s * merge + i) * CORES + p.core, SEGS : SEGS + 1, :]
            parts.append([r[:, k * width : (k + 1) * width] for k in range(3)])
        row = lambda k: jnp.concatenate([v[k] for v in parts], axis=1) if merge > 1 else parts[0][k]
        qb[s], vb[s], ehs_ref[s] = row(0), row(1), row(2)

    lists = seen_lists(steps, tok)
    for qi in range(CORES):
        owner = owners[qi]
        item, rank = ranks_at(len_ref, owner, tok, (tok, LANES), 0)
        lo, hi = item[:, :1] * 16, rank[:, :1]
        for j, b in enumerate(lists[qi]):
            _, e = ranks_at(len_ref, owners[b], tok, (8, tok), 1)
            e = e[:1]
            masks[qi, j] = jnp.where((e >= lo) & (e <= hi), 0.0, -1e30)
    own_item, _ = ranks_at(len_ref, owners[0], tok, (tok, 8), 0)
    picks = (own_item == lax.broadcasted_iota(jnp.int32, (tok, 8), 1)).astype(bf16)

    gwide_ref[0] = (per_token(picks, table(GAMMA_TWO)) * grad_ref[...].astype(f32)).astype(bf16)
    cross = [
        remote(gwide_ref.at[0], gwide_ref.at[1], ms.at[0], mr.at[0], p.twin()),
        remote(theirs, got, ms.at[1], mr.at[1], p.twin()),
        remote(nwide_ref.at[0], nwide_ref.at[1], ms.at[2], mr.at[2], p.twin()),
    ]
    cross[0].start()

    owns[0].wait()
    twins[0].wait()

    def norm_block(b):
        owner = owners[0]
        for i in range(1, blocks):
            owner = jnp.where(b == i, owners[i], owner)
        item, _ = ranks_at(len_ref, owner, tok, (tok, 8), 0)
        pick = (item == lax.broadcasted_iota(jnp.int32, (tok, 8), 1)).astype(bf16)
        normal, _ = norm_parts(win[b].astype(f32))
        scale = per_token(pick, table(SCALE_ONE))
        shift = per_token(pick, table(SHIFT_ONE))
        at = pl.ds(pl.multiple_of(b * tok, tok), tok)
        normed[at, :] = (normal * (1.0 + scale) + shift).astype(bf16)

    def weight(s, k, count=1):
        if merge == 1:
            return wa[s, k * width : (k + count) * width, :]
        rows_of = [
            wa[s * merge + i, (k + j) * width : (k + j + 1) * width, :]
            for j in range(count)
            for i in range(merge)
        ]
        return jnp.concatenate(rows_of, axis=0)

    def keys_block(b):
        at = pl.ds(pl.multiple_of(b * tok, tok), tok)

        def slot(s, _):
            r = dot(normed[at, :], weight(s, 1, 2), 1, 1)
            kv[s, at, :] = r[:, :LANES]
            vv[s, at, :] = (r[:, LANES:] + vb[s]).astype(bf16)
            return 0

        lax.fori_loop(0, pairs, slot, 0)

    @pl.loop(0, CORES)
    def _(b):
        norm_block(b)

    for level in range(bits_of(nd)):
        for step in range(1, nz):
            al.each(step, lambda w, chip: a_spread(w, step, chip).step(level))
    owns[1].wait()
    wout = pltpu.make_async_copy(wa, wa_out, out_sem.at[0])
    wout.start()

    @pl.loop(0, CORES)
    def _(b):
        keys_block(b)
        at = pl.ds(pl.multiple_of(b * tok, tok), tok)

        def slot(s, _):
            qv[s, at, :] = dot(normed[at, :], weight(s, 0), 1, 1) + qb[s]
            return 0

        lax.fori_loop(0, pairs, slot, 0)

    for i in range(rounds):
        any_got = p.core < 0
        for j, go, have, copy in moves:
            if j == i:
                pl.when(have)(copy.wait_recv)
                any_got = any_got | have

        @pl.when(jnp.logical_not(any_got))
        def _():
            win[2 * i + 2] = jnp.zeros((tok, D), bf16)

        twins[i + 1].start()
    for i in range(rounds):
        twins[i + 1].wait()

    @pl.loop(CORES, blocks)
    def _(b):
        norm_block(b)
        keys_block(b)

    outs = [wout]
    for i, (src, dst) in enumerate(((normed, n_out), (qv, q_out), (kv, k_out), (vv, v_out))):
        outs.append(pltpu.make_async_copy(src, dst, out_sem.at[i + 1]))
        outs[-1].start()

    ml.got(1, lambda w, chip: m_spread(w, 1, chip).begin())
    trips = pairs * CORES
    agenda = {}
    for step in range(1, nz):
        at = min(trips - 1, (step * trips) // nz)
        agenda.setdefault(at, []).append(step)

    @pl.loop(0, trips)
    def _(it):
        s, qi = it // CORES, lax.rem(it, CORES)

        @pl.when(qi == 0)
        def _():
            k = kv[s]
            ku[...] = (k * lax.rsqrt(half_sums(k * k) + epsilon)).astype(bf16)
            v = vv[s]
            low = half_lanes(v.shape[0])
            one = jnp.ones_like(v)
            v0[...] = jnp.where(low, v, one)
            v1[...] = jnp.where(low, one, v)

        at = pl.ds(pl.multiple_of(qi * tok, tok), tok)
        q = qv[s, at, :]
        qu = (q * lax.rsqrt(half_sums(q * q) + epsilon) * ehs_ref[s]).astype(bf16)
        qs = [one_half(qu, h) for h in range(2)]
        acc = [None, None]
        for j in range(len(lists[0])):
            b = block_at(lists, qi, j)
            cols = pl.ds(pl.multiple_of(b * tok, tok), tok)
            mask = masks[qi, j]
            for h in range(2):
                w = jnp.exp(dot(qs[h], ku[cols, :], 1, 1) + mask).astype(bf16)
                r = dot(w, (v0 if h == 0 else v1)[cols, :])
                acc[h] = r if acc[h] is None else acc[h] + r
        low = half_lanes(tok)
        other = jnp.where(low, pltpu.roll(acc[0], HEAD, 1), pltpu.roll(acc[1], HEAD, 1))
        o_ref[s, at, :] = (jnp.where(low, acc[0], acc[1]) / other).astype(bf16)
        turned = other.T
        l_ref[s, 0:1, at] = turned[0:1, :]
        l_ref[s, 1:2, at] = turned[HEAD : HEAD + 1, :]

        for when, todo in agenda.items():

            @pl.when(it == when)
            def _():
                for step in todo:
                    if step + 1 < nz:
                        ml.got(step + 1, lambda w, chip: m_spread(w, step + 1, chip).begin())
                    ml.each(step, lambda w, chip: m_spread(w, step, chip).step(0))

    def project(at):
        total = dot(o_ref[0, at, :], weight(0, 3))
        for s in range(1, pairs):
            total += dot(o_ref[s, at, :], weight(s, 3))
        return total

    theirs[...] = project(pl.ds(tok, tok)).astype(bf16)
    cross[1].start()
    first = project(pl.ds(0, tok)) + pb_ref[...]
    cross[1].wait()
    branch = first + got[...].astype(f32)
    branch_ref[...] = branch
    resid = win[0].astype(f32) + per_token(picks, table(GAMMA_ONE)) * branch
    resid_ref[...] = resid
    normal, _ = norm_parts(resid)
    scale = per_token(picks, table(SCALE_TWO))
    shift = per_token(picks, table(SHIFT_TWO))
    nwide_ref[0] = (normal * (1.0 + scale) + shift).astype(bf16)
    cross[2].start()

    for level in range(1, bits_of(nd)):
        for step in range(1, nz):
            ml.each(step, lambda w, chip: m_spread(w, step, chip).step(level))
    cross[0].wait()
    cross[2].wait()
    for step in range(1, nz):
        al.each(step, lambda w, chip: a_spread(w, step, chip).end())
        ml.each(step, lambda w, chip: m_spread(w, step, chip).end())
    al.end()
    ml.end()
    for i, go, have, copy in moves:
        pl.when(go)(copy.wait_send)
    owns[2].wait()
    for c in outs:
        c.wait()


def forward(lengths, tokens, out_grad, part, extra, abias, proj_bias, apack, mpack, steps, nd, width):
    n, _, cols = part.shape
    nz = n // CORES
    tok = tokens.shape[0]
    rounds = len(steps)
    blocks = 2 * rounds + 2
    t, w = CORES * tok, blocks * tok
    pairs = nz * width // LANES
    seen = len(seen_lists(steps, tok)[0])
    dma = pltpu.SemaphoreType.DMA
    vmem = pl.BlockSpec(memory_space=pltpu.VMEM)
    anywhere = pl.BlockSpec(memory_space=pl.ANY)
    out = lambda *shape: jax.ShapeDtypeStruct(shape, f32)
    low = lambda *shape: jax.ShapeDtypeStruct(shape, bf16)
    v = pltpu.VMEM
    return pl.pallas_call(
        functools.partial(forward_body, n, nd, steps, width),
        out_shape=[
            low(w, D),
            out(pairs, t, LANES),
            out(pairs, w, LANES),
            low(pairs, w, LANES),
            low(pairs, t, LANES),
            out(pairs, 8, t),
            low(nz, 4 * width, D),
            low(nz, *mpack.shape),
            out(tok, D),
            out(tok, D),
            low(CORES, tok, D),
            low(CORES, tok, D),
            out(8, 6 * D),
            out(pairs, 1, LANES),
        ],
        in_specs=[pl.BlockSpec(memory_space=pltpu.SMEM), anywhere]
        + [vmem] * 5
        + [anywhere] * 2,
        out_specs=[anywhere] * 4 + [vmem] * 2 + [anywhere] * 2 + [vmem] * 6,
        scratch_shapes=[
            v((blocks, tok, D), bf16),
            v((nz, 4 * width, D), bf16),
            v(part.shape, f32),
            v((n - 1,) + part.shape[1:], f32),
            v((w, D), bf16),
            v((pairs, t, LANES), f32),
            v((pairs, w, LANES), f32),
            v((pairs, w, LANES), bf16),
            v((pairs, 1, LANES), f32),
            v((pairs, 1, LANES), f32),
            v((CORES, seen, tok, tok), f32),
            v((w, LANES), bf16),
            v((w, LANES), bf16),
            v((w, LANES), bf16),
            v((tok, D), bf16),
            v((tok, D), bf16),
            dma((n - 1,)),
            dma((n - 1,)),
            dma((n - 1,)),
            dma((n - 1,)),
            dma((rounds, CORES)),
            dma((rounds, CORES)),
            dma((rounds + 1,)),
            dma((rounds + 1,)),
            dma((2, nz)),
            dma((2, nz)),
            dma((2, nz)),
            dma((2, nz)),
            dma((3,)),
            dma((5,)),
            dma((2, nz, 2, nd)),
            dma((2, nz, 2, nd)),
            dma((2, nz, 2, nd)),
            dma((2, nz, 2, nd)),
            dma((3,)),
            dma((3,)),
        ],
        compiler_params=pltpu.CompilerParams(
            collective_id=0, has_side_effects=True, vmem_limit_bytes=VMEM_LIMIT
        ),
        name="forward",
    )(lengths, tokens, out_grad, part, extra, abias, proj_bias, apack, mpack)


def turn_body(
    n, nd, gx_ref, mlp_ref, resid_ref, branch_ref, g_ref, seg_ref, mod_ref, db_ref, w_ref, gw_ref,
    mid_ref, wide_ref, hg_ref, out_ref, items_ref, sums_ref, theirs, got, send, recv,
):
    p = Place(n, nd)
    tok = g_ref.shape[0]
    greet([p.twin()])
    theirs[0] = gx_ref[pl.ds(tok, tok), :].astype(bf16)
    theirs[1] = mlp_ref[pl.ds(tok, tok), :].astype(bf16)
    copies = [remote(theirs.at[i], got.at[i], send.at[i], recv.at[i], p.twin()) for i in range(2)]
    for c in copies:
        c.start()
    picks = picks_of(seg_ref[...])
    normal, rstd = norm_parts(resid_ref[...])
    scale = per_token(picks, mod_ref[SCALE_TWO])
    grad_final = g_ref[...].astype(f32)
    copies[0].wait()
    second = gx_ref[pl.ds(0, tok), :] + got[0].astype(f32)
    mid = grad_final + norm_back(normal, rstd, second * (1.0 + scale))
    mid_ref[...] = mid
    attn = (per_token(picks, mod_ref[GAMMA_ONE]) * mid).astype(bf16)
    wide_ref[0] = attn
    copies.append(remote(wide_ref.at[0], wide_ref.at[1], send.at[2], recv.at[2], p.twin()))
    copies[2].start()
    copies[1].wait()
    branch = mlp_ref[pl.ds(0, tok), :] + got[1].astype(f32) + db_ref[...]
    gamma = per_token(picks, mod_ref[GAMMA_TWO])
    out_ref[...] = (resid_ref[...] + gamma * branch).astype(bf16)
    items_ref[0] = per_item(picks, mid * branch_ref[...])
    items_ref[1] = per_item(picks, grad_final * branch)
    items_ref[2] = per_item(picks, second * normal)
    items_ref[3] = per_item(picks, second)
    sums_ref[...] = jnp.zeros_like(sums_ref)
    sums_ref[0:1, :] = jnp.sum(attn.astype(f32), axis=0, keepdims=True)
    sums_ref[1:2, :] = jnp.sum(gw_ref[0].astype(f32), axis=0, keepdims=True)
    copies[2].wait()
    for s in range(w_ref.shape[0]):
        for c in range(CORES):
            hg_ref[s, pl.ds(c * tok, tok), :] = dot(
                wide_ref[c], w_ref[s, 3 * LANES :, :], 1, 1
            ).astype(bf16)


def turn(gx, mlp_part, resid, branch, out_grad, seg, mod, down_bias, weights, gwide, n, nd):
    tok = out_grad.shape[0]
    pairs = weights.shape[0]
    dma = pltpu.SemaphoreType.DMA
    vmem = pl.BlockSpec(memory_space=pltpu.VMEM)
    return pl.pallas_call(
        functools.partial(turn_body, n, nd),
        out_shape=[
            jax.ShapeDtypeStruct((tok, D), f32),
            jax.ShapeDtypeStruct((CORES, tok, D), bf16),
            jax.ShapeDtypeStruct((pairs, CORES * tok, LANES), bf16),
            jax.ShapeDtypeStruct((tok, D), bf16),
            jax.ShapeDtypeStruct((4, 8, D), f32),
            jax.ShapeDtypeStruct((8, D), f32),
        ],
        in_specs=[vmem] * 10,
        out_specs=[vmem] * 6,
        scratch_shapes=[
            pltpu.VMEM((2, tok, D), bf16),
            pltpu.VMEM((2, tok, D), bf16),
            dma((3,)),
            dma((3,)),
        ],
        compiler_params=pltpu.CompilerParams(
            collective_id=2, has_side_effects=True, vmem_limit_bytes=48 << 20
        ),
        name="turn",
    )(gx, mlp_part, resid, branch, out_grad, seg, mod, down_bias, weights, gwide)


def mlp_body(x_ref, g_ref, w_ref, bias_ref, mlp_ref, gx_ref, dw_ref, dbias_ref):
    x, g = x_ref[...], g_ref[...]
    units = w_ref.shape[2] * w_ref.shape[3]
    up = w_ref[0, 0].reshape(units, D)
    down = w_ref[0, 1].reshape(units, D)
    pre = dot(x, up, 1, 1) + bias_ref[0]
    square = pre * pre
    th = jnp.tanh(0.7978845608028654 * pre * (1.0 + 0.044715 * square))
    half = 0.5 * (1.0 + th)
    hidden = (pre * half).astype(bf16)
    slope = half + 0.5 * pre * (1.0 - th * th) * (
        0.7978845608028654 * (1.0 + 3.0 * 0.044715 * square)
    )
    gp = (dot(g, down, 1, 1) * slope).astype(bf16)

    @pl.when(pl.program_id(0) == 0)
    def _():
        mlp_ref[...] = jnp.zeros_like(mlp_ref)
        gx_ref[...] = jnp.zeros_like(gx_ref)

    mlp_ref[...] += dot(hidden, down)
    gx_ref[...] += dot(gp, up)
    dw_ref[0, 0] = dot(gp, x, 0, 0).astype(bf16).reshape(dw_ref.shape[2:])
    dw_ref[0, 1] = dot(hidden, g, 0, 0).astype(bf16).reshape(dw_ref.shape[2:])
    dbias_ref[0] = jnp.sum(gp.astype(f32), axis=0, keepdims=True)


def mlp(x, g, weights, bias):
    t = x.shape[0]
    nz, _, nd, piece, _ = weights.shape
    count = min(nd, max(1, 256 // piece))
    per = nd // count
    steps, units = nz * per, count * piece
    whole = lambda *shape: pl.BlockSpec(shape, lambda i: (0,) * len(shape))
    block = pl.BlockSpec((1, 2, count, piece, D), lambda i: (i // per, 0, i % per, 0, 0))
    row = pl.BlockSpec((1, 1, units), lambda i: (i, 0, 0))
    return pl.pallas_call(
        mlp_body,
        grid=(steps,),
        in_specs=[whole(t, D), whole(t, D), block, row],
        out_specs=[whole(t, D), whole(t, D), block, row],
        out_shape=[
            jax.ShapeDtypeStruct((t, D), f32),
            jax.ShapeDtypeStruct((t, D), f32),
            jax.ShapeDtypeStruct(weights.shape, bf16),
            jax.ShapeDtypeStruct((steps, 1, units), f32),
        ],
        compiler_params=pltpu.CompilerParams(vmem_limit_bytes=VMEM_LIMIT),
        name="mlp",
    )(x, g, weights, bias.reshape(steps, 1, units))


class Reduce:
    def __init__(self, place, first, stage, zstage, out, sems):
        self.p, self.first, self.stage, self.zstage, self.out = place, first, stage, zstage, out
        self.ps, self.pr, self.zs, self.zr, self.os, self.or_ = sems
        self.copies, self.all = {}, []

    def held(self, part, level):
        rels = list(range(self.p.nd))
        for bit in self.p.orders[part][:level]:
            rels = [r for r in rels if not (r >> bit) & 1]
        return rels

    def current(self, part, level, chip, rel):
        if level == 0:
            return self.first(part, chip, self.p.dp ^ rel)
        return self.stage(part, level - 1, chip, self.held(part, level).index(rel))

    def send_plane(self, level, o):
        p = self.p
        chip = p.chip(o)
        for part, order in enumerate(p.orders):
            bit = order[level]
            for rel in self.held(part, level):
                if (rel >> bit) & 1:
                    slot = self.held(part, level + 1).index(rel ^ (1 << bit))
                    c = remote(
                        self.current(part, level, chip, rel),
                        self.stage(part, level, chip, slot),
                        self.ps.at[part, level, o, slot],
                        self.pr.at[part, level, o, slot],
                        p.flip(bit),
                    )
                    c.start()
                    self.copies[part, level, o, slot] = c
                    self.all.append(c)

    def add_plane(self, level, o):
        p = self.p
        chip = p.chip(o)
        for part in range(2):
            for slot, rel in enumerate(self.held(part, level + 1)):
                self.copies[part, level, o, slot].wait_recv()
                room = self.stage(part, level, chip, slot)
                mine = self.current(part, level, chip, rel)
                room[...] = (room[...].astype(f32) + mine[...].astype(f32)).astype(bf16)

    def send_line(self, o):
        p = self.p
        m = bits_of(p.nd)
        for part in range(2):
            c = remote(
                self.stage(part, m - 1, p.chip(o), 0),
                self.zstage(part, o),
                self.zs.at[part, o],
                self.zr.at[part, o],
                p.on_chip(o),
            )
            c.start()
            self.copies["z", part, o] = c
            self.all.append(c)

    def end_line(self):
        p = self.p
        m = bits_of(p.nd)
        for part in range(2):
            total = self.stage(part, m - 1, p.z, 0)[...].astype(f32)
            for o in p.far:
                self.copies["z", part, o].wait_recv()
                total = total + self.zstage(part, o)[...].astype(f32)
            self.out(part, p.dp)[...] = total.astype(bf16)
        self.back = Spread(p, self.out, self.os, self.or_)
        self.back.begin()

    def end(self):
        for c in self.all:
            c.wait_send()
        self.back.end()


def finish_body(
    n, nd, steps, dm_ref, da_ref, gn_ref, x_ref, mid_ref, seg_ref, mod_ref, part_ref, extra_ref,
    ym_ref, ya_ref, tg_ref, small_ref,
    mstage, astage, mz, az, gswap, gmine, ghalo, part, held,
    mps, mpr, mzs, mzr, mos, mor, aps, apr, azs, azr, aos, aor,
    gs, gr, hs, hr, s1, r1, s2, r2, s3, r3, s4, r4,
):
    p = Place(n, nd)
    nz, tok = p.nz, x_ref.shape[0]
    rounds = len(steps)
    half = D // 2
    m = bits_of(nd)
    p.greet_all()

    def room(buffer, narrow):
        def at(p_, level, chip, slot):
            base = sum(nd >> (i + 1) for i in range(level))
            return buffer.at[p_, base + slot, chip]

        return at

    cut = lambda part_: pl.ds(part_ * half, half)
    rm = Reduce(
        p,
        lambda q, chip, d: dm_ref.at[chip, q, d],
        room(mstage, False),
        lambda q, o: mz.at[q, o],
        lambda q, d: ym_ref.at[q, d],
        (mps, mpr, mzs, mzr, mos, mor),
    )
    ra = Reduce(
        p,
        lambda q, chip, d: da_ref.at[chip, d, :, cut(q)],
        room(astage, True),
        lambda q, o: az.at[q, o],
        lambda q, d: ya_ref.at[d, :, cut(q)],
        (aps, apr, azs, azr, aos, aor),
    )
    far = p.far + [0]
    gcopies = []
    for i in range(rounds + 1):
        gswap[i] = gn_ref[i, 1].astype(bf16)
        c = remote(gswap.at[i], gmine.at[i], gs.at[i], gr.at[i], p.twin())
        c.start()
        gcopies.append(c)
    for o in far:
        rm.send_plane(0, o)
    moves = []
    for i, per_core in enumerate(steps):
        gcopies[i + 1].wait()
        gmine[i + 1] = (gn_ref[i + 1, 0] + gmine[i + 1].astype(f32)).astype(bf16)
        for c, step in enumerate(per_core):
            if step is None:
                continue
            go = (p.core == c) & (p.z - step >= 0) & (p.z - step < nz)
            got = (p.core == c) & (p.z + step >= 0) & (p.z + step < nz)
            copy = remote(gmine.at[i + 1], ghalo.at[i], hs.at[i, c], hr.at[i, c], p.on_chip(-step))
            pl.when(go)(copy.start)
            moves.append((i, go, got, copy))
    gcopies[0].wait()
    first = gn_ref[0, 0] + gmine[0].astype(f32)
    tg_ref[...] = first
    for i, go, got, copy in moves:

        @pl.when(got)
        def _():
            copy.wait_recv()
            tg_ref[...] += ghalo[i].astype(f32)

    first = tg_ref[...]
    picks = picks_of(seg_ref[...])
    normal, rstd = norm_parts(x_ref[...].astype(f32))
    scale = per_token(picks, mod_ref[SCALE_ONE])
    tg_ref[...] = mid_ref[...] + norm_back(normal, rstd, first * (1.0 + scale))
    part[...] = part_ref[...]
    chunk = 6 * D // n
    for which, values in ((SCALE_ONE, first * normal), (SHIFT_ONE, first)):
        items = per_item(picks, values)
        begin, end = which * D, (which + 1) * D
        for j in range(n):
            a, b = max(begin, j * chunk), min(end, (j + 1) * chunk)
            if a < b:
                part[j, :, a - j * chunk : b - j * chunk] += items[:, a - begin : b - begin]
    line = p.line()
    sums = [remote(part.at[q[1]], held.at[o], s1.at[o], r1.at[o], q) for o, q in enumerate(line)]
    for c in sums:
        c.start()

    def advance(r, level):
        for o in far:
            r.add_plane(level, o)
            if level + 1 < m:
                r.send_plane(level + 1, o)
            elif o:
                r.send_line(o)

    advance(rm, 0)
    for o in far:
        ra.send_plane(0, o)
    for c in sums:
        c.wait()
    total = part[p.me] + extra_ref[...]
    for o in range(n - 1):
        total = total + held[o]
    small_ref[p.core, p.z, p.dp] = total
    mine = small_ref.at[p.core, p.z, p.dp]
    plane = [(lax.rem(p.dp + o, nd), p.me) for o in range(1, nd)]
    sums = [remote(mine, mine, s2.at[o], r2.at[o], q) for o, q in enumerate(plane)]
    for c in sums:
        c.start()
    for level in range(1, m):
        advance(rm, level)
    for c in sums:
        c.wait()
    mine = small_ref.at[p.core, p.z]
    sums = [remote(mine, mine, s3.at[o], r3.at[o], p.on_chip(o)) for o in p.far]
    for c in sums:
        c.start()
    advance(ra, 0)
    rm.end_line()
    for level in range(1, m):
        advance(ra, level)
    for c in sums:
        c.wait()
    mine = small_ref.at[p.core]
    last = remote(mine, mine, s4, r4, p.twin())
    last.start()
    ra.end_line()
    for level in range(m):
        rm.back.step(level)
        ra.back.step(level)
    last.wait()
    rm.end()
    ra.end()
    for i, go, got, copy in moves:
        pl.when(go)(copy.wait_send)


def finish(dm, da, gn, tokens, mid, seg, mod, part, extra, steps, nd):
    n, rows, cols = part.shape
    nz = n // CORES
    tok = tokens.shape[0]
    rounds = len(steps)
    piece, arows = dm.shape[3], da.shape[2]
    dma = pltpu.SemaphoreType.DMA
    vmem = pl.BlockSpec(memory_space=pltpu.VMEM)
    m = bits_of(nd)
    levels = max(1, nd // 2)
    plane = (2, m, nz, levels)
    wide = lambda: [
        dma(plane),
        dma(plane),
        dma((2, nz)),
        dma((2, nz)),
        dma((2, nd)),
        dma((2, nd)),
    ]
    return pl.pallas_call(
        functools.partial(finish_body, n, nd, steps),
        out_shape=[
            jax.ShapeDtypeStruct(dm.shape[1:], bf16),
            jax.ShapeDtypeStruct(da.shape[1:], bf16),
            jax.ShapeDtypeStruct((tok, D), f32),
            jax.ShapeDtypeStruct((CORES, nz, nd, rows, cols), f32),
        ],
        in_specs=[vmem] * 9,
        out_specs=[vmem] * 4,
        scratch_shapes=[
            pltpu.VMEM((2, nd - 1, nz, piece, D), bf16),
            pltpu.VMEM((2, nd - 1, nz, arows, D // 2), bf16),
            pltpu.VMEM((2, nz, piece, D), bf16),
            pltpu.VMEM((2, nz, arows, D // 2), bf16),
            pltpu.VMEM((rounds + 1, tok, D), bf16),
            pltpu.VMEM((rounds + 1, tok, D), bf16),
            pltpu.VMEM((rounds, tok, D), bf16),
            pltpu.VMEM((n, rows, cols), f32),
            pltpu.VMEM((n - 1, rows, cols), f32),
        ]
        + wide()
        + wide()
        + [
            dma((rounds + 1,)),
            dma((rounds + 1,)),
            dma((rounds, CORES)),
            dma((rounds, CORES)),
            dma((n - 1,)),
            dma((n - 1,)),
            dma((nd - 1,)),
            dma((nd - 1,)),
            dma((nz,)),
            dma((nz,)),
            dma,
            dma,
        ],
        compiler_params=pltpu.CompilerParams(
            collective_id=3, has_side_effects=True, vmem_limit_bytes=VMEM_LIMIT
        ),
        name="finish",
    )(dm, da, gn, tokens, mid, seg, mod, part, extra)


def local(
    nd,
    nt,
    tokens,
    class_embed,
    item_lengths,
    token_codes,
    ada_weight,
    ada_bias,
    qkv_weight,
    query_bias,
    value_bias,
    head_scale,
    proj_weight,
    proj_bias,
    up_weight,
    up_bias,
    down_weight,
    down_bias,
    out_grad,
):
    d, t = lax.axis_index("dp"), lax.axis_index("tensor")
    nz = nt // CORES
    z, core = t // CORES, t % CORES
    tok = tokens.shape[0]
    heads = head_scale.shape[0]
    width = heads * HEAD
    wide = nz * width
    pairs = wide // LANES
    units = up_weight.shape[1]
    feat = class_embed.shape[2]

    per_chip = CORES * tok
    seen = [[], []]
    for c in range(CORES):
        for step in range(1, nz):
            if step * per_chip - c * tok - tok < BEHIND:
                seen[c].append(step)
        for step in range(1, nz):
            if (step - 1) * per_chip + c * tok < AHEAD:
                seen[c].append(-step)
    rounds = max(len(s) for s in seen)
    steps = [
        tuple(s[len(s) - 1 - i] if i < len(s) else None for s in seen) for i in range(rounds)
    ]

    chunk = ada_weight.shape[1] // nt
    cond_act = jax.nn.silu(class_embed[0]).astype(bf16)
    ada_part = jnp.dot(cond_act, ada_weight, preferred_element_type=f32)
    part = jnp.pad(ada_part.reshape(SEGS, nt, chunk).transpose(1, 0, 2), ((0, 0), (0, 2), (0, 0)))
    bias_row = jnp.concatenate(
        [
            query_bias,
            value_bias,
            jnp.broadcast_to(jnp.exp(head_scale)[:, None], (heads, HEAD)).reshape(width),
            jnp.zeros((chunk - 3 * width,), f32),
        ]
    )
    extra = jnp.pad(bias_row[None], ((SEGS, 7 - SEGS), (0, 0)))
    abias = jnp.pad(
        jnp.broadcast_to(ada_bias.reshape(nt, 1, chunk), (nt, SEGS, chunk)),
        ((0, 0), (0, 8 - SEGS), (0, 0)),
    )
    apack = jnp.concatenate(
        [qkv_weight.transpose(1, 2, 0).reshape(3 * width, D), proj_weight], axis=0
    )
    mpack = jnp.stack([up_weight.T, down_weight]).reshape(2, nd, units // nd, D)
    (
        normed, q_raw, k_raw, v_in, heads_out, weight_sums, wattn, wmlp, branch, resid, nwide,
        gwide, mod_wide, ehs,
    ) = forward(
        item_lengths[0], tokens, out_grad, part, extra, abias, proj_bias[None], apack, mpack,
        steps, nd, width,
    )
    mod = mod_wide.reshape(8, 6, D).transpose(1, 0, 2)

    segment, scale_ids = item_layout(item_lengths[0])
    rank = segment * 16 + scale_ids
    owners = []
    for s in [(0, 0)] + steps:
        for flip in range(CORES):
            c = core ^ flip
            step = jnp.where(c == 0, nz if s[0] is None else s[0], nz if s[1] is None else s[1])
            chip = z - step
            owners.append(jnp.where((chip >= 0) & (chip < nz), chip * CORES + c, -1))
    blocks = len(owners)
    seg_blocks, rank_blocks = segment.reshape(nt, tok), rank.reshape(nt, tok)
    take = lambda a, o: lax.dynamic_index_in_dim(a, jnp.maximum(o, 0), 0, keepdims=False)
    seg_win = jnp.concatenate([take(seg_blocks, o) for o in owners])
    e_win = jnp.concatenate([jnp.where(o >= 0, take(rank_blocks, o), -1) for o in owners])
    lo = seg_win[: CORES * tok] * 16
    hi = e_win[: CORES * tok]
    e_blocks = e_win.reshape(blocks, tok)
    e_max, e_min = jnp.max(e_blocks, axis=1), jnp.min(e_blocks, axis=1)
    need = (
        (e_max[None, :] >= jnp.min(lo.reshape(CORES, tok), axis=1)[:, None])
        & (e_min[None, :] <= jnp.max(hi.reshape(CORES, tok), axis=1)[:, None])
        & (e_max[None, :] >= 0)
    ).astype(jnp.int32).reshape(CORES * blocks)
    seg_own = seg_win[:tok, None]

    merge = nz // pairs
    weights = (
        wattn.reshape(pairs, merge, 4, width, D)
        .transpose(0, 2, 1, 3, 4)
        .reshape(pairs, 4 * LANES, D)
    )

    up_own = lax.dynamic_index_in_dim(
        up_bias.reshape(nz, CORES, units), core, 1, keepdims=False
    )
    mlp_part, gx_part, dmlp, dbias = mlp(
        nwide.reshape(CORES * tok, D), gwide.reshape(CORES * tok, D), wmlp, up_own
    )
    mid, awide, heads_grad, layer_out, items, sums = turn(
        gx_part, mlp_part, resid, branch, out_grad, seg_own, mod, down_bias[None], weights,
        gwide, nt, nd,
    )
    dattn, gn, head_sums = attend_back(
        need, q_raw, k_raw, v_in, heads_grad, heads_out, weight_sums, ehs, lo[None, :],
        hi[None, :], e_win[:, None], normed, awide.reshape(CORES * tok, D), weights, tok,
    )

    low_codes = 64
    hot = lambda v, k: (v[:, None] == jnp.arange(k, dtype=jnp.int32)[None, :]).astype(bf16)
    hist = dot(
        hot(token_codes // low_codes, NBINS // low_codes),
        hot(token_codes % low_codes, low_codes),
        0,
        0,
    ).reshape(NBINS)
    row_six = jnp.concatenate([sums[0], sums[1], hist])
    to_all = lambda v: jnp.where(
        (jnp.arange(CORES) == core)[None, :, None], v[:, None, :], 0.0
    ).reshape(-1)
    row_seven = jnp.concatenate(
        [
            to_all(dbias.reshape(nz, units)),
            to_all(head_sums[:, 0].reshape(nz, width)),
            to_all(head_sums[:, 1].reshape(nz, width)),
        ]
    )
    hs_part = to_all(jnp.sum(head_sums[:, 2].reshape(nz, heads, HEAD), axis=2)).reshape(nt, heads)
    none = jnp.zeros((SEGS, D), f32)
    mod_part = jnp.concatenate(
        [items[0, :SEGS], items[1, :SEGS], none, items[2, :SEGS], none, items[3, :SEGS]], axis=1
    )
    payload = jnp.concatenate([mod_part, row_six[None], row_seven[None]], axis=0)
    payload = payload.reshape(8, nt, chunk).transpose(1, 0, 2)
    tail = jnp.pad(hs_part[:, None, :], ((0, 0), (7, 0), (0, LANES - heads)))
    own_tail = jnp.pad(
        cond_act.astype(f32), ((0, 8 - SEGS), (chunk, LANES - feat))
    )
    dattn = (
        dattn.reshape(pairs, 4, merge, width, D)
        .transpose(0, 2, 1, 3, 4)
        .reshape(nz, nd, 4 * width // nd, D)
    )
    ymlp, yattn, tokens_grad, small = finish(
        dmlp,
        dattn,
        gn.reshape(rounds + 1, CORES, tok, D),
        tokens,
        mid,
        seg_own,
        mod,
        jnp.concatenate([payload, tail], axis=2),
        own_tail,
        steps,
        nd,
    )

    rows_all = small[..., :chunk].transpose(2, 3, 1, 0, 4).reshape(nd, 8, 6 * D)
    mod_all = rows_all[:, :SEGS].reshape(nd * SEGS, 6 * D)
    mod_own = lax.dynamic_index_in_dim(rows_all, d, 0, keepdims=False)[:SEGS]
    bias_sums = jnp.sum(rows_all[:, SEGS:], axis=0)
    own_small = lax.dynamic_index_in_dim(small, core, 0, keepdims=False)
    own_small = lax.dynamic_index_in_dim(own_small, z, 0, keepdims=False)
    cond_all = own_small[:, :SEGS, chunk : chunk + feat].reshape(nd * SEGS, feat)
    hscale_grad = jnp.sum(own_small[:, 7, chunk : chunk + heads], axis=0)
    adaw_grad = dot(cond_all, mod_all, 0, 0, highest)
    adab_grad = jnp.sum(mod_all, axis=0)
    cond_grad = dot(mod_own, ada_weight.astype(f32), 1, 1, highest)
    embed_grad = jax.vjp(jax.nn.silu, class_embed)[1](cond_grad[None])[0]
    projb_grad, downb_grad = bias_sums[0, :D], bias_sums[0, D : 2 * D]
    code_hist = bias_sums[0, 2 * D :]
    at = lambda base, k: lax.dynamic_slice_in_dim(bias_sums[1], base + t * k, k, 0)
    upb_grad = at(0, units)
    qbias_grad = at(nt * units, width)
    vbias_grad = at(nt * (units + width), width)
    yattn = yattn.reshape(4 * width, D)
    qkvw_grad = yattn[: 3 * width].astype(f32).reshape(3, width, D).transpose(2, 0, 1)
    projw_grad = yattn[3 * width :].astype(f32)
    upw_grad = ymlp[0].reshape(units, D).astype(f32).T
    downw_grad = ymlp[1].reshape(units, D).astype(f32)
    return (
        layer_out,
        tokens_grad,
        embed_grad,
        adaw_grad,
        adab_grad,
        qkvw_grad,
        qbias_grad,
        vbias_grad,
        hscale_grad,
        projw_grad,
        projb_grad,
        upw_grad,
        upb_grad,
        downw_grad,
        downb_grad,
        code_hist,
    )


def solution(mesh):
    placed = (
        P(("dp", "tensor"), None),
        P("dp", None, "tensor"),
        P("dp", None),
        P(("dp", "tensor")),
        P("tensor", None),
        P(),
        P(None, None, "tensor"),
        P("tensor"),
        P("tensor"),
        P("tensor"),
        P("tensor", None),
        P(),
        P(None, "tensor"),
        P(),
        P("tensor", None),
        P(),
        P(("dp", "tensor"), None),
    )
    return jax.shard_map(
        functools.partial(local, mesh.shape["dp"], mesh.shape["tensor"]),
        mesh=mesh,
        in_specs=placed,
        out_specs=(
            P(("dp", "tensor"), None),
            P(("dp", "tensor"), None),
            P("dp", None, "tensor"),
            P("tensor", None),
            P(),
            P(None, None, "tensor"),
            P("tensor"),
            P("tensor"),
            P("tensor"),
            P("tensor", None),
            P(),
            P(None, "tensor"),
            P("tensor"),
            P("tensor", None),
            P(),
            P(),
        ),
        check_vma=False,
    )
```

```python
import functools

import jax
import jax.numpy as jnp
from jax import lax
from jax.experimental import pallas as pl
from jax.experimental.pallas import tpu as pltpu
from jax.sharding import PartitionSpec as P

HEAD = 64
NBINS = 4096
ROW_LEN = 2048
SEGS = 6
D = 1024
ITEM_MAX = 680
CORES = 2
LANES = 128

epsilon = 1e-06
scale_starts = (1, 5, 14, 30, 55, 91, 155, 255, 424)
AHEAD = ITEM_MAX - scale_starts[-1] - 1
BEHIND = ITEM_MAX - 1
highest = lax.Precision.HIGHEST
f32 = jnp.float32
bf16 = jnp.bfloat16
MESH = pl.DeviceIdType.MESH
VMEM_LIMIT = 56 << 20


def dot(a, b, ca=1, cb=0, precision=None):
    return lax.dot_general(
        a, b, (((ca,), (cb,)), ((), ())), preferred_element_type=f32, precision=precision
    )


def item_layout(lengths):
    ends = jnp.cumsum(lengths, dtype=jnp.int32)
    begin = ends - lengths
    position = jnp.arange(ROW_LEN, dtype=jnp.int32)
    segment = jnp.sum((position[:, None] >= ends[None, :]).astype(jnp.int32), axis=1)
    chosen = segment[:, None] == jnp.arange(SEGS, dtype=jnp.int32)[None, :]
    inside = position - jnp.sum(jnp.where(chosen, begin[None, :], 0), axis=1)
    scale_ids = jnp.zeros_like(inside)
    for threshold in scale_starts:
        scale_ids = scale_ids + (inside >= threshold).astype(jnp.int32)
    return segment, scale_ids


def greet(peers):
    barrier = pltpu.get_barrier_semaphore()
    for p in peers:
        pl.semaphore_signal(barrier, inc=1, device_id=p, device_id_type=MESH)
    pl.semaphore_wait(barrier, len(peers))


def remote(src, dst, send, recv, to):
    return pltpu.make_async_remote_copy(
        src_ref=src,
        dst_ref=dst,
        send_sem=send,
        recv_sem=recv,
        device_id=to,
        device_id_type=MESH,
    )


class Place:
    def __init__(self, n, nd):
        self.n, self.nd, self.nz = n, nd, n // CORES
        self.dp, self.me = lax.axis_index("dp"), lax.axis_index("tensor")
        self.z, self.core = self.me // CORES, lax.rem(self.me, CORES)
        self.orders = orders_of(nd)
        self.far = sorted(range(1, self.nz), key=lambda o: min(o, self.nz - o))

    def chip(self, step):
        return lax.rem(self.z + step + self.nz, self.nz)

    def on_chip(self, step):
        return (self.dp, self.chip(step) * CORES + self.core)

    def twin(self):
        return (self.dp, self.z * CORES + 1 - self.core)

    def flip(self, bit):
        return (self.dp ^ (1 << bit), self.me)

    def line(self):
        return [(self.dp, lax.rem(self.me + o, self.n)) for o in range(1, self.n)]

    def greet_all(self):
        greet(self.line() + [self.flip(b) for b in range(bits_of(self.nd))])


def bits_of(nd):
    return nd.bit_length() - 1


def orders_of(nd):
    m = bits_of(nd)
    return [list(range(m)), [(m // 2 + i) % m for i in range(m)]]


def spread_plan(order):
    plan = [(0, list(order))]
    for i, bit in enumerate(order):
        plan += [(rel | (1 << bit), list(order[i + 1 :])) for rel, _ in list(plan)]
    return plan


class Spread:
    def __init__(self, place, ref_of, send, recv):
        self.place, self.ref_of, self.send, self.recv = place, ref_of, send, recv
        self.levels = bits_of(place.nd)

    def sends(self, part, rel, bits):
        p = self.place
        ref = self.ref_of(part, p.dp ^ rel)
        for bit in bits:
            to = rel | (1 << bit)
            yield remote(ref, ref, self.send.at[part, to], self.recv.at[part, to], p.flip(bit))

    def arrived(self, level):
        for part, order in enumerate(self.place.orders):
            for rel, bits in spread_plan(order):
                if rel and len(order) - 1 - len(bits) == level:
                    yield part, rel, bits

    def begin(self):
        for part, order in enumerate(self.place.orders):
            for c in self.sends(part, 0, order):
                c.start()

    def step(self, level):
        p = self.place
        for part, rel, bits in self.arrived(level):
            ref = self.ref_of(part, p.dp ^ rel)
            remote(
                ref, ref, self.send.at[part, rel], self.recv.at[part, rel], p.flip(0)
            ).wait_recv()
            for c in self.sends(part, rel, bits):
                c.start()

    def end(self):
        for part, order in enumerate(self.place.orders):
            for rel, bits in spread_plan(order):
                for c in self.sends(part, rel, bits):
                    c.wait_send()


class Line:
    def __init__(self, place, own, ref_of, send, recv):
        self.p, self.own, self.ref_of, self.send, self.recv = place, own, ref_of, send, recv
        self.ways = (1, -1)

    def inside(self, z):
        return (z >= 0) & (z < self.p.nz)

    def source(self, w, step):
        z = self.p.z - self.ways[w] * step
        return jnp.clip(z, 0, self.p.nz - 1), self.inside(z)

    def copy(self, w, step):
        p = self.p
        to = p.z + self.ways[w]
        chip, have = self.source(w, step - 1)
        src = self.own if step == 1 else self.ref_of(chip)
        c = remote(
            src,
            self.ref_of(chip),
            self.send.at[w, step],
            self.recv.at[w, step],
            (p.dp, jnp.clip(to, 0, p.nz - 1) * CORES + p.core),
        )
        return c, have & self.inside(to)

    def start(self, step=1):
        for w in range(2):
            c, do = self.copy(w, step)
            pl.when(do)(c.start)

    def got(self, step, then):
        for w in range(2):
            chip, have = self.source(w, step)
            to = self.p.z + self.ways[w]
            ref = self.ref_of(chip)
            wait = remote(
                ref, ref, self.send.at[w, step], self.recv.at[w, step], self.p.twin()
            )
            on, more = None, None
            if step + 1 < self.p.nz:
                on, more = self.copy(w, step + 1)

            @pl.when(have)
            def _():
                wait.wait_recv()
                if on is not None:
                    pl.when(more)(on.start)
                then(w, chip)

    def each(self, step, do):
        for w in range(2):
            chip, have = self.source(w, step)
            pl.when(have)(functools.partial(do, w, chip))

    def end(self):
        for step in range(1, self.p.nz):
            for w in range(2):
                c, do = self.copy(w, step)
                pl.when(do)(c.wait_send)


def picks_of(seg):
    return (seg == lax.broadcasted_iota(jnp.int32, (seg.shape[0], 8), 1)).astype(bf16)


def two(x):
    high = x.astype(bf16)
    return high, (x - high.astype(f32)).astype(bf16)


def per_token(picks, table):
    high, low = two(table)
    return dot(picks, high) + dot(picks, low)


def per_item(picks, values):
    high, low = two(values)
    return dot(picks, high, 0, 0) + dot(picks, low, 0, 0)


def norm_parts(values):
    centred = values - jnp.mean(values, axis=-1, keepdims=True)
    rstd = lax.rsqrt(jnp.mean(centred * centred, axis=-1, keepdims=True) + epsilon)
    return centred * rstd, rstd


def norm_back(normal, rstd, scaled):
    return rstd * (
        scaled
        - jnp.mean(scaled, axis=-1, keepdims=True)
        - normal * jnp.mean(scaled * normal, axis=-1, keepdims=True)
    )


GAMMA_ONE, GAMMA_TWO, SCALE_ONE, SCALE_TWO, SHIFT_ONE, SHIFT_TWO = range(6)


def half_lanes(rows):
    return lax.broadcasted_iota(jnp.int32, (rows, LANES), 1) < HEAD


def half_sums(x):
    low = half_lanes(x.shape[0])
    a = jnp.sum(jnp.where(low, x, 0.0), axis=1, keepdims=True)
    b = jnp.sum(jnp.where(low, 0.0, x), axis=1, keepdims=True)
    return jnp.where(low, a, b)


def one_half(x, h):
    low = half_lanes(x.shape[0])
    return jnp.where(low if h == 0 else jnp.logical_not(low), x, jnp.zeros_like(x))


def ranks_at(lengths_ref, owner, tok, shape, axis):
    place = jnp.maximum(owner, 0) * tok + lax.broadcasted_iota(jnp.int32, shape, axis)
    item = jnp.zeros(shape, jnp.int32)
    begin = jnp.zeros(shape, jnp.int32)
    end = jnp.int32(0)
    for i in range(SEGS):
        end = end + lengths_ref[i]
        past = place >= end
        item = item + past.astype(jnp.int32)
        begin = jnp.where(past, end, begin)
    rank = item * 16
    for threshold in scale_starts:
        rank = rank + (place - begin >= threshold).astype(jnp.int32)
    there = owner >= 0
    return item, jnp.where(there, rank, -1)


def owners_of(p, steps):
    owners = []
    for s in [(0, 0)] + list(steps):
        for flip in range(CORES):
            c = p.core ^ flip
            far = [p.nz if v is None else v for v in s]
            chip = p.z - jnp.where(c == 0, far[0], far[1])
            owners.append(jnp.where((chip >= 0) & (chip < p.nz), chip * CORES + c, -1))
    return owners


def seen_lists(steps, tok):
    lists = []
    for qi in range(CORES):
        seen = set()
        for c in range(CORES):
            query = c ^ qi
            for i, s in enumerate([(0, 0)] + list(steps)):
                for flip in range(CORES):
                    owner = c ^ flip
                    if s[owner] is None:
                        continue
                    off = owner - s[owner] * CORES - query
                    near = off == 0
                    behind = off < 0 and (-off - 1) * tok + 1 <= BEHIND
                    ahead = off > 0 and (off - 1) * tok + 1 <= AHEAD
                    if near or behind or ahead:
                        seen.add(2 * i + flip)
        lists.append(seen)
    both = sorted(lists[0] & lists[1])
    rest = [sorted(v - set(both)) for v in lists]
    size = max(len(r) for r in rest)
    for r in rest:
        spare = [b for b in range(2 * len(steps) + 2) if b not in both and b not in r]
        r += spare[: size - len(r)]
    return [both + rest[0], both + rest[1]]


def block_at(lists, qi, j):
    a, b = lists[0][j], lists[1][j]
    return a if a == b else jnp.where(qi == 0, a, b)


def forward_body(
    n, nd, steps, width, len_ref, tok_ref, grad_ref, part_ref, extra_ref, abias_ref, pb_ref,
    apack_ref, mpack_ref,
    n_out, q_out, k_out, v_out, o_ref, l_ref, wa_out, wm_ref, branch_ref, resid_ref, nwide_ref,
    gwide_ref, mod_ref, ehs_ref,
    win, wa, modc, held, normed, qv, kv, vv, qb, vb, masks, ku, v0, v1, theirs, got,
    s1, r1, s2, r2, ts, tr, cs, cr, azs, azr, mzs, mzr, local_sem, out_sem, das, dar, dms, dmr,
    ms, mr,
):
    p = Place(n, nd)
    nz, tok = p.nz, grad_ref.shape[0]
    rounds = len(steps)
    blocks = 2 * rounds + 2
    pairs = qv.shape[0]
    merge = LANES // width
    rows = 4 * width // nd
    half = D // 2
    chunk = modc.shape[2]
    owners = owners_of(p, steps)
    p.greet_all()
    line = p.line()

    a_at = lambda chip, d: wa.at[chip, pl.ds(d * rows, rows)]
    mine = pl.ds(p.dp * rows, rows)
    al = Line(p, apack_ref.at[mine], lambda chip: wa.at[chip, mine], azs, azr)
    ml = Line(p, mpack_ref.at[:, p.dp], lambda chip: wm_ref.at[chip, :, p.dp], mzs, mzr)

    def a_spread(w, step, chip):
        return Spread(
            p,
            lambda part, d: wa.at[chip, pl.ds(d * rows, rows), pl.ds(part * half, half)],
            das.at[w, step],
            dar.at[w, step],
        )

    def m_spread(w, step, chip):
        return Spread(
            p, lambda part, d: wm_ref.at[chip, part, d], dms.at[w, step], dmr.at[w, step]
        )

    al.start()
    owns = [
        pltpu.make_async_copy(tok_ref, win.at[0], local_sem.at[0]),
        pltpu.make_async_copy(apack_ref, wa.at[p.z], local_sem.at[1]),
        pltpu.make_async_copy(mpack_ref, wm_ref.at[p.z], local_sem.at[2]),
    ]
    for c in owns:
        c.start()
    sums = [
        remote(part_ref.at[q[1]], held.at[o], s1.at[o], r1.at[o], q) for o, q in enumerate(line)
    ]
    for c in sums:
        c.start()
    twins = [
        remote(tok_ref if i == 0 else win.at[2 * i], win.at[2 * i + 1], cs.at[i], cr.at[i], p.twin())
        for i in range(rounds + 1)
    ]
    twins[0].start()
    for c in sums:
        c.wait()
    total = part_ref[p.me] + extra_ref[...] + abias_ref[p.me]
    for o in range(n - 1):
        total = total + held[o]
    modc[p.me] = total
    sums = [
        remote(modc.at[p.me], modc.at[p.me], s2.at[o], r2.at[o], q) for o, q in enumerate(line)
    ]
    for c in sums:
        c.start()
    moves = []
    for i, per_core in enumerate(steps):
        for c, step in enumerate(per_core):
            if step is None:
                continue
            go = (p.core == c) & (p.z + step >= 0) & (p.z + step < nz)
            have = (p.core == c) & (p.z - step >= 0) & (p.z - step < nz)
            to = (p.dp, jnp.clip(p.z + step, 0, nz - 1) * CORES + p.core)
            moves.append((i, go, have, remote(tok_ref, win.at[2 * i + 2], ts.at[i, c], tr.at[i, c], to)))
    al.got(1, lambda w, chip: a_spread(w, 1, chip).begin())
    for i, go, have, copy in moves:
        pl.when(go)(copy.start)
    for step in range(2, nz):
        al.got(step, lambda w, chip: a_spread(w, step, chip).begin())
    ml.start()

    for c in sums:
        c.wait()
    for j in range(n):
        mod_ref[:, j * chunk : (j + 1) * chunk] = modc[j]
    table = lambda which: mod_ref[:, which * D : (which + 1) * D]
    for s in range(pairs):
        parts = []
        for i in range(merge):
            r = modc[(s * merge + i) * CORES + p.core, SEGS : SEGS + 1, :]
            parts.append([r[:, k * width : (k + 1) * width] for k in range(3)])
        row = lambda k: jnp.concatenate([v[k] for v in parts], axis=1) if merge > 1 else parts[0][k]
        qb[s], vb[s], ehs_ref[s] = row(0), row(1), row(2)

    lists = seen_lists(steps, tok)
    for qi in range(CORES):
        owner = owners[qi]
        item, rank = ranks_at(len_ref, owner, tok, (tok, LANES), 0)
        lo, hi = item[:, :1] * 16, rank[:, :1]
        for j, b in enumerate(lists[qi]):
            _, e = ranks_at(len_ref, owners[b], tok, (8, tok), 1)
            e = e[:1]
            masks[qi, j] = jnp.where((e >= lo) & (e <= hi), 0.0, -1e30)
    own_item, _ = ranks_at(len_ref, owners[0], tok, (tok, 8), 0)
    picks = (own_item == lax.broadcasted_iota(jnp.int32, (tok, 8), 1)).astype(bf16)

    gwide_ref[0] = (per_token(picks, table(GAMMA_TWO)) * grad_ref[...].astype(f32)).astype(bf16)
    cross = [
        remote(gwide_ref.at[0], gwide_ref.at[1], ms.at[0], mr.at[0], p.twin()),
        remote(theirs, got, ms.at[1], mr.at[1], p.twin()),
        remote(nwide_ref.at[0], nwide_ref.at[1], ms.at[2], mr.at[2], p.twin()),
    ]
    cross[0].start()

    owns[0].wait()
    twins[0].wait()

    def norm_block(b):
        owner = owners[0]
        for i in range(1, blocks):
            owner = jnp.where(b == i, owners[i], owner)
        item, _ = ranks_at(len_ref, owner, tok, (tok, 8), 0)
        pick = (item == lax.broadcasted_iota(jnp.int32, (tok, 8), 1)).astype(bf16)
        normal, _ = norm_parts(win[b].astype(f32))
        scale = per_token(pick, table(SCALE_ONE))
        shift = per_token(pick, table(SHIFT_ONE))
        at = pl.ds(pl.multiple_of(b * tok, tok), tok)
        normed[at, :] = (normal * (1.0 + scale) + shift).astype(bf16)

    def weight(s, k, count=1):
        if merge == 1:
            return wa[s, k * width : (k + count) * width, :]
        rows_of = [
            wa[s * merge + i, (k + j) * width : (k + j + 1) * width, :]
            for j in range(count)
            for i in range(merge)
        ]
        return jnp.concatenate(rows_of, axis=0)

    def keys_block(b):
        at = pl.ds(pl.multiple_of(b * tok, tok), tok)

        def slot(s, _):
            r = dot(normed[at, :], weight(s, 1, 2), 1, 1)
            kv[s, at, :] = r[:, :LANES]
            vv[s, at, :] = (r[:, LANES:] + vb[s]).astype(bf16)
            return 0

        lax.fori_loop(0, pairs, slot, 0)

    @pl.loop(0, CORES)
    def _(b):
        norm_block(b)

    for level in range(bits_of(nd)):
        for step in range(1, nz):
            al.each(step, lambda w, chip: a_spread(w, step, chip).step(level))
    owns[1].wait()
    wout = pltpu.make_async_copy(wa, wa_out, out_sem.at[0])
    wout.start()

    @pl.loop(0, CORES)
    def _(b):
        keys_block(b)
        at = pl.ds(pl.multiple_of(b * tok, tok), tok)

        def slot(s, _):
            qv[s, at, :] = dot(normed[at, :], weight(s, 0), 1, 1) + qb[s]
            return 0

        lax.fori_loop(0, pairs, slot, 0)

    for i in range(rounds):
        any_got = p.core < 0
        for j, go, have, copy in moves:
            if j == i:
                pl.when(have)(copy.wait_recv)
                any_got = any_got | have

        @pl.when(jnp.logical_not(any_got))
        def _():
            win[2 * i + 2] = jnp.zeros((tok, D), bf16)

        twins[i + 1].start()
    for i in range(rounds):
        twins[i + 1].wait()

    @pl.loop(CORES, blocks)
    def _(b):
        norm_block(b)
        keys_block(b)

    outs = [wout]
    for i, (src, dst) in enumerate(((normed, n_out), (qv, q_out), (kv, k_out), (vv, v_out))):
        outs.append(pltpu.make_async_copy(src, dst, out_sem.at[i + 1]))
        outs[-1].start()

    ml.got(1, lambda w, chip: m_spread(w, 1, chip).begin())
    trips = pairs * CORES
    agenda = {}
    for step in range(1, nz):
        at = min(trips - 1, (step * trips) // nz)
        agenda.setdefault(at, []).append(step)

    @pl.loop(0, trips)
    def _(it):
        s, qi = it // CORES, lax.rem(it, CORES)

        @pl.when(qi == 0)
        def _():
            k = kv[s]
            ku[...] = (k * lax.rsqrt(half_sums(k * k) + epsilon)).astype(bf16)
            v = vv[s]
            low = half_lanes(v.shape[0])
            one = jnp.ones_like(v)
            v0[...] = jnp.where(low, v, one)
            v1[...] = jnp.where(low, one, v)

        at = pl.ds(pl.multiple_of(qi * tok, tok), tok)
        q = qv[s, at, :]
        qu = (q * lax.rsqrt(half_sums(q * q) + epsilon) * ehs_ref[s]).astype(bf16)
        qs = [one_half(qu, h) for h in range(2)]
        acc = [None, None]
        for j in range(len(lists[0])):
            b = block_at(lists, qi, j)
            cols = pl.ds(pl.multiple_of(b * tok, tok), tok)
            mask = masks[qi, j]
            for h in range(2):
                w = jnp.exp(dot(qs[h], ku[cols, :], 1, 1) + mask).astype(bf16)
                r = dot(w, (v0 if h == 0 else v1)[cols, :])
                acc[h] = r if acc[h] is None else acc[h] + r
        low = half_lanes(tok)
        other = jnp.where(low, pltpu.roll(acc[0], HEAD, 1), pltpu.roll(acc[1], HEAD, 1))
        o_ref[s, at, :] = (jnp.where(low, acc[0], acc[1]) / other).astype(bf16)
        turned = other.T
        l_ref[s, 0:1, at] = turned[0:1, :]
        l_ref[s, 1:2, at] = turned[HEAD : HEAD + 1, :]

        for when, todo in agenda.items():

            @pl.when(it == when)
            def _():
                for step in todo:
                    if step + 1 < nz:
                        ml.got(step + 1, lambda w, chip: m_spread(w, step + 1, chip).begin())
                    ml.each(step, lambda w, chip: m_spread(w, step, chip).step(0))

    def project(at):
        total = dot(o_ref[0, at, :], weight(0, 3))
        for s in range(1, pairs):
            total += dot(o_ref[s, at, :], weight(s, 3))
        return total

    theirs[...] = project(pl.ds(tok, tok)).astype(bf16)
    cross[1].start()
    first = project(pl.ds(0, tok)) + pb_ref[...]
    cross[1].wait()
    branch = first + got[...].astype(f32)
    branch_ref[...] = branch
    resid = win[0].astype(f32) + per_token(picks, table(GAMMA_ONE)) * branch
    resid_ref[...] = resid
    normal, _ = norm_parts(resid)
    scale = per_token(picks, table(SCALE_TWO))
    shift = per_token(picks, table(SHIFT_TWO))
    nwide_ref[0] = (normal * (1.0 + scale) + shift).astype(bf16)
    cross[2].start()

    for level in range(1, bits_of(nd)):
        for step in range(1, nz):
            ml.each(step, lambda w, chip: m_spread(w, step, chip).step(level))
    cross[0].wait()
    cross[2].wait()
    for step in range(1, nz):
        al.each(step, lambda w, chip: a_spread(w, step, chip).end())
        ml.each(step, lambda w, chip: m_spread(w, step, chip).end())
    al.end()
    ml.end()
    for i, go, have, copy in moves:
        pl.when(go)(copy.wait_send)
    owns[2].wait()
    for c in outs:
        c.wait()


def forward(lengths, tokens, out_grad, part, extra, abias, proj_bias, apack, mpack, steps, nd, width):
    n, _, cols = part.shape
    nz = n // CORES
    tok = tokens.shape[0]
    rounds = len(steps)
    blocks = 2 * rounds + 2
    t, w = CORES * tok, blocks * tok
    pairs = nz * width // LANES
    seen = len(seen_lists(steps, tok)[0])
    dma = pltpu.SemaphoreType.DMA
    vmem = pl.BlockSpec(memory_space=pltpu.VMEM)
    anywhere = pl.BlockSpec(memory_space=pl.ANY)
    out = lambda *shape: jax.ShapeDtypeStruct(shape, f32)
    low = lambda *shape: jax.ShapeDtypeStruct(shape, bf16)
    v = pltpu.VMEM
    return pl.pallas_call(
        functools.partial(forward_body, n, nd, steps, width),
        out_shape=[
            low(w, D),
            out(pairs, t, LANES),
            out(pairs, w, LANES),
            low(pairs, w, LANES),
            low(pairs, t, LANES),
            out(pairs, 8, t),
            low(nz, 4 * width, D),
            low(nz, *mpack.shape),
            out(tok, D),
            out(tok, D),
            low(CORES, tok, D),
            low(CORES, tok, D),
            out(8, 6 * D),
            out(pairs, 1, LANES),
        ],
        in_specs=[pl.BlockSpec(memory_space=pltpu.SMEM), anywhere]
        + [vmem] * 5
        + [anywhere] * 2,
        out_specs=[anywhere] * 4 + [vmem] * 2 + [anywhere] * 2 + [vmem] * 6,
        scratch_shapes=[
            v((blocks, tok, D), bf16),
            v((nz, 4 * width, D), bf16),
            v(part.shape, f32),
            v((n - 1,) + part.shape[1:], f32),
            v((w, D), bf16),
            v((pairs, t, LANES), f32),
            v((pairs, w, LANES), f32),
            v((pairs, w, LANES), bf16),
            v((pairs, 1, LANES), f32),
            v((pairs, 1, LANES), f32),
            v((CORES, seen, tok, tok), f32),
            v((w, LANES), bf16),
            v((w, LANES), bf16),
            v((w, LANES), bf16),
            v((tok, D), bf16),
            v((tok, D), bf16),
            dma((n - 1,)),
            dma((n - 1,)),
            dma((n - 1,)),
            dma((n - 1,)),
            dma((rounds, CORES)),
            dma((rounds, CORES)),
            dma((rounds + 1,)),
            dma((rounds + 1,)),
            dma((2, nz)),
            dma((2, nz)),
            dma((2, nz)),
            dma((2, nz)),
            dma((3,)),
            dma((5,)),
            dma((2, nz, 2, nd)),
            dma((2, nz, 2, nd)),
            dma((2, nz, 2, nd)),
            dma((2, nz, 2, nd)),
            dma((3,)),
            dma((3,)),
        ],
        compiler_params=pltpu.CompilerParams(
            collective_id=0, has_side_effects=True, vmem_limit_bytes=VMEM_LIMIT
        ),
        name="forward",
    )(lengths, tokens, out_grad, part, extra, abias, proj_bias, apack, mpack)


def mlp_body(x_ref, g_ref, w_ref, bias_ref, mine_ref, theirs_ref, dw_ref, dbias_ref, mlp, gx):
    x, g = x_ref[...], g_ref[...]
    tok = mine_ref.shape[1]
    units = w_ref.shape[2] * w_ref.shape[3]
    up = w_ref[0, 0].reshape(units, D)
    down = w_ref[0, 1].reshape(units, D)
    pre = dot(x, up, 1, 1) + bias_ref[0]
    square = pre * pre
    th = jnp.tanh(0.7978845608028654 * pre * (1.0 + 0.044715 * square))
    half = 0.5 * (1.0 + th)
    hidden = (pre * half).astype(bf16)
    slope = half + 0.5 * pre * (1.0 - th * th) * (
        0.7978845608028654 * (1.0 + 3.0 * 0.044715 * square)
    )
    gp = (dot(g, down, 1, 1) * slope).astype(bf16)

    @pl.when(pl.program_id(0) == 0)
    def _():
        mlp[...] = jnp.zeros_like(mlp)
        gx[...] = jnp.zeros_like(gx)

    mlp[...] += dot(hidden, down)
    gx[...] += dot(gp, up)
    dw_ref[0, 0] = dot(gp, x, 0, 0).astype(bf16).reshape(dw_ref.shape[2:])
    dw_ref[0, 1] = dot(hidden, g, 0, 0).astype(bf16).reshape(dw_ref.shape[2:])
    dbias_ref[0] = jnp.sum(gp.astype(f32), axis=0, keepdims=True)

    @pl.when(pl.program_id(0) == pl.num_programs(0) - 1)
    def _():
        for i, v in enumerate((gx, mlp)):
            mine_ref[i] = v[:tok, :]
            theirs_ref[i] = v[tok:, :].astype(bf16)


def mlp(x, g, weights, bias):
    t = x.shape[0]
    tok = t // CORES
    nz, _, nd, piece, _ = weights.shape
    count = min(nd, max(1, 256 // piece))
    per = nd // count
    steps, units = nz * per, count * piece
    whole = lambda *shape: pl.BlockSpec(shape, lambda i: (0,) * len(shape))
    block = pl.BlockSpec((1, 2, count, piece, D), lambda i: (i // per, 0, i % per, 0, 0))
    row = pl.BlockSpec((1, 1, units), lambda i: (i, 0, 0))
    return pl.pallas_call(
        mlp_body,
        grid=(steps,),
        in_specs=[whole(t, D), whole(t, D), block, row],
        out_specs=[whole(2, tok, D), whole(2, tok, D), block, row],
        out_shape=[
            jax.ShapeDtypeStruct((2, tok, D), f32),
            jax.ShapeDtypeStruct((2, tok, D), bf16),
            jax.ShapeDtypeStruct(weights.shape, bf16),
            jax.ShapeDtypeStruct((steps, 1, units), f32),
        ],
        scratch_shapes=[pltpu.VMEM((t, D), f32), pltpu.VMEM((t, D), f32)],
        compiler_params=pltpu.CompilerParams(vmem_limit_bytes=VMEM_LIMIT),
        name="mlp",
    )(x, g, weights, bias.reshape(steps, 1, units))


class Reduce:
    def __init__(self, place, sent, kept, stage, zstage, final, out, sems):
        self.p, self.sent, self.kept = place, sent, kept
        self.stage, self.zstage, self.final = stage, zstage, final
        self.ps, self.pr, self.zs, self.zr, self.os, self.or_, self.fs = sems
        self.m = bits_of(place.nd)
        self.back = Spread(place, out, self.os, self.or_)
        self.out = out

    def held(self, part, level):
        rels = list(range(self.p.nd))
        for bit in self.p.orders[part][:level]:
            rels = [r for r in rels if not (r >> bit) & 1]
        return rels

    def current(self, part, level, chip, rel):
        if level == 0:
            bit = self.p.orders[part][0]
            return (self.sent if (rel >> bit) & 1 else self.kept)(part, chip, self.p.dp ^ rel)
        return self.stage(part, level - 1, chip, self.held(part, level).index(rel))

    def plane(self, level, chip):
        for part, order in enumerate(self.p.orders):
            bit = order[level]
            for rel in self.held(part, level):
                if (rel >> bit) & 1:
                    slot = self.held(part, level + 1).index(rel ^ (1 << bit))
                    yield remote(
                        self.current(part, level, chip, rel),
                        self.stage(part, level, chip, slot),
                        self.ps.at[part, level, chip, slot],
                        self.pr.at[part, level, chip, slot],
                        self.p.flip(bit),
                    )

    def send_plane(self, level, chip):
        for c in self.plane(level, chip):
            c.start()

    def add_plane(self, level, chip):
        for c in self.plane(level, chip):
            c.wait_recv()
        for part in range(2):
            for slot, rel in enumerate(self.held(part, level + 1)):
                room = self.stage(part, level, chip, slot)
                mine = self.current(part, level, chip, rel)
                room[...] = (room[...].astype(f32) + mine[...].astype(f32)).astype(bf16)

    def line(self, o):
        for part in range(2):
            yield part, remote(
                self.stage(part, self.m - 1, self.p.chip(o), 0),
                self.zstage(part, o),
                self.zs.at[part, o],
                self.zr.at[part, o],
                self.p.on_chip(o),
            )

    def advance(self, level, then=None):
        for o in self.p.far + [0]:
            self.add_plane(level, self.p.chip(o))
            if level + 1 < self.m:
                self.send_plane(level + 1, self.p.chip(o))
            elif o:
                for _, c in self.line(o):
                    c.start()

    def end_line(self):
        p = self.p
        for o in p.far:
            for _, c in self.line(o):
                c.wait_recv()
        puts = []
        for part in range(2):
            total = self.stage(part, self.m - 1, p.z, 0)[...].astype(f32)
            for o in p.far:
                total = total + self.zstage(part, o)[...].astype(f32)
            self.final(part)[...] = total.astype(bf16)
            puts.append(
                pltpu.make_async_copy(self.final(part), self.out(part, p.dp), self.fs.at[part])
            )
            puts[-1].start()
        for c in puts:
            c.wait()
        self.back.begin()

    def end(self):
        for level in range(self.m):
            for chip in range(self.p.nz):
                for c in self.plane(level, chip):
                    c.wait_send()
        for o in self.p.far:
            for _, c in self.line(o):
                c.wait_send()
        self.back.end()


def backward_body(
    n, nd, steps, width, len_ref, mine_ref, theirs_ref, x_ref, g_ref, gm_ref, branch_ref, mod_ref,
    db_ref, dbias_ref, hist_ref, extra_ref, l_ref, ehs_ref, dm_ref, n_hbm, q_hbm, k_hbm, v_hbm,
    o_hbm, wa_hbm,
    out_ref, ym_ref, ya_ref, tg_ref, small_ref,
    got, awide, spare, normed, wp, qs_, ks_, vs_, os_, ku, kut, dk, dv, gqs, gkv, masks,
    dmk, mstage, mz, mfinal, da, astage, az, afinal, gmine, ghalo, pay, part, held,
    xs, xr, load, wl, ld, mks,
    mps, mpr, mzs, mzr, mos, mor, mfs, aps, apr, azs, azr, aos, aor, afs,
    gs, gr, hs, hr, s1, r1, s2, r2, s3, r3, s4, r4,
):
    p = Place(n, nd)
    nz, tok = p.nz, x_ref.shape[0]
    rounds = len(steps)
    blocks = 2 * rounds + 2
    pairs = l_ref.shape[0]
    merge = LANES // width
    arows = 4 * width // nd
    units = dbias_ref.shape[1]
    t = CORES * tok
    half = D // 2
    m = bits_of(nd)
    chunk = 6 * D // n
    owners = owners_of(p, steps)
    table = lambda which: mod_ref[:, which * D : (which + 1) * D]

    def base(level):
        return sum(nd >> (i + 1) for i in range(level))

    def kept_slot(q, d):
        bit = p.orders[q][0]
        return ((d >> (bit + 1)) << bit) | (d & ((1 << bit) - 1))

    cut = lambda q: pl.ds(q * half, half)
    rm = Reduce(
        p,
        lambda q, chip, d: dm_ref.at[chip, q, d],
        lambda q, chip, d: dmk.at[q, chip, kept_slot(q, d)],
        lambda q, level, chip, slot: mstage.at[q, base(level) + slot, chip],
        lambda q, o: mz.at[q, o - 1],
        lambda q: mfinal.at[q],
        lambda q, d: ym_ref.at[q, d],
        (mps, mpr, mzs, mzr, mos, mor, mfs),
    )
    a_own = lambda q, chip, d: da.at[chip, pl.ds(d * arows, arows), cut(q)]
    ra = Reduce(
        p,
        a_own,
        a_own,
        lambda q, level, chip, slot: astage.at[q, base(level) + slot, chip],
        lambda q, o: az.at[q, o - 1],
        lambda q: afinal.at[q],
        lambda q, d: ya_ref.at[pl.ds(d * arows, arows), cut(q)],
        (aps, apr, azs, azr, aos, aor, afs),
    )
    p.greet_all()
    far = p.far + [0]
    swaps = [remote(theirs_ref.at[i], got.at[i], xs.at[i], xr.at[i], p.twin()) for i in range(2)]
    swaps.append(remote(awide.at[0], awide.at[1], xs.at[2], xr.at[2], p.twin()))
    swaps[0].start()
    swaps[1].start()
    for o in far:
        rm.send_plane(0, p.chip(o))
    loads = [
        pltpu.make_async_copy(wa_hbm.at[:, pl.ds(3 * width, width)], wp, load.at[0]),
        pltpu.make_async_copy(n_hbm, normed.at[pl.ds(0, blocks * tok)], load.at[1]),
    ]
    for c in loads:
        c.start()

    def fetch(s, slot):
        return [
            pltpu.make_async_copy(src.at[s], dst.at[slot], ld.at[i, slot])
            for i, (src, dst) in enumerate(
                ((q_hbm, qs_), (k_hbm, ks_), (v_hbm, vs_), (o_hbm, os_))
            )
        ]

    for c in fetch(0, 0):
        c.start()
    keeps = []
    for q in range(2):
        for rel in rm.held(q, 1):
            d = p.dp ^ rel
            keeps.append(
                pltpu.make_async_copy(
                    dm_ref.at[:, q, d], dmk.at[q, :, kept_slot(q, d)], mks.at[q, rel]
                )
            )
            keeps[-1].start()

    item, _ = ranks_at(len_ref, owners[0], tok, (tok, 8), 0)
    picks = (item == lax.broadcasted_iota(jnp.int32, (tok, 8), 1)).astype(bf16)
    gamma_one = per_token(picks, table(GAMMA_ONE))
    resid = x_ref[...].astype(f32) + gamma_one * branch_ref[...]
    normal, rstd = norm_parts(resid)
    scale = per_token(picks, table(SCALE_TWO))
    grad_final = g_ref[...].astype(f32)
    swaps[0].wait()
    second = mine_ref[0] + got[0].astype(f32)
    mid = grad_final + norm_back(normal, rstd, second * (1.0 + scale))
    tg_ref[...] = mid
    attn = (gamma_one * mid).astype(bf16)
    awide[0] = attn
    swaps[2].start()
    pay[...] = jnp.zeros_like(pay)

    def put_items(which, values):
        pay[:, which * D : (which + 1) * D] = per_item(picks, values)

    put_items(SCALE_TWO, second * normal)
    put_items(SHIFT_TWO, second)
    put_items(GAMMA_ONE, mid * branch_ref[...])
    swaps[1].wait()
    mlp_branch = mine_ref[1] + got[1].astype(f32) + db_ref[...]
    out_ref[...] = (resid + per_token(picks, table(GAMMA_TWO)) * mlp_branch).astype(bf16)
    put_items(GAMMA_TWO, grad_final * mlp_branch)
    row_six = SEGS
    pay[row_six : row_six + 1, :D] = jnp.sum(attn.astype(f32), axis=0, keepdims=True)
    pay[row_six : row_six + 1, D : 2 * D] = jnp.sum(
        gm_ref[...].astype(f32), axis=0, keepdims=True
    )
    pay[row_six : row_six + 1, 2 * D :] = hist_ref[...]
    row = pl.ds(SEGS + 1, 1)
    for z in range(nz):
        at = pl.multiple_of((p.core * nz + z) * units, LANES)
        pay[row, pl.ds(at, units)] = dbias_ref[z : z + 1, :]
    part[:, :, chunk:] = jnp.zeros((n, 8, LANES), f32)

    lists = seen_lists(steps, tok)
    for qi in range(CORES):
        item, rank = ranks_at(len_ref, owners[qi], tok, (8, tok), 1)
        lo, hi = item[:1] * 16, rank[:1]
        for j, b in enumerate(lists[qi]):
            _, e = ranks_at(len_ref, owners[b], tok, (tok, LANES), 0)
            e = e[:, :1]
            masks[qi, j] = jnp.where((e >= lo) & (e <= hi), 0.0, -1e30).astype(bf16)

    def proj_rows(s):
        if merge == 1:
            return wp[s]
        return jnp.concatenate([wp[s * merge + i] for i in range(merge)], axis=0)

    def weight(s, k, count=1):
        at = lambda i, j: normed[((s * merge + i) * 3 + j) * width : ((s * merge + i) * 3 + j + 1) * width, :]
        if merge == 1:
            return normed[(s * 3 + k) * width : (s * 3 + k + count) * width, :]
        rows_of = [at(i, k + j) for j in range(count) for i in range(merge)]
        return jnp.concatenate(rows_of, axis=0)

    def put_grad(s, k, value):
        for i in range(merge):
            da[s * merge + i, k * width : (k + 1) * width, :] = value[
                i * width : (i + 1) * width
            ].astype(bf16)

    loads[0].wait()
    loads[1].wait()
    swaps[2].wait()

    @pl.loop(0, pairs * CORES)
    def _(it):
        s, qi = it // CORES, lax.rem(it, CORES)
        slot = lax.rem(s, 2)

        @pl.when(qi == 0)
        def _():
            for c in fetch(s, slot):
                c.wait()

            @pl.when(s + 1 < pairs)
            def _():
                for c in fetch(s + 1, 1 - slot):
                    c.start()

            k = ks_[slot]
            unit = k * lax.rsqrt(half_sums(k * k) + epsilon)
            ku[...] = unit.astype(bf16)
            kut[...] = unit.T.astype(bf16)
            dk[...] = jnp.zeros_like(dk)
            dv[...] = jnp.zeros_like(dv)

        at = pl.ds(pl.multiple_of(qi * tok, tok), tok)
        ehs = ehs_ref[s]
        q = qs_[slot, at, :]
        rq = lax.rsqrt(half_sums(q * q) + epsilon)
        qhat = q * rq
        qu = (qhat * ehs).astype(bf16)
        qs = [one_half(qu, h) for h in range(2)]
        g = dot(awide[qi], proj_rows(s), 1, 1).astype(bf16)
        gs_h = [one_half(g, h) for h in range(2)]
        turned = (g.astype(f32) * os_[slot, at, :].astype(f32)).T
        deltas = [
            jnp.sum(turned[:HEAD], axis=0, keepdims=True),
            jnp.sum(turned[HEAD:], axis=0, keepdims=True),
        ]
        invs = [1.0 / l_ref[s, h : h + 1, at] for h in range(2)]
        dqt = [None, None]
        for j in range(len(lists[0])):
            b = block_at(lists, qi, j)
            cols = pl.ds(pl.multiple_of(b * tok, tok), tok)
            mask = masks[qi, j].astype(f32)
            kb, vb = ku[cols, :], vs_[slot, cols, :]
            dvs, dks = None, None
            for h in range(2):
                w = jnp.exp(dot(kb, qs[h], 1, 1) + mask) * invs[h]
                dp = dot(vb, gs_h[h], 1, 1)
                ds = (w * (dp - deltas[h])).astype(bf16)
                a = dot(w.astype(bf16), gs_h[h])
                c = dot(ds, qs[h])
                dvs = a if h == 0 else dvs + a
                dks = c if h == 0 else dks + c
                r = dot(kut[h * HEAD : (h + 1) * HEAD, cols], ds)
                dqt[h] = r if dqt[h] is None else dqt[h] + r
            dv[cols, :] += dvs
            dk[cols, :] += dks
        d = jnp.concatenate(dqt, axis=0).T
        hsum = jnp.sum(d * qhat * ehs, axis=0, keepdims=True)
        gq = (ehs * rq * (d - qhat * half_sums(qhat * d))).astype(bf16)
        gqs[s, at, :] = gq
        qsum = jnp.sum(gq.astype(f32), axis=0, keepdims=True)
        qcol = pl.ds(pl.multiple_of(nz * CORES * units + p.core * nz * width + s * LANES, LANES), LANES)
        vcol = pl.ds(
            pl.multiple_of(
                nz * CORES * (units + width) + p.core * nz * width + s * LANES, LANES
            ),
            LANES,
        )
        pay[row, qcol] += qsum
        for i in range(merge):
            chip = (s * merge + i) * CORES + p.core
            part[chip, SEGS + 1 : SEGS + 2, chunk : chunk + width] += hsum[
                :, i * width : (i + 1) * width
            ]

        @pl.when(qi == CORES - 1)
        def _():
            k = ks_[slot]
            rk = lax.rsqrt(half_sums(k * k) + epsilon)
            khat = k * rk
            d = dk[...]
            gkv[s, :, :LANES] = (rk * (d - khat * half_sums(khat * d))).astype(bf16)
            gv = dv[...].astype(bf16)
            gkv[s, :, LANES:] = gv
            pay[row, vcol] = jnp.sum(gv.astype(f32), axis=0, keepdims=True)
            put_grad(s, 0, dot(gqs[s], normed[:t, :], 0, 0))
            kvg = dot(gkv[s], normed[: blocks * tok, :], 0, 0)
            put_grad(s, 1, kvg[:LANES])
            put_grad(s, 2, kvg[LANES:])
            both = dot(os_[slot, :tok, :], awide[0], 0, 0)
            both = both + dot(os_[slot, tok:, :], awide[1], 0, 0)
            put_grad(s, 3, both)

    def norm_grad(b):
        at = pl.ds(b * tok, tok)
        total = None
        for s in range(pairs):
            r = dot(gkv[s, at, :], weight(s, 1, 2))
            if b < CORES:
                r = r + dot(gqs[s, at, :], weight(s, 0))
            total = r if total is None else total + r
        return total

    wloads = [
        pltpu.make_async_copy(
            wa_hbm.at[c, pl.ds(0, 3 * width)],
            normed.at[pl.ds(c * 3 * width, 3 * width)],
            wl.at[c],
        )
        for c in range(nz)
    ]
    for c in wloads:
        c.start()
    rooms = [awide.at[0], awide.at[1], got.at[0], got.at[1]]
    rooms += [spare.at[i] for i in range(spare.shape[0])]
    swap_at = lambda i: rooms[i]
    for c in wloads:
        c.wait()
    gcopies = [
        remote(swap_at(i), gmine.at[i], gs.at[i], gr.at[i], p.twin()) for i in range(rounds + 1)
    ]
    for i in range(rounds, -1, -1):
        swap_at(i)[...] = norm_grad(2 * i + 1).astype(bf16)
        gcopies[i].start()
    for c in keeps:
        c.wait()
    rm.advance(0)
    for chip in range(nz):
        ra.send_plane(0, chip)
    moves = []
    for i, per_core in enumerate(steps):
        own = norm_grad(2 * i + 2)
        gcopies[i + 1].wait()
        gmine[i + 1] = (own + gmine[i + 1].astype(f32)).astype(bf16)
        for c, step in enumerate(per_core):
            if step is None:
                continue
            go = (p.core == c) & (p.z - step >= 0) & (p.z - step < nz)
            have = (p.core == c) & (p.z + step >= 0) & (p.z + step < nz)
            to = (p.dp, jnp.clip(p.z - step, 0, nz - 1) * CORES + p.core)
            copy = remote(gmine.at[i + 1], ghalo.at[i], hs.at[i, c], hr.at[i, c], to)
            pl.when(go)(copy.start)
            moves.append((i, go, have, copy))
    own = norm_grad(0)
    gcopies[0].wait()
    own = own + gmine[0].astype(f32)
    for level in range(1, m):
        rm.advance(level)
    for i, go, have, copy in moves:
        pl.when(have)(copy.wait_recv)
    for i in range(rounds):
        any_have = p.core < 0
        for j, go, have, copy in moves:
            if j == i:
                any_have = any_have | have

        @pl.when(jnp.logical_not(any_have))
        def _():
            ghalo[i] = jnp.zeros((tok, D), bf16)

    first = own
    for i in range(rounds):
        first = first + ghalo[i].astype(f32)
    normal, rstd = norm_parts(x_ref[...].astype(f32))
    scale = per_token(picks, table(SCALE_ONE))
    tg_ref[...] += norm_back(normal, rstd, first * (1.0 + scale))
    for which, values in ((SCALE_ONE, first * normal), (SHIFT_ONE, first)):
        pay[:SEGS, which * D : (which + 1) * D] = per_item(picks, values)[:SEGS]
    for j in range(n):
        part[j, :, :chunk] = pay[:, j * chunk : (j + 1) * chunk]
    line = p.line()
    sums = [remote(part.at[q[1]], held.at[o], s1.at[o], r1.at[o], q) for o, q in enumerate(line)]
    for c in sums:
        c.start()
    ra.advance(0)
    for c in sums:
        c.wait()
    total = part[p.me] + extra_ref[...]
    for o in range(n - 1):
        total = total + held[o]
    small_ref[p.core, p.z, p.dp] = total
    mine = small_ref.at[p.core, p.z, p.dp]
    plane = [(lax.rem(p.dp + o, nd), p.me) for o in range(1, nd)]
    sums = [remote(mine, mine, s2.at[o], r2.at[o], q) for o, q in enumerate(plane)]
    for c in sums:
        c.start()
    for level in range(1, m):
        ra.advance(level)
    for c in sums:
        c.wait()
    mine = small_ref.at[p.core, p.z]
    sums = [remote(mine, mine, s3.at[o], r3.at[o], p.on_chip(o)) for o in p.far]
    for c in sums:
        c.start()
    rm.end_line()
    for c in sums:
        c.wait()
    mine = small_ref.at[p.core]
    last = remote(mine, mine, s4, r4, p.twin())
    last.start()
    ra.end_line()
    for level in range(m):
        rm.back.step(level)
        ra.back.step(level)
    last.wait()
    rm.end()
    ra.end()
    for i, go, have, copy in moves:
        pl.when(go)(copy.wait_send)


def backward(
    lengths, mine, theirs, tokens, out_grad, gmlp, branch, mod, down_bias, dbias, hist, extra, l,
    ehs, dm, normed, q, k, v, o, wa, steps, nd, width,
):
    n = wa.shape[0] * CORES
    nz = n // CORES
    tok = tokens.shape[0]
    rounds = len(steps)
    t, w = CORES * tok, k.shape[1]
    pairs = k.shape[0]
    piece, arows = dm.shape[3], 4 * width // nd
    rows, cols = extra.shape
    seen = len(seen_lists(steps, tok)[0])
    dma = pltpu.SemaphoreType.DMA
    vmem = pl.BlockSpec(memory_space=pltpu.VMEM)
    anywhere = pl.BlockSpec(memory_space=pl.ANY)
    m = bits_of(nd)
    scr = pltpu.VMEM
    plane = (2, m, nz, max(1, nd // 2))
    sems = lambda: [
        dma(plane),
        dma(plane),
        dma((2, nz)),
        dma((2, nz)),
        dma((2, nd)),
        dma((2, nd)),
        dma((2,)),
    ]
    return pl.pallas_call(
        functools.partial(backward_body, n, nd, steps, width),
        out_shape=[
            jax.ShapeDtypeStruct((tok, D), bf16),
            jax.ShapeDtypeStruct(dm.shape[1:], bf16),
            jax.ShapeDtypeStruct((4 * width, D), bf16),
            jax.ShapeDtypeStruct((tok, D), f32),
            jax.ShapeDtypeStruct((CORES, nz, nd, rows, cols), f32),
        ],
        in_specs=[pl.BlockSpec(memory_space=pltpu.SMEM)] + [vmem] * 13 + [anywhere] * 7,
        out_specs=[vmem, anywhere, anywhere, vmem, vmem],
        scratch_shapes=[
            scr((2, tok, D), bf16),
            scr((CORES, tok, D), bf16),
            scr((max(1, rounds - 3), tok if rounds > 3 else 16, D), bf16),
            scr((max(w, pairs * 3 * LANES), D), bf16),
            scr((nz, width, D), bf16),
            scr((2, t, LANES), f32),
            scr((2, w, LANES), f32),
            scr((2, w, LANES), bf16),
            scr((2, t, LANES), bf16),
            scr((w, LANES), bf16),
            scr((LANES, w), bf16),
            scr((w, LANES), f32),
            scr((w, LANES), f32),
            scr((pairs, t, LANES), bf16),
            scr((pairs, w, 2 * LANES), bf16),
            scr((CORES, seen, tok, tok), bf16),
            scr((2, nz, max(1, nd // 2), piece, D), bf16),
            scr((2, nd - 1, nz, piece, D), bf16),
            scr((2, nz - 1, piece, D), bf16),
            scr((2, piece, D), bf16),
            scr((nz, 4 * width, D), bf16),
            scr((2, nd - 1, nz, arows, D // 2), bf16),
            scr((2, nz - 1, arows, D // 2), bf16),
            scr((2, arows, D // 2), bf16),
            scr((rounds + 1, tok, D), bf16),
            scr((rounds, tok, D), bf16),
            scr((8, 6 * D), f32),
            scr((n, rows, cols), f32),
            scr((n - 1, rows, cols), f32),
            dma((3,)),
            dma((3,)),
            dma((2,)),
            dma((nz,)),
            dma((4, 2)),
            dma((2, nd)),
        ]
        + sems()
        + sems()
        + [
            dma((rounds + 1,)),
            dma((rounds + 1,)),
            dma((rounds, CORES)),
            dma((rounds, CORES)),
            dma((n - 1,)),
            dma((n - 1,)),
            dma((nd - 1,)),
            dma((nd - 1,)),
            dma((nz,)),
            dma((nz,)),
            dma,
            dma,
        ],
        compiler_params=pltpu.CompilerParams(
            collective_id=1, has_side_effects=True, vmem_limit_bytes=60 << 20
        ),
        name="backward",
    )(
        lengths, mine, theirs, tokens, out_grad, gmlp, branch, mod, down_bias, dbias, hist, extra,
        l, ehs, dm, normed, q, k, v, o, wa,
    )


def local(
    nd,
    nt,
    tokens,
    class_embed,
    item_lengths,
    token_codes,
    ada_weight,
    ada_bias,
    qkv_weight,
    query_bias,
    value_bias,
    head_scale,
    proj_weight,
    proj_bias,
    up_weight,
    up_bias,
    down_weight,
    down_bias,
    out_grad,
):
    d, t = lax.axis_index("dp"), lax.axis_index("tensor")
    nz = nt // CORES
    z, core = t // CORES, t % CORES
    tok = tokens.shape[0]
    heads = head_scale.shape[0]
    width = heads * HEAD
    wide = nz * width
    pairs = wide // LANES
    units = up_weight.shape[1]
    feat = class_embed.shape[2]

    per_chip = CORES * tok
    seen = [[], []]
    for c in range(CORES):
        for step in range(1, nz):
            if step * per_chip - c * tok - tok < BEHIND:
                seen[c].append(step)
        for step in range(1, nz):
            if (step - 1) * per_chip + c * tok < AHEAD:
                seen[c].append(-step)
    rounds = max(len(s) for s in seen)
    steps = [
        tuple(s[len(s) - 1 - i] if i < len(s) else None for s in seen) for i in range(rounds)
    ]

    chunk = ada_weight.shape[1] // nt
    cond_act = jax.nn.silu(class_embed[0]).astype(bf16)
    ada_part = jnp.dot(cond_act, ada_weight, preferred_element_type=f32)
    part = jnp.pad(ada_part.reshape(SEGS, nt, chunk).transpose(1, 0, 2), ((0, 0), (0, 2), (0, 0)))
    bias_row = jnp.concatenate(
        [
            query_bias,
            value_bias,
            jnp.broadcast_to(jnp.exp(head_scale)[:, None], (heads, HEAD)).reshape(width),
            jnp.zeros((chunk - 3 * width,), f32),
        ]
    )
    extra = jnp.pad(bias_row[None], ((SEGS, 7 - SEGS), (0, 0)))
    abias = jnp.pad(
        jnp.broadcast_to(ada_bias.reshape(nt, 1, chunk), (nt, SEGS, chunk)),
        ((0, 0), (0, 8 - SEGS), (0, 0)),
    )
    apack = jnp.concatenate(
        [qkv_weight.transpose(1, 2, 0).reshape(3 * width, D), proj_weight], axis=0
    )
    mpack = jnp.stack([up_weight.T, down_weight]).reshape(2, nd, units // nd, D)
    (
        normed, q_raw, k_raw, v_in, heads_out, weight_sums, wattn, wmlp, branch, resid, nwide,
        gwide, mod_wide, ehs,
    ) = forward(
        item_lengths[0], tokens, out_grad, part, extra, abias, proj_bias[None], apack, mpack,
        steps, nd, width,
    )
    up_own = lax.dynamic_index_in_dim(
        up_bias.reshape(nz, CORES, units), core, 1, keepdims=False
    )
    mine, theirs, dmlp, dbias = mlp(
        nwide.reshape(CORES * tok, D), gwide.reshape(CORES * tok, D), wmlp, up_own
    )
    low_codes = 64
    hot = lambda v, k: (v[:, None] == jnp.arange(k, dtype=jnp.int32)[None, :]).astype(bf16)
    hist = dot(
        hot(token_codes // low_codes, NBINS // low_codes),
        hot(token_codes % low_codes, low_codes),
        0,
        0,
    ).reshape(1, NBINS)
    own_tail = jnp.pad(cond_act.astype(f32), ((0, 8 - SEGS), (chunk, LANES - feat)))
    layer_out, ymlp, yattn, tokens_grad, small = backward(
        item_lengths[0], mine, theirs, tokens, out_grad, gwide[0], branch, mod_wide,
        down_bias[None], dbias.reshape(nz, units), hist, own_tail, weight_sums, ehs, dmlp,
        normed, q_raw, k_raw, v_in, heads_out, wattn, steps, nd, width,
    )

    rows_all = small[..., :chunk].transpose(2, 3, 1, 0, 4).reshape(nd, 8, 6 * D)
    mod_all = rows_all[:, :SEGS].reshape(nd * SEGS, 6 * D)
    mod_own = lax.dynamic_index_in_dim(rows_all, d, 0, keepdims=False)[:SEGS]
    bias_sums = jnp.sum(rows_all[:, SEGS:], axis=0)
    own_small = lax.dynamic_index_in_dim(small, core, 0, keepdims=False)
    own_small = lax.dynamic_index_in_dim(own_small, z, 0, keepdims=False)
    cond_all = own_small[:, :SEGS, chunk : chunk + feat].reshape(nd * SEGS, feat)
    hscale_grad = jnp.sum(own_small[:, 7, chunk : chunk + width].reshape(nd, heads, HEAD), axis=(0, 2))
    adaw_grad = dot(cond_all, mod_all, 0, 0, highest)
    adab_grad = jnp.sum(mod_all, axis=0)
    cond_grad = dot(mod_own, ada_weight.astype(f32), 1, 1, highest)
    embed_grad = jax.vjp(jax.nn.silu, class_embed)[1](cond_grad[None])[0]
    projb_grad, downb_grad = bias_sums[0, :D], bias_sums[0, D : 2 * D]
    code_hist = bias_sums[0, 2 * D :]
    at = lambda base, k: lax.dynamic_slice_in_dim(bias_sums[1], base + (core * nz + z) * k, k, 0)
    upb_grad = at(0, units)
    qbias_grad = at(nt * units, width)
    vbias_grad = at(nt * (units + width), width)
    qkvw_grad = yattn[: 3 * width].astype(f32).reshape(3, width, D).transpose(2, 0, 1)
    projw_grad = yattn[3 * width :].astype(f32)
    upw_grad = ymlp[0].reshape(units, D).astype(f32).T
    downw_grad = ymlp[1].reshape(units, D).astype(f32)
    return (
        layer_out,
        tokens_grad,
        embed_grad,
        adaw_grad,
        adab_grad,
        qkvw_grad,
        qbias_grad,
        vbias_grad,
        hscale_grad,
        projw_grad,
        projb_grad,
        upw_grad,
        upb_grad,
        downw_grad,
        downb_grad,
        code_hist,
    )


def solution(mesh):
    placed = (
        P(("dp", "tensor"), None),
        P("dp", None, "tensor"),
        P("dp", None),
        P(("dp", "tensor")),
        P("tensor", None),
        P(),
        P(None, None, "tensor"),
        P("tensor"),
        P("tensor"),
        P("tensor"),
        P("tensor", None),
        P(),
        P(None, "tensor"),
        P(),
        P("tensor", None),
        P(),
        P(("dp", "tensor"), None),
    )
    return jax.shard_map(
        functools.partial(local, mesh.shape["dp"], mesh.shape["tensor"]),
        mesh=mesh,
        in_specs=placed,
        out_specs=(
            P(("dp", "tensor"), None),
            P(("dp", "tensor"), None),
            P("dp", None, "tensor"),
            P("tensor", None),
            P(),
            P(None, None, "tensor"),
            P("tensor"),
            P("tensor"),
            P("tensor"),
            P("tensor", None),
            P(),
            P(None, "tensor"),
            P("tensor"),
            P("tensor", None),
            P(),
            P(),
        ),
        check_vma=False,
    )
```

```python
import functools

import jax
import jax.numpy as jnp
from jax import lax
from jax.experimental import pallas as pl
from jax.experimental.pallas import tpu as pltpu
from jax.sharding import PartitionSpec as P

HEAD = 64
NBINS = 4096
ROW_LEN = 2048
SEGS = 6
D = 1024
ITEM_MAX = 680
CORES = 2
LANES = 128

epsilon = 1e-06
scale_starts = (1, 5, 14, 30, 55, 91, 155, 255, 424)
AHEAD = ITEM_MAX - scale_starts[-1] - 1
BEHIND = ITEM_MAX - 1
highest = lax.Precision.HIGHEST
f32 = jnp.float32
bf16 = jnp.bfloat16
MESH = pl.DeviceIdType.MESH
VMEM_LIMIT = 56 << 20


def dot(a, b, ca=1, cb=0, precision=None):
    return lax.dot_general(
        a, b, (((ca,), (cb,)), ((), ())), preferred_element_type=f32, precision=precision
    )


def item_layout(lengths):
    ends = jnp.cumsum(lengths, dtype=jnp.int32)
    begin = ends - lengths
    position = jnp.arange(ROW_LEN, dtype=jnp.int32)
    segment = jnp.sum((position[:, None] >= ends[None, :]).astype(jnp.int32), axis=1)
    chosen = segment[:, None] == jnp.arange(SEGS, dtype=jnp.int32)[None, :]
    inside = position - jnp.sum(jnp.where(chosen, begin[None, :], 0), axis=1)
    scale_ids = jnp.zeros_like(inside)
    for threshold in scale_starts:
        scale_ids = scale_ids + (inside >= threshold).astype(jnp.int32)
    return segment, scale_ids


def greet(peers):
    barrier = pltpu.get_barrier_semaphore()
    for p in peers:
        pl.semaphore_signal(barrier, inc=1, device_id=p, device_id_type=MESH)
    pl.semaphore_wait(barrier, len(peers))


def remote(src, dst, send, recv, to):
    return pltpu.make_async_remote_copy(
        src_ref=src,
        dst_ref=dst,
        send_sem=send,
        recv_sem=recv,
        device_id=to,
        device_id_type=MESH,
    )


class Place:
    def __init__(self, n, nd):
        self.n, self.nd, self.nz = n, nd, n // CORES
        self.dp, self.me = lax.axis_index("dp"), lax.axis_index("tensor")
        self.z, self.core = self.me // CORES, lax.rem(self.me, CORES)
        self.orders = orders_of(nd)
        self.far = sorted(range(1, self.nz), key=lambda o: min(o, self.nz - o))

    def chip(self, step):
        return lax.rem(self.z + step + self.nz, self.nz)

    def on_chip(self, step):
        return (self.dp, self.chip(step) * CORES + self.core)

    def twin(self):
        return (self.dp, self.z * CORES + 1 - self.core)

    def flip(self, bit):
        return (self.dp ^ (1 << bit), self.me)

    def line(self):
        return [(self.dp, lax.rem(self.me + o, self.n)) for o in range(1, self.n)]

    def greet_all(self):
        greet(self.line() + [self.flip(b) for b in range(bits_of(self.nd))])


def bits_of(nd):
    return nd.bit_length() - 1


def orders_of(nd):
    m = bits_of(nd)
    return [list(range(m)), [(m // 2 + i) % m for i in range(m)]]


def spread_plan(order):
    plan = [(0, list(order))]
    for i, bit in enumerate(order):
        plan += [(rel | (1 << bit), list(order[i + 1 :])) for rel, _ in list(plan)]
    return plan


class Spread:
    def __init__(self, place, ref_of, send, recv):
        self.place, self.ref_of, self.send, self.recv = place, ref_of, send, recv
        self.levels = bits_of(place.nd)

    def sends(self, part, rel, bits):
        p = self.place
        ref = self.ref_of(part, p.dp ^ rel)
        for bit in bits:
            to = rel | (1 << bit)
            yield remote(ref, ref, self.send.at[part, to], self.recv.at[part, to], p.flip(bit))

    def arrived(self, level):
        for part, order in enumerate(self.place.orders):
            for rel, bits in spread_plan(order):
                if rel and len(order) - 1 - len(bits) == level:
                    yield part, rel, bits

    def begin(self):
        for part, order in enumerate(self.place.orders):
            for c in self.sends(part, 0, order):
                c.start()

    def step(self, level):
        p = self.place
        for part, rel, bits in self.arrived(level):
            ref = self.ref_of(part, p.dp ^ rel)
            remote(
                ref, ref, self.send.at[part, rel], self.recv.at[part, rel], p.flip(0)
            ).wait_recv()
            for c in self.sends(part, rel, bits):
                c.start()

    def end(self):
        for part, order in enumerate(self.place.orders):
            for rel, bits in spread_plan(order):
                for c in self.sends(part, rel, bits):
                    c.wait_send()


class Line:
    def __init__(self, place, own, ref_of, send, recv):
        self.p, self.own, self.ref_of, self.send, self.recv = place, own, ref_of, send, recv
        self.ways = (1, -1)

    def inside(self, z):
        return (z >= 0) & (z < self.p.nz)

    def source(self, w, step):
        z = self.p.z - self.ways[w] * step
        return jnp.clip(z, 0, self.p.nz - 1), self.inside(z)

    def copy(self, w, step):
        p = self.p
        to = p.z + self.ways[w]
        chip, have = self.source(w, step - 1)
        src = self.own if step == 1 else self.ref_of(chip)
        c = remote(
            src,
            self.ref_of(chip),
            self.send.at[w, step],
            self.recv.at[w, step],
            (p.dp, jnp.clip(to, 0, p.nz - 1) * CORES + p.core),
        )
        return c, have & self.inside(to)

    def start(self, step=1):
        for w in range(2):
            c, do = self.copy(w, step)
            pl.when(do)(c.start)

    def got(self, step, then):
        for w in range(2):
            chip, have = self.source(w, step)
            to = self.p.z + self.ways[w]
            ref = self.ref_of(chip)
            wait = remote(
                ref, ref, self.send.at[w, step], self.recv.at[w, step], self.p.twin()
            )
            on, more = None, None
            if step + 1 < self.p.nz:
                on, more = self.copy(w, step + 1)

            @pl.when(have)
            def _():
                wait.wait_recv()
                if on is not None:
                    pl.when(more)(on.start)
                then(w, chip)

    def each(self, step, do):
        for w in range(2):
            chip, have = self.source(w, step)
            pl.when(have)(functools.partial(do, w, chip))

    def end(self):
        for step in range(1, self.p.nz):
            for w in range(2):
                c, do = self.copy(w, step)
                pl.when(do)(c.wait_send)


def picks_of(seg):
    return (seg == lax.broadcasted_iota(jnp.int32, (seg.shape[0], 8), 1)).astype(bf16)


def two(x):
    high = x.astype(bf16)
    return high, (x - high.astype(f32)).astype(bf16)


def per_token(picks, table):
    high, low = two(table)
    return dot(picks, high) + dot(picks, low)


def per_item(picks, values):
    high, low = two(values)
    return dot(picks, high, 0, 0) + dot(picks, low, 0, 0)


def norm_parts(values):
    centred = values - jnp.mean(values, axis=-1, keepdims=True)
    rstd = lax.rsqrt(jnp.mean(centred * centred, axis=-1, keepdims=True) + epsilon)
    return centred * rstd, rstd


def norm_back(normal, rstd, scaled):
    return rstd * (
        scaled
        - jnp.mean(scaled, axis=-1, keepdims=True)
        - normal * jnp.mean(scaled * normal, axis=-1, keepdims=True)
    )


GAMMA_ONE, GAMMA_TWO, SCALE_ONE, SCALE_TWO, SHIFT_ONE, SHIFT_TWO = range(6)


def half_lanes(rows):
    return lax.broadcasted_iota(jnp.int32, (rows, LANES), 1) < HEAD


def half_sums(x):
    low = half_lanes(x.shape[0])
    a = jnp.sum(jnp.where(low, x, 0.0), axis=1, keepdims=True)
    b = jnp.sum(jnp.where(low, 0.0, x), axis=1, keepdims=True)
    return jnp.where(low, a, b)


def one_half(x, h):
    low = half_lanes(x.shape[0])
    return jnp.where(low if h == 0 else jnp.logical_not(low), x, jnp.zeros_like(x))


def ranks_at(lengths_ref, owner, tok, shape, axis):
    place = jnp.maximum(owner, 0) * tok + lax.broadcasted_iota(jnp.int32, shape, axis)
    item = jnp.zeros(shape, jnp.int32)
    begin = jnp.zeros(shape, jnp.int32)
    end = jnp.int32(0)
    for i in range(SEGS):
        end = end + lengths_ref[i]
        past = place >= end
        item = item + past.astype(jnp.int32)
        begin = jnp.where(past, end, begin)
    rank = item * 16
    for threshold in scale_starts:
        rank = rank + (place - begin >= threshold).astype(jnp.int32)
    there = owner >= 0
    return item, jnp.where(there, rank, -1)


def owners_of(p, steps):
    owners = []
    for s in [(0, 0)] + list(steps):
        for flip in range(CORES):
            c = p.core ^ flip
            far = [p.nz if v is None else v for v in s]
            chip = p.z - jnp.where(c == 0, far[0], far[1])
            owners.append(jnp.where((chip >= 0) & (chip < p.nz), chip * CORES + c, -1))
    return owners


def seen_lists(steps, tok):
    lists = []
    for qi in range(CORES):
        seen = set()
        for c in range(CORES):
            query = c ^ qi
            for i, s in enumerate([(0, 0)] + list(steps)):
                for flip in range(CORES):
                    owner = c ^ flip
                    if s[owner] is None:
                        continue
                    off = owner - s[owner] * CORES - query
                    near = off == 0
                    behind = off < 0 and (-off - 1) * tok + 1 <= BEHIND
                    ahead = off > 0 and (off - 1) * tok + 1 <= AHEAD
                    if near or behind or ahead:
                        seen.add(2 * i + flip)
        lists.append(seen)
    both = sorted(lists[0] & lists[1])
    rest = [sorted(v - set(both)) for v in lists]
    size = max(len(r) for r in rest)
    for r in rest:
        spare = [b for b in range(2 * len(steps) + 2) if b not in both and b not in r]
        r += spare[: size - len(r)]
    return [both + rest[0], both + rest[1]]


def block_at(lists, qi, j):
    a, b = lists[0][j], lists[1][j]
    return a if a == b else jnp.where(qi == 0, a, b)


def forward_body(
    n, nd, steps, width, len_ref, tok_ref, grad_ref, part_ref, extra_ref, abias_ref, pb_ref,
    apack_ref, mpack_ref,
    n_out, q_out, k_out, v_out, o_ref, l_ref, wa_out, wm_ref, branch_ref, resid_ref, nwide_ref,
    gwide_ref, mod_ref, ehs_ref,
    win, wa, modc, held, normed, qv, kv, vv, qb, vb, masks, ku, v0, v1, theirs, got,
    s1, r1, s2, r2, ts, tr, cs, cr, azs, azr, mzs, mzr, local_sem, out_sem, das, dar, dms, dmr,
    ms, mr,
):
    p = Place(n, nd)
    nz, tok = p.nz, grad_ref.shape[0]
    rounds = len(steps)
    blocks = 2 * rounds + 2
    pairs = qv.shape[0]
    merge = LANES // width
    rows = 4 * width // nd
    half = D // 2
    chunk = modc.shape[2]
    owners = owners_of(p, steps)
    p.greet_all()
    line = p.line()

    a_at = lambda chip, d: wa.at[chip, pl.ds(d * rows, rows)]
    mine = pl.ds(p.dp * rows, rows)
    al = Line(p, apack_ref.at[mine], lambda chip: wa.at[chip, mine], azs, azr)
    ml = Line(p, mpack_ref.at[:, p.dp], lambda chip: wm_ref.at[chip, :, p.dp], mzs, mzr)

    def a_spread(w, step, chip):
        return Spread(
            p,
            lambda part, d: wa.at[chip, pl.ds(d * rows, rows), pl.ds(part * half, half)],
            das.at[w, step],
            dar.at[w, step],
        )

    def m_spread(w, step, chip):
        return Spread(
            p, lambda part, d: wm_ref.at[chip, part, d], dms.at[w, step], dmr.at[w, step]
        )

    al.start()
    owns = [
        pltpu.make_async_copy(tok_ref, win.at[0], local_sem.at[0]),
        pltpu.make_async_copy(apack_ref, wa.at[p.z], local_sem.at[1]),
        pltpu.make_async_copy(mpack_ref, wm_ref.at[p.z], local_sem.at[2]),
    ]
    for c in owns:
        c.start()
    sums = [
        remote(part_ref.at[q[1]], held.at[o], s1.at[o], r1.at[o], q) for o, q in enumerate(line)
    ]
    for c in sums:
        c.start()
    twins = [
        remote(tok_ref if i == 0 else win.at[2 * i], win.at[2 * i + 1], cs.at[i], cr.at[i], p.twin())
        for i in range(rounds + 1)
    ]
    twins[0].start()
    for c in sums:
        c.wait()
    total = part_ref[p.me] + extra_ref[...] + abias_ref[p.me]
    for o in range(n - 1):
        total = total + held[o]
    modc[p.me] = total
    sums = [
        remote(modc.at[p.me], modc.at[p.me], s2.at[o], r2.at[o], q) for o, q in enumerate(line)
    ]
    for c in sums:
        c.start()
    moves = []
    for i, per_core in enumerate(steps):
        for c, step in enumerate(per_core):
            if step is None:
                continue
            go = (p.core == c) & (p.z + step >= 0) & (p.z + step < nz)
            have = (p.core == c) & (p.z - step >= 0) & (p.z - step < nz)
            to = (p.dp, jnp.clip(p.z + step, 0, nz - 1) * CORES + p.core)
            moves.append((i, go, have, remote(tok_ref, win.at[2 * i + 2], ts.at[i, c], tr.at[i, c], to)))
    al.got(1, lambda w, chip: a_spread(w, 1, chip).begin())
    for i, go, have, copy in moves:
        pl.when(go)(copy.start)
    for step in range(2, nz):
        al.got(step, lambda w, chip: a_spread(w, step, chip).begin())
    ml.start()

    for c in sums:
        c.wait()
    for j in range(n):
        mod_ref[:, j * chunk : (j + 1) * chunk] = modc[j]
    table = lambda which: mod_ref[:, which * D : (which + 1) * D]
    for s in range(pairs):
        parts = []
        for i in range(merge):
            r = modc[(s * merge + i) * CORES + p.core, SEGS : SEGS + 1, :]
            parts.append([r[:, k * width : (k + 1) * width] for k in range(3)])
        row = lambda k: jnp.concatenate([v[k] for v in parts], axis=1) if merge > 1 else parts[0][k]
        qb[s], vb[s], ehs_ref[s] = row(0), row(1), row(2)

    lists = seen_lists(steps, tok)
    for qi in range(CORES):
        owner = owners[qi]
        item, rank = ranks_at(len_ref, owner, tok, (tok, LANES), 0)
        lo, hi = item[:, :1] * 16, rank[:, :1]
        for j, b in enumerate(lists[qi]):
            _, e = ranks_at(len_ref, owners[b], tok, (8, tok), 1)
            e = e[:1]
            masks[qi, j] = jnp.where((e >= lo) & (e <= hi), 0.0, -1e30)
    own_item, _ = ranks_at(len_ref, owners[0], tok, (tok, 8), 0)
    picks = (own_item == lax.broadcasted_iota(jnp.int32, (tok, 8), 1)).astype(bf16)

    gwide_ref[0] = (per_token(picks, table(GAMMA_TWO)) * grad_ref[...].astype(f32)).astype(bf16)
    cross = [
        remote(gwide_ref.at[0], gwide_ref.at[1], ms.at[0], mr.at[0], p.twin()),
        remote(theirs, got, ms.at[1], mr.at[1], p.twin()),
        remote(nwide_ref.at[0], nwide_ref.at[1], ms.at[2], mr.at[2], p.twin()),
    ]
    cross[0].start()

    owns[0].wait()
    twins[0].wait()

    def norm_block(b):
        owner = owners[0]
        for i in range(1, blocks):
            owner = jnp.where(b == i, owners[i], owner)
        item, _ = ranks_at(len_ref, owner, tok, (tok, 8), 0)
        pick = (item == lax.broadcasted_iota(jnp.int32, (tok, 8), 1)).astype(bf16)
        normal, _ = norm_parts(win[b].astype(f32))
        scale = per_token(pick, table(SCALE_ONE))
        shift = per_token(pick, table(SHIFT_ONE))
        at = pl.ds(pl.multiple_of(b * tok, tok), tok)
        normed[at, :] = (normal * (1.0 + scale) + shift).astype(bf16)

    def weight(s, k, count=1):
        if merge == 1:
            return wa[s, k * width : (k + count) * width, :]
        rows_of = [
            wa[s * merge + i, (k + j) * width : (k + j + 1) * width, :]
            for j in range(count)
            for i in range(merge)
        ]
        return jnp.concatenate(rows_of, axis=0)

    def keys_block(b):
        at = pl.ds(pl.multiple_of(b * tok, tok), tok)

        def slot(s, _):
            r = dot(normed[at, :], weight(s, 1, 2), 1, 1)
            kv[s, at, :] = r[:, :LANES]
            vv[s, at, :] = (r[:, LANES:] + vb[s]).astype(bf16)
            return 0

        lax.fori_loop(0, pairs, slot, 0)

    @pl.loop(0, CORES)
    def _(b):
        norm_block(b)

    for level in range(bits_of(nd)):
        for step in range(1, nz):
            al.each(step, lambda w, chip: a_spread(w, step, chip).step(level))
    owns[1].wait()
    wout = pltpu.make_async_copy(wa, wa_out, out_sem.at[0])
    wout.start()

    @pl.loop(0, CORES)
    def _(b):
        keys_block(b)
        at = pl.ds(pl.multiple_of(b * tok, tok), tok)

        def slot(s, _):
            qv[s, at, :] = dot(normed[at, :], weight(s, 0), 1, 1) + qb[s]
            return 0

        lax.fori_loop(0, pairs, slot, 0)

    for i in range(rounds):
        any_got = p.core < 0
        for j, go, have, copy in moves:
            if j == i:
                pl.when(have)(copy.wait_recv)
                any_got = any_got | have

        @pl.when(jnp.logical_not(any_got))
        def _():
            win[2 * i + 2] = jnp.zeros((tok, D), bf16)

        twins[i + 1].start()
    for i in range(rounds):
        twins[i + 1].wait()

    ml.got(1, lambda w, chip: m_spread(w, 1, chip).begin())

    @pl.loop(CORES, blocks)
    def _(b):
        norm_block(b)
        keys_block(b)

    outs = [wout]
    for i, (src, dst) in enumerate(((normed, n_out), (qv, q_out), (kv, k_out), (vv, v_out))):
        outs.append(pltpu.make_async_copy(src, dst, out_sem.at[i + 1]))
        outs[-1].start()

    trips = pairs * CORES
    agenda = {}
    for step in range(1, nz):
        if step + 1 < nz:
            at = min(trips - 1, ((step - 1) * trips) // nz)
            agenda.setdefault(at, []).append((step + 1, 0))
        at = min(trips - 1, (step * trips) // nz)
        agenda.setdefault(at, []).append((0, step))

    @pl.loop(0, trips)
    def _(it):
        s, qi = it // CORES, lax.rem(it, CORES)

        @pl.when(qi == 0)
        def _():
            k = kv[s]
            ku[...] = (k * lax.rsqrt(half_sums(k * k) + epsilon)).astype(bf16)
            v = vv[s]
            low = half_lanes(v.shape[0])
            one = jnp.ones_like(v)
            v0[...] = jnp.where(low, v, one)
            v1[...] = jnp.where(low, one, v)

        at = pl.ds(pl.multiple_of(qi * tok, tok), tok)
        q = qv[s, at, :]
        qu = (q * lax.rsqrt(half_sums(q * q) + epsilon) * ehs_ref[s]).astype(bf16)
        qs = [one_half(qu, h) for h in range(2)]
        acc = [None, None]
        for j in range(len(lists[0])):
            b = block_at(lists, qi, j)
            cols = pl.ds(pl.multiple_of(b * tok, tok), tok)
            mask = masks[qi, j]
            for h in range(2):
                w = jnp.exp(dot(qs[h], ku[cols, :], 1, 1) + mask).astype(bf16)
                r = dot(w, (v0 if h == 0 else v1)[cols, :])
                acc[h] = r if acc[h] is None else acc[h] + r
        low = half_lanes(tok)
        other = jnp.where(low, pltpu.roll(acc[0], HEAD, 1), pltpu.roll(acc[1], HEAD, 1))
        o_ref[s, at, :] = (jnp.where(low, acc[0], acc[1]) / other).astype(bf16)
        turned = other.T
        l_ref[s, 0:1, at] = turned[0:1, :]
        l_ref[s, 1:2, at] = turned[HEAD : HEAD + 1, :]

        for when, todo in agenda.items():

            @pl.when(it == when)
            def _():
                for get, step in todo:
                    if get:
                        ml.got(get, lambda w, chip: m_spread(w, get, chip).begin())
                    else:
                        ml.each(step, lambda w, chip: m_spread(w, step, chip).step(0))

    def project(at):
        total = dot(o_ref[0, at, :], weight(0, 3))
        for s in range(1, pairs):
            total += dot(o_ref[s, at, :], weight(s, 3))
        return total

    theirs[...] = project(pl.ds(tok, tok)).astype(bf16)
    cross[1].start()
    first = project(pl.ds(0, tok)) + pb_ref[...]
    cross[1].wait()
    branch = first + got[...].astype(f32)
    branch_ref[...] = branch
    resid = win[0].astype(f32) + per_token(picks, table(GAMMA_ONE)) * branch
    resid_ref[...] = resid
    normal, _ = norm_parts(resid)
    scale = per_token(picks, table(SCALE_TWO))
    shift = per_token(picks, table(SHIFT_TWO))
    nwide_ref[0] = (normal * (1.0 + scale) + shift).astype(bf16)
    cross[2].start()

    for level in range(1, bits_of(nd)):
        for step in range(1, nz):
            ml.each(step, lambda w, chip: m_spread(w, step, chip).step(level))
    cross[0].wait()
    cross[2].wait()
    for step in range(1, nz):
        al.each(step, lambda w, chip: a_spread(w, step, chip).end())
        ml.each(step, lambda w, chip: m_spread(w, step, chip).end())
    al.end()
    ml.end()
    for i, go, have, copy in moves:
        pl.when(go)(copy.wait_send)
    owns[2].wait()
    for c in outs:
        c.wait()


def forward(lengths, tokens, out_grad, part, extra, abias, proj_bias, apack, mpack, steps, nd, width):
    n, _, cols = part.shape
    nz = n // CORES
    tok = tokens.shape[0]
    rounds = len(steps)
    blocks = 2 * rounds + 2
    t, w = CORES * tok, blocks * tok
    pairs = nz * width // LANES
    seen = len(seen_lists(steps, tok)[0])
    dma = pltpu.SemaphoreType.DMA
    vmem = pl.BlockSpec(memory_space=pltpu.VMEM)
    anywhere = pl.BlockSpec(memory_space=pl.ANY)
    out = lambda *shape: jax.ShapeDtypeStruct(shape, f32)
    low = lambda *shape: jax.ShapeDtypeStruct(shape, bf16)
    v = pltpu.VMEM
    return pl.pallas_call(
        functools.partial(forward_body, n, nd, steps, width),
        out_shape=[
            low(w, D),
            out(pairs, t, LANES),
            out(pairs, w, LANES),
            low(pairs, w, LANES),
            low(pairs, t, LANES),
            out(pairs, 8, t),
            low(nz, 4 * width, D),
            low(nz, *mpack.shape),
            out(tok, D),
            out(tok, D),
            low(CORES, tok, D),
            low(CORES, tok, D),
            out(8, 6 * D),
            out(pairs, 1, LANES),
        ],
        in_specs=[pl.BlockSpec(memory_space=pltpu.SMEM), anywhere]
        + [vmem] * 5
        + [anywhere] * 2,
        out_specs=[anywhere] * 4 + [vmem] * 2 + [anywhere] * 2 + [vmem] * 6,
        scratch_shapes=[
            v((blocks, tok, D), bf16),
            v((nz, 4 * width, D), bf16),
            v(part.shape, f32),
            v((n - 1,) + part.shape[1:], f32),
            v((w, D), bf16),
            v((pairs, t, LANES), f32),
            v((pairs, w, LANES), f32),
            v((pairs, w, LANES), bf16),
            v((pairs, 1, LANES), f32),
            v((pairs, 1, LANES), f32),
            v((CORES, seen, tok, tok), f32),
            v((w, LANES), bf16),
            v((w, LANES), bf16),
            v((w, LANES), bf16),
            v((tok, D), bf16),
            v((tok, D), bf16),
            dma((n - 1,)),
            dma((n - 1,)),
            dma((n - 1,)),
            dma((n - 1,)),
            dma((rounds, CORES)),
            dma((rounds, CORES)),
            dma((rounds + 1,)),
            dma((rounds + 1,)),
            dma((2, nz)),
            dma((2, nz)),
            dma((2, nz)),
            dma((2, nz)),
            dma((3,)),
            dma((5,)),
            dma((2, nz, 2, nd)),
            dma((2, nz, 2, nd)),
            dma((2, nz, 2, nd)),
            dma((2, nz, 2, nd)),
            dma((3,)),
            dma((3,)),
        ],
        compiler_params=pltpu.CompilerParams(
            collective_id=0, has_side_effects=True, vmem_limit_bytes=VMEM_LIMIT
        ),
        name="forward",
    )(lengths, tokens, out_grad, part, extra, abias, proj_bias, apack, mpack)


def mlp_body(x_ref, g_ref, w_ref, bias_ref, mine_ref, theirs_ref, dw_ref, dbias_ref, mlp, gx):
    x, g = x_ref[...], g_ref[...]
    tok = mine_ref.shape[1]
    units = w_ref.shape[2] * w_ref.shape[3]
    up = w_ref[0, 0].reshape(units, D)
    down = w_ref[0, 1].reshape(units, D)
    pre = dot(x, up, 1, 1) + bias_ref[0]
    square = pre * pre
    th = jnp.tanh(0.7978845608028654 * pre * (1.0 + 0.044715 * square))
    half = 0.5 * (1.0 + th)
    hidden = (pre * half).astype(bf16)
    slope = half + 0.5 * pre * (1.0 - th * th) * (
        0.7978845608028654 * (1.0 + 3.0 * 0.044715 * square)
    )
    gp = (dot(g, down, 1, 1) * slope).astype(bf16)

    @pl.when(pl.program_id(0) == 0)
    def _():
        mlp[...] = jnp.zeros_like(mlp)
        gx[...] = jnp.zeros_like(gx)

    mlp[...] += dot(hidden, down)
    gx[...] += dot(gp, up)
    dw_ref[0, 0] = dot(gp, x, 0, 0).astype(bf16).reshape(dw_ref.shape[2:])
    dw_ref[0, 1] = dot(hidden, g, 0, 0).astype(bf16).reshape(dw_ref.shape[2:])
    dbias_ref[0] = jnp.sum(gp.astype(f32), axis=0, keepdims=True)

    @pl.when(pl.program_id(0) == pl.num_programs(0) - 1)
    def _():
        for i, v in enumerate((gx, mlp)):
            mine_ref[i] = v[:tok, :]
            theirs_ref[i] = v[tok:, :].astype(bf16)


def mlp(x, g, weights, bias):
    t = x.shape[0]
    tok = t // CORES
    nz, _, nd, piece, _ = weights.shape
    count = min(nd, max(1, 512 // piece))
    per = nd // count
    steps, units = nz * per, count * piece
    whole = lambda *shape: pl.BlockSpec(shape, lambda i: (0,) * len(shape))
    block = pl.BlockSpec((1, 2, count, piece, D), lambda i: (i // per, 0, i % per, 0, 0))
    row = pl.BlockSpec((1, 1, units), lambda i: (i, 0, 0))
    return pl.pallas_call(
        mlp_body,
        grid=(steps,),
        in_specs=[whole(t, D), whole(t, D), block, row],
        out_specs=[whole(2, tok, D), whole(2, tok, D), block, row],
        out_shape=[
            jax.ShapeDtypeStruct((2, tok, D), f32),
            jax.ShapeDtypeStruct((2, tok, D), bf16),
            jax.ShapeDtypeStruct(weights.shape, bf16),
            jax.ShapeDtypeStruct((steps, 1, units), f32),
        ],
        scratch_shapes=[pltpu.VMEM((t, D), f32), pltpu.VMEM((t, D), f32)],
        compiler_params=pltpu.CompilerParams(vmem_limit_bytes=VMEM_LIMIT),
        name="mlp",
    )(x, g, weights, bias.reshape(steps, 1, units))


class Reduce:
    def __init__(self, place, sent, kept, stage, zstage, final, out, sems):
        self.p, self.sent, self.kept = place, sent, kept
        self.stage, self.zstage, self.final = stage, zstage, final
        self.ps, self.pr, self.zs, self.zr, self.os, self.or_, self.fs = sems
        self.m = bits_of(place.nd)
        self.back = Spread(place, out, self.os, self.or_)
        self.out = out

    def held(self, part, level):
        rels = list(range(self.p.nd))
        for bit in self.p.orders[part][:level]:
            rels = [r for r in rels if not (r >> bit) & 1]
        return rels

    def current(self, part, level, chip, rel):
        if level == 0:
            bit = self.p.orders[part][0]
            return (self.sent if (rel >> bit) & 1 else self.kept)(part, chip, self.p.dp ^ rel)
        return self.stage(part, level - 1, chip, self.held(part, level).index(rel))

    def plane(self, level, chip):
        for part, order in enumerate(self.p.orders):
            bit = order[level]
            for rel in self.held(part, level):
                if (rel >> bit) & 1:
                    slot = self.held(part, level + 1).index(rel ^ (1 << bit))
                    yield remote(
                        self.current(part, level, chip, rel),
                        self.stage(part, level, chip, slot),
                        self.ps.at[part, level, chip, slot],
                        self.pr.at[part, level, chip, slot],
                        self.p.flip(bit),
                    )

    def send_plane(self, level, chip):
        for c in self.plane(level, chip):
            c.start()

    def add_plane(self, level, chip):
        for c in self.plane(level, chip):
            c.wait_recv()
        for part in range(2):
            for slot, rel in enumerate(self.held(part, level + 1)):
                room = self.stage(part, level, chip, slot)
                mine = self.current(part, level, chip, rel)
                room[...] = (room[...].astype(f32) + mine[...].astype(f32)).astype(bf16)

    def line(self, o):
        for part in range(2):
            yield part, remote(
                self.stage(part, self.m - 1, self.p.chip(o), 0),
                self.zstage(part, o),
                self.zs.at[part, o],
                self.zr.at[part, o],
                self.p.on_chip(o),
            )

    def advance(self, level, then=None):
        for o in self.p.far + [0]:
            self.add_plane(level, self.p.chip(o))
            if level + 1 < self.m:
                self.send_plane(level + 1, self.p.chip(o))
            elif o:
                self.send_line(o)

    def send_line(self, o):
        for _, c in self.line(o):
            c.start()

    def end_line(self):
        p = self.p
        for o in p.far:
            for _, c in self.line(o):
                c.wait_recv()
        puts = []
        for part in range(2):
            total = self.stage(part, self.m - 1, p.z, 0)[...].astype(f32)
            for o in p.far:
                total = total + self.zstage(part, o)[...].astype(f32)
            self.final(part)[...] = total.astype(bf16)
            puts.append(
                pltpu.make_async_copy(self.final(part), self.out(part, p.dp), self.fs.at[part])
            )
            puts[-1].start()
        for c in puts:
            c.wait()
        self.back.begin()

    def end(self):
        for level in range(self.m):
            for chip in range(self.p.nz):
                for c in self.plane(level, chip):
                    c.wait_send()
        for o in self.p.far:
            for _, c in self.line(o):
                c.wait_send()
        self.back.end()


def backward_body(
    n, nd, steps, width, len_ref, mine_ref, theirs_ref, x_ref, g_ref, gm_ref, branch_ref, mod_ref,
    db_ref, dbias_ref, hist_ref, extra_ref, l_ref, ehs_ref, dm_ref, n_hbm, q_hbm, k_hbm, v_hbm,
    o_hbm, wa_hbm,
    out_ref, ym_ref, ya_ref, tg_ref, small_ref,
    got, awide, spare, normed, wp, qs_, ks_, vs_, os_, ku, kut, dk, dv, gqs, gkv, masks,
    dmk, mstage, mz, mfinal, da, astage, az, afinal, gmine, ghalo, pay, part, held,
    xs, xr, load, wl, ld, mks,
    mps, mpr, mzs, mzr, mos, mor, mfs, aps, apr, azs, azr, aos, aor, afs,
    gs, gr, hs, hr, s1, r1, s2, r2, s3, r3, s4, r4,
):
    p = Place(n, nd)
    nz, tok = p.nz, x_ref.shape[0]
    rounds = len(steps)
    blocks = 2 * rounds + 2
    pairs = l_ref.shape[0]
    merge = LANES // width
    arows = 4 * width // nd
    units = dbias_ref.shape[1]
    t = CORES * tok
    half = D // 2
    m = bits_of(nd)
    chunk = 6 * D // n
    owners = owners_of(p, steps)
    table = lambda which: mod_ref[:, which * D : (which + 1) * D]

    def base(level):
        return sum(nd >> (i + 1) for i in range(level))

    def kept_slot(q, d):
        bit = p.orders[q][0]
        return ((d >> (bit + 1)) << bit) | (d & ((1 << bit) - 1))

    cut = lambda q: pl.ds(q * half, half)
    rm = Reduce(
        p,
        lambda q, chip, d: dm_ref.at[chip, q, d],
        lambda q, chip, d: dmk.at[q, chip, kept_slot(q, d)],
        lambda q, level, chip, slot: mstage.at[q, base(level) + slot, chip],
        lambda q, o: mz.at[q, o - 1],
        lambda q: mfinal.at[q],
        lambda q, d: ym_ref.at[q, d],
        (mps, mpr, mzs, mzr, mos, mor, mfs),
    )
    a_own = lambda q, chip, d: da.at[chip, pl.ds(d * arows, arows), cut(q)]
    ra = Reduce(
        p,
        a_own,
        a_own,
        lambda q, level, chip, slot: astage.at[q, base(level) + slot, chip],
        lambda q, o: az.at[q, o - 1],
        lambda q: afinal.at[q],
        lambda q, d: ya_ref.at[pl.ds(d * arows, arows), cut(q)],
        (aps, apr, azs, azr, aos, aor, afs),
    )
    p.greet_all()
    far = p.far + [0]
    swaps = [remote(theirs_ref.at[i], got.at[i], xs.at[i], xr.at[i], p.twin()) for i in range(2)]
    swaps.append(remote(awide.at[0], awide.at[1], xs.at[2], xr.at[2], p.twin()))
    swaps[0].start()
    swaps[1].start()
    early = far[: nz // 2]
    for o in early:
        rm.send_plane(0, p.chip(o))
    loads = [
        pltpu.make_async_copy(wa_hbm.at[:, pl.ds(3 * width, width)], wp, load.at[0]),
        pltpu.make_async_copy(n_hbm, normed.at[pl.ds(0, blocks * tok)], load.at[1]),
    ]
    for c in loads:
        c.start()

    def fetch(s, slot):
        return [
            pltpu.make_async_copy(src.at[s], dst.at[slot], ld.at[i, slot])
            for i, (src, dst) in enumerate(
                ((q_hbm, qs_), (k_hbm, ks_), (v_hbm, vs_), (o_hbm, os_))
            )
        ]

    for c in fetch(0, 0):
        c.start()
    keeps = []
    for q in range(2):
        for rel in rm.held(q, 1):
            d = p.dp ^ rel
            keeps.append(
                pltpu.make_async_copy(
                    dm_ref.at[:, q, d], dmk.at[q, :, kept_slot(q, d)], mks.at[q, rel]
                )
            )
            keeps[-1].start()

    item, _ = ranks_at(len_ref, owners[0], tok, (tok, 8), 0)
    picks = (item == lax.broadcasted_iota(jnp.int32, (tok, 8), 1)).astype(bf16)
    gamma_one = per_token(picks, table(GAMMA_ONE))
    resid = x_ref[...].astype(f32) + gamma_one * branch_ref[...]
    normal, rstd = norm_parts(resid)
    scale = per_token(picks, table(SCALE_TWO))
    grad_final = g_ref[...].astype(f32)
    swaps[0].wait()
    second = mine_ref[0] + got[0].astype(f32)
    mid = grad_final + norm_back(normal, rstd, second * (1.0 + scale))
    tg_ref[...] = mid
    attn = (gamma_one * mid).astype(bf16)
    awide[0] = attn
    swaps[2].start()
    pay[...] = jnp.zeros_like(pay)

    def put_items(which, values):
        pay[:, which * D : (which + 1) * D] = per_item(picks, values)

    put_items(SCALE_TWO, second * normal)
    put_items(SHIFT_TWO, second)
    put_items(GAMMA_ONE, mid * branch_ref[...])
    swaps[1].wait()
    mlp_branch = mine_ref[1] + got[1].astype(f32) + db_ref[...]
    out_ref[...] = (resid + per_token(picks, table(GAMMA_TWO)) * mlp_branch).astype(bf16)
    put_items(GAMMA_TWO, grad_final * mlp_branch)
    row_six = SEGS
    pay[row_six : row_six + 1, :D] = jnp.sum(attn.astype(f32), axis=0, keepdims=True)
    pay[row_six : row_six + 1, D : 2 * D] = jnp.sum(
        gm_ref[...].astype(f32), axis=0, keepdims=True
    )
    pay[row_six : row_six + 1, 2 * D :] = hist_ref[...]
    row = pl.ds(SEGS + 1, 1)
    for z in range(nz):
        at = pl.multiple_of((p.core * nz + z) * units, LANES)
        pay[row, pl.ds(at, units)] = dbias_ref[z : z + 1, :]
    part[:, :, chunk:] = jnp.zeros((n, 8, LANES), f32)

    lists = seen_lists(steps, tok)
    for qi in range(CORES):
        item, rank = ranks_at(len_ref, owners[qi], tok, (8, tok), 1)
        lo, hi = item[:1] * 16, rank[:1]
        for j, b in enumerate(lists[qi]):
            _, e = ranks_at(len_ref, owners[b], tok, (tok, LANES), 0)
            e = e[:, :1]
            masks[qi, j] = jnp.where((e >= lo) & (e <= hi), 0.0, -1e30).astype(bf16)

    def proj_rows(s):
        if merge == 1:
            return wp[s]
        return jnp.concatenate([wp[s * merge + i] for i in range(merge)], axis=0)

    def weight(s, k, count=1):
        at = lambda i, j: normed[((s * merge + i) * 3 + j) * width : ((s * merge + i) * 3 + j + 1) * width, :]
        if merge == 1:
            return normed[(s * 3 + k) * width : (s * 3 + k + count) * width, :]
        rows_of = [at(i, k + j) for j in range(count) for i in range(merge)]
        return jnp.concatenate(rows_of, axis=0)

    def put_grad(s, k, value):
        for i in range(merge):
            da[s * merge + i, k * width : (k + 1) * width, :] = value[
                i * width : (i + 1) * width
            ].astype(bf16)

    for c in loads + keeps:
        c.wait()
    swaps[2].wait()

    trips = pairs * CORES
    agenda = {}

    def at_trip(it, do):
        agenda.setdefault(min(it, trips - 1), []).append(do)

    def pass_on(level, o):
        rm.add_plane(level, p.chip(o))
        if level + 1 < m:
            rm.send_plane(level + 1, p.chip(o))
        elif o:
            rm.send_line(o)

    per_trip = max(1, nz // 4)
    for k, o in enumerate(early):
        at_trip(1 + k // per_trip, functools.partial(pass_on, 0, o))
        if k + len(early) < nz:
            at_trip(
                1 + k // per_trip,
                functools.partial(rm.send_plane, 0, p.chip(far[k + len(early)])),
            )
    if m > 1:
        for k, o in enumerate(early):
            at_trip(5 + k // per_trip, functools.partial(pass_on, 1, o))
    late = far[len(early) :]
    at_trip(6, functools.partial(pass_on, 0, late[0]))

    @pl.loop(0, pairs * CORES)
    def _(it):
        s, qi = it // CORES, lax.rem(it, CORES)
        slot = lax.rem(s, 2)

        @pl.when(qi == 0)
        def _():
            for c in fetch(s, slot):
                c.wait()

            @pl.when(s + 1 < pairs)
            def _():
                for c in fetch(s + 1, 1 - slot):
                    c.start()

            k = ks_[slot]
            unit = k * lax.rsqrt(half_sums(k * k) + epsilon)
            ku[...] = unit.astype(bf16)
            kut[...] = unit.T.astype(bf16)
            dk[...] = jnp.zeros_like(dk)
            dv[...] = jnp.zeros_like(dv)

        at = pl.ds(pl.multiple_of(qi * tok, tok), tok)
        ehs = ehs_ref[s]
        q = qs_[slot, at, :]
        rq = lax.rsqrt(half_sums(q * q) + epsilon)
        qhat = q * rq
        qu = (qhat * ehs).astype(bf16)
        qs = [one_half(qu, h) for h in range(2)]
        g = dot(awide[qi], proj_rows(s), 1, 1).astype(bf16)
        gs_h = [one_half(g, h) for h in range(2)]
        turned = (g.astype(f32) * os_[slot, at, :].astype(f32)).T
        deltas = [
            jnp.sum(turned[:HEAD], axis=0, keepdims=True),
            jnp.sum(turned[HEAD:], axis=0, keepdims=True),
        ]
        invs = [1.0 / l_ref[s, h : h + 1, at] for h in range(2)]
        dqt = [None, None]
        for j in range(len(lists[0])):
            b = block_at(lists, qi, j)
            cols = pl.ds(pl.multiple_of(b * tok, tok), tok)
            mask = masks[qi, j].astype(f32)
            kb, vb = ku[cols, :], vs_[slot, cols, :]
            dvs, dks = None, None
            for h in range(2):
                w = jnp.exp(dot(kb, qs[h], 1, 1) + mask) * invs[h]
                dp = dot(vb, gs_h[h], 1, 1)
                ds = (w * (dp - deltas[h])).astype(bf16)
                a = dot(w.astype(bf16), gs_h[h])
                c = dot(ds, qs[h])
                dvs = a if h == 0 else dvs + a
                dks = c if h == 0 else dks + c
                r = dot(kut[h * HEAD : (h + 1) * HEAD, cols], ds)
                dqt[h] = r if dqt[h] is None else dqt[h] + r
            dv[cols, :] += dvs
            dk[cols, :] += dks
        d = jnp.concatenate(dqt, axis=0).T
        hsum = jnp.sum(d * qhat * ehs, axis=0, keepdims=True)
        gq = (ehs * rq * (d - qhat * half_sums(qhat * d))).astype(bf16)
        gqs[s, at, :] = gq
        qsum = jnp.sum(gq.astype(f32), axis=0, keepdims=True)
        qcol = pl.ds(pl.multiple_of(nz * CORES * units + p.core * nz * width + s * LANES, LANES), LANES)
        vcol = pl.ds(
            pl.multiple_of(
                nz * CORES * (units + width) + p.core * nz * width + s * LANES, LANES
            ),
            LANES,
        )
        pay[row, qcol] += qsum
        for i in range(merge):
            chip = (s * merge + i) * CORES + p.core
            part[chip, SEGS + 1 : SEGS + 2, chunk : chunk + width] += hsum[
                :, i * width : (i + 1) * width
            ]

        @pl.when(qi == CORES - 1)
        def _():
            k = ks_[slot]
            rk = lax.rsqrt(half_sums(k * k) + epsilon)
            khat = k * rk
            d = dk[...]
            gkv[s, :, :LANES] = (rk * (d - khat * half_sums(khat * d))).astype(bf16)
            gv = dv[...].astype(bf16)
            gkv[s, :, LANES:] = gv
            pay[row, vcol] = jnp.sum(gv.astype(f32), axis=0, keepdims=True)
            put_grad(s, 0, dot(gqs[s], normed[:t, :], 0, 0))
            kvg = dot(gkv[s], normed[: blocks * tok, :], 0, 0)
            put_grad(s, 1, kvg[:LANES])
            put_grad(s, 2, kvg[LANES:])
            both = dot(os_[slot, :tok, :], awide[0], 0, 0)
            both = both + dot(os_[slot, tok:, :], awide[1], 0, 0)
            put_grad(s, 3, both)

        for when, todo in agenda.items():

            @pl.when(it == when)
            def _():
                for do in todo:
                    do()

    def norm_grad(b):
        at = pl.ds(b * tok, tok)
        total = None
        for s in range(pairs):
            r = dot(gkv[s, at, :], weight(s, 1, 2))
            if b < CORES:
                r = r + dot(gqs[s, at, :], weight(s, 0))
            total = r if total is None else total + r
        return total

    wloads = [
        pltpu.make_async_copy(
            wa_hbm.at[c, pl.ds(0, 3 * width)],
            normed.at[pl.ds(c * 3 * width, 3 * width)],
            wl.at[c],
        )
        for c in range(nz)
    ]
    for c in wloads:
        c.start()
    rooms = [awide.at[0], awide.at[1], got.at[0], got.at[1]]
    rooms += [spare.at[i] for i in range(spare.shape[0])]
    swap_at = lambda i: rooms[i]
    for c in wloads:
        c.wait()
    gcopies = [
        remote(swap_at(i), gmine.at[i], gs.at[i], gr.at[i], p.twin()) for i in range(rounds + 1)
    ]
    for i in range(rounds, -1, -1):
        swap_at(i)[...] = norm_grad(2 * i + 1).astype(bf16)
        gcopies[i].start()
    for o in late[1:]:
        pass_on(0, o)
    for o in far[: nz // 2]:
        ra.send_plane(0, p.chip(o))
    moves = []
    for i, per_core in enumerate(steps):
        own = norm_grad(2 * i + 2)
        gcopies[i + 1].wait()
        gmine[i + 1] = (own + gmine[i + 1].astype(f32)).astype(bf16)
        for c, step in enumerate(per_core):
            if step is None:
                continue
            go = (p.core == c) & (p.z - step >= 0) & (p.z - step < nz)
            have = (p.core == c) & (p.z + step >= 0) & (p.z + step < nz)
            to = (p.dp, jnp.clip(p.z - step, 0, nz - 1) * CORES + p.core)
            copy = remote(gmine.at[i + 1], ghalo.at[i], hs.at[i, c], hr.at[i, c], to)
            pl.when(go)(copy.start)
            moves.append((i, go, have, copy))
    own = norm_grad(0)
    gcopies[0].wait()
    own = own + gmine[0].astype(f32)
    if m > 1:
        for o in late:
            pass_on(1, o)
    for level in range(2, m):
        for o in far:
            pass_on(level, o)
    for o in far[nz // 2 :]:
        ra.send_plane(0, p.chip(o))
    rm.end_line()
    for o in far[: nz // 2]:
        ra.add_plane(0, p.chip(o))
        if m > 1:
            ra.send_plane(1, p.chip(o))
        elif o:
            ra.send_line(o)
    for i, go, have, copy in moves:
        pl.when(have)(copy.wait_recv)
    for i in range(rounds):
        any_have = p.core < 0
        for j, go, have, copy in moves:
            if j == i:
                any_have = any_have | have

        @pl.when(jnp.logical_not(any_have))
        def _():
            ghalo[i] = jnp.zeros((tok, D), bf16)

    first = own
    for i in range(rounds):
        first = first + ghalo[i].astype(f32)
    normal, rstd = norm_parts(x_ref[...].astype(f32))
    scale = per_token(picks, table(SCALE_ONE))
    tg_ref[...] += norm_back(normal, rstd, first * (1.0 + scale))
    for which, values in ((SCALE_ONE, first * normal), (SHIFT_ONE, first)):
        pay[:SEGS, which * D : (which + 1) * D] = per_item(picks, values)[:SEGS]
    for j in range(n):
        part[j, :, :chunk] = pay[:, j * chunk : (j + 1) * chunk]
    line = p.line()
    sums = [remote(part.at[q[1]], held.at[o], s1.at[o], r1.at[o], q) for o, q in enumerate(line)]
    for c in sums:
        c.start()
    for o in far[nz // 2 :]:
        ra.add_plane(0, p.chip(o))
        if m > 1:
            ra.send_plane(1, p.chip(o))
        elif o:
            ra.send_line(o)
    for c in sums:
        c.wait()
    total = part[p.me] + extra_ref[...]
    for o in range(n - 1):
        total = total + held[o]
    small_ref[p.core, p.z, p.dp] = total
    mine = small_ref.at[p.core, p.z, p.dp]
    plane = [(lax.rem(p.dp + o, nd), p.me) for o in range(1, nd)]
    sums = [remote(mine, mine, s2.at[o], r2.at[o], q) for o, q in enumerate(plane)]
    for c in sums:
        c.start()
    for level in range(1, m):
        ra.advance(level)
    for c in sums:
        c.wait()
    mine = small_ref.at[p.core, p.z]
    sums = [remote(mine, mine, s3.at[o], r3.at[o], p.on_chip(o)) for o in p.far]
    for c in sums:
        c.start()
    rm.back.step(0)
    ra.end_line()
    for c in sums:
        c.wait()
    mine = small_ref.at[p.core]
    last = remote(mine, mine, s4, r4, p.twin())
    last.start()
    for level in range(m):
        if level:
            rm.back.step(level)
        ra.back.step(level)
    last.wait()
    rm.end()
    ra.end()
    for i, go, have, copy in moves:
        pl.when(go)(copy.wait_send)


def backward(
    lengths, mine, theirs, tokens, out_grad, gmlp, branch, mod, down_bias, dbias, hist, extra, l,
    ehs, dm, normed, q, k, v, o, wa, steps, nd, width,
):
    n = wa.shape[0] * CORES
    nz = n // CORES
    tok = tokens.shape[0]
    rounds = len(steps)
    t, w = CORES * tok, k.shape[1]
    pairs = k.shape[0]
    piece, arows = dm.shape[3], 4 * width // nd
    rows, cols = extra.shape
    seen = len(seen_lists(steps, tok)[0])
    dma = pltpu.SemaphoreType.DMA
    vmem = pl.BlockSpec(memory_space=pltpu.VMEM)
    anywhere = pl.BlockSpec(memory_space=pl.ANY)
    m = bits_of(nd)
    scr = pltpu.VMEM
    plane = (2, m, nz, max(1, nd // 2))
    sems = lambda: [
        dma(plane),
        dma(plane),
        dma((2, nz)),
        dma((2, nz)),
        dma((2, nd)),
        dma((2, nd)),
        dma((2,)),
    ]
    return pl.pallas_call(
        functools.partial(backward_body, n, nd, steps, width),
        out_shape=[
            jax.ShapeDtypeStruct((tok, D), bf16),
            jax.ShapeDtypeStruct(dm.shape[1:], bf16),
            jax.ShapeDtypeStruct((4 * width, D), bf16),
            jax.ShapeDtypeStruct((tok, D), f32),
            jax.ShapeDtypeStruct((CORES, nz, nd, rows, cols), f32),
        ],
        in_specs=[pl.BlockSpec(memory_space=pltpu.SMEM)] + [vmem] * 13 + [anywhere] * 7,
        out_specs=[vmem, anywhere, anywhere, vmem, vmem],
        scratch_shapes=[
            scr((2, tok, D), bf16),
            scr((CORES, tok, D), bf16),
            scr((max(1, rounds - 3), tok if rounds > 3 else 16, D), bf16),
            scr((max(w, pairs * 3 * LANES), D), bf16),
            scr((nz, width, D), bf16),
            scr((2, t, LANES), f32),
            scr((2, w, LANES), f32),
            scr((2, w, LANES), bf16),
            scr((2, t, LANES), bf16),
            scr((w, LANES), bf16),
            scr((LANES, w), bf16),
            scr((w, LANES), f32),
            scr((w, LANES), f32),
            scr((pairs, t, LANES), bf16),
            scr((pairs, w, 2 * LANES), bf16),
            scr((CORES, seen, tok, tok), bf16),
            scr((2, nz, max(1, nd // 2), piece, D), bf16),
            scr((2, nd - 1, nz, piece, D), bf16),
            scr((2, nz - 1, piece, D), bf16),
            scr((2, piece, D), bf16),
            scr((nz, 4 * width, D), bf16),
            scr((2, nd - 1, nz, arows, D // 2), bf16),
            scr((2, nz - 1, arows, D // 2), bf16),
            scr((2, arows, D // 2), bf16),
            scr((rounds + 1, tok, D), bf16),
            scr((rounds, tok, D), bf16),
            scr((8, 6 * D), f32),
            scr((n, rows, cols), f32),
            scr((n - 1, rows, cols), f32),
            dma((3,)),
            dma((3,)),
            dma((2,)),
            dma((nz,)),
            dma((4, 2)),
            dma((2, nd)),
        ]
        + sems()
        + sems()
        + [
            dma((rounds + 1,)),
            dma((rounds + 1,)),
            dma((rounds, CORES)),
            dma((rounds, CORES)),
            dma((n - 1,)),
            dma((n - 1,)),
            dma((nd - 1,)),
            dma((nd - 1,)),
            dma((nz,)),
            dma((nz,)),
            dma,
            dma,
        ],
        compiler_params=pltpu.CompilerParams(
            collective_id=1, has_side_effects=True, vmem_limit_bytes=60 << 20
        ),
        name="backward",
    )(
        lengths, mine, theirs, tokens, out_grad, gmlp, branch, mod, down_bias, dbias, hist, extra,
        l, ehs, dm, normed, q, k, v, o, wa,
    )


def local(
    nd,
    nt,
    tokens,
    class_embed,
    item_lengths,
    token_codes,
    ada_weight,
    ada_bias,
    qkv_weight,
    query_bias,
    value_bias,
    head_scale,
    proj_weight,
    proj_bias,
    up_weight,
    up_bias,
    down_weight,
    down_bias,
    out_grad,
):
    d, t = lax.axis_index("dp"), lax.axis_index("tensor")
    nz = nt // CORES
    z, core = t // CORES, t % CORES
    tok = tokens.shape[0]
    heads = head_scale.shape[0]
    width = heads * HEAD
    wide = nz * width
    pairs = wide // LANES
    units = up_weight.shape[1]
    feat = class_embed.shape[2]

    per_chip = CORES * tok
    seen = [[], []]
    for c in range(CORES):
        for step in range(1, nz):
            if step * per_chip - c * tok - tok < BEHIND:
                seen[c].append(step)
        for step in range(1, nz):
            if (step - 1) * per_chip + c * tok < AHEAD:
                seen[c].append(-step)
    rounds = max(len(s) for s in seen)
    steps = [
        tuple(s[len(s) - 1 - i] if i < len(s) else None for s in seen) for i in range(rounds)
    ]

    chunk = ada_weight.shape[1] // nt
    cond_act = jax.nn.silu(class_embed[0]).astype(bf16)
    ada_part = jnp.dot(cond_act, ada_weight, preferred_element_type=f32)
    part = jnp.pad(ada_part.reshape(SEGS, nt, chunk).transpose(1, 0, 2), ((0, 0), (0, 2), (0, 0)))
    bias_row = jnp.concatenate(
        [
            query_bias,
            value_bias,
            jnp.broadcast_to(jnp.exp(head_scale)[:, None], (heads, HEAD)).reshape(width),
            jnp.zeros((chunk - 3 * width,), f32),
        ]
    )
    extra = jnp.pad(bias_row[None], ((SEGS, 7 - SEGS), (0, 0)))
    abias = jnp.pad(
        jnp.broadcast_to(ada_bias.reshape(nt, 1, chunk), (nt, SEGS, chunk)),
        ((0, 0), (0, 8 - SEGS), (0, 0)),
    )
    apack = jnp.concatenate(
        [qkv_weight.transpose(1, 2, 0).reshape(3 * width, D), proj_weight], axis=0
    )
    mpack = jnp.stack([up_weight.T, down_weight]).reshape(2, nd, units // nd, D)
    (
        normed, q_raw, k_raw, v_in, heads_out, weight_sums, wattn, wmlp, branch, resid, nwide,
        gwide, mod_wide, ehs,
    ) = forward(
        item_lengths[0], tokens, out_grad, part, extra, abias, proj_bias[None], apack, mpack,
        steps, nd, width,
    )
    up_own = lax.dynamic_index_in_dim(
        up_bias.reshape(nz, CORES, units), core, 1, keepdims=False
    )
    mine, theirs, dmlp, dbias = mlp(
        nwide.reshape(CORES * tok, D), gwide.reshape(CORES * tok, D), wmlp, up_own
    )
    low_codes = 64
    hot = lambda v, k: (v[:, None] == jnp.arange(k, dtype=jnp.int32)[None, :]).astype(bf16)
    hist = dot(
        hot(token_codes // low_codes, NBINS // low_codes),
        hot(token_codes % low_codes, low_codes),
        0,
        0,
    ).reshape(1, NBINS)
    own_tail = jnp.pad(cond_act.astype(f32), ((0, 8 - SEGS), (chunk, LANES - feat)))
    layer_out, ymlp, yattn, tokens_grad, small = backward(
        item_lengths[0], mine, theirs, tokens, out_grad, gwide[0], branch, mod_wide,
        down_bias[None], dbias.reshape(nz, units), hist, own_tail, weight_sums, ehs, dmlp,
        normed, q_raw, k_raw, v_in, heads_out, wattn, steps, nd, width,
    )

    rows_all = small[..., :chunk].transpose(2, 3, 1, 0, 4).reshape(nd, 8, 6 * D)
    mod_all = rows_all[:, :SEGS].reshape(nd * SEGS, 6 * D)
    mod_own = lax.dynamic_index_in_dim(rows_all, d, 0, keepdims=False)[:SEGS]
    bias_sums = jnp.sum(rows_all[:, SEGS:], axis=0)
    own_small = lax.dynamic_index_in_dim(small, core, 0, keepdims=False)
    own_small = lax.dynamic_index_in_dim(own_small, z, 0, keepdims=False)
    cond_all = own_small[:, :SEGS, chunk : chunk + feat].reshape(nd * SEGS, feat)
    hscale_grad = jnp.sum(own_small[:, 7, chunk : chunk + width].reshape(nd, heads, HEAD), axis=(0, 2))
    adaw_grad = dot(cond_all, mod_all, 0, 0, highest)
    adab_grad = jnp.sum(mod_all, axis=0)
    cond_grad = dot(mod_own, ada_weight.astype(f32), 1, 1, highest)
    embed_grad = jax.vjp(jax.nn.silu, class_embed)[1](cond_grad[None])[0]
    projb_grad, downb_grad = bias_sums[0, :D], bias_sums[0, D : 2 * D]
    code_hist = bias_sums[0, 2 * D :]
    at = lambda base, k: lax.dynamic_slice_in_dim(bias_sums[1], base + (core * nz + z) * k, k, 0)
    upb_grad = at(0, units)
    qbias_grad = at(nt * units, width)
    vbias_grad = at(nt * (units + width), width)
    qkvw_grad = yattn[: 3 * width].astype(f32).reshape(3, width, D).transpose(2, 0, 1)
    projw_grad = yattn[3 * width :].astype(f32)
    upw_grad = ymlp[0].reshape(units, D).astype(f32).T
    downw_grad = ymlp[1].reshape(units, D).astype(f32)
    return (
        layer_out,
        tokens_grad,
        embed_grad,
        adaw_grad,
        adab_grad,
        qkvw_grad,
        qbias_grad,
        vbias_grad,
        hscale_grad,
        projw_grad,
        projb_grad,
        upw_grad,
        upb_grad,
        downw_grad,
        downb_grad,
        code_hist,
    )


def solution(mesh):
    placed = (
        P(("dp", "tensor"), None),
        P("dp", None, "tensor"),
        P("dp", None),
        P(("dp", "tensor")),
        P("tensor", None),
        P(),
        P(None, None, "tensor"),
        P("tensor"),
        P("tensor"),
        P("tensor"),
        P("tensor", None),
        P(),
        P(None, "tensor"),
        P(),
        P("tensor", None),
        P(),
        P(("dp", "tensor"), None),
    )
    return jax.shard_map(
        functools.partial(local, mesh.shape["dp"], mesh.shape["tensor"]),
        mesh=mesh,
        in_specs=placed,
        out_specs=(
            P(("dp", "tensor"), None),
            P(("dp", "tensor"), None),
            P("dp", None, "tensor"),
            P("tensor", None),
            P(),
            P(None, None, "tensor"),
            P("tensor"),
            P("tensor"),
            P("tensor"),
            P("tensor", None),
            P(),
            P(None, "tensor"),
            P("tensor"),
            P("tensor", None),
            P(),
            P(),
        ),
        check_vma=False,
    )
```

```python
import functools

import jax
import jax.numpy as jnp
from jax import lax
from jax.experimental import pallas as pl
from jax.experimental.pallas import tpu as pltpu
from jax.sharding import PartitionSpec as P

HEAD = 64
NBINS = 4096
ROW_LEN = 2048
SEGS = 6
D = 1024
ITEM_MAX = 680
CORES = 2
LANES = 128

epsilon = 1e-06
scale_starts = (1, 5, 14, 30, 55, 91, 155, 255, 424)
AHEAD = ITEM_MAX - scale_starts[-1] - 1
BEHIND = ITEM_MAX - 1
highest = lax.Precision.HIGHEST
f32 = jnp.float32
bf16 = jnp.bfloat16
MESH = pl.DeviceIdType.MESH
VMEM_LIMIT = 56 << 20


def dot(a, b, ca=1, cb=0, precision=None):
    return lax.dot_general(
        a, b, (((ca,), (cb,)), ((), ())), preferred_element_type=f32, precision=precision
    )


def item_layout(lengths):
    ends = jnp.cumsum(lengths, dtype=jnp.int32)
    begin = ends - lengths
    position = jnp.arange(ROW_LEN, dtype=jnp.int32)
    segment = jnp.sum((position[:, None] >= ends[None, :]).astype(jnp.int32), axis=1)
    chosen = segment[:, None] == jnp.arange(SEGS, dtype=jnp.int32)[None, :]
    inside = position - jnp.sum(jnp.where(chosen, begin[None, :], 0), axis=1)
    scale_ids = jnp.zeros_like(inside)
    for threshold in scale_starts:
        scale_ids = scale_ids + (inside >= threshold).astype(jnp.int32)
    return segment, scale_ids


def greet(peers):
    barrier = pltpu.get_barrier_semaphore()
    for p in peers:
        pl.semaphore_signal(barrier, inc=1, device_id=p, device_id_type=MESH)
    pl.semaphore_wait(barrier, len(peers))


def remote(src, dst, send, recv, to):
    return pltpu.make_async_remote_copy(
        src_ref=src,
        dst_ref=dst,
        send_sem=send,
        recv_sem=recv,
        device_id=to,
        device_id_type=MESH,
    )


class Place:
    def __init__(self, n, nd):
        self.n, self.nd, self.nz = n, nd, n // CORES
        self.dp, self.me = lax.axis_index("dp"), lax.axis_index("tensor")
        self.z, self.core = self.me // CORES, lax.rem(self.me, CORES)
        self.orders = orders_of(nd)
        self.far = sorted(range(1, self.nz), key=lambda o: min(o, self.nz - o))

    def chip(self, step):
        return lax.rem(self.z + step + self.nz, self.nz)

    def on_chip(self, step):
        return (self.dp, self.chip(step) * CORES + self.core)

    def turn(self, k):
        return jnp.where(self.z < self.nz // 2, self.nz - 1 - k, k)

    def twin(self):
        return (self.dp, self.z * CORES + 1 - self.core)

    def flip(self, bit):
        return (self.dp ^ (1 << bit), self.me)

    def line(self):
        return [(self.dp, lax.rem(self.me + o, self.n)) for o in range(1, self.n)]

    def greet_all(self):
        greet(self.line() + [self.flip(b) for b in range(bits_of(self.nd))])


def bits_of(nd):
    return nd.bit_length() - 1


def orders_of(nd):
    m = bits_of(nd)
    return [list(range(m)), [(m // 2 + i) % m for i in range(m)]]


def spread_plan(order):
    plan = [(0, list(order))]
    for i, bit in enumerate(order):
        plan += [(rel | (1 << bit), list(order[i + 1 :])) for rel, _ in list(plan)]
    return plan


class Spread:
    def __init__(self, place, ref_of, send, recv):
        self.place, self.ref_of, self.send, self.recv = place, ref_of, send, recv
        self.levels = bits_of(place.nd)

    def sends(self, part, rel, bits):
        p = self.place
        ref = self.ref_of(part, p.dp ^ rel)
        for bit in bits:
            to = rel | (1 << bit)
            yield remote(ref, ref, self.send.at[part, to], self.recv.at[part, to], p.flip(bit))

    def arrived(self, level):
        for part, order in enumerate(self.place.orders):
            for rel, bits in spread_plan(order):
                if rel and len(order) - 1 - len(bits) == level:
                    yield part, rel, bits

    def begin(self):
        for part, order in enumerate(self.place.orders):
            for c in self.sends(part, 0, order):
                c.start()

    def step(self, level):
        p = self.place
        for part, rel, bits in self.arrived(level):
            ref = self.ref_of(part, p.dp ^ rel)
            remote(
                ref, ref, self.send.at[part, rel], self.recv.at[part, rel], p.flip(0)
            ).wait_recv()
            for c in self.sends(part, rel, bits):
                c.start()

    def end(self):
        for part, order in enumerate(self.place.orders):
            for rel, bits in spread_plan(order):
                for c in self.sends(part, rel, bits):
                    c.wait_send()


class Line:
    def __init__(self, place, own, ref_of, send, recv):
        self.p, self.own, self.ref_of, self.send, self.recv = place, own, ref_of, send, recv
        self.ways = (1, -1)

    def inside(self, z):
        return (z >= 0) & (z < self.p.nz)

    def source(self, w, step):
        z = self.p.z - self.ways[w] * step
        return jnp.clip(z, 0, self.p.nz - 1), self.inside(z)

    def copy(self, w, step):
        p = self.p
        to = p.z + self.ways[w]
        chip, have = self.source(w, step - 1)
        src = self.own if step == 1 else self.ref_of(chip)
        c = remote(
            src,
            self.ref_of(chip),
            self.send.at[w, step],
            self.recv.at[w, step],
            (p.dp, jnp.clip(to, 0, p.nz - 1) * CORES + p.core),
        )
        return c, have & self.inside(to)

    def start(self, step=1):
        for w in range(2):
            c, do = self.copy(w, step)
            pl.when(do)(c.start)

    def got(self, step, then):
        for w in range(2):
            chip, have = self.source(w, step)
            to = self.p.z + self.ways[w]
            ref = self.ref_of(chip)
            wait = remote(
                ref, ref, self.send.at[w, step], self.recv.at[w, step], self.p.twin()
            )
            on, more = None, None
            if step + 1 < self.p.nz:
                on, more = self.copy(w, step + 1)

            @pl.when(have)
            def _():
                wait.wait_recv()
                if on is not None:
                    pl.when(more)(on.start)
                then(w, chip)

    def each(self, step, do):
        for w in range(2):
            chip, have = self.source(w, step)
            pl.when(have)(functools.partial(do, w, chip))

    def end(self):
        for step in range(1, self.p.nz):
            for w in range(2):
                c, do = self.copy(w, step)
                pl.when(do)(c.wait_send)


def picks_of(seg):
    return (seg == lax.broadcasted_iota(jnp.int32, (seg.shape[0], 8), 1)).astype(bf16)


def two(x):
    high = x.astype(bf16)
    return high, (x - high.astype(f32)).astype(bf16)


def per_token(picks, table):
    high, low = two(table)
    return dot(picks, high) + dot(picks, low)


def per_item(picks, values):
    high, low = two(values)
    return dot(picks, high, 0, 0) + dot(picks, low, 0, 0)


def norm_parts(values):
    centred = values - jnp.mean(values, axis=-1, keepdims=True)
    rstd = lax.rsqrt(jnp.mean(centred * centred, axis=-1, keepdims=True) + epsilon)
    return centred * rstd, rstd


def norm_back(normal, rstd, scaled):
    return rstd * (
        scaled
        - jnp.mean(scaled, axis=-1, keepdims=True)
        - normal * jnp.mean(scaled * normal, axis=-1, keepdims=True)
    )


GAMMA_ONE, GAMMA_TWO, SCALE_ONE, SCALE_TWO, SHIFT_ONE, SHIFT_TWO = range(6)


def half_lanes(rows):
    return lax.broadcasted_iota(jnp.int32, (rows, LANES), 1) < HEAD


def half_sums(x):
    low = half_lanes(x.shape[0])
    a = jnp.sum(jnp.where(low, x, 0.0), axis=1, keepdims=True)
    b = jnp.sum(jnp.where(low, 0.0, x), axis=1, keepdims=True)
    return jnp.where(low, a, b)


def one_half(x, h):
    low = half_lanes(x.shape[0])
    return jnp.where(low if h == 0 else jnp.logical_not(low), x, jnp.zeros_like(x))


def ranks_at(lengths_ref, owner, tok, shape, axis):
    place = jnp.maximum(owner, 0) * tok + lax.broadcasted_iota(jnp.int32, shape, axis)
    item = jnp.zeros(shape, jnp.int32)
    begin = jnp.zeros(shape, jnp.int32)
    end = jnp.int32(0)
    for i in range(SEGS):
        end = end + lengths_ref[i]
        past = place >= end
        item = item + past.astype(jnp.int32)
        begin = jnp.where(past, end, begin)
    rank = item * 16
    for threshold in scale_starts:
        rank = rank + (place - begin >= threshold).astype(jnp.int32)
    there = owner >= 0
    return item, jnp.where(there, rank, -1)


def owners_of(p, steps):
    owners = []
    for s in [(0, 0)] + list(steps):
        for flip in range(CORES):
            c = p.core ^ flip
            far = [p.nz if v is None else v for v in s]
            chip = p.z - jnp.where(c == 0, far[0], far[1])
            owners.append(jnp.where((chip >= 0) & (chip < p.nz), chip * CORES + c, -1))
    return owners


def seen_lists(steps, tok):
    lists = []
    for qi in range(CORES):
        seen = set()
        for c in range(CORES):
            query = c ^ qi
            for i, s in enumerate([(0, 0)] + list(steps)):
                for flip in range(CORES):
                    owner = c ^ flip
                    if s[owner] is None:
                        continue
                    off = owner - s[owner] * CORES - query
                    near = off == 0
                    behind = off < 0 and (-off - 1) * tok + 1 <= BEHIND
                    ahead = off > 0 and (off - 1) * tok + 1 <= AHEAD
                    if near or behind or ahead:
                        seen.add(2 * i + flip)
        lists.append(seen)
    both = sorted(lists[0] & lists[1])
    rest = [sorted(v - set(both)) for v in lists]
    size = max(len(r) for r in rest)
    for r in rest:
        spare = [b for b in range(2 * len(steps) + 2) if b not in both and b not in r]
        r += spare[: size - len(r)]
    return [both + rest[0], both + rest[1]]


def block_at(lists, qi, j):
    a, b = lists[0][j], lists[1][j]
    return a if a == b else jnp.where(qi == 0, a, b)


def forward_body(
    n, nd, steps, width, len_ref, tok_ref, grad_ref, part_ref, extra_ref, abias_ref, pb_ref,
    apack_ref, mpack_ref,
    n_out, q_out, k_out, v_out, o_ref, l_ref, wa_out, wm_ref, branch_ref, resid_ref, nwide_ref,
    gwide_ref, mod_ref, ehs_ref,
    win, wa, modc, held, normed, qv, kv, vv, qb, vb, masks, ku, v0, v1, theirs, got,
    s1, r1, s2, r2, ts, tr, cs, cr, azs, azr, mzs, mzr, local_sem, out_sem, das, dar, dms, dmr,
    ms, mr,
):
    p = Place(n, nd)
    nz, tok = p.nz, grad_ref.shape[0]
    rounds = len(steps)
    blocks = 2 * rounds + 2
    pairs = qv.shape[0]
    merge = LANES // width
    rows = 4 * width // nd
    half = D // 2
    chunk = modc.shape[2]
    owners = owners_of(p, steps)
    p.greet_all()
    line = p.line()

    a_at = lambda chip, d: wa.at[chip, pl.ds(d * rows, rows)]
    mine = pl.ds(p.dp * rows, rows)
    al = Line(p, apack_ref.at[mine], lambda chip: wa.at[chip, mine], azs, azr)
    ml = Line(p, mpack_ref.at[:, p.dp], lambda chip: wm_ref.at[chip, :, p.dp], mzs, mzr)

    def a_spread(w, step, chip):
        return Spread(
            p,
            lambda part, d: wa.at[chip, pl.ds(d * rows, rows), pl.ds(part * half, half)],
            das.at[w, step],
            dar.at[w, step],
        )

    def m_spread(w, step, chip):
        return Spread(
            p, lambda part, d: wm_ref.at[chip, part, d], dms.at[w, step], dmr.at[w, step]
        )

    al.start()
    owns = [
        pltpu.make_async_copy(tok_ref, win.at[0], local_sem.at[0]),
        pltpu.make_async_copy(apack_ref, wa.at[p.z], local_sem.at[1]),
        pltpu.make_async_copy(mpack_ref, wm_ref.at[p.z], local_sem.at[2]),
    ]
    for c in owns:
        c.start()
    sums = [
        remote(part_ref.at[q[1]], held.at[o], s1.at[o], r1.at[o], q) for o, q in enumerate(line)
    ]
    for c in sums:
        c.start()
    twins = [
        remote(tok_ref if i == 0 else win.at[2 * i], win.at[2 * i + 1], cs.at[i], cr.at[i], p.twin())
        for i in range(rounds + 1)
    ]
    twins[0].start()
    for c in sums:
        c.wait()
    total = part_ref[p.me] + extra_ref[...] + abias_ref[p.me]
    for o in range(n - 1):
        total = total + held[o]
    modc[p.me] = total
    sums = [
        remote(modc.at[p.me], modc.at[p.me], s2.at[o], r2.at[o], q) for o, q in enumerate(line)
    ]
    for c in sums:
        c.start()
    moves = []
    for i, per_core in enumerate(steps):
        for c, step in enumerate(per_core):
            if step is None:
                continue
            go = (p.core == c) & (p.z + step >= 0) & (p.z + step < nz)
            have = (p.core == c) & (p.z - step >= 0) & (p.z - step < nz)
            to = (p.dp, jnp.clip(p.z + step, 0, nz - 1) * CORES + p.core)
            moves.append((i, go, have, remote(tok_ref, win.at[2 * i + 2], ts.at[i, c], tr.at[i, c], to)))
    al.got(1, lambda w, chip: a_spread(w, 1, chip).begin())
    for i, go, have, copy in moves:
        pl.when(go)(copy.start)
    for step in range(2, nz):
        al.got(step, lambda w, chip: a_spread(w, step, chip).begin())
    ml.start()

    for c in sums:
        c.wait()
    for j in range(n):
        mod_ref[:, j * chunk : (j + 1) * chunk] = modc[j]
    table = lambda which: mod_ref[:, which * D : (which + 1) * D]
    for s in range(pairs):
        parts = []
        for i in range(merge):
            r = modc[(s * merge + i) * CORES + p.core, SEGS : SEGS + 1, :]
            parts.append([r[:, k * width : (k + 1) * width] for k in range(3)])
        row = lambda k: jnp.concatenate([v[k] for v in parts], axis=1) if merge > 1 else parts[0][k]
        qb[s], vb[s], ehs_ref[s] = row(0), row(1), row(2)

    lists = seen_lists(steps, tok)
    for qi in range(CORES):
        owner = owners[qi]
        item, rank = ranks_at(len_ref, owner, tok, (tok, LANES), 0)
        lo, hi = item[:, :1] * 16, rank[:, :1]
        for j, b in enumerate(lists[qi]):
            _, e = ranks_at(len_ref, owners[b], tok, (8, tok), 1)
            e = e[:1]
            masks[qi, j] = jnp.where((e >= lo) & (e <= hi), 0.0, -1e30)
    own_item, _ = ranks_at(len_ref, owners[0], tok, (tok, 8), 0)
    picks = (own_item == lax.broadcasted_iota(jnp.int32, (tok, 8), 1)).astype(bf16)

    gwide_ref[0] = (per_token(picks, table(GAMMA_TWO)) * grad_ref[...].astype(f32)).astype(bf16)
    cross = [
        remote(gwide_ref.at[0], gwide_ref.at[1], ms.at[0], mr.at[0], p.twin()),
        remote(theirs, got, ms.at[1], mr.at[1], p.twin()),
        remote(nwide_ref.at[0], nwide_ref.at[1], ms.at[2], mr.at[2], p.twin()),
    ]
    cross[0].start()

    owns[0].wait()
    twins[0].wait()

    def norm_block(b):
        owner = owners[0]
        for i in range(1, blocks):
            owner = jnp.where(b == i, owners[i], owner)
        item, _ = ranks_at(len_ref, owner, tok, (tok, 8), 0)
        pick = (item == lax.broadcasted_iota(jnp.int32, (tok, 8), 1)).astype(bf16)
        normal, _ = norm_parts(win[b].astype(f32))
        scale = per_token(pick, table(SCALE_ONE))
        shift = per_token(pick, table(SHIFT_ONE))
        at = pl.ds(pl.multiple_of(b * tok, tok), tok)
        normed[at, :] = (normal * (1.0 + scale) + shift).astype(bf16)

    def weight(s, k, count=1):
        if merge == 1:
            return wa[s, k * width : (k + count) * width, :]
        rows_of = [
            wa[s * merge + i, (k + j) * width : (k + j + 1) * width, :]
            for j in range(count)
            for i in range(merge)
        ]
        return jnp.concatenate(rows_of, axis=0)

    def keys_block(b):
        at = pl.ds(pl.multiple_of(b * tok, tok), tok)

        def slot(s, _):
            r = dot(normed[at, :], weight(s, 1, 2), 1, 1)
            kv[s, at, :] = r[:, :LANES]
            vv[s, at, :] = (r[:, LANES:] + vb[s]).astype(bf16)
            return 0

        lax.fori_loop(0, pairs, slot, 0)

    @pl.loop(0, CORES)
    def _(b):
        norm_block(b)

    for level in range(bits_of(nd)):
        for step in range(1, nz):
            al.each(step, lambda w, chip: a_spread(w, step, chip).step(level))
    owns[1].wait()
    wout = pltpu.make_async_copy(wa, wa_out, out_sem.at[0])
    wout.start()

    @pl.loop(0, CORES)
    def _(b):
        keys_block(b)
        at = pl.ds(pl.multiple_of(b * tok, tok), tok)

        def slot(s, _):
            qv[s, at, :] = dot(normed[at, :], weight(s, 0), 1, 1) + qb[s]
            return 0

        lax.fori_loop(0, pairs, slot, 0)

    for i in range(rounds):
        any_got = p.core < 0
        for j, go, have, copy in moves:
            if j == i:
                pl.when(have)(copy.wait_recv)
                any_got = any_got | have

        @pl.when(jnp.logical_not(any_got))
        def _():
            win[2 * i + 2] = jnp.zeros((tok, D), bf16)

        twins[i + 1].start()
    for i in range(rounds):
        twins[i + 1].wait()

    ml.got(1, lambda w, chip: m_spread(w, 1, chip).begin())

    @pl.loop(CORES, blocks)
    def _(b):
        norm_block(b)
        keys_block(b)

    outs = [wout]
    for i, (src, dst) in enumerate(((normed, n_out), (qv, q_out), (kv, k_out), (vv, v_out))):
        outs.append(pltpu.make_async_copy(src, dst, out_sem.at[i + 1]))
        outs[-1].start()

    trips = pairs * CORES
    agenda = {}
    for step in range(1, nz):
        if step + 1 < nz:
            at = min(trips - 1, ((step - 1) * trips) // nz)
            agenda.setdefault(at, []).append((step + 1, 0))
        at = min(trips - 1, (step * trips) // nz)
        agenda.setdefault(at, []).append((0, step))

    @pl.loop(0, trips)
    def _(it):
        s, qi = it // CORES, lax.rem(it, CORES)

        @pl.when(qi == 0)
        def _():
            k = kv[s]
            ku[...] = (k * lax.rsqrt(half_sums(k * k) + epsilon)).astype(bf16)
            v = vv[s]
            low = half_lanes(v.shape[0])
            one = jnp.ones_like(v)
            v0[...] = jnp.where(low, v, one)
            v1[...] = jnp.where(low, one, v)

        at = pl.ds(pl.multiple_of(qi * tok, tok), tok)
        q = qv[s, at, :]
        qu = (q * lax.rsqrt(half_sums(q * q) + epsilon) * ehs_ref[s]).astype(bf16)
        qs = [one_half(qu, h) for h in range(2)]
        acc = [None, None]
        for j in range(len(lists[0])):
            b = block_at(lists, qi, j)
            cols = pl.ds(pl.multiple_of(b * tok, tok), tok)
            mask = masks[qi, j]
            for h in range(2):
                w = jnp.exp(dot(qs[h], ku[cols, :], 1, 1) + mask).astype(bf16)
                r = dot(w, (v0 if h == 0 else v1)[cols, :])
                acc[h] = r if acc[h] is None else acc[h] + r
        low = half_lanes(tok)
        other = jnp.where(low, pltpu.roll(acc[0], HEAD, 1), pltpu.roll(acc[1], HEAD, 1))
        o_ref[s, at, :] = (jnp.where(low, acc[0], acc[1]) / other).astype(bf16)
        turned = other.T
        l_ref[s, 0:1, at] = turned[0:1, :]
        l_ref[s, 1:2, at] = turned[HEAD : HEAD + 1, :]

        for when, todo in agenda.items():

            @pl.when(it == when)
            def _():
                for get, step in todo:
                    if get:
                        ml.got(get, lambda w, chip: m_spread(w, get, chip).begin())
                    else:
                        ml.each(step, lambda w, chip: m_spread(w, step, chip).step(0))

    def project(at):
        total = dot(o_ref[0, at, :], weight(0, 3))
        for s in range(1, pairs):
            total += dot(o_ref[s, at, :], weight(s, 3))
        return total

    theirs[...] = project(pl.ds(tok, tok)).astype(bf16)
    cross[1].start()
    first = project(pl.ds(0, tok)) + pb_ref[...]
    cross[1].wait()
    branch = first + got[...].astype(f32)
    branch_ref[...] = branch
    resid = win[0].astype(f32) + per_token(picks, table(GAMMA_ONE)) * branch
    resid_ref[...] = resid
    normal, _ = norm_parts(resid)
    scale = per_token(picks, table(SCALE_TWO))
    shift = per_token(picks, table(SHIFT_TWO))
    nwide_ref[0] = (normal * (1.0 + scale) + shift).astype(bf16)
    cross[2].start()

    for level in range(1, bits_of(nd)):
        for step in range(1, nz):
            ml.each(step, lambda w, chip: m_spread(w, step, chip).step(level))
    cross[0].wait()
    cross[2].wait()
    for step in range(1, nz):
        al.each(step, lambda w, chip: a_spread(w, step, chip).end())
        ml.each(step, lambda w, chip: m_spread(w, step, chip).end())
    al.end()
    ml.end()
    for i, go, have, copy in moves:
        pl.when(go)(copy.wait_send)
    owns[2].wait()
    for c in outs:
        c.wait()


def forward(lengths, tokens, out_grad, part, extra, abias, proj_bias, apack, mpack, steps, nd, width):
    n, _, cols = part.shape
    nz = n // CORES
    tok = tokens.shape[0]
    rounds = len(steps)
    blocks = 2 * rounds + 2
    t, w = CORES * tok, blocks * tok
    pairs = nz * width // LANES
    seen = len(seen_lists(steps, tok)[0])
    dma = pltpu.SemaphoreType.DMA
    vmem = pl.BlockSpec(memory_space=pltpu.VMEM)
    anywhere = pl.BlockSpec(memory_space=pl.ANY)
    out = lambda *shape: jax.ShapeDtypeStruct(shape, f32)
    low = lambda *shape: jax.ShapeDtypeStruct(shape, bf16)
    v = pltpu.VMEM
    return pl.pallas_call(
        functools.partial(forward_body, n, nd, steps, width),
        out_shape=[
            low(w, D),
            out(pairs, t, LANES),
            out(pairs, w, LANES),
            low(pairs, w, LANES),
            low(pairs, t, LANES),
            out(pairs, 8, t),
            low(nz, 4 * width, D),
            low(nz, *mpack.shape),
            out(tok, D),
            out(tok, D),
            low(CORES, tok, D),
            low(CORES, tok, D),
            out(8, 6 * D),
            out(pairs, 1, LANES),
        ],
        in_specs=[pl.BlockSpec(memory_space=pltpu.SMEM), anywhere]
        + [vmem] * 5
        + [anywhere] * 2,
        out_specs=[anywhere] * 4 + [vmem] * 2 + [anywhere] * 2 + [vmem] * 6,
        scratch_shapes=[
            v((blocks, tok, D), bf16),
            v((nz, 4 * width, D), bf16),
            v(part.shape, f32),
            v((n - 1,) + part.shape[1:], f32),
            v((w, D), bf16),
            v((pairs, t, LANES), f32),
            v((pairs, w, LANES), f32),
            v((pairs, w, LANES), bf16),
            v((pairs, 1, LANES), f32),
            v((pairs, 1, LANES), f32),
            v((CORES, seen, tok, tok), f32),
            v((w, LANES), bf16),
            v((w, LANES), bf16),
            v((w, LANES), bf16),
            v((tok, D), bf16),
            v((tok, D), bf16),
            dma((n - 1,)),
            dma((n - 1,)),
            dma((n - 1,)),
            dma((n - 1,)),
            dma((rounds, CORES)),
            dma((rounds, CORES)),
            dma((rounds + 1,)),
            dma((rounds + 1,)),
            dma((2, nz)),
            dma((2, nz)),
            dma((2, nz)),
            dma((2, nz)),
            dma((3,)),
            dma((5,)),
            dma((2, nz, 2, nd)),
            dma((2, nz, 2, nd)),
            dma((2, nz, 2, nd)),
            dma((2, nz, 2, nd)),
            dma((3,)),
            dma((3,)),
        ],
        compiler_params=pltpu.CompilerParams(
            collective_id=0, has_side_effects=True, vmem_limit_bytes=VMEM_LIMIT
        ),
        name="forward",
    )(lengths, tokens, out_grad, part, extra, abias, proj_bias, apack, mpack)


def mlp_body(x_ref, g_ref, w_ref, bias_ref, mine_ref, theirs_ref, dw_ref, dbias_ref, mlp, gx):
    x, g = x_ref[...], g_ref[...]
    tok = mine_ref.shape[1]
    units = w_ref.shape[2] * w_ref.shape[3]
    up = w_ref[0, 0].reshape(units, D)
    down = w_ref[0, 1].reshape(units, D)
    pre = dot(x, up, 1, 1) + bias_ref[0]
    square = pre * pre
    th = jnp.tanh(0.7978845608028654 * pre * (1.0 + 0.044715 * square))
    half = 0.5 * (1.0 + th)
    hidden = (pre * half).astype(bf16)
    slope = half + 0.5 * pre * (1.0 - th * th) * (
        0.7978845608028654 * (1.0 + 3.0 * 0.044715 * square)
    )
    gp = (dot(g, down, 1, 1) * slope).astype(bf16)

    @pl.when(pl.program_id(0) == 0)
    def _():
        mlp[...] = jnp.zeros_like(mlp)
        gx[...] = jnp.zeros_like(gx)

    mlp[...] += dot(hidden, down)
    gx[...] += dot(gp, up)
    dw_ref[0, 0] = dot(gp, x, 0, 0).astype(bf16).reshape(dw_ref.shape[2:])
    dw_ref[0, 1] = dot(hidden, g, 0, 0).astype(bf16).reshape(dw_ref.shape[2:])
    dbias_ref[0] = jnp.sum(gp.astype(f32), axis=0, keepdims=True)

    @pl.when(pl.program_id(0) == pl.num_programs(0) - 1)
    def _():
        for i, v in enumerate((gx, mlp)):
            mine_ref[i] = v[:tok, :]
            theirs_ref[i] = v[tok:, :].astype(bf16)


def mlp(x, g, weights, bias):
    t = x.shape[0]
    tok = t // CORES
    nz, _, nd, piece, _ = weights.shape
    count = min(nd, max(1, 512 // piece))
    per = nd // count
    steps, units = nz * per, count * piece
    whole = lambda *shape: pl.BlockSpec(shape, lambda i: (0,) * len(shape))
    block = pl.BlockSpec((1, 2, count, piece, D), lambda i: (i // per, 0, i % per, 0, 0))
    row = pl.BlockSpec((1, 1, units), lambda i: (i, 0, 0))
    return pl.pallas_call(
        mlp_body,
        grid=(steps,),
        in_specs=[whole(t, D), whole(t, D), block, row],
        out_specs=[whole(2, tok, D), whole(2, tok, D), block, row],
        out_shape=[
            jax.ShapeDtypeStruct((2, tok, D), f32),
            jax.ShapeDtypeStruct((2, tok, D), bf16),
            jax.ShapeDtypeStruct(weights.shape, bf16),
            jax.ShapeDtypeStruct((steps, 1, units), f32),
        ],
        scratch_shapes=[pltpu.VMEM((t, D), f32), pltpu.VMEM((t, D), f32)],
        compiler_params=pltpu.CompilerParams(vmem_limit_bytes=VMEM_LIMIT),
        name="mlp",
    )(x, g, weights, bias.reshape(steps, 1, units))


class Reduce:
    def __init__(self, place, sent, kept, stage, zstage, out, sems):
        self.p, self.sent, self.kept = place, sent, kept
        self.stage, self.zstage = stage, zstage
        self.ps, self.pr, self.zs, self.zr, self.os, self.or_, self.fs = sems
        self.m = bits_of(place.nd)
        self.back = Spread(place, out, self.os, self.or_)
        self.out = out

    def held(self, part, level):
        rels = list(range(self.p.nd))
        for bit in self.p.orders[part][:level]:
            rels = [r for r in rels if not (r >> bit) & 1]
        return rels

    def current(self, part, level, chip, rel):
        if level == 0:
            bit = self.p.orders[part][0]
            return (self.sent if (rel >> bit) & 1 else self.kept)(part, chip, self.p.dp ^ rel)
        return self.stage(part, level - 1, chip, self.held(part, level).index(rel))

    def plane(self, level, chip):
        for part, order in enumerate(self.p.orders):
            bit = order[level]
            for rel in self.held(part, level):
                if (rel >> bit) & 1:
                    slot = self.held(part, level + 1).index(rel ^ (1 << bit))
                    yield remote(
                        self.current(part, level, chip, rel),
                        self.stage(part, level, chip, slot),
                        self.ps.at[part, level, chip, slot],
                        self.pr.at[part, level, chip, slot],
                        self.p.flip(bit),
                    )

    def send_plane(self, level, chip):
        for c in self.plane(level, chip):
            c.start()

    def add_plane(self, level, chip):
        for c in self.plane(level, chip):
            c.wait_recv()
        for part in range(2):
            for slot, rel in enumerate(self.held(part, level + 1)):
                room = self.stage(part, level, chip, slot)
                mine = self.current(part, level, chip, rel)
                room[...] = (room[...].astype(f32) + mine[...].astype(f32)).astype(bf16)

    def hop(self, chip):
        p = self.p
        right = chip > p.z
        way, room = jnp.where(right, 0, 1), jnp.abs(chip - p.z)
        to = (p.dp, jnp.clip(jnp.where(right, p.z + 1, p.z - 1), 0, p.nz - 1) * CORES + p.core)
        behind = (chip != p.z) & jnp.where(right, p.z > 0, p.z < p.nz - 1)
        before = jnp.maximum(room - 1, 0)
        copies = [
            remote(
                self.stage(part, self.m - 1, chip, 0),
                self.zstage(part, way, before),
                self.zs.at[part, way, before],
                self.zr.at[part, way, before],
                to,
            )
            for part in range(2)
        ]
        return copies, behind, way, jnp.minimum(room, p.nz - 2)

    def arrive(self, part, way, room):
        p = self.p
        ref = self.zstage(part, way, room)
        remote(ref, ref, self.zs.at[part, way, room], self.zr.at[part, way, room], p.twin()).wait_recv()

    def send_line(self, chip):
        copies, behind, _, _ = self.hop(chip)

        @pl.when((chip != self.p.z) & jnp.logical_not(behind))
        def _():
            for c in copies:
                c.start()

    def forward_line(self, chip):
        copies, behind, way, room = self.hop(chip)

        @pl.when(behind)
        def _():
            for part, c in enumerate(copies):
                self.arrive(part, way, room)
                mine = self.stage(part, self.m - 1, chip, 0)
                got = self.zstage(part, way, room)
                mine[...] = (mine[...].astype(f32) + got[...].astype(f32)).astype(bf16)
                c.start()

    def pass_on(self, level, chip):
        self.add_plane(level, chip)
        if level + 1 < self.m:
            self.send_plane(level + 1, chip)
        else:
            self.send_line(chip)

    def end_line(self):
        p = self.p
        puts = []
        for way, there in ((0, p.z > 0), (1, p.z < p.nz - 1)):

            @pl.when(there)
            def _():
                for part in range(2):
                    self.arrive(part, way, 0)
                    mine = self.stage(part, self.m - 1, p.z, 0)
                    got = self.zstage(part, way, 0)
                    mine[...] = (mine[...].astype(f32) + got[...].astype(f32)).astype(bf16)

        for part in range(2):
            puts.append(
                pltpu.make_async_copy(
                    self.stage(part, self.m - 1, p.z, 0), self.out(part, p.dp), self.fs.at[part]
                )
            )
            puts[-1].start()
        for c in puts:
            c.wait()
        self.back.begin()

    def end(self):
        for level in range(self.m):
            for chip in range(self.p.nz):
                for c in self.plane(level, chip):
                    c.wait_send()
        for chip in range(self.p.nz):
            copies, _, _, _ = self.hop(chip)

            @pl.when(chip != self.p.z)
            def _():
                for c in copies:
                    c.wait_send()

        self.back.end()


def backward_body(
    n, nd, steps, width, len_ref, mine_ref, theirs_ref, x_ref, g_ref, gm_ref, branch_ref, mod_ref,
    db_ref, dbias_ref, hist_ref, extra_ref, l_ref, ehs_ref, dm_ref, n_hbm, q_hbm, k_hbm, v_hbm,
    o_hbm, wa_hbm,
    out_ref, ym_ref, ya_ref, tg_ref, small_ref,
    got, awide, spare, normed, wp, qs_, ks_, vs_, os_, ku, kut, dk, dv, gqs, gkv, masks,
    dmk, mstage, mz, da, astage, az, gmine, ghalo, pay, part, held,
    xs, xr, load, wl, ld, mks,
    mps, mpr, mzs, mzr, mos, mor, mfs, aps, apr, azs, azr, aos, aor, afs,
    gs, gr, hs, hr, s1, r1, s2, r2, s3, r3, s4, r4,
):
    p = Place(n, nd)
    nz, tok = p.nz, x_ref.shape[0]
    rounds = len(steps)
    blocks = 2 * rounds + 2
    pairs = l_ref.shape[0]
    merge = LANES // width
    arows = 4 * width // nd
    units = dbias_ref.shape[1]
    t = CORES * tok
    half = D // 2
    m = bits_of(nd)
    chunk = 6 * D // n
    owners = owners_of(p, steps)
    table = lambda which: mod_ref[:, which * D : (which + 1) * D]

    def base(level):
        return sum(nd >> (i + 1) for i in range(level))

    def kept_slot(q, d):
        bit = p.orders[q][0]
        return ((d >> (bit + 1)) << bit) | (d & ((1 << bit) - 1))

    cut = lambda q: pl.ds(q * half, half)
    rm = Reduce(
        p,
        lambda q, chip, d: dm_ref.at[chip, q, d],
        lambda q, chip, d: dmk.at[q, chip, kept_slot(q, d)],
        lambda q, level, chip, slot: mstage.at[q, base(level) + slot, chip],
        lambda q, way, room: mz.at[q, way, room],
        lambda q, d: ym_ref.at[q, d],
        (mps, mpr, mzs, mzr, mos, mor, mfs),
    )
    a_own = lambda q, chip, d: da.at[chip, pl.ds(d * arows, arows), cut(q)]
    ra = Reduce(
        p,
        a_own,
        a_own,
        lambda q, level, chip, slot: astage.at[q, base(level) + slot, chip],
        lambda q, way, room: az.at[q, way, room],
        lambda q, d: ya_ref.at[pl.ds(d * arows, arows), cut(q)],
        (aps, apr, azs, azr, aos, aor, afs),
    )
    p.greet_all()
    far = [p.turn(k) for k in range(nz)]
    swaps = [remote(theirs_ref.at[i], got.at[i], xs.at[i], xr.at[i], p.twin()) for i in range(2)]
    swaps.append(remote(awide.at[0], awide.at[1], xs.at[2], xr.at[2], p.twin()))
    swaps[0].start()
    swaps[1].start()
    early = far[: nz // 2]
    for o in early:
        rm.send_plane(0, o)
    loads = [
        pltpu.make_async_copy(wa_hbm.at[:, pl.ds(3 * width, width)], wp, load.at[0]),
        pltpu.make_async_copy(n_hbm, normed.at[pl.ds(0, blocks * tok)], load.at[1]),
    ]
    for c in loads:
        c.start()

    def fetch(s, slot):
        return [
            pltpu.make_async_copy(src.at[s], dst.at[slot], ld.at[i, slot])
            for i, (src, dst) in enumerate(
                ((q_hbm, qs_), (k_hbm, ks_), (v_hbm, vs_), (o_hbm, os_))
            )
        ]

    for c in fetch(0, 0):
        c.start()
    keeps = []
    for q in range(2):
        for rel in rm.held(q, 1):
            d = p.dp ^ rel
            keeps.append(
                pltpu.make_async_copy(
                    dm_ref.at[:, q, d], dmk.at[q, :, kept_slot(q, d)], mks.at[q, rel]
                )
            )
            keeps[-1].start()

    item, _ = ranks_at(len_ref, owners[0], tok, (tok, 8), 0)
    picks = (item == lax.broadcasted_iota(jnp.int32, (tok, 8), 1)).astype(bf16)
    gamma_one = per_token(picks, table(GAMMA_ONE))
    resid = x_ref[...].astype(f32) + gamma_one * branch_ref[...]
    normal, rstd = norm_parts(resid)
    scale = per_token(picks, table(SCALE_TWO))
    grad_final = g_ref[...].astype(f32)
    swaps[0].wait()
    second = mine_ref[0] + got[0].astype(f32)
    mid = grad_final + norm_back(normal, rstd, second * (1.0 + scale))
    tg_ref[...] = mid
    attn = (gamma_one * mid).astype(bf16)
    awide[0] = attn
    swaps[2].start()
    pay[...] = jnp.zeros_like(pay)

    def put_items(which, values):
        pay[:, which * D : (which + 1) * D] = per_item(picks, values)

    put_items(SCALE_TWO, second * normal)
    put_items(SHIFT_TWO, second)
    put_items(GAMMA_ONE, mid * branch_ref[...])
    swaps[1].wait()
    mlp_branch = mine_ref[1] + got[1].astype(f32) + db_ref[...]
    out_ref[...] = (resid + per_token(picks, table(GAMMA_TWO)) * mlp_branch).astype(bf16)
    put_items(GAMMA_TWO, grad_final * mlp_branch)
    row_six = SEGS
    pay[row_six : row_six + 1, :D] = jnp.sum(attn.astype(f32), axis=0, keepdims=True)
    pay[row_six : row_six + 1, D : 2 * D] = jnp.sum(
        gm_ref[...].astype(f32), axis=0, keepdims=True
    )
    pay[row_six : row_six + 1, 2 * D :] = hist_ref[...]
    row = pl.ds(SEGS + 1, 1)
    for z in range(nz):
        at = pl.multiple_of((p.core * nz + z) * units, LANES)
        pay[row, pl.ds(at, units)] = dbias_ref[z : z + 1, :]
    part[:, :, chunk:] = jnp.zeros((n, 8, LANES), f32)

    lists = seen_lists(steps, tok)
    for qi in range(CORES):
        item, rank = ranks_at(len_ref, owners[qi], tok, (8, tok), 1)
        lo, hi = item[:1] * 16, rank[:1]
        for j, b in enumerate(lists[qi]):
            _, e = ranks_at(len_ref, owners[b], tok, (tok, LANES), 0)
            e = e[:, :1]
            masks[qi, j] = jnp.where((e >= lo) & (e <= hi), 0.0, -1e30).astype(bf16)

    def proj_rows(s):
        if merge == 1:
            return wp[s]
        return jnp.concatenate([wp[s * merge + i] for i in range(merge)], axis=0)

    def weight(s, k, count=1):
        at = lambda i, j: normed[((s * merge + i) * 3 + j) * width : ((s * merge + i) * 3 + j + 1) * width, :]
        if merge == 1:
            return normed[(s * 3 + k) * width : (s * 3 + k + count) * width, :]
        rows_of = [at(i, k + j) for j in range(count) for i in range(merge)]
        return jnp.concatenate(rows_of, axis=0)

    def put_grad(s, k, value):
        for i in range(merge):
            da[s * merge + i, k * width : (k + 1) * width, :] = value[
                i * width : (i + 1) * width
            ].astype(bf16)

    for c in loads + keeps:
        c.wait()
    swaps[2].wait()

    trips = pairs * CORES
    agenda = {}

    def at_trip(it, do):
        agenda.setdefault(min(it, trips - 1), []).append(do)

    per_trip = max(1, nz // 4)
    for k, o in enumerate(early):
        at_trip(1 + k // per_trip, functools.partial(rm.pass_on, 0, o))
        if k + len(early) < nz:
            at_trip(
                1 + k // per_trip,
                functools.partial(rm.send_plane, 0, far[k + len(early)]),
            )
    if m > 1:
        for k, o in enumerate(early):
            at_trip(4 + k // per_trip, functools.partial(rm.pass_on, 1, o))
    late = far[len(early) :]
    at_trip(5, functools.partial(rm.pass_on, 0, late[0]))
    if nz == 4 and m == 2:
        at_trip(7, functools.partial(rm.pass_on, 0, late[1]))
        at_trip(6, functools.partial(rm.forward_line, early[0]))

    @pl.loop(0, pairs * CORES)
    def _(it):
        s, qi = it // CORES, lax.rem(it, CORES)
        slot = lax.rem(s, 2)

        @pl.when(qi == 0)
        def _():
            for c in fetch(s, slot):
                c.wait()

            @pl.when(s + 1 < pairs)
            def _():
                for c in fetch(s + 1, 1 - slot):
                    c.start()

            k = ks_[slot]
            unit = k * lax.rsqrt(half_sums(k * k) + epsilon)
            ku[...] = unit.astype(bf16)
            kut[...] = unit.T.astype(bf16)
            dk[...] = jnp.zeros_like(dk)
            dv[...] = jnp.zeros_like(dv)

        at = pl.ds(pl.multiple_of(qi * tok, tok), tok)
        ehs = ehs_ref[s]
        q = qs_[slot, at, :]
        rq = lax.rsqrt(half_sums(q * q) + epsilon)
        qhat = q * rq
        qu = (qhat * ehs).astype(bf16)
        qs = [one_half(qu, h) for h in range(2)]
        g = dot(awide[qi], proj_rows(s), 1, 1).astype(bf16)
        gs_h = [one_half(g, h) for h in range(2)]
        turned = (g.astype(f32) * os_[slot, at, :].astype(f32)).T
        deltas = [
            jnp.sum(turned[:HEAD], axis=0, keepdims=True),
            jnp.sum(turned[HEAD:], axis=0, keepdims=True),
        ]
        invs = [1.0 / l_ref[s, h : h + 1, at] for h in range(2)]
        dqt = [None, None]
        for j in range(len(lists[0])):
            b = block_at(lists, qi, j)
            cols = pl.ds(pl.multiple_of(b * tok, tok), tok)
            mask = masks[qi, j].astype(f32)
            kb, vb = ku[cols, :], vs_[slot, cols, :]
            dvs, dks = None, None
            for h in range(2):
                w = jnp.exp(dot(kb, qs[h], 1, 1) + mask) * invs[h]
                dp = dot(vb, gs_h[h], 1, 1)
                ds = (w * (dp - deltas[h])).astype(bf16)
                a = dot(w.astype(bf16), gs_h[h])
                c = dot(ds, qs[h])
                dvs = a if h == 0 else dvs + a
                dks = c if h == 0 else dks + c
                r = dot(kut[h * HEAD : (h + 1) * HEAD, cols], ds)
                dqt[h] = r if dqt[h] is None else dqt[h] + r
            dv[cols, :] += dvs
            dk[cols, :] += dks
        d = jnp.concatenate(dqt, axis=0).T
        hsum = jnp.sum(d * qhat * ehs, axis=0, keepdims=True)
        gq = (ehs * rq * (d - qhat * half_sums(qhat * d))).astype(bf16)
        gqs[s, at, :] = gq
        qsum = jnp.sum(gq.astype(f32), axis=0, keepdims=True)
        qcol = pl.ds(pl.multiple_of(nz * CORES * units + p.core * nz * width + s * LANES, LANES), LANES)
        vcol = pl.ds(
            pl.multiple_of(
                nz * CORES * (units + width) + p.core * nz * width + s * LANES, LANES
            ),
            LANES,
        )
        pay[row, qcol] += qsum
        for i in range(merge):
            chip = (s * merge + i) * CORES + p.core
            part[chip, SEGS + 1 : SEGS + 2, chunk : chunk + width] += hsum[
                :, i * width : (i + 1) * width
            ]

        @pl.when(qi == CORES - 1)
        def _():
            k = ks_[slot]
            rk = lax.rsqrt(half_sums(k * k) + epsilon)
            khat = k * rk
            d = dk[...]
            gkv[s, :, :LANES] = (rk * (d - khat * half_sums(khat * d))).astype(bf16)
            gv = dv[...].astype(bf16)
            gkv[s, :, LANES:] = gv
            pay[row, vcol] = jnp.sum(gv.astype(f32), axis=0, keepdims=True)
            put_grad(s, 0, dot(gqs[s], normed[:t, :], 0, 0))
            kvg = dot(gkv[s], normed[: blocks * tok, :], 0, 0)
            put_grad(s, 1, kvg[:LANES])
            put_grad(s, 2, kvg[LANES:])
            both = dot(os_[slot, :tok, :], awide[0], 0, 0)
            both = both + dot(os_[slot, tok:, :], awide[1], 0, 0)
            put_grad(s, 3, both)

        for when, todo in agenda.items():

            @pl.when(it == when)
            def _():
                for do in todo:
                    do()

    def norm_grad(b):
        at = pl.ds(b * tok, tok)
        total = None
        for s in range(pairs):
            r = dot(gkv[s, at, :], weight(s, 1, 2))
            if b < CORES:
                r = r + dot(gqs[s, at, :], weight(s, 0))
            total = r if total is None else total + r
        return total

    wloads = [
        pltpu.make_async_copy(
            wa_hbm.at[c, pl.ds(0, 3 * width)],
            normed.at[pl.ds(c * 3 * width, 3 * width)],
            wl.at[c],
        )
        for c in range(nz)
    ]
    for c in wloads:
        c.start()
    rooms = [awide.at[0], awide.at[1], got.at[0], got.at[1]]
    rooms += [spare.at[i] for i in range(spare.shape[0])]
    swap_at = lambda i: rooms[i]
    for c in wloads:
        c.wait()
    gcopies = [
        remote(swap_at(i), gmine.at[i], gs.at[i], gr.at[i], p.twin()) for i in range(rounds + 1)
    ]
    for i in range(rounds, -1, -1):
        swap_at(i)[...] = norm_grad(2 * i + 1).astype(bf16)
        gcopies[i].start()
    for o in late[1:]:
        if not (nz == 4 and m == 2):
            rm.pass_on(0, o)
    for o in far[: nz // 2]:
        ra.send_plane(0, o)
    if m == 2 and nz != 4:
        rm.forward_line(early[0])
    moves = []
    for i, per_core in enumerate(steps):
        own = norm_grad(2 * i + 2)
        gcopies[i + 1].wait()
        gmine[i + 1] = (own + gmine[i + 1].astype(f32)).astype(bf16)
        for c, step in enumerate(per_core):
            if step is None:
                continue
            go = (p.core == c) & (p.z - step >= 0) & (p.z - step < nz)
            have = (p.core == c) & (p.z + step >= 0) & (p.z + step < nz)
            to = (p.dp, jnp.clip(p.z - step, 0, nz - 1) * CORES + p.core)
            copy = remote(gmine.at[i + 1], ghalo.at[i], hs.at[i, c], hr.at[i, c], to)
            pl.when(go)(copy.start)
            moves.append((i, go, have, copy))
    own = norm_grad(0)
    gcopies[0].wait()
    own = own + gmine[0].astype(f32)
    if m > 1:
        for o in late:
            rm.pass_on(1, o)
    for level in range(2, m):
        for o in far:
            rm.pass_on(level, o)
    for o in far[nz // 2 :]:
        ra.send_plane(0, o)
    for k, o in enumerate(far):
        if k or m != 2:
            rm.forward_line(o)
    for o in far[: nz // 2]:
        ra.pass_on(0, o)
    for i, go, have, copy in moves:
        pl.when(have)(copy.wait_recv)
    for i in range(rounds):
        any_have = p.core < 0
        for j, go, have, copy in moves:
            if j == i:
                any_have = any_have | have

        @pl.when(jnp.logical_not(any_have))
        def _():
            ghalo[i] = jnp.zeros((tok, D), bf16)

    first = own
    for i in range(rounds):
        first = first + ghalo[i].astype(f32)
    normal, rstd = norm_parts(x_ref[...].astype(f32))
    scale = per_token(picks, table(SCALE_ONE))
    tg_ref[...] += norm_back(normal, rstd, first * (1.0 + scale))
    for which, values in ((SCALE_ONE, first * normal), (SHIFT_ONE, first)):
        pay[:SEGS, which * D : (which + 1) * D] = per_item(picks, values)[:SEGS]
    for j in range(n):
        part[j, :, :chunk] = pay[:, j * chunk : (j + 1) * chunk]
    line = p.line()
    sums = [remote(part.at[q[1]], held.at[o], s1.at[o], r1.at[o], q) for o, q in enumerate(line)]
    for c in sums:
        c.start()
    for o in far[nz // 2 :]:
        ra.pass_on(0, o)
    for c in sums:
        c.wait()
    total = part[p.me] + extra_ref[...]
    for o in range(n - 1):
        total = total + held[o]
    small_ref[p.core, p.dp, p.z] = total
    mine = small_ref.at[p.core, p.dp, p.z]
    sums = [remote(mine, mine, s3.at[o], r3.at[o], p.on_chip(o)) for o in p.far]
    for c in sums:
        c.start()
    for level in range(1, m):
        for o in far:
            ra.pass_on(level, o)
    for c in sums:
        c.wait()
    mine = small_ref.at[p.core, p.dp]
    plane = [(lax.rem(p.dp + o, nd), p.me) for o in range(1, nd)]
    sums = [remote(mine, mine, s2.at[o], r2.at[o], q) for o, q in enumerate(plane)]
    for c in sums:
        c.start()
    rm.end_line()
    for o in far:
        ra.forward_line(o)
    rm.back.step(0)
    ra.end_line()
    for c in sums:
        c.wait()
    mine = small_ref.at[p.core]
    last = remote(mine, mine, s4, r4, p.twin())
    last.start()
    for level in range(m):
        if level:
            rm.back.step(level)
        ra.back.step(level)
    last.wait()
    rm.end()
    ra.end()
    for i, go, have, copy in moves:
        pl.when(go)(copy.wait_send)


def backward(
    lengths, mine, theirs, tokens, out_grad, gmlp, branch, mod, down_bias, dbias, hist, extra, l,
    ehs, dm, normed, q, k, v, o, wa, steps, nd, width,
):
    n = wa.shape[0] * CORES
    nz = n // CORES
    tok = tokens.shape[0]
    rounds = len(steps)
    t, w = CORES * tok, k.shape[1]
    pairs = k.shape[0]
    piece, arows = dm.shape[3], 4 * width // nd
    rows, cols = extra.shape
    seen = len(seen_lists(steps, tok)[0])
    dma = pltpu.SemaphoreType.DMA
    vmem = pl.BlockSpec(memory_space=pltpu.VMEM)
    anywhere = pl.BlockSpec(memory_space=pl.ANY)
    m = bits_of(nd)
    scr = pltpu.VMEM
    plane = (2, m, nz, max(1, nd // 2))
    sems = lambda: [
        dma(plane),
        dma(plane),
        dma((2, 2, nz)),
        dma((2, 2, nz)),
        dma((2, nd)),
        dma((2, nd)),
        dma((2,)),
    ]
    return pl.pallas_call(
        functools.partial(backward_body, n, nd, steps, width),
        out_shape=[
            jax.ShapeDtypeStruct((tok, D), bf16),
            jax.ShapeDtypeStruct(dm.shape[1:], bf16),
            jax.ShapeDtypeStruct((4 * width, D), bf16),
            jax.ShapeDtypeStruct((tok, D), f32),
            jax.ShapeDtypeStruct((CORES, nd, nz, rows, cols), f32),
        ],
        in_specs=[pl.BlockSpec(memory_space=pltpu.SMEM)] + [vmem] * 13 + [anywhere] * 7,
        out_specs=[vmem, anywhere, anywhere, vmem, vmem],
        scratch_shapes=[
            scr((2, tok, D), bf16),
            scr((CORES, tok, D), bf16),
            scr((max(1, rounds - 3), tok if rounds > 3 else 16, D), bf16),
            scr((max(w, pairs * 3 * LANES), D), bf16),
            scr((nz, width, D), bf16),
            scr((2, t, LANES), f32),
            scr((2, w, LANES), f32),
            scr((2, w, LANES), bf16),
            scr((2, t, LANES), bf16),
            scr((w, LANES), bf16),
            scr((LANES, w), bf16),
            scr((w, LANES), f32),
            scr((w, LANES), f32),
            scr((pairs, t, LANES), bf16),
            scr((pairs, w, 2 * LANES), bf16),
            scr((CORES, seen, tok, tok), bf16),
            scr((2, nz, max(1, nd // 2), piece, D), bf16),
            scr((2, nd - 1, nz, piece, D), bf16),
            scr((2, 2, nz - 1, piece, D), bf16),
            scr((nz, 4 * width, D), bf16),
            scr((2, nd - 1, nz, arows, D // 2), bf16),
            scr((2, 2, nz - 1, arows, D // 2), bf16),
            scr((rounds + 1, tok, D), bf16),
            scr((rounds, tok, D), bf16),
            scr((8, 6 * D), f32),
            scr((n, rows, cols), f32),
            scr((n - 1, rows, cols), f32),
            dma((3,)),
            dma((3,)),
            dma((2,)),
            dma((nz,)),
            dma((4, 2)),
            dma((2, nd)),
        ]
        + sems()
        + sems()
        + [
            dma((rounds + 1,)),
            dma((rounds + 1,)),
            dma((rounds, CORES)),
            dma((rounds, CORES)),
            dma((n - 1,)),
            dma((n - 1,)),
            dma((nd - 1,)),
            dma((nd - 1,)),
            dma((nz,)),
            dma((nz,)),
            dma,
            dma,
        ],
        compiler_params=pltpu.CompilerParams(
            collective_id=1, has_side_effects=True, vmem_limit_bytes=60 << 20
        ),
        name="backward",
    )(
        lengths, mine, theirs, tokens, out_grad, gmlp, branch, mod, down_bias, dbias, hist, extra,
        l, ehs, dm, normed, q, k, v, o, wa,
    )


def local(
    nd,
    nt,
    tokens,
    class_embed,
    item_lengths,
    token_codes,
    ada_weight,
    ada_bias,
    qkv_weight,
    query_bias,
    value_bias,
    head_scale,
    proj_weight,
    proj_bias,
    up_weight,
    up_bias,
    down_weight,
    down_bias,
    out_grad,
):
    d, t = lax.axis_index("dp"), lax.axis_index("tensor")
    nz = nt // CORES
    z, core = t // CORES, t % CORES
    tok = tokens.shape[0]
    heads = head_scale.shape[0]
    width = heads * HEAD
    wide = nz * width
    pairs = wide // LANES
    units = up_weight.shape[1]
    feat = class_embed.shape[2]

    per_chip = CORES * tok
    seen = [[], []]
    for c in range(CORES):
        for step in range(1, nz):
            if step * per_chip - c * tok - tok < BEHIND:
                seen[c].append(step)
        for step in range(1, nz):
            if (step - 1) * per_chip + c * tok < AHEAD:
                seen[c].append(-step)
    rounds = max(len(s) for s in seen)
    steps = [
        tuple(s[len(s) - 1 - i] if i < len(s) else None for s in seen) for i in range(rounds)
    ]

    chunk = ada_weight.shape[1] // nt
    cond_act = jax.nn.silu(class_embed[0]).astype(bf16)
    ada_part = jnp.dot(cond_act, ada_weight, preferred_element_type=f32)
    part = jnp.pad(ada_part.reshape(SEGS, nt, chunk).transpose(1, 0, 2), ((0, 0), (0, 2), (0, 0)))
    bias_row = jnp.concatenate(
        [
            query_bias,
            value_bias,
            jnp.broadcast_to(jnp.exp(head_scale)[:, None], (heads, HEAD)).reshape(width),
            jnp.zeros((chunk - 3 * width,), f32),
        ]
    )
    extra = jnp.pad(bias_row[None], ((SEGS, 7 - SEGS), (0, 0)))
    abias = jnp.pad(
        jnp.broadcast_to(ada_bias.reshape(nt, 1, chunk), (nt, SEGS, chunk)),
        ((0, 0), (0, 8 - SEGS), (0, 0)),
    )
    apack = jnp.concatenate(
        [qkv_weight.transpose(1, 2, 0).reshape(3 * width, D), proj_weight], axis=0
    )
    mpack = jnp.stack([up_weight.T, down_weight]).reshape(2, nd, units // nd, D)
    (
        normed, q_raw, k_raw, v_in, heads_out, weight_sums, wattn, wmlp, branch, resid, nwide,
        gwide, mod_wide, ehs,
    ) = forward(
        item_lengths[0], tokens, out_grad, part, extra, abias, proj_bias[None], apack, mpack,
        steps, nd, width,
    )
    up_own = lax.dynamic_index_in_dim(
        up_bias.reshape(nz, CORES, units), core, 1, keepdims=False
    )
    mine, theirs, dmlp, dbias = mlp(
        nwide.reshape(CORES * tok, D), gwide.reshape(CORES * tok, D), wmlp, up_own
    )
    low_codes = 64
    hot = lambda v, k: (v[:, None] == jnp.arange(k, dtype=jnp.int32)[None, :]).astype(bf16)
    hist = dot(
        hot(token_codes // low_codes, NBINS // low_codes),
        hot(token_codes % low_codes, low_codes),
        0,
        0,
    ).reshape(1, NBINS)
    own_tail = jnp.pad(cond_act.astype(f32), ((0, 8 - SEGS), (chunk, LANES - feat)))
    layer_out, ymlp, yattn, tokens_grad, small = backward(
        item_lengths[0], mine, theirs, tokens, out_grad, gwide[0], branch, mod_wide,
        down_bias[None], dbias.reshape(nz, units), hist, own_tail, weight_sums, ehs, dmlp,
        normed, q_raw, k_raw, v_in, heads_out, wattn, steps, nd, width,
    )

    rows_all = small[..., :chunk].transpose(1, 3, 2, 0, 4).reshape(nd, 8, 6 * D)
    mod_all = rows_all[:, :SEGS].reshape(nd * SEGS, 6 * D)
    mod_own = lax.dynamic_index_in_dim(rows_all, d, 0, keepdims=False)[:SEGS]
    bias_sums = jnp.sum(rows_all[:, SEGS:], axis=0)
    own_small = lax.dynamic_index_in_dim(small, core, 0, keepdims=False)
    own_small = lax.dynamic_index_in_dim(own_small, z, 1, keepdims=False)
    cond_all = own_small[:, :SEGS, chunk : chunk + feat].reshape(nd * SEGS, feat)
    hscale_grad = jnp.sum(own_small[:, 7, chunk : chunk + width].reshape(nd, heads, HEAD), axis=(0, 2))
    adaw_grad = dot(cond_all, mod_all, 0, 0, highest)
    adab_grad = jnp.sum(mod_all, axis=0)
    cond_grad = dot(mod_own, ada_weight.astype(f32), 1, 1, highest)
    embed_grad = jax.vjp(jax.nn.silu, class_embed)[1](cond_grad[None])[0]
    projb_grad, downb_grad = bias_sums[0, :D], bias_sums[0, D : 2 * D]
    code_hist = bias_sums[0, 2 * D :]
    at = lambda base, k: lax.dynamic_slice_in_dim(bias_sums[1], base + (core * nz + z) * k, k, 0)
    upb_grad = at(0, units)
    qbias_grad = at(nt * units, width)
    vbias_grad = at(nt * (units + width), width)
    qkvw_grad = yattn[: 3 * width].astype(f32).reshape(3, width, D).transpose(2, 0, 1)
    projw_grad = yattn[3 * width :].astype(f32)
    upw_grad = ymlp[0].reshape(units, D).astype(f32).T
    downw_grad = ymlp[1].reshape(units, D).astype(f32)
    return (
        layer_out,
        tokens_grad,
        embed_grad,
        adaw_grad,
        adab_grad,
        qkvw_grad,
        qbias_grad,
        vbias_grad,
        hscale_grad,
        projw_grad,
        projb_grad,
        upw_grad,
        upb_grad,
        downw_grad,
        downb_grad,
        code_hist,
    )


def solution(mesh):
    placed = (
        P(("dp", "tensor"), None),
        P("dp", None, "tensor"),
        P("dp", None),
        P(("dp", "tensor")),
        P("tensor", None),
        P(),
        P(None, None, "tensor"),
        P("tensor"),
        P("tensor"),
        P("tensor"),
        P("tensor", None),
        P(),
        P(None, "tensor"),
        P(),
        P("tensor", None),
        P(),
        P(("dp", "tensor"), None),
    )
    return jax.shard_map(
        functools.partial(local, mesh.shape["dp"], mesh.shape["tensor"]),
        mesh=mesh,
        in_specs=placed,
        out_specs=(
            P(("dp", "tensor"), None),
            P(("dp", "tensor"), None),
            P("dp", None, "tensor"),
            P("tensor", None),
            P(),
            P(None, None, "tensor"),
            P("tensor"),
            P("tensor"),
            P("tensor"),
            P("tensor", None),
            P(),
            P(None, "tensor"),
            P("tensor"),
            P("tensor", None),
            P(),
            P(),
        ),
        check_vma=False,
    )
```

```python
import functools

import jax
import jax.numpy as jnp
from jax import lax
from jax.experimental import pallas as pl
from jax.experimental.pallas import tpu as pltpu
from jax.sharding import PartitionSpec as P

HEAD = 64
NBINS = 4096
ROW_LEN = 2048
SEGS = 6
D = 1024
ITEM_MAX = 680
CORES = 2
LANES = 128

epsilon = 1e-06
scale_starts = (1, 5, 14, 30, 55, 91, 155, 255, 424)
AHEAD = ITEM_MAX - scale_starts[-1] - 1
BEHIND = ITEM_MAX - 1
highest = lax.Precision.HIGHEST
f32 = jnp.float32
bf16 = jnp.bfloat16
MESH = pl.DeviceIdType.MESH
VMEM_LIMIT = 56 << 20


def dot(a, b, ca=1, cb=0, precision=None):
    return lax.dot_general(
        a, b, (((ca,), (cb,)), ((), ())), preferred_element_type=f32, precision=precision
    )


def item_layout(lengths):
    ends = jnp.cumsum(lengths, dtype=jnp.int32)
    begin = ends - lengths
    position = jnp.arange(ROW_LEN, dtype=jnp.int32)
    segment = jnp.sum((position[:, None] >= ends[None, :]).astype(jnp.int32), axis=1)
    chosen = segment[:, None] == jnp.arange(SEGS, dtype=jnp.int32)[None, :]
    inside = position - jnp.sum(jnp.where(chosen, begin[None, :], 0), axis=1)
    scale_ids = jnp.zeros_like(inside)
    for threshold in scale_starts:
        scale_ids = scale_ids + (inside >= threshold).astype(jnp.int32)
    return segment, scale_ids


def greet(peers):
    barrier = pltpu.get_barrier_semaphore()
    for p in peers:
        pl.semaphore_signal(barrier, inc=1, device_id=p, device_id_type=MESH)
    pl.semaphore_wait(barrier, len(peers))


def remote(src, dst, send, recv, to):
    return pltpu.make_async_remote_copy(
        src_ref=src,
        dst_ref=dst,
        send_sem=send,
        recv_sem=recv,
        device_id=to,
        device_id_type=MESH,
    )


class Place:
    def __init__(self, n, nd):
        self.n, self.nd, self.nz = n, nd, n // CORES
        self.dp, self.me = lax.axis_index("dp"), lax.axis_index("tensor")
        self.z, self.core = self.me // CORES, lax.rem(self.me, CORES)
        self.orders = orders_of(nd)
        self.far = sorted(range(1, self.nz), key=lambda o: min(o, self.nz - o))

    def chip(self, step):
        return lax.rem(self.z + step + self.nz, self.nz)

    def on_chip(self, step):
        return (self.dp, self.chip(step) * CORES + self.core)

    def turn(self, k):
        return jnp.where(self.z < self.nz // 2, self.nz - 1 - k, k)

    def twin(self):
        return (self.dp, self.z * CORES + 1 - self.core)

    def flip(self, bit):
        return (self.dp ^ (1 << bit), self.me)

    def line(self):
        return [(self.dp, lax.rem(self.me + o, self.n)) for o in range(1, self.n)]

    def greet_all(self):
        greet(self.line() + [self.flip(b) for b in range(bits_of(self.nd))])


def bits_of(nd):
    return nd.bit_length() - 1


def orders_of(nd):
    m = bits_of(nd)
    return [list(range(m)), [(m // 2 + i) % m for i in range(m)]]


def spread_plan(order):
    plan = [(0, list(order))]
    for i, bit in enumerate(order):
        plan += [(rel | (1 << bit), list(order[i + 1 :])) for rel, _ in list(plan)]
    return plan


class Spread:
    def __init__(self, place, ref_of, send, recv):
        self.place, self.ref_of, self.send, self.recv = place, ref_of, send, recv
        self.levels = bits_of(place.nd)

    def sends(self, part, rel, bits):
        p = self.place
        ref = self.ref_of(part, p.dp ^ rel)
        for bit in bits:
            to = rel | (1 << bit)
            yield remote(ref, ref, self.send.at[part, to], self.recv.at[part, to], p.flip(bit))

    def arrived(self, level):
        for part, order in enumerate(self.place.orders):
            for rel, bits in spread_plan(order):
                if rel and len(order) - 1 - len(bits) == level:
                    yield part, rel, bits

    def begin(self):
        for part, order in enumerate(self.place.orders):
            for c in self.sends(part, 0, order):
                c.start()

    def step(self, level):
        p = self.place
        for part, rel, bits in self.arrived(level):
            ref = self.ref_of(part, p.dp ^ rel)
            remote(
                ref, ref, self.send.at[part, rel], self.recv.at[part, rel], p.flip(0)
            ).wait_recv()
            for c in self.sends(part, rel, bits):
                c.start()

    def end(self):
        for part, order in enumerate(self.place.orders):
            for rel, bits in spread_plan(order):
                for c in self.sends(part, rel, bits):
                    c.wait_send()


class Line:
    def __init__(self, place, own, ref_of, send, recv):
        self.p, self.own, self.ref_of, self.send, self.recv = place, own, ref_of, send, recv
        self.ways = (1, -1)

    def inside(self, z):
        return (z >= 0) & (z < self.p.nz)

    def source(self, w, step):
        z = self.p.z - self.ways[w] * step
        return jnp.clip(z, 0, self.p.nz - 1), self.inside(z)

    def copies(self, w, step):
        p = self.p
        to = p.z + self.ways[w]
        chip, have = self.source(w, step - 1)
        there = self.ref_of(chip)
        cs = [
            remote(
                src,
                dst,
                self.send.at[w, step, i],
                self.recv.at[w, step, i],
                (p.dp, jnp.clip(to, 0, p.nz - 1) * CORES + p.core),
            )
            for i, (src, dst) in enumerate(zip(self.own if step == 1 else there, there))
        ]
        return cs, have & self.inside(to)

    def start(self, step=1):
        for w in range(2):
            cs, do = self.copies(w, step)

            @pl.when(do)
            def _():
                for c in cs:
                    c.start()

    def got(self, step, then):
        for w in range(2):
            chip, have = self.source(w, step)
            waits = [
                remote(ref, ref, self.send.at[w, step, i], self.recv.at[w, step, i], self.p.twin())
                for i, ref in enumerate(self.ref_of(chip))
            ]
            on, more = [], None
            if step + 1 < self.p.nz:
                on, more = self.copies(w, step + 1)

            @pl.when(have)
            def _():
                for c in waits:
                    c.wait_recv()
                if on:

                    @pl.when(more)
                    def _():
                        for c in on:
                            c.start()

                then(w, chip)

    def each(self, step, do):
        for w in range(2):
            chip, have = self.source(w, step)
            pl.when(have)(functools.partial(do, w, chip))

    def end(self):
        for step in range(1, self.p.nz):
            for w in range(2):
                cs, do = self.copies(w, step)

                @pl.when(do)
                def _():
                    for c in cs:
                        c.wait_send()


def picks_of(seg):
    return (seg == lax.broadcasted_iota(jnp.int32, (seg.shape[0], 8), 1)).astype(bf16)


def two(x):
    high = x.astype(bf16)
    return high, (x - high.astype(f32)).astype(bf16)


def per_token(picks, table):
    high, low = two(table)
    return dot(picks, high) + dot(picks, low)


def per_item(picks, values):
    high, low = two(values)
    return dot(picks, high, 0, 0) + dot(picks, low, 0, 0)


def norm_parts(values):
    centred = values - jnp.mean(values, axis=-1, keepdims=True)
    rstd = lax.rsqrt(jnp.mean(centred * centred, axis=-1, keepdims=True) + epsilon)
    return centred * rstd, rstd


def norm_back(normal, rstd, scaled):
    return rstd * (
        scaled
        - jnp.mean(scaled, axis=-1, keepdims=True)
        - normal * jnp.mean(scaled * normal, axis=-1, keepdims=True)
    )


GAMMA_ONE, GAMMA_TWO, SCALE_ONE, SCALE_TWO, SHIFT_ONE, SHIFT_TWO = range(6)


def half_lanes(rows):
    return lax.broadcasted_iota(jnp.int32, (rows, LANES), 1) < HEAD


def half_sums(x):
    low = half_lanes(x.shape[0])
    a = jnp.sum(jnp.where(low, x, 0.0), axis=1, keepdims=True)
    b = jnp.sum(jnp.where(low, 0.0, x), axis=1, keepdims=True)
    return jnp.where(low, a, b)


def one_half(x, h):
    low = half_lanes(x.shape[0])
    return jnp.where(low if h == 0 else jnp.logical_not(low), x, jnp.zeros_like(x))


def ranks_at(lengths_ref, owner, tok, shape, axis):
    place = jnp.maximum(owner, 0) * tok + lax.broadcasted_iota(jnp.int32, shape, axis)
    item = jnp.zeros(shape, jnp.int32)
    begin = jnp.zeros(shape, jnp.int32)
    end = jnp.int32(0)
    for i in range(SEGS):
        end = end + lengths_ref[i]
        past = place >= end
        item = item + past.astype(jnp.int32)
        begin = jnp.where(past, end, begin)
    rank = item * 16
    for threshold in scale_starts:
        rank = rank + (place - begin >= threshold).astype(jnp.int32)
    there = owner >= 0
    return item, jnp.where(there, rank, -1)


def owners_of(p, steps):
    owners = []
    for s in [(0, 0)] + list(steps):
        for flip in range(CORES):
            c = p.core ^ flip
            far = [p.nz if v is None else v for v in s]
            chip = p.z - jnp.where(c == 0, far[0], far[1])
            owners.append(jnp.where((chip >= 0) & (chip < p.nz), chip * CORES + c, -1))
    return owners


def seen_lists(steps, tok):
    lists = []
    for qi in range(CORES):
        seen = set()
        for c in range(CORES):
            query = c ^ qi
            for i, s in enumerate([(0, 0)] + list(steps)):
                for flip in range(CORES):
                    owner = c ^ flip
                    if s[owner] is None:
                        continue
                    off = owner - s[owner] * CORES - query
                    near = off == 0
                    behind = off < 0 and (-off - 1) * tok + 1 <= BEHIND
                    ahead = off > 0 and (off - 1) * tok + 1 <= AHEAD
                    if near or behind or ahead:
                        seen.add(2 * i + flip)
        lists.append(seen)
    both = sorted(lists[0] & lists[1])
    rest = [sorted(v - set(both)) for v in lists]
    size = max(len(r) for r in rest)
    for r in rest:
        spare = [b for b in range(2 * len(steps) + 2) if b not in both and b not in r]
        r += spare[: size - len(r)]
    return [both + rest[0], both + rest[1]]


def block_at(lists, qi, j):
    a, b = lists[0][j], lists[1][j]
    return a if a == b else jnp.where(qi == 0, a, b)


def forward_body(
    n, nd, steps, width, len_ref, hs_ref, tok_ref, grad_ref, part_ref, abias_ref, qbias_ref,
    vbias_ref, pb_ref,
    apack_ref, up_ref, down_ref,
    n_out, q_out, k_out, v_out, o_ref, l_ref, wa_out, wm_ref, branch_ref, resid_ref, nwide_ref,
    gwide_ref, mod_ref, ehs_ref,
    win, wa, modc, held, normed, qv, kv, vv, qb, vb, masks, ku, v0, v1, theirs, got,
    s1, r1, s2, r2, ts, tr, cs, cr, azs, azr, mzs, mzr, local_sem, out_sem, das, dar, dms, dmr,
    ms, mr,
):
    p = Place(n, nd)
    nz, tok = p.nz, grad_ref.shape[0]
    rounds = len(steps)
    blocks = 2 * rounds + 2
    pairs = qv.shape[0]
    merge = LANES // width
    rows = 4 * width // nd
    half = D // 2
    chunk = modc.shape[2]
    owners = owners_of(p, steps)
    p.greet_all()
    line = p.line()

    a_at = lambda chip, d: wa.at[chip, pl.ds(d * rows, rows)]
    mine = pl.ds(p.dp * rows, rows)
    al = Line(p, [apack_ref.at[mine]], lambda chip: [wa.at[chip, mine]], azs, azr)
    ml = Line(
        p,
        [up_ref.at[p.dp], down_ref.at[p.dp]],
        lambda chip: [wm_ref.at[chip, i, p.dp] for i in range(2)],
        mzs,
        mzr,
    )

    def a_spread(w, step, chip):
        return Spread(
            p,
            lambda part, d: wa.at[chip, pl.ds(d * rows, rows), pl.ds(part * half, half)],
            das.at[w, step],
            dar.at[w, step],
        )

    def m_spread(w, step, chip):
        return Spread(
            p, lambda part, d: wm_ref.at[chip, part, d], dms.at[w, step], dmr.at[w, step]
        )

    al.start()
    owns = [
        pltpu.make_async_copy(tok_ref, win.at[0], local_sem.at[0]),
        pltpu.make_async_copy(apack_ref, wa.at[p.z], local_sem.at[1]),
        pltpu.make_async_copy(up_ref, wm_ref.at[p.z, 0], local_sem.at[2]),
        pltpu.make_async_copy(down_ref, wm_ref.at[p.z, 1], local_sem.at[3]),
    ]
    for c in owns:
        c.start()
    sums = [
        remote(part_ref.at[q[1]], held.at[o], s1.at[o], r1.at[o], q) for o, q in enumerate(line)
    ]
    for c in sums:
        c.start()
    twins = [
        remote(tok_ref if i == 0 else win.at[2 * i], win.at[2 * i + 1], cs.at[i], cr.at[i], p.twin())
        for i in range(rounds + 1)
    ]
    twins[0].start()
    for c in sums:
        c.wait()
    own = pl.ds(pl.multiple_of(p.me * chunk, LANES), chunk)
    total = part_ref[p.me] + abias_ref[:, own]
    for o in range(n - 1):
        total = total + held[o]
    modc[p.me] = total
    modc[p.me, SEGS : SEGS + 1, :width] = qbias_ref[...]
    modc[p.me, SEGS : SEGS + 1, width : 2 * width] = vbias_ref[...]
    for h in range(width // HEAD):
        at = 2 * width + h * HEAD
        modc[p.me, SEGS : SEGS + 1, at : at + HEAD] = jnp.exp(jnp.full((1, HEAD), hs_ref[h], f32))
    sums = [
        remote(modc.at[p.me], modc.at[p.me], s2.at[o], r2.at[o], q) for o, q in enumerate(line)
    ]
    for c in sums:
        c.start()
    moves = []
    for i, per_core in enumerate(steps):
        for c, step in enumerate(per_core):
            if step is None:
                continue
            go = (p.core == c) & (p.z + step >= 0) & (p.z + step < nz)
            have = (p.core == c) & (p.z - step >= 0) & (p.z - step < nz)
            to = (p.dp, jnp.clip(p.z + step, 0, nz - 1) * CORES + p.core)
            moves.append((i, go, have, remote(tok_ref, win.at[2 * i + 2], ts.at[i, c], tr.at[i, c], to)))
    al.got(1, lambda w, chip: a_spread(w, 1, chip).begin())
    for i, go, have, copy in moves:
        pl.when(go)(copy.start)
    for step in range(2, nz):
        al.got(step, lambda w, chip: a_spread(w, step, chip).begin())
    ml.start()

    for c in sums:
        c.wait()
    for j in range(n):
        mod_ref[:, j * chunk : (j + 1) * chunk] = modc[j]
    table = lambda which: mod_ref[:, which * D : (which + 1) * D]
    for s in range(pairs):
        parts = []
        for i in range(merge):
            r = modc[(s * merge + i) * CORES + p.core, SEGS : SEGS + 1, :]
            parts.append([r[:, k * width : (k + 1) * width] for k in range(3)])
        row = lambda k: jnp.concatenate([v[k] for v in parts], axis=1) if merge > 1 else parts[0][k]
        qb[s], vb[s], ehs_ref[s] = row(0), row(1), row(2)

    lists = seen_lists(steps, tok)
    for qi in range(CORES):
        owner = owners[qi]
        item, rank = ranks_at(len_ref, owner, tok, (tok, LANES), 0)
        lo, hi = item[:, :1] * 16, rank[:, :1]
        for j, b in enumerate(lists[qi]):
            _, e = ranks_at(len_ref, owners[b], tok, (8, tok), 1)
            e = e[:1]
            masks[qi, j] = jnp.where((e >= lo) & (e <= hi), 0.0, -1e30)
    own_item, _ = ranks_at(len_ref, owners[0], tok, (tok, 8), 0)
    picks = (own_item == lax.broadcasted_iota(jnp.int32, (tok, 8), 1)).astype(bf16)

    gwide_ref[0] = (per_token(picks, table(GAMMA_TWO)) * grad_ref[...].astype(f32)).astype(bf16)
    cross = [
        remote(gwide_ref.at[0], gwide_ref.at[1], ms.at[0], mr.at[0], p.twin()),
        remote(theirs, got, ms.at[1], mr.at[1], p.twin()),
        remote(nwide_ref.at[0], nwide_ref.at[1], ms.at[2], mr.at[2], p.twin()),
    ]
    cross[0].start()

    owns[0].wait()
    twins[0].wait()

    def norm_block(b):
        owner = owners[0]
        for i in range(1, blocks):
            owner = jnp.where(b == i, owners[i], owner)
        item, _ = ranks_at(len_ref, owner, tok, (tok, 8), 0)
        pick = (item == lax.broadcasted_iota(jnp.int32, (tok, 8), 1)).astype(bf16)
        normal, _ = norm_parts(win[b].astype(f32))
        scale = per_token(pick, table(SCALE_ONE))
        shift = per_token(pick, table(SHIFT_ONE))
        at = pl.ds(pl.multiple_of(b * tok, tok), tok)
        normed[at, :] = (normal * (1.0 + scale) + shift).astype(bf16)

    def weight(s, k, count=1):
        if merge == 1:
            return wa[s, k * width : (k + count) * width, :]
        rows_of = [
            wa[s * merge + i, (k + j) * width : (k + j + 1) * width, :]
            for j in range(count)
            for i in range(merge)
        ]
        return jnp.concatenate(rows_of, axis=0)

    def keys_block(b):
        at = pl.ds(pl.multiple_of(b * tok, tok), tok)

        def slot(s, _):
            r = dot(normed[at, :], weight(s, 1, 2), 1, 1)
            kv[s, at, :] = r[:, :LANES]
            vv[s, at, :] = (r[:, LANES:] + vb[s]).astype(bf16)
            return 0

        lax.fori_loop(0, pairs, slot, 0)

    @pl.loop(0, CORES)
    def _(b):
        norm_block(b)

    for level in range(bits_of(nd)):
        for step in range(1, nz):
            al.each(step, lambda w, chip: a_spread(w, step, chip).step(level))
    owns[1].wait()
    wout = pltpu.make_async_copy(wa, wa_out, out_sem.at[0])
    wout.start()

    @pl.loop(0, CORES)
    def _(b):
        keys_block(b)
        at = pl.ds(pl.multiple_of(b * tok, tok), tok)

        def slot(s, _):
            qv[s, at, :] = dot(normed[at, :], weight(s, 0), 1, 1) + qb[s]
            return 0

        lax.fori_loop(0, pairs, slot, 0)

    for i in range(rounds):
        any_got = p.core < 0
        for j, go, have, copy in moves:
            if j == i:
                pl.when(have)(copy.wait_recv)
                any_got = any_got | have

        @pl.when(jnp.logical_not(any_got))
        def _():
            win[2 * i + 2] = jnp.zeros((tok, D), bf16)

        twins[i + 1].start()
    for i in range(rounds):
        twins[i + 1].wait()

    ml.got(1, lambda w, chip: m_spread(w, 1, chip).begin())

    @pl.loop(CORES, blocks)
    def _(b):
        norm_block(b)
        keys_block(b)

    outs = [wout]
    for i, (src, dst) in enumerate(((normed, n_out), (qv, q_out), (kv, k_out), (vv, v_out))):
        outs.append(pltpu.make_async_copy(src, dst, out_sem.at[i + 1]))
        outs[-1].start()

    trips = pairs * CORES
    agenda = {}
    for step in range(1, nz):
        if step + 1 < nz:
            at = min(trips - 1, ((step - 1) * trips) // nz)
            agenda.setdefault(at, []).append((step + 1, 0))
        at = min(trips - 1, (step * trips) // nz)
        agenda.setdefault(at, []).append((0, step))

    @pl.loop(0, trips)
    def _(it):
        s, qi = it // CORES, lax.rem(it, CORES)

        @pl.when(qi == 0)
        def _():
            k = kv[s]
            ku[...] = (k * lax.rsqrt(half_sums(k * k) + epsilon)).astype(bf16)
            v = vv[s]
            low = half_lanes(v.shape[0])
            one = jnp.ones_like(v)
            v0[...] = jnp.where(low, v, one)
            v1[...] = jnp.where(low, one, v)

        at = pl.ds(pl.multiple_of(qi * tok, tok), tok)
        q = qv[s, at, :]
        qu = (q * lax.rsqrt(half_sums(q * q) + epsilon) * ehs_ref[s]).astype(bf16)
        qs = [one_half(qu, h) for h in range(2)]
        acc = [None, None]
        for j in range(len(lists[0])):
            b = block_at(lists, qi, j)
            cols = pl.ds(pl.multiple_of(b * tok, tok), tok)
            mask = masks[qi, j]
            for h in range(2):
                w = jnp.exp(dot(qs[h], ku[cols, :], 1, 1) + mask).astype(bf16)
                r = dot(w, (v0 if h == 0 else v1)[cols, :])
                acc[h] = r if acc[h] is None else acc[h] + r
        low = half_lanes(tok)
        other = jnp.where(low, pltpu.roll(acc[0], HEAD, 1), pltpu.roll(acc[1], HEAD, 1))
        o_ref[s, at, :] = (jnp.where(low, acc[0], acc[1]) / other).astype(bf16)
        turned = other.T
        l_ref[s, 0:1, at] = turned[0:1, :]
        l_ref[s, 1:2, at] = turned[HEAD : HEAD + 1, :]

        for when, todo in agenda.items():

            @pl.when(it == when)
            def _():
                for get, step in todo:
                    if get:
                        ml.got(get, lambda w, chip: m_spread(w, get, chip).begin())
                    else:
                        ml.each(step, lambda w, chip: m_spread(w, step, chip).step(0))

    def project(at):
        total = dot(o_ref[0, at, :], weight(0, 3))
        for s in range(1, pairs):
            total += dot(o_ref[s, at, :], weight(s, 3))
        return total

    theirs[...] = project(pl.ds(tok, tok)).astype(bf16)
    cross[1].start()
    first = project(pl.ds(0, tok)) + pb_ref[...]
    cross[1].wait()
    branch = first + got[...].astype(f32)
    branch_ref[...] = branch
    resid = win[0].astype(f32) + per_token(picks, table(GAMMA_ONE)) * branch
    resid_ref[...] = resid
    normal, _ = norm_parts(resid)
    scale = per_token(picks, table(SCALE_TWO))
    shift = per_token(picks, table(SHIFT_TWO))
    nwide_ref[0] = (normal * (1.0 + scale) + shift).astype(bf16)
    cross[2].start()

    for level in range(1, bits_of(nd)):
        for step in range(1, nz):
            ml.each(step, lambda w, chip: m_spread(w, step, chip).step(level))
    cross[0].wait()
    cross[2].wait()
    for step in range(1, nz):
        al.each(step, lambda w, chip: a_spread(w, step, chip).end())
        ml.each(step, lambda w, chip: m_spread(w, step, chip).end())
    al.end()
    ml.end()
    for i, go, have, copy in moves:
        pl.when(go)(copy.wait_send)
    owns[2].wait()
    owns[3].wait()
    for c in outs:
        c.wait()


def forward(
    lengths, scales, tokens, out_grad, part, abias, qbias, vbias, proj_bias, apack, up, down,
    steps, nd, width,
):
    n, _, cols = part.shape
    nz = n // CORES
    tok = tokens.shape[0]
    rounds = len(steps)
    blocks = 2 * rounds + 2
    t, w = CORES * tok, blocks * tok
    pairs = nz * width // LANES
    seen = len(seen_lists(steps, tok)[0])
    dma = pltpu.SemaphoreType.DMA
    vmem = pl.BlockSpec(memory_space=pltpu.VMEM)
    anywhere = pl.BlockSpec(memory_space=pl.ANY)
    out = lambda *shape: jax.ShapeDtypeStruct(shape, f32)
    low = lambda *shape: jax.ShapeDtypeStruct(shape, bf16)
    v = pltpu.VMEM
    return pl.pallas_call(
        functools.partial(forward_body, n, nd, steps, width),
        out_shape=[
            low(w, D),
            out(pairs, t, LANES),
            out(pairs, w, LANES),
            low(pairs, w, LANES),
            low(pairs, t, LANES),
            out(pairs, 8, t),
            low(nz, 4 * width, D),
            low(nz, 2, *up.shape),
            out(tok, D),
            out(tok, D),
            low(CORES, tok, D),
            low(CORES, tok, D),
            out(8, 6 * D),
            out(pairs, 1, LANES),
        ],
        in_specs=[pl.BlockSpec(memory_space=pltpu.SMEM)] * 2
        + [anywhere]
        + [vmem] * 6
        + [anywhere] * 3,
        out_specs=[anywhere] * 4 + [vmem] * 2 + [anywhere] * 2 + [vmem] * 6,
        scratch_shapes=[
            v((blocks, tok, D), bf16),
            v((nz, 4 * width, D), bf16),
            v(part.shape, f32),
            v((n - 1,) + part.shape[1:], f32),
            v((w, D), bf16),
            v((pairs, t, LANES), f32),
            v((pairs, w, LANES), f32),
            v((pairs, w, LANES), bf16),
            v((pairs, 1, LANES), f32),
            v((pairs, 1, LANES), f32),
            v((CORES, seen, tok, tok), f32),
            v((w, LANES), bf16),
            v((w, LANES), bf16),
            v((w, LANES), bf16),
            v((tok, D), bf16),
            v((tok, D), bf16),
            dma((n - 1,)),
            dma((n - 1,)),
            dma((n - 1,)),
            dma((n - 1,)),
            dma((rounds, CORES)),
            dma((rounds, CORES)),
            dma((rounds + 1,)),
            dma((rounds + 1,)),
            dma((2, nz, 1)),
            dma((2, nz, 1)),
            dma((2, nz, 2)),
            dma((2, nz, 2)),
            dma((4,)),
            dma((5,)),
            dma((2, nz, 2, nd)),
            dma((2, nz, 2, nd)),
            dma((2, nz, 2, nd)),
            dma((2, nz, 2, nd)),
            dma((3,)),
            dma((3,)),
        ],
        compiler_params=pltpu.CompilerParams(
            collective_id=0, has_side_effects=True, vmem_limit_bytes=VMEM_LIMIT
        ),
        name="forward",
    )(
        lengths, scales, tokens, out_grad, part, abias, qbias, vbias, proj_bias, apack, up, down
    )


def mlp_body(x_ref, g_ref, w_ref, bias_ref, mine_ref, theirs_ref, dw_ref, dbias_ref, gsum_ref, mlp, gx):
    x, g = x_ref[...], g_ref[...]
    tok = mine_ref.shape[1]
    units = w_ref.shape[2] * w_ref.shape[3]
    up = w_ref[0, 0].reshape(units, D)
    down = w_ref[0, 1].reshape(units, D)
    pre = dot(x, up, 1, 1) + bias_ref[0]
    square = pre * pre
    th = jnp.tanh(0.7978845608028654 * pre * (1.0 + 0.044715 * square))
    half = 0.5 * (1.0 + th)
    hidden = (pre * half).astype(bf16)
    slope = half + 0.5 * pre * (1.0 - th * th) * (
        0.7978845608028654 * (1.0 + 3.0 * 0.044715 * square)
    )
    gp = (dot(g, down, 1, 1) * slope).astype(bf16)

    @pl.when(pl.program_id(0) == 0)
    def _():
        gsum_ref[...] = jnp.sum(g[:tok].astype(f32), axis=0, keepdims=True)
        mlp[...] = jnp.zeros_like(mlp)
        gx[...] = jnp.zeros_like(gx)

    mlp[...] += dot(hidden, down)
    gx[...] += dot(gp, up)
    dw_ref[0, 0] = dot(gp, x, 0, 0).astype(bf16).reshape(dw_ref.shape[2:])
    dw_ref[0, 1] = dot(hidden, g, 0, 0).astype(bf16).reshape(dw_ref.shape[2:])
    dbias_ref[0] = jnp.sum(gp.astype(f32), axis=0, keepdims=True)

    @pl.when(pl.program_id(0) == pl.num_programs(0) - 1)
    def _():
        for i, v in enumerate((gx, mlp)):
            mine_ref[i] = v[:tok, :]
            theirs_ref[i] = v[tok:, :].astype(bf16)


def mlp(x, g, weights, bias):
    t = x.shape[0]
    tok = t // CORES
    nz, _, nd, piece, _ = weights.shape
    count = min(nd, max(1, 512 // piece))
    per = nd // count
    steps, units = nz * per, count * piece
    whole = lambda *shape: pl.BlockSpec(shape, lambda i: (0,) * len(shape))
    block = pl.BlockSpec((1, 2, count, piece, D), lambda i: (i // per, 0, i % per, 0, 0))
    row = pl.BlockSpec((1, 1, units), lambda i: (i, 0, 0))
    return pl.pallas_call(
        mlp_body,
        grid=(steps,),
        in_specs=[whole(t, D), whole(t, D), block, row],
        out_specs=[whole(2, tok, D), whole(2, tok, D), block, row, whole(1, D)],
        out_shape=[
            jax.ShapeDtypeStruct((2, tok, D), f32),
            jax.ShapeDtypeStruct((2, tok, D), bf16),
            jax.ShapeDtypeStruct(weights.shape, bf16),
            jax.ShapeDtypeStruct((steps, 1, units), f32),
            jax.ShapeDtypeStruct((1, D), f32),
        ],
        scratch_shapes=[pltpu.VMEM((t, D), f32), pltpu.VMEM((t, D), f32)],
        compiler_params=pltpu.CompilerParams(vmem_limit_bytes=VMEM_LIMIT),
        name="mlp",
    )(x, g, weights, bias.reshape(steps, 1, units))


class Reduce:
    def __init__(self, place, sent, kept, stage, zstage, out, sems):
        self.p, self.sent, self.kept = place, sent, kept
        self.stage, self.zstage = stage, zstage
        self.ps, self.pr, self.zs, self.zr, self.os, self.or_, self.fs = sems
        self.m = bits_of(place.nd)
        self.back = Spread(place, out, self.os, self.or_)
        self.out = out

    def held(self, part, level):
        rels = list(range(self.p.nd))
        for bit in self.p.orders[part][:level]:
            rels = [r for r in rels if not (r >> bit) & 1]
        return rels

    def current(self, part, level, chip, rel):
        if level == 0:
            bit = self.p.orders[part][0]
            return (self.sent if (rel >> bit) & 1 else self.kept)(part, chip, self.p.dp ^ rel)
        return self.stage(part, level - 1, chip, self.held(part, level).index(rel))

    def plane(self, level, chip):
        for part, order in enumerate(self.p.orders):
            bit = order[level]
            for rel in self.held(part, level):
                if (rel >> bit) & 1:
                    slot = self.held(part, level + 1).index(rel ^ (1 << bit))
                    yield remote(
                        self.current(part, level, chip, rel),
                        self.stage(part, level, chip, slot),
                        self.ps.at[part, level, chip, slot],
                        self.pr.at[part, level, chip, slot],
                        self.p.flip(bit),
                    )

    def send_plane(self, level, chip):
        for c in self.plane(level, chip):
            c.start()

    def add_plane(self, level, chip):
        for c in self.plane(level, chip):
            c.wait_recv()
        for part in range(2):
            for slot, rel in enumerate(self.held(part, level + 1)):
                room = self.stage(part, level, chip, slot)
                mine = self.current(part, level, chip, rel)
                room[...] = (room[...].astype(f32) + mine[...].astype(f32)).astype(bf16)

    def hop(self, chip):
        p = self.p
        right = chip > p.z
        way, room = jnp.where(right, 0, 1), jnp.abs(chip - p.z)
        to = (p.dp, jnp.clip(jnp.where(right, p.z + 1, p.z - 1), 0, p.nz - 1) * CORES + p.core)
        behind = (chip != p.z) & jnp.where(right, p.z > 0, p.z < p.nz - 1)
        before = jnp.maximum(room - 1, 0)
        copies = [
            remote(
                self.stage(part, self.m - 1, chip, 0),
                self.zstage(part, way, before),
                self.zs.at[part, way, before],
                self.zr.at[part, way, before],
                to,
            )
            for part in range(2)
        ]
        return copies, behind, way, jnp.minimum(room, p.nz - 2)

    def arrive(self, part, way, room):
        p = self.p
        ref = self.zstage(part, way, room)
        remote(ref, ref, self.zs.at[part, way, room], self.zr.at[part, way, room], p.twin()).wait_recv()

    def send_line(self, chip):
        copies, behind, _, _ = self.hop(chip)

        @pl.when((chip != self.p.z) & jnp.logical_not(behind))
        def _():
            for c in copies:
                c.start()

    def forward_line(self, chip):
        copies, behind, way, room = self.hop(chip)

        @pl.when(behind)
        def _():
            for part, c in enumerate(copies):
                self.arrive(part, way, room)
                mine = self.stage(part, self.m - 1, chip, 0)
                got = self.zstage(part, way, room)
                mine[...] = (mine[...].astype(f32) + got[...].astype(f32)).astype(bf16)
                c.start()

    def pass_on(self, level, chip):
        self.add_plane(level, chip)
        if level + 1 < self.m:
            self.send_plane(level + 1, chip)
        else:
            self.send_line(chip)

    def end_line(self):
        p = self.p
        puts = []
        for way, there in ((0, p.z > 0), (1, p.z < p.nz - 1)):

            @pl.when(there)
            def _():
                for part in range(2):
                    self.arrive(part, way, 0)
                    mine = self.stage(part, self.m - 1, p.z, 0)
                    got = self.zstage(part, way, 0)
                    mine[...] = (mine[...].astype(f32) + got[...].astype(f32)).astype(bf16)

        for part in range(2):
            puts.append(
                pltpu.make_async_copy(
                    self.stage(part, self.m - 1, p.z, 0), self.out(part, p.dp), self.fs.at[part]
                )
            )
            puts[-1].start()
        for c in puts:
            c.wait()
        self.back.begin()

    def end(self):
        for level in range(self.m):
            for chip in range(self.p.nz):
                for c in self.plane(level, chip):
                    c.wait_send()
        for chip in range(self.p.nz):
            copies, _, _, _ = self.hop(chip)

            @pl.when(chip != self.p.z)
            def _():
                for c in copies:
                    c.wait_send()

        self.back.end()


def backward_body(
    n, nd, steps, width, len_ref, mine_ref, theirs_ref, x_ref, g_ref, gm_ref, branch_ref, mod_ref,
    db_ref, dbias_ref, code_ref, extra_ref, l_ref, ehs_ref, dm_ref, n_hbm, q_hbm, k_hbm, v_hbm,
    o_hbm, wa_hbm,
    out_ref, ym_ref, ya_ref, tg_ref, small_ref,
    got, awide, spare, normed, wp, qs_, ks_, vs_, os_, ku, kut, dk, dv, gqs, gkv, masks,
    dmk, mstage, mz, da, astage, az, gmine, ghalo, pay, part, held,
    xs, xr, load, wl, ld, mks,
    mps, mpr, mzs, mzr, mos, mor, mfs, aps, apr, azs, azr, aos, aor, afs,
    gs, gr, hs, hr, s1, r1, s2, r2, s3, r3, s4, r4,
):
    p = Place(n, nd)
    nz, tok = p.nz, x_ref.shape[0]
    rounds = len(steps)
    blocks = 2 * rounds + 2
    pairs = l_ref.shape[0]
    merge = LANES // width
    arows = 4 * width // nd
    units = dbias_ref.shape[1]
    t = CORES * tok
    half = D // 2
    m = bits_of(nd)
    chunk = 6 * D // n
    owners = owners_of(p, steps)
    table = lambda which: mod_ref[:, which * D : (which + 1) * D]

    def base(level):
        return sum(nd >> (i + 1) for i in range(level))

    def kept_slot(q, d):
        bit = p.orders[q][0]
        return ((d >> (bit + 1)) << bit) | (d & ((1 << bit) - 1))

    cut = lambda q: pl.ds(q * half, half)
    rm = Reduce(
        p,
        lambda q, chip, d: dm_ref.at[chip, q, d],
        lambda q, chip, d: dmk.at[q, chip, kept_slot(q, d)],
        lambda q, level, chip, slot: mstage.at[q, base(level) + slot, chip],
        lambda q, way, room: mz.at[q, way, room],
        lambda q, d: ym_ref.at[q, d],
        (mps, mpr, mzs, mzr, mos, mor, mfs),
    )
    a_own = lambda q, chip, d: da.at[chip, pl.ds(d * arows, arows), cut(q)]
    ra = Reduce(
        p,
        a_own,
        a_own,
        lambda q, level, chip, slot: astage.at[q, base(level) + slot, chip],
        lambda q, way, room: az.at[q, way, room],
        lambda q, d: ya_ref.at[pl.ds(d * arows, arows), cut(q)],
        (aps, apr, azs, azr, aos, aor, afs),
    )
    p.greet_all()
    far = [p.turn(k) for k in range(nz)]
    swaps = [remote(theirs_ref.at[i], got.at[i], xs.at[i], xr.at[i], p.twin()) for i in range(2)]
    swaps.append(remote(awide.at[0], awide.at[1], xs.at[2], xr.at[2], p.twin()))
    swaps[0].start()
    swaps[1].start()
    early = far[: nz // 2]
    for o in early:
        rm.send_plane(0, o)
    loads = [
        pltpu.make_async_copy(wa_hbm.at[:, pl.ds(3 * width, width)], wp, load.at[0]),
        pltpu.make_async_copy(n_hbm, normed.at[pl.ds(0, blocks * tok)], load.at[1]),
    ]
    for c in loads:
        c.start()

    def fetch(s, slot):
        return [
            pltpu.make_async_copy(src.at[s], dst.at[slot], ld.at[i, slot])
            for i, (src, dst) in enumerate(
                ((q_hbm, qs_), (k_hbm, ks_), (v_hbm, vs_), (o_hbm, os_))
            )
        ]

    for c in fetch(0, 0):
        c.start()
    keeps = []
    for q in range(2):
        for rel in rm.held(q, 1):
            d = p.dp ^ rel
            keeps.append(
                pltpu.make_async_copy(
                    dm_ref.at[:, q, d], dmk.at[q, :, kept_slot(q, d)], mks.at[q, rel]
                )
            )
            keeps[-1].start()

    item, _ = ranks_at(len_ref, owners[0], tok, (tok, 8), 0)
    picks = (item == lax.broadcasted_iota(jnp.int32, (tok, 8), 1)).astype(bf16)
    gamma_one = per_token(picks, table(GAMMA_ONE))
    resid = x_ref[...].astype(f32) + gamma_one * branch_ref[...]
    normal, rstd = norm_parts(resid)
    scale = per_token(picks, table(SCALE_TWO))
    grad_final = g_ref[...].astype(f32)
    swaps[0].wait()
    second = mine_ref[0] + got[0].astype(f32)
    mid = grad_final + norm_back(normal, rstd, second * (1.0 + scale))
    tg_ref[...] = mid
    attn = (gamma_one * mid).astype(bf16)
    awide[0] = attn
    swaps[2].start()
    pay[...] = jnp.zeros_like(pay)

    def put_items(which, values):
        pay[:, which * D : (which + 1) * D] = per_item(picks, values)

    put_items(SCALE_TWO, second * normal)
    put_items(SHIFT_TWO, second)
    put_items(GAMMA_ONE, mid * branch_ref[...])
    swaps[1].wait()
    mlp_branch = mine_ref[1] + got[1].astype(f32) + db_ref[...]
    out_ref[...] = (resid + per_token(picks, table(GAMMA_TWO)) * mlp_branch).astype(bf16)
    put_items(GAMMA_TWO, grad_final * mlp_branch)
    row_six = SEGS
    pay[row_six : row_six + 1, :D] = jnp.sum(attn.astype(f32), axis=0, keepdims=True)
    pay[row_six : row_six + 1, D : 2 * D] = gm_ref[...]
    codes = code_ref[...]
    bins = NBINS // LANES
    high = lax.broadcasted_iota(jnp.int32, (bins, tok), 0) == codes // LANES
    low = lax.broadcasted_iota(jnp.int32, (LANES, tok), 0) == lax.rem(codes, LANES)
    counts = dot(high.astype(f32).astype(bf16), low.astype(f32).astype(bf16), 1, 1)
    for i in range(bins):
        at = 2 * D + i * LANES
        pay[row_six : row_six + 1, at : at + LANES] = counts[i : i + 1, :]
    row = pl.ds(SEGS + 1, 1)
    for z in range(nz):
        at = pl.multiple_of((p.core * nz + z) * units, LANES)
        pay[row, pl.ds(at, units)] = dbias_ref[z : z + 1, :]
    part[:, :, chunk:] = jnp.zeros((n, 8, LANES), f32)

    lists = seen_lists(steps, tok)
    for qi in range(CORES):
        item, rank = ranks_at(len_ref, owners[qi], tok, (8, tok), 1)
        lo, hi = item[:1] * 16, rank[:1]
        for j, b in enumerate(lists[qi]):
            _, e = ranks_at(len_ref, owners[b], tok, (tok, LANES), 0)
            e = e[:, :1]
            masks[qi, j] = jnp.where((e >= lo) & (e <= hi), 0.0, -1e30).astype(bf16)

    def proj_rows(s):
        if merge == 1:
            return wp[s]
        return jnp.concatenate([wp[s * merge + i] for i in range(merge)], axis=0)

    def weight(s, k, count=1):
        at = lambda i, j: normed[((s * merge + i) * 3 + j) * width : ((s * merge + i) * 3 + j + 1) * width, :]
        if merge == 1:
            return normed[(s * 3 + k) * width : (s * 3 + k + count) * width, :]
        rows_of = [at(i, k + j) for j in range(count) for i in range(merge)]
        return jnp.concatenate(rows_of, axis=0)

    def put_grad(s, k, value):
        for i in range(merge):
            da[s * merge + i, k * width : (k + 1) * width, :] = value[
                i * width : (i + 1) * width
            ].astype(bf16)

    for c in loads + keeps:
        c.wait()
    swaps[2].wait()

    trips = pairs * CORES
    agenda = {}

    def at_trip(it, do):
        agenda.setdefault(min(it, trips - 1), []).append(do)

    per_trip = max(1, nz // 4)
    for k, o in enumerate(early):
        at_trip(1 + k // per_trip, functools.partial(rm.pass_on, 0, o))
        if k + len(early) < nz:
            at_trip(
                1 + k // per_trip,
                functools.partial(rm.send_plane, 0, far[k + len(early)]),
            )
    if m > 1:
        for k, o in enumerate(early):
            at_trip(4 + k // per_trip, functools.partial(rm.pass_on, 1, o))
    late = far[len(early) :]
    at_trip(5, functools.partial(rm.pass_on, 0, late[0]))
    if nz == 4 and m == 2:
        at_trip(7, functools.partial(rm.pass_on, 0, late[1]))
        at_trip(6, functools.partial(rm.forward_line, early[0]))

    @pl.loop(0, pairs * CORES)
    def _(it):
        s, qi = it // CORES, lax.rem(it, CORES)
        slot = lax.rem(s, 2)

        @pl.when(qi == 0)
        def _():
            for c in fetch(s, slot):
                c.wait()

            @pl.when(s + 1 < pairs)
            def _():
                for c in fetch(s + 1, 1 - slot):
                    c.start()

            k = ks_[slot]
            unit = k * lax.rsqrt(half_sums(k * k) + epsilon)
            ku[...] = unit.astype(bf16)
            kut[...] = unit.T.astype(bf16)
            dk[...] = jnp.zeros_like(dk)
            dv[...] = jnp.zeros_like(dv)

        at = pl.ds(pl.multiple_of(qi * tok, tok), tok)
        ehs = ehs_ref[s]
        q = qs_[slot, at, :]
        rq = lax.rsqrt(half_sums(q * q) + epsilon)
        qhat = q * rq
        qu = (qhat * ehs).astype(bf16)
        qs = [one_half(qu, h) for h in range(2)]
        g = dot(awide[qi], proj_rows(s), 1, 1).astype(bf16)
        gs_h = [one_half(g, h) for h in range(2)]
        turned = (g.astype(f32) * os_[slot, at, :].astype(f32)).T
        deltas = [
            jnp.sum(turned[:HEAD], axis=0, keepdims=True),
            jnp.sum(turned[HEAD:], axis=0, keepdims=True),
        ]
        invs = [1.0 / l_ref[s, h : h + 1, at] for h in range(2)]
        dqt = [None, None]
        for j in range(len(lists[0])):
            b = block_at(lists, qi, j)
            cols = pl.ds(pl.multiple_of(b * tok, tok), tok)
            mask = masks[qi, j].astype(f32)
            kb, vb = ku[cols, :], vs_[slot, cols, :]
            dvs, dks = None, None
            for h in range(2):
                w = jnp.exp(dot(kb, qs[h], 1, 1) + mask) * invs[h]
                dp = dot(vb, gs_h[h], 1, 1)
                ds = (w * (dp - deltas[h])).astype(bf16)
                a = dot(w.astype(bf16), gs_h[h])
                c = dot(ds, qs[h])
                dvs = a if h == 0 else dvs + a
                dks = c if h == 0 else dks + c
                r = dot(kut[h * HEAD : (h + 1) * HEAD, cols], ds)
                dqt[h] = r if dqt[h] is None else dqt[h] + r
            dv[cols, :] += dvs
            dk[cols, :] += dks
        d = jnp.concatenate(dqt, axis=0).T
        hsum = jnp.sum(d * qhat * ehs, axis=0, keepdims=True)
        gq = (ehs * rq * (d - qhat * half_sums(qhat * d))).astype(bf16)
        gqs[s, at, :] = gq
        qsum = jnp.sum(gq.astype(f32), axis=0, keepdims=True)
        qcol = pl.ds(pl.multiple_of(nz * CORES * units + p.core * nz * width + s * LANES, LANES), LANES)
        vcol = pl.ds(
            pl.multiple_of(
                nz * CORES * (units + width) + p.core * nz * width + s * LANES, LANES
            ),
            LANES,
        )
        pay[row, qcol] += qsum
        for i in range(merge):
            chip = (s * merge + i) * CORES + p.core
            part[chip, SEGS + 1 : SEGS + 2, chunk : chunk + width] += hsum[
                :, i * width : (i + 1) * width
            ]

        @pl.when(qi == CORES - 1)
        def _():
            k = ks_[slot]
            rk = lax.rsqrt(half_sums(k * k) + epsilon)
            khat = k * rk
            d = dk[...]
            gkv[s, :, :LANES] = (rk * (d - khat * half_sums(khat * d))).astype(bf16)
            gv = dv[...].astype(bf16)
            gkv[s, :, LANES:] = gv
            pay[row, vcol] = jnp.sum(gv.astype(f32), axis=0, keepdims=True)
            put_grad(s, 0, dot(gqs[s], normed[:t, :], 0, 0))
            kvg = dot(gkv[s], normed[: blocks * tok, :], 0, 0)
            put_grad(s, 1, kvg[:LANES])
            put_grad(s, 2, kvg[LANES:])
            both = dot(os_[slot, :tok, :], awide[0], 0, 0)
            both = both + dot(os_[slot, tok:, :], awide[1], 0, 0)
            put_grad(s, 3, both)

        for when, todo in agenda.items():

            @pl.when(it == when)
            def _():
                for do in todo:
                    do()

    def norm_grad(b):
        at = pl.ds(b * tok, tok)
        total = None
        for s in range(pairs):
            r = dot(gkv[s, at, :], weight(s, 1, 2))
            if b < CORES:
                r = r + dot(gqs[s, at, :], weight(s, 0))
            total = r if total is None else total + r
        return total

    wloads = [
        pltpu.make_async_copy(
            wa_hbm.at[c, pl.ds(0, 3 * width)],
            normed.at[pl.ds(c * 3 * width, 3 * width)],
            wl.at[c],
        )
        for c in range(nz)
    ]
    for c in wloads:
        c.start()
    rooms = [awide.at[0], awide.at[1], got.at[0], got.at[1]]
    rooms += [spare.at[i] for i in range(spare.shape[0])]
    swap_at = lambda i: rooms[i]
    for c in wloads:
        c.wait()
    gcopies = [
        remote(swap_at(i), gmine.at[i], gs.at[i], gr.at[i], p.twin()) for i in range(rounds + 1)
    ]
    for i in range(rounds, -1, -1):
        swap_at(i)[...] = norm_grad(2 * i + 1).astype(bf16)
        gcopies[i].start()
    for o in late[1:]:
        if not (nz == 4 and m == 2):
            rm.pass_on(0, o)
    for o in far[: nz // 2]:
        ra.send_plane(0, o)
    if m == 2 and nz != 4:
        rm.forward_line(early[0])
    moves = []
    for i, per_core in enumerate(steps):
        own = norm_grad(2 * i + 2)
        gcopies[i + 1].wait()
        gmine[i + 1] = (own + gmine[i + 1].astype(f32)).astype(bf16)
        for c, step in enumerate(per_core):
            if step is None:
                continue
            go = (p.core == c) & (p.z - step >= 0) & (p.z - step < nz)
            have = (p.core == c) & (p.z + step >= 0) & (p.z + step < nz)
            to = (p.dp, jnp.clip(p.z - step, 0, nz - 1) * CORES + p.core)
            copy = remote(gmine.at[i + 1], ghalo.at[i], hs.at[i, c], hr.at[i, c], to)
            pl.when(go)(copy.start)
            moves.append((i, go, have, copy))
    own = norm_grad(0)
    gcopies[0].wait()
    own = own + gmine[0].astype(f32)
    if m > 1:
        for o in late:
            rm.pass_on(1, o)
    for level in range(2, m):
        for o in far:
            rm.pass_on(level, o)
    for o in far[nz // 2 :]:
        ra.send_plane(0, o)
    for k, o in enumerate(far):
        if k or m != 2:
            rm.forward_line(o)
    for o in far[: nz // 2]:
        ra.pass_on(0, o)
    for i, go, have, copy in moves:
        pl.when(have)(copy.wait_recv)
    for i in range(rounds):
        any_have = p.core < 0
        for j, go, have, copy in moves:
            if j == i:
                any_have = any_have | have

        @pl.when(jnp.logical_not(any_have))
        def _():
            ghalo[i] = jnp.zeros((tok, D), bf16)

    first = own
    for i in range(rounds):
        first = first + ghalo[i].astype(f32)
    normal, rstd = norm_parts(x_ref[...].astype(f32))
    scale = per_token(picks, table(SCALE_ONE))
    tg_ref[...] += norm_back(normal, rstd, first * (1.0 + scale))
    for which, values in ((SCALE_ONE, first * normal), (SHIFT_ONE, first)):
        pay[:SEGS, which * D : (which + 1) * D] = per_item(picks, values)[:SEGS]
    for j in range(n):
        part[j, :, :chunk] = pay[:, j * chunk : (j + 1) * chunk]
    line = p.line()
    sums = [remote(part.at[q[1]], held.at[o], s1.at[o], r1.at[o], q) for o, q in enumerate(line)]
    for c in sums:
        c.start()
    for o in far[nz // 2 :]:
        ra.pass_on(0, o)
    for c in sums:
        c.wait()
    total = part[p.me] + extra_ref[...]
    for o in range(n - 1):
        total = total + held[o]
    small_ref[p.core, p.dp, p.z] = total
    mine = small_ref.at[p.core, p.dp, p.z]
    sums = [remote(mine, mine, s3.at[o], r3.at[o], p.on_chip(o)) for o in p.far]
    for c in sums:
        c.start()
    for level in range(1, m):
        for o in far:
            ra.pass_on(level, o)
    for c in sums:
        c.wait()
    mine = small_ref.at[p.core, p.dp]
    plane = [(lax.rem(p.dp + o, nd), p.me) for o in range(1, nd)]
    sums = [remote(mine, mine, s2.at[o], r2.at[o], q) for o, q in enumerate(plane)]
    for c in sums:
        c.start()
    rm.end_line()
    for o in far:
        ra.forward_line(o)
    rm.back.step(0)
    ra.end_line()
    for c in sums:
        c.wait()
    mine = small_ref.at[p.core]
    last = remote(mine, mine, s4, r4, p.twin())
    last.start()
    for level in range(m):
        if level:
            rm.back.step(level)
        ra.back.step(level)
    last.wait()
    rm.end()
    ra.end()
    for i, go, have, copy in moves:
        pl.when(go)(copy.wait_send)


def backward(
    lengths, mine, theirs, tokens, out_grad, gmlp, branch, mod, down_bias, dbias, codes, extra, l,
    ehs, dm, normed, q, k, v, o, wa, steps, nd, width,
):
    n = wa.shape[0] * CORES
    nz = n // CORES
    tok = tokens.shape[0]
    rounds = len(steps)
    t, w = CORES * tok, k.shape[1]
    pairs = k.shape[0]
    piece, arows = dm.shape[3], 4 * width // nd
    rows, cols = extra.shape
    seen = len(seen_lists(steps, tok)[0])
    dma = pltpu.SemaphoreType.DMA
    vmem = pl.BlockSpec(memory_space=pltpu.VMEM)
    anywhere = pl.BlockSpec(memory_space=pl.ANY)
    m = bits_of(nd)
    scr = pltpu.VMEM
    plane = (2, m, nz, max(1, nd // 2))
    sems = lambda: [
        dma(plane),
        dma(plane),
        dma((2, 2, nz)),
        dma((2, 2, nz)),
        dma((2, nd)),
        dma((2, nd)),
        dma((2,)),
    ]
    return pl.pallas_call(
        functools.partial(backward_body, n, nd, steps, width),
        out_shape=[
            jax.ShapeDtypeStruct((tok, D), bf16),
            jax.ShapeDtypeStruct(dm.shape[1:], bf16),
            jax.ShapeDtypeStruct((4 * width, D), bf16),
            jax.ShapeDtypeStruct((tok, D), f32),
            jax.ShapeDtypeStruct((CORES, nd, nz, rows, cols), f32),
        ],
        in_specs=[pl.BlockSpec(memory_space=pltpu.SMEM)]
        + [vmem] * 13
        + [anywhere] * 7,
        out_specs=[vmem, anywhere, anywhere, vmem, vmem],
        scratch_shapes=[
            scr((2, tok, D), bf16),
            scr((CORES, tok, D), bf16),
            scr((max(1, rounds - 3), tok if rounds > 3 else 16, D), bf16),
            scr((max(w, pairs * 3 * LANES), D), bf16),
            scr((nz, width, D), bf16),
            scr((2, t, LANES), f32),
            scr((2, w, LANES), f32),
            scr((2, w, LANES), bf16),
            scr((2, t, LANES), bf16),
            scr((w, LANES), bf16),
            scr((LANES, w), bf16),
            scr((w, LANES), f32),
            scr((w, LANES), f32),
            scr((pairs, t, LANES), bf16),
            scr((pairs, w, 2 * LANES), bf16),
            scr((CORES, seen, tok, tok), bf16),
            scr((2, nz, max(1, nd // 2), piece, D), bf16),
            scr((2, nd - 1, nz, piece, D), bf16),
            scr((2, 2, nz - 1, piece, D), bf16),
            scr((nz, 4 * width, D), bf16),
            scr((2, nd - 1, nz, arows, D // 2), bf16),
            scr((2, 2, nz - 1, arows, D // 2), bf16),
            scr((rounds + 1, tok, D), bf16),
            scr((rounds, tok, D), bf16),
            scr((8, 6 * D), f32),
            scr((n, rows, cols), f32),
            scr((n - 1, rows, cols), f32),
            dma((3,)),
            dma((3,)),
            dma((2,)),
            dma((nz,)),
            dma((4, 2)),
            dma((2, nd)),
        ]
        + sems()
        + sems()
        + [
            dma((rounds + 1,)),
            dma((rounds + 1,)),
            dma((rounds, CORES)),
            dma((rounds, CORES)),
            dma((n - 1,)),
            dma((n - 1,)),
            dma((nd - 1,)),
            dma((nd - 1,)),
            dma((nz,)),
            dma((nz,)),
            dma,
            dma,
        ],
        compiler_params=pltpu.CompilerParams(
            collective_id=1, has_side_effects=True, vmem_limit_bytes=60 << 20
        ),
        name="backward",
    )(
        lengths, mine, theirs, tokens, out_grad, gmlp, branch, mod, down_bias, dbias, codes, extra,
        l, ehs, dm, normed, q, k, v, o, wa,
    )


def local(
    nd,
    nt,
    tokens,
    class_embed,
    item_lengths,
    token_codes,
    ada_weight,
    ada_bias,
    qkv_weight,
    query_bias,
    value_bias,
    head_scale,
    proj_weight,
    proj_bias,
    up_weight,
    up_bias,
    down_weight,
    down_bias,
    out_grad,
):
    d, t = lax.axis_index("dp"), lax.axis_index("tensor")
    nz = nt // CORES
    z, core = t // CORES, t % CORES
    tok = tokens.shape[0]
    heads = head_scale.shape[0]
    width = heads * HEAD
    wide = nz * width
    pairs = wide // LANES
    units = up_weight.shape[1]
    feat = class_embed.shape[2]

    per_chip = CORES * tok
    seen = [[], []]
    for c in range(CORES):
        for step in range(1, nz):
            if step * per_chip - c * tok - tok < BEHIND:
                seen[c].append(step)
        for step in range(1, nz):
            if (step - 1) * per_chip + c * tok < AHEAD:
                seen[c].append(-step)
    rounds = max(len(s) for s in seen)
    steps = [
        tuple(s[len(s) - 1 - i] if i < len(s) else None for s in seen) for i in range(rounds)
    ]

    chunk = ada_weight.shape[1] // nt
    cond_act = jax.nn.silu(class_embed[0]).astype(bf16)
    ada_part = jnp.dot(cond_act, ada_weight, preferred_element_type=f32)
    part = jnp.pad(ada_part.reshape(SEGS, nt, chunk).transpose(1, 0, 2), ((0, 0), (0, 2), (0, 0)))
    apack = jnp.concatenate(
        [qkv_weight.transpose(1, 2, 0).reshape(3 * width, D), proj_weight], axis=0
    )
    up_pack = up_weight.T.reshape(nd, units // nd, D)
    down_pack = down_weight.reshape(nd, units // nd, D)
    (
        normed, q_raw, k_raw, v_in, heads_out, weight_sums, wattn, wmlp, branch, resid, nwide,
        gwide, mod_wide, ehs,
    ) = forward(
        item_lengths[0], head_scale, tokens, out_grad, part, ada_bias[None], query_bias[None],
        value_bias[None], proj_bias[None], apack, up_pack, down_pack, steps, nd, width,
    )
    up_own = lax.dynamic_index_in_dim(
        up_bias.reshape(nz, CORES, units), core, 1, keepdims=False
    )
    mine, theirs, dmlp, dbias, gsum = mlp(
        nwide.reshape(CORES * tok, D), gwide.reshape(CORES * tok, D), wmlp, up_own
    )
    own_tail = jnp.pad(cond_act.astype(f32), ((0, 8 - SEGS), (chunk, LANES - feat)))
    layer_out, ymlp, yattn, tokens_grad, small = backward(
        item_lengths[0], mine, theirs, tokens, out_grad, gsum, branch, mod_wide,
        down_bias[None], dbias.reshape(nz, units), token_codes.reshape(1, tok), own_tail, weight_sums, ehs, dmlp,
        normed, q_raw, k_raw, v_in, heads_out, wattn, steps, nd, width,
    )

    rows_all = small[..., :chunk].transpose(1, 3, 2, 0, 4).reshape(nd, 8, 6 * D)
    mod_all = rows_all[:, :SEGS].reshape(nd * SEGS, 6 * D)
    mod_own = lax.dynamic_index_in_dim(rows_all, d, 0, keepdims=False)[:SEGS]
    bias_sums = jnp.sum(rows_all[:, SEGS:], axis=0)
    own_small = lax.dynamic_index_in_dim(small, core, 0, keepdims=False)
    own_small = lax.dynamic_index_in_dim(own_small, z, 1, keepdims=False)
    cond_all = own_small[:, :SEGS, chunk : chunk + feat].reshape(nd * SEGS, feat)
    hscale_grad = jnp.sum(own_small[:, 7, chunk : chunk + width].reshape(nd, heads, HEAD), axis=(0, 2))
    adaw_grad = dot(cond_all, mod_all, 0, 0, lax.Precision.HIGH)
    adab_grad = jnp.sum(mod_all, axis=0)
    cond_grad = dot(mod_own, ada_weight.astype(f32), 1, 1, lax.Precision.HIGH)
    embed_grad = jax.vjp(jax.nn.silu, class_embed)[1](cond_grad[None])[0]
    projb_grad, downb_grad = bias_sums[0, :D], bias_sums[0, D : 2 * D]
    code_hist = bias_sums[0, 2 * D :]
    at = lambda base, k: lax.dynamic_slice_in_dim(bias_sums[1], base + (core * nz + z) * k, k, 0)
    upb_grad = at(0, units)
    qbias_grad = at(nt * units, width)
    vbias_grad = at(nt * (units + width), width)
    qkvw_grad = yattn[: 3 * width].astype(f32).reshape(3, width, D).transpose(2, 0, 1)
    projw_grad = yattn[3 * width :].astype(f32)
    upw_grad = ymlp[0].reshape(units, D).astype(f32).T
    downw_grad = ymlp[1].reshape(units, D).astype(f32)
    return (
        layer_out,
        tokens_grad,
        embed_grad,
        adaw_grad,
        adab_grad,
        qkvw_grad,
        qbias_grad,
        vbias_grad,
        hscale_grad,
        projw_grad,
        projb_grad,
        upw_grad,
        upb_grad,
        downw_grad,
        downb_grad,
        code_hist,
    )


def solution(mesh):
    placed = (
        P(("dp", "tensor"), None),
        P("dp", None, "tensor"),
        P("dp", None),
        P(("dp", "tensor")),
        P("tensor", None),
        P(),
        P(None, None, "tensor"),
        P("tensor"),
        P("tensor"),
        P("tensor"),
        P("tensor", None),
        P(),
        P(None, "tensor"),
        P(),
        P("tensor", None),
        P(),
        P(("dp", "tensor"), None),
    )
    return jax.shard_map(
        functools.partial(local, mesh.shape["dp"], mesh.shape["tensor"]),
        mesh=mesh,
        in_specs=placed,
        out_specs=(
            P(("dp", "tensor"), None),
            P(("dp", "tensor"), None),
            P("dp", None, "tensor"),
            P("tensor", None),
            P(),
            P(None, None, "tensor"),
            P("tensor"),
            P("tensor"),
            P("tensor"),
            P("tensor", None),
            P(),
            P(None, "tensor"),
            P("tensor"),
            P("tensor", None),
            P(),
            P(),
        ),
        check_vma=False,
    )
```

```python
import functools

import jax
import jax.numpy as jnp
from jax import lax
from jax.experimental import pallas as pl
from jax.experimental.pallas import tpu as pltpu
from jax.sharding import PartitionSpec as P

HEAD = 64
NBINS = 4096
ROW_LEN = 2048
SEGS = 6
D = 1024
ITEM_MAX = 680
CORES = 2
LANES = 128

epsilon = 1e-06
scale_starts = (1, 5, 14, 30, 55, 91, 155, 255, 424)
AHEAD = ITEM_MAX - scale_starts[-1] - 1
BEHIND = ITEM_MAX - 1
highest = lax.Precision.HIGHEST
f32 = jnp.float32
bf16 = jnp.bfloat16
MESH = pl.DeviceIdType.MESH
VMEM_LIMIT = 56 << 20


def dot(a, b, ca=1, cb=0, precision=None):
    return lax.dot_general(
        a, b, (((ca,), (cb,)), ((), ())), preferred_element_type=f32, precision=precision
    )


def item_layout(lengths):
    ends = jnp.cumsum(lengths, dtype=jnp.int32)
    begin = ends - lengths
    position = jnp.arange(ROW_LEN, dtype=jnp.int32)
    segment = jnp.sum((position[:, None] >= ends[None, :]).astype(jnp.int32), axis=1)
    chosen = segment[:, None] == jnp.arange(SEGS, dtype=jnp.int32)[None, :]
    inside = position - jnp.sum(jnp.where(chosen, begin[None, :], 0), axis=1)
    scale_ids = jnp.zeros_like(inside)
    for threshold in scale_starts:
        scale_ids = scale_ids + (inside >= threshold).astype(jnp.int32)
    return segment, scale_ids


def greet(peers):
    barrier = pltpu.get_barrier_semaphore()
    for p in peers:
        pl.semaphore_signal(barrier, inc=1, device_id=p, device_id_type=MESH)
    pl.semaphore_wait(barrier, len(peers))


def remote(src, dst, send, recv, to):
    return pltpu.make_async_remote_copy(
        src_ref=src,
        dst_ref=dst,
        send_sem=send,
        recv_sem=recv,
        device_id=to,
        device_id_type=MESH,
    )


class Place:
    def __init__(self, n, nd):
        self.n, self.nd, self.nz = n, nd, n // CORES
        self.dp, self.me = lax.axis_index("dp"), lax.axis_index("tensor")
        self.z, self.core = self.me // CORES, lax.rem(self.me, CORES)
        self.orders = orders_of(nd)
        self.far = sorted(range(1, self.nz), key=lambda o: min(o, self.nz - o))

    def chip(self, step):
        return lax.rem(self.z + step + self.nz, self.nz)

    def on_chip(self, step):
        return (self.dp, self.chip(step) * CORES + self.core)

    def turn(self, k):
        return jnp.where(self.z < self.nz // 2, self.nz - 1 - k, k)

    def twin(self):
        return (self.dp, self.z * CORES + 1 - self.core)

    def flip(self, bit):
        return (self.dp ^ (1 << bit), self.me)

    def line(self):
        return [(self.dp, lax.rem(self.me + o, self.n)) for o in range(1, self.n)]

    def greet_all(self):
        greet(self.line() + [self.flip(b) for b in range(bits_of(self.nd))])


def bits_of(nd):
    return nd.bit_length() - 1


def orders_of(nd):
    m = bits_of(nd)
    return [list(range(m)), [(m // 2 + i) % m for i in range(m)]]


def spread_plan(order):
    plan = [(0, list(order))]
    for i, bit in enumerate(order):
        plan += [(rel | (1 << bit), list(order[i + 1 :])) for rel, _ in list(plan)]
    return plan


class Spread:
    def __init__(self, place, ref_of, send, recv):
        self.place, self.ref_of, self.send, self.recv = place, ref_of, send, recv
        self.levels = bits_of(place.nd)

    def sends(self, part, rel, bits):
        p = self.place
        ref = self.ref_of(part, p.dp ^ rel)
        for bit in bits:
            to = rel | (1 << bit)
            yield remote(ref, ref, self.send.at[part, to], self.recv.at[part, to], p.flip(bit))

    def arrived(self, level):
        for part, order in enumerate(self.place.orders):
            for rel, bits in spread_plan(order):
                if rel and len(order) - 1 - len(bits) == level:
                    yield part, rel, bits

    def begin(self):
        for part, order in enumerate(self.place.orders):
            for c in self.sends(part, 0, order):
                c.start()

    def step(self, level):
        p = self.place
        for part, rel, bits in self.arrived(level):
            ref = self.ref_of(part, p.dp ^ rel)
            remote(
                ref, ref, self.send.at[part, rel], self.recv.at[part, rel], p.flip(0)
            ).wait_recv()
            for c in self.sends(part, rel, bits):
                c.start()

    def end(self):
        for part, order in enumerate(self.place.orders):
            for rel, bits in spread_plan(order):
                for c in self.sends(part, rel, bits):
                    c.wait_send()


class Line:
    def __init__(self, place, own, ref_of, send, recv):
        self.p, self.own, self.ref_of, self.send, self.recv = place, own, ref_of, send, recv
        self.ways = (1, -1)

    def inside(self, z):
        return (z >= 0) & (z < self.p.nz)

    def source(self, w, step):
        z = self.p.z - self.ways[w] * step
        return jnp.clip(z, 0, self.p.nz - 1), self.inside(z)

    def copies(self, w, step):
        p = self.p
        to = p.z + self.ways[w]
        chip, have = self.source(w, step - 1)
        there = self.ref_of(chip)
        cs = [
            remote(
                src,
                dst,
                self.send.at[w, step, i],
                self.recv.at[w, step, i],
                (p.dp, jnp.clip(to, 0, p.nz - 1) * CORES + p.core),
            )
            for i, (src, dst) in enumerate(zip(self.own if step == 1 else there, there))
        ]
        return cs, have & self.inside(to)

    def start(self, step=1):
        for w in range(2):
            cs, do = self.copies(w, step)

            @pl.when(do)
            def _():
                for c in cs:
                    c.start()

    def got(self, step, then):
        for w in range(2):
            chip, have = self.source(w, step)
            waits = [
                remote(ref, ref, self.send.at[w, step, i], self.recv.at[w, step, i], self.p.twin())
                for i, ref in enumerate(self.ref_of(chip))
            ]
            on, more = [], None
            if step + 1 < self.p.nz:
                on, more = self.copies(w, step + 1)

            @pl.when(have)
            def _():
                for c in waits:
                    c.wait_recv()
                if on:

                    @pl.when(more)
                    def _():
                        for c in on:
                            c.start()

                then(w, chip)

    def each(self, step, do):
        for w in range(2):
            chip, have = self.source(w, step)
            pl.when(have)(functools.partial(do, w, chip))

    def end(self):
        for step in range(1, self.p.nz):
            for w in range(2):
                cs, do = self.copies(w, step)

                @pl.when(do)
                def _():
                    for c in cs:
                        c.wait_send()


def picks_of(seg):
    return (seg == lax.broadcasted_iota(jnp.int32, (seg.shape[0], 8), 1)).astype(bf16)


def two(x):
    high = x.astype(bf16)
    return high, (x - high.astype(f32)).astype(bf16)


def per_token(picks, table):
    high, low = two(table)
    return dot(picks, high) + dot(picks, low)


def per_item(picks, values):
    high, low = two(values)
    return dot(picks, high, 0, 0) + dot(picks, low, 0, 0)


def norm_parts(values):
    centred = values - jnp.mean(values, axis=-1, keepdims=True)
    rstd = lax.rsqrt(jnp.mean(centred * centred, axis=-1, keepdims=True) + epsilon)
    return centred * rstd, rstd


def norm_back(normal, rstd, scaled):
    return rstd * (
        scaled
        - jnp.mean(scaled, axis=-1, keepdims=True)
        - normal * jnp.mean(scaled * normal, axis=-1, keepdims=True)
    )


GAMMA_ONE, GAMMA_TWO, SCALE_ONE, SCALE_TWO, SHIFT_ONE, SHIFT_TWO = range(6)


def half_lanes(rows):
    return lax.broadcasted_iota(jnp.int32, (rows, LANES), 1) < HEAD


def half_sums(x):
    low = half_lanes(x.shape[0])
    a = jnp.sum(jnp.where(low, x, 0.0), axis=1, keepdims=True)
    b = jnp.sum(jnp.where(low, 0.0, x), axis=1, keepdims=True)
    return jnp.where(low, a, b)


def one_half(x, h):
    low = half_lanes(x.shape[0])
    return jnp.where(low if h == 0 else jnp.logical_not(low), x, jnp.zeros_like(x))


def ranks_at(lengths_ref, owner, tok, shape, axis):
    place = jnp.maximum(owner, 0) * tok + lax.broadcasted_iota(jnp.int32, shape, axis)
    item = jnp.zeros(shape, jnp.int32)
    begin = jnp.zeros(shape, jnp.int32)
    end = jnp.int32(0)
    for i in range(SEGS):
        end = end + lengths_ref[i]
        past = place >= end
        item = item + past.astype(jnp.int32)
        begin = jnp.where(past, end, begin)
    rank = item * 16
    for threshold in scale_starts:
        rank = rank + (place - begin >= threshold).astype(jnp.int32)
    there = owner >= 0
    return item, jnp.where(there, rank, -1)


def owners_of(p, steps):
    owners = []
    for s in [(0, 0)] + list(steps):
        for flip in range(CORES):
            c = p.core ^ flip
            far = [p.nz if v is None else v for v in s]
            chip = p.z - jnp.where(c == 0, far[0], far[1])
            owners.append(jnp.where((chip >= 0) & (chip < p.nz), chip * CORES + c, -1))
    return owners


def seen_lists(steps, tok):
    lists = []
    for qi in range(CORES):
        seen = set()
        for c in range(CORES):
            query = c ^ qi
            for i, s in enumerate([(0, 0)] + list(steps)):
                for flip in range(CORES):
                    owner = c ^ flip
                    if s[owner] is None:
                        continue
                    off = owner - s[owner] * CORES - query
                    near = off == 0
                    behind = off < 0 and (-off - 1) * tok + 1 <= BEHIND
                    ahead = off > 0 and (off - 1) * tok + 1 <= AHEAD
                    if near or behind or ahead:
                        seen.add(2 * i + flip)
        lists.append(seen)
    both = sorted(lists[0] & lists[1])
    rest = [sorted(v - set(both)) for v in lists]
    size = max(len(r) for r in rest)
    for r in rest:
        spare = [b for b in range(2 * len(steps) + 2) if b not in both and b not in r]
        r += spare[: size - len(r)]
    return [both + rest[0], both + rest[1]]


def block_at(lists, qi, j):
    a, b = lists[0][j], lists[1][j]
    return a if a == b else jnp.where(qi == 0, a, b)


def forward_body(
    n, nd, steps, width, len_ref, hs_ref, tok_ref, grad_ref, emb_ref, ada_ref, abias_ref, qbias_ref,
    vbias_ref, pb_ref,
    apack_ref, up_ref, down_ref,
    n_out, q_out, k_out, v_out, o_ref, l_ref, wa_out, wm_ref, branch_ref, resid_ref, nwide_ref,
    gwide_ref, mod_ref, ehs_ref,
    win, wa, modc, held, part_ref, normed, qv, kv, vv, qb, vb, masks, ku, v0, v1, theirs, got,
    s1, r1, s2, r2, ts, tr, cs, cr, azs, azr, mzs, mzr, local_sem, out_sem, das, dar, dms, dmr,
    ms, mr,
):
    p = Place(n, nd)
    nz, tok = p.nz, grad_ref.shape[0]
    rounds = len(steps)
    blocks = 2 * rounds + 2
    pairs = qv.shape[0]
    merge = LANES // width
    rows = 4 * width // nd
    half = D // 2
    chunk = modc.shape[2]
    owners = owners_of(p, steps)
    p.greet_all()
    line = p.line()

    a_at = lambda chip, d: wa.at[chip, pl.ds(d * rows, rows)]
    mine = pl.ds(p.dp * rows, rows)
    al = Line(p, [apack_ref.at[mine]], lambda chip: [wa.at[chip, mine]], azs, azr)
    ml = Line(
        p,
        [up_ref.at[p.dp], down_ref.at[p.dp]],
        lambda chip: [wm_ref.at[chip, i, p.dp] for i in range(2)],
        mzs,
        mzr,
    )

    def a_spread(w, step, chip):
        return Spread(
            p,
            lambda part, d: wa.at[chip, pl.ds(d * rows, rows), pl.ds(part * half, half)],
            das.at[w, step],
            dar.at[w, step],
        )

    def m_spread(w, step, chip):
        return Spread(
            p, lambda part, d: wm_ref.at[chip, part, d], dms.at[w, step], dmr.at[w, step]
        )

    al.start()
    owns = [
        pltpu.make_async_copy(tok_ref, win.at[0], local_sem.at[0]),
        pltpu.make_async_copy(apack_ref, wa.at[p.z], local_sem.at[1]),
        pltpu.make_async_copy(up_ref, wm_ref.at[p.z, 0], local_sem.at[2]),
        pltpu.make_async_copy(down_ref, wm_ref.at[p.z, 1], local_sem.at[3]),
    ]
    for c in owns:
        c.start()
    x = emb_ref[...]
    cond = (x / (1.0 + jnp.exp(-x))).astype(bf16)
    part_ref[...] = jnp.zeros_like(part_ref)
    for j in range(n):
        part_ref[j, :SEGS, :] = dot(cond, ada_ref[:, j * chunk : (j + 1) * chunk])
    sums = [
        remote(part_ref.at[q[1]], held.at[o], s1.at[o], r1.at[o], q) for o, q in enumerate(line)
    ]
    for c in sums:
        c.start()
    twins = [
        remote(tok_ref if i == 0 else win.at[2 * i], win.at[2 * i + 1], cs.at[i], cr.at[i], p.twin())
        for i in range(rounds + 1)
    ]
    twins[0].start()
    for c in sums:
        c.wait()
    own = pl.ds(pl.multiple_of(p.me * chunk, LANES), chunk)
    total = part_ref[p.me] + abias_ref[:, own]
    for o in range(n - 1):
        total = total + held[o]
    modc[p.me] = total
    modc[p.me, SEGS : SEGS + 1, :width] = qbias_ref[...]
    modc[p.me, SEGS : SEGS + 1, width : 2 * width] = vbias_ref[...]
    for h in range(width // HEAD):
        at = 2 * width + h * HEAD
        modc[p.me, SEGS : SEGS + 1, at : at + HEAD] = jnp.exp(jnp.full((1, HEAD), hs_ref[h], f32))
    sums = [
        remote(modc.at[p.me], modc.at[p.me], s2.at[o], r2.at[o], q) for o, q in enumerate(line)
    ]
    for c in sums:
        c.start()
    moves = []
    for i, per_core in enumerate(steps):
        for c, step in enumerate(per_core):
            if step is None:
                continue
            go = (p.core == c) & (p.z + step >= 0) & (p.z + step < nz)
            have = (p.core == c) & (p.z - step >= 0) & (p.z - step < nz)
            to = (p.dp, jnp.clip(p.z + step, 0, nz - 1) * CORES + p.core)
            moves.append((i, go, have, remote(tok_ref, win.at[2 * i + 2], ts.at[i, c], tr.at[i, c], to)))
    al.got(1, lambda w, chip: a_spread(w, 1, chip).begin())
    for i, go, have, copy in moves:
        pl.when(go)(copy.start)
    for step in range(2, nz):
        al.got(step, lambda w, chip: a_spread(w, step, chip).begin())
    ml.start()

    for c in sums:
        c.wait()
    for j in range(n):
        mod_ref[:, j * chunk : (j + 1) * chunk] = modc[j]
    table = lambda which: mod_ref[:, which * D : (which + 1) * D]
    for s in range(pairs):
        parts = []
        for i in range(merge):
            r = modc[(s * merge + i) * CORES + p.core, SEGS : SEGS + 1, :]
            parts.append([r[:, k * width : (k + 1) * width] for k in range(3)])
        row = lambda k: jnp.concatenate([v[k] for v in parts], axis=1) if merge > 1 else parts[0][k]
        qb[s], vb[s], ehs_ref[s] = row(0), row(1), row(2)

    lists = seen_lists(steps, tok)
    for qi in range(CORES):
        owner = owners[qi]
        item, rank = ranks_at(len_ref, owner, tok, (tok, LANES), 0)
        lo, hi = item[:, :1] * 16, rank[:, :1]
        for j, b in enumerate(lists[qi]):
            _, e = ranks_at(len_ref, owners[b], tok, (8, tok), 1)
            e = e[:1]
            masks[qi, j] = jnp.where((e >= lo) & (e <= hi), 0.0, -1e30)
    own_item, _ = ranks_at(len_ref, owners[0], tok, (tok, 8), 0)
    picks = (own_item == lax.broadcasted_iota(jnp.int32, (tok, 8), 1)).astype(bf16)

    gwide_ref[0] = (per_token(picks, table(GAMMA_TWO)) * grad_ref[...].astype(f32)).astype(bf16)
    cross = [
        remote(gwide_ref.at[0], gwide_ref.at[1], ms.at[0], mr.at[0], p.twin()),
        remote(theirs, got, ms.at[1], mr.at[1], p.twin()),
        remote(nwide_ref.at[0], nwide_ref.at[1], ms.at[2], mr.at[2], p.twin()),
    ]
    cross[0].start()

    owns[0].wait()
    twins[0].wait()

    def norm_block(b):
        owner = owners[0]
        for i in range(1, blocks):
            owner = jnp.where(b == i, owners[i], owner)
        item, _ = ranks_at(len_ref, owner, tok, (tok, 8), 0)
        pick = (item == lax.broadcasted_iota(jnp.int32, (tok, 8), 1)).astype(bf16)
        normal, _ = norm_parts(win[b].astype(f32))
        scale = per_token(pick, table(SCALE_ONE))
        shift = per_token(pick, table(SHIFT_ONE))
        at = pl.ds(pl.multiple_of(b * tok, tok), tok)
        normed[at, :] = (normal * (1.0 + scale) + shift).astype(bf16)

    def weight(s, k, count=1):
        if merge == 1:
            return wa[s, k * width : (k + count) * width, :]
        rows_of = [
            wa[s * merge + i, (k + j) * width : (k + j + 1) * width, :]
            for j in range(count)
            for i in range(merge)
        ]
        return jnp.concatenate(rows_of, axis=0)

    def keys_block(b):
        at = pl.ds(pl.multiple_of(b * tok, tok), tok)

        def slot(s, _):
            r = dot(normed[at, :], weight(s, 1, 2), 1, 1)
            kv[s, at, :] = r[:, :LANES]
            vv[s, at, :] = (r[:, LANES:] + vb[s]).astype(bf16)
            return 0

        lax.fori_loop(0, pairs, slot, 0)

    @pl.loop(0, CORES)
    def _(b):
        norm_block(b)

    for level in range(bits_of(nd)):
        for step in range(1, nz):
            al.each(step, lambda w, chip: a_spread(w, step, chip).step(level))
    owns[1].wait()
    wout = pltpu.make_async_copy(wa, wa_out, out_sem.at[0])
    wout.start()

    @pl.loop(0, CORES)
    def _(b):
        keys_block(b)
        at = pl.ds(pl.multiple_of(b * tok, tok), tok)

        def slot(s, _):
            qv[s, at, :] = dot(normed[at, :], weight(s, 0), 1, 1) + qb[s]
            return 0

        lax.fori_loop(0, pairs, slot, 0)

    for i in range(rounds):
        any_got = p.core < 0
        for j, go, have, copy in moves:
            if j == i:
                pl.when(have)(copy.wait_recv)
                any_got = any_got | have

        @pl.when(jnp.logical_not(any_got))
        def _():
            win[2 * i + 2] = jnp.zeros((tok, D), bf16)

        twins[i + 1].start()
    for i in range(rounds):
        twins[i + 1].wait()

    ml.got(1, lambda w, chip: m_spread(w, 1, chip).begin())

    @pl.loop(CORES, blocks)
    def _(b):
        norm_block(b)
        keys_block(b)

    outs = [wout]
    for i, (src, dst) in enumerate(((normed, n_out), (qv, q_out), (kv, k_out), (vv, v_out))):
        outs.append(pltpu.make_async_copy(src, dst, out_sem.at[i + 1]))
        outs[-1].start()

    trips = pairs * CORES
    agenda = {}
    for step in range(1, nz):
        if step + 1 < nz:
            at = min(trips - 1, ((step - 1) * trips) // nz)
            agenda.setdefault(at, []).append((step + 1, 0))
        at = min(trips - 1, (step * trips) // nz)
        agenda.setdefault(at, []).append((0, step))

    @pl.loop(0, trips)
    def _(it):
        s, qi = it // CORES, lax.rem(it, CORES)

        @pl.when(qi == 0)
        def _():
            k = kv[s]
            ku[...] = (k * lax.rsqrt(half_sums(k * k) + epsilon)).astype(bf16)
            v = vv[s]
            low = half_lanes(v.shape[0])
            one = jnp.ones_like(v)
            v0[...] = jnp.where(low, v, one)
            v1[...] = jnp.where(low, one, v)

        at = pl.ds(pl.multiple_of(qi * tok, tok), tok)
        q = qv[s, at, :]
        qu = (q * lax.rsqrt(half_sums(q * q) + epsilon) * ehs_ref[s]).astype(bf16)
        qs = [one_half(qu, h) for h in range(2)]
        acc = [None, None]
        for j in range(len(lists[0])):
            b = block_at(lists, qi, j)
            cols = pl.ds(pl.multiple_of(b * tok, tok), tok)
            mask = masks[qi, j]
            for h in range(2):
                w = jnp.exp(dot(qs[h], ku[cols, :], 1, 1) + mask).astype(bf16)
                r = dot(w, (v0 if h == 0 else v1)[cols, :])
                acc[h] = r if acc[h] is None else acc[h] + r
        low = half_lanes(tok)
        other = jnp.where(low, pltpu.roll(acc[0], HEAD, 1), pltpu.roll(acc[1], HEAD, 1))
        o_ref[s, at, :] = (jnp.where(low, acc[0], acc[1]) / other).astype(bf16)
        turned = other.T
        l_ref[s, 0:1, at] = turned[0:1, :]
        l_ref[s, 1:2, at] = turned[HEAD : HEAD + 1, :]

        for when, todo in agenda.items():

            @pl.when(it == when)
            def _():
                for get, step in todo:
                    if get:
                        ml.got(get, lambda w, chip: m_spread(w, get, chip).begin())
                    else:
                        ml.each(step, lambda w, chip: m_spread(w, step, chip).step(0))

    def project(at):
        total = dot(o_ref[0, at, :], weight(0, 3))
        for s in range(1, pairs):
            total += dot(o_ref[s, at, :], weight(s, 3))
        return total

    theirs[...] = project(pl.ds(tok, tok)).astype(bf16)
    cross[1].start()
    first = project(pl.ds(0, tok)) + pb_ref[...]
    cross[1].wait()
    branch = first + got[...].astype(f32)
    branch_ref[...] = branch
    resid = win[0].astype(f32) + per_token(picks, table(GAMMA_ONE)) * branch
    resid_ref[...] = resid
    normal, _ = norm_parts(resid)
    scale = per_token(picks, table(SCALE_TWO))
    shift = per_token(picks, table(SHIFT_TWO))
    nwide_ref[0] = (normal * (1.0 + scale) + shift).astype(bf16)
    cross[2].start()

    for level in range(1, bits_of(nd)):
        for step in range(1, nz):
            ml.each(step, lambda w, chip: m_spread(w, step, chip).step(level))
    cross[0].wait()
    cross[2].wait()
    for step in range(1, nz):
        al.each(step, lambda w, chip: a_spread(w, step, chip).end())
        ml.each(step, lambda w, chip: m_spread(w, step, chip).end())
    al.end()
    ml.end()
    for i, go, have, copy in moves:
        pl.when(go)(copy.wait_send)
    owns[2].wait()
    owns[3].wait()
    for c in outs:
        c.wait()


def forward(
    lengths, scales, tokens, out_grad, embed, ada, abias, qbias, vbias, proj_bias, apack, up, down,
    steps, n, nd, width,
):
    part_shape = (n, 8, ada.shape[1] // n)
    nz = n // CORES
    tok = tokens.shape[0]
    rounds = len(steps)
    blocks = 2 * rounds + 2
    t, w = CORES * tok, blocks * tok
    pairs = nz * width // LANES
    seen = len(seen_lists(steps, tok)[0])
    dma = pltpu.SemaphoreType.DMA
    vmem = pl.BlockSpec(memory_space=pltpu.VMEM)
    anywhere = pl.BlockSpec(memory_space=pl.ANY)
    out = lambda *shape: jax.ShapeDtypeStruct(shape, f32)
    low = lambda *shape: jax.ShapeDtypeStruct(shape, bf16)
    v = pltpu.VMEM
    return pl.pallas_call(
        functools.partial(forward_body, n, nd, steps, width),
        out_shape=[
            low(w, D),
            out(pairs, t, LANES),
            out(pairs, w, LANES),
            low(pairs, w, LANES),
            low(pairs, t, LANES),
            out(pairs, 8, t),
            low(nz, 4 * width, D),
            low(nz, 2, *up.shape),
            out(tok, D),
            out(tok, D),
            low(CORES, tok, D),
            low(CORES, tok, D),
            out(8, 6 * D),
            out(pairs, 1, LANES),
        ],
        in_specs=[pl.BlockSpec(memory_space=pltpu.SMEM)] * 2
        + [anywhere]
        + [vmem] * 7
        + [anywhere] * 3,
        out_specs=[anywhere] * 4 + [vmem] * 2 + [anywhere] * 2 + [vmem] * 6,
        scratch_shapes=[
            v((blocks, tok, D), bf16),
            v((nz, 4 * width, D), bf16),
            v(part_shape, f32),
            v((n - 1,) + part_shape[1:], f32),
            v(part_shape, f32),
            v((w, D), bf16),
            v((pairs, t, LANES), f32),
            v((pairs, w, LANES), f32),
            v((pairs, w, LANES), bf16),
            v((pairs, 1, LANES), f32),
            v((pairs, 1, LANES), f32),
            v((CORES, seen, tok, tok), f32),
            v((w, LANES), bf16),
            v((w, LANES), bf16),
            v((w, LANES), bf16),
            v((tok, D), bf16),
            v((tok, D), bf16),
            dma((n - 1,)),
            dma((n - 1,)),
            dma((n - 1,)),
            dma((n - 1,)),
            dma((rounds, CORES)),
            dma((rounds, CORES)),
            dma((rounds + 1,)),
            dma((rounds + 1,)),
            dma((2, nz, 1)),
            dma((2, nz, 1)),
            dma((2, nz, 2)),
            dma((2, nz, 2)),
            dma((4,)),
            dma((5,)),
            dma((2, nz, 2, nd)),
            dma((2, nz, 2, nd)),
            dma((2, nz, 2, nd)),
            dma((2, nz, 2, nd)),
            dma((3,)),
            dma((3,)),
        ],
        compiler_params=pltpu.CompilerParams(
            collective_id=0, has_side_effects=True, vmem_limit_bytes=VMEM_LIMIT
        ),
        name="forward",
    )(
        lengths, scales, tokens, out_grad, embed, ada, abias, qbias, vbias, proj_bias, apack, up,
        down,
    )


def mlp_body(x_ref, g_ref, w_ref, bias_ref, mine_ref, theirs_ref, dw_ref, dbias_ref, gsum_ref, mlp, gx):
    x, g = x_ref[...], g_ref[...]
    tok = mine_ref.shape[1]
    units = w_ref.shape[2] * w_ref.shape[3]
    up = w_ref[0, 0].reshape(units, D)
    down = w_ref[0, 1].reshape(units, D)
    pre = dot(x, up, 1, 1) + bias_ref[0]
    square = pre * pre
    th = jnp.tanh(0.7978845608028654 * pre * (1.0 + 0.044715 * square))
    half = 0.5 * (1.0 + th)
    hidden = (pre * half).astype(bf16)
    slope = half + 0.5 * pre * (1.0 - th * th) * (
        0.7978845608028654 * (1.0 + 3.0 * 0.044715 * square)
    )
    gp = (dot(g, down, 1, 1) * slope).astype(bf16)

    @pl.when(pl.program_id(0) == 0)
    def _():
        gsum_ref[...] = jnp.sum(g[:tok].astype(f32), axis=0, keepdims=True)
        mlp[...] = jnp.zeros_like(mlp)
        gx[...] = jnp.zeros_like(gx)

    mlp[...] += dot(hidden, down)
    gx[...] += dot(gp, up)
    dw_ref[0, 0] = dot(gp, x, 0, 0).astype(bf16).reshape(dw_ref.shape[2:])
    dw_ref[0, 1] = dot(hidden, g, 0, 0).astype(bf16).reshape(dw_ref.shape[2:])
    dbias_ref[0] = jnp.sum(gp.astype(f32), axis=0, keepdims=True)

    @pl.when(pl.program_id(0) == pl.num_programs(0) - 1)
    def _():
        for i, v in enumerate((gx, mlp)):
            mine_ref[i] = v[:tok, :]
            theirs_ref[i] = v[tok:, :].astype(bf16)


def mlp(x, g, weights, bias):
    t = x.shape[0]
    tok = t // CORES
    nz, _, nd, piece, _ = weights.shape
    count = min(nd, max(1, 512 // piece))
    per = nd // count
    steps, units = nz * per, count * piece
    whole = lambda *shape: pl.BlockSpec(shape, lambda i: (0,) * len(shape))
    block = pl.BlockSpec((1, 2, count, piece, D), lambda i: (i // per, 0, i % per, 0, 0))
    row = pl.BlockSpec((1, 1, units), lambda i: (i, 0, 0))
    return pl.pallas_call(
        mlp_body,
        grid=(steps,),
        in_specs=[whole(t, D), whole(t, D), block, row],
        out_specs=[whole(2, tok, D), whole(2, tok, D), block, row, whole(1, D)],
        out_shape=[
            jax.ShapeDtypeStruct((2, tok, D), f32),
            jax.ShapeDtypeStruct((2, tok, D), bf16),
            jax.ShapeDtypeStruct(weights.shape, bf16),
            jax.ShapeDtypeStruct((steps, 1, units), f32),
            jax.ShapeDtypeStruct((1, D), f32),
        ],
        scratch_shapes=[pltpu.VMEM((t, D), f32), pltpu.VMEM((t, D), f32)],
        compiler_params=pltpu.CompilerParams(vmem_limit_bytes=VMEM_LIMIT),
        name="mlp",
    )(x, g, weights, bias.reshape(steps, 1, units))


class Reduce:
    def __init__(self, place, sent, kept, stage, zstage, out, sems):
        self.p, self.sent, self.kept = place, sent, kept
        self.stage, self.zstage = stage, zstage
        self.ps, self.pr, self.zs, self.zr, self.os, self.or_, self.fs = sems
        self.m = bits_of(place.nd)
        self.back = Spread(place, out, self.os, self.or_)
        self.out = out

    def held(self, part, level):
        rels = list(range(self.p.nd))
        for bit in self.p.orders[part][:level]:
            rels = [r for r in rels if not (r >> bit) & 1]
        return rels

    def current(self, part, level, chip, rel):
        if level == 0:
            bit = self.p.orders[part][0]
            return (self.sent if (rel >> bit) & 1 else self.kept)(part, chip, self.p.dp ^ rel)
        return self.stage(part, level - 1, chip, self.held(part, level).index(rel))

    def plane(self, level, chip):
        for part, order in enumerate(self.p.orders):
            bit = order[level]
            for rel in self.held(part, level):
                if (rel >> bit) & 1:
                    slot = self.held(part, level + 1).index(rel ^ (1 << bit))
                    yield remote(
                        self.current(part, level, chip, rel),
                        self.stage(part, level, chip, slot),
                        self.ps.at[part, level, chip, slot],
                        self.pr.at[part, level, chip, slot],
                        self.p.flip(bit),
                    )

    def send_plane(self, level, chip):
        for c in self.plane(level, chip):
            c.start()

    def add_plane(self, level, chip):
        for c in self.plane(level, chip):
            c.wait_recv()
        for part in range(2):
            for slot, rel in enumerate(self.held(part, level + 1)):
                room = self.stage(part, level, chip, slot)
                mine = self.current(part, level, chip, rel)
                room[...] = (room[...].astype(f32) + mine[...].astype(f32)).astype(bf16)

    def hop(self, chip):
        p = self.p
        right = chip > p.z
        way, room = jnp.where(right, 0, 1), jnp.abs(chip - p.z)
        to = (p.dp, jnp.clip(jnp.where(right, p.z + 1, p.z - 1), 0, p.nz - 1) * CORES + p.core)
        behind = (chip != p.z) & jnp.where(right, p.z > 0, p.z < p.nz - 1)
        before = jnp.maximum(room - 1, 0)
        copies = [
            remote(
                self.stage(part, self.m - 1, chip, 0),
                self.zstage(part, way, before),
                self.zs.at[part, way, before],
                self.zr.at[part, way, before],
                to,
            )
            for part in range(2)
        ]
        return copies, behind, way, jnp.minimum(room, p.nz - 2)

    def arrive(self, part, way, room):
        p = self.p
        ref = self.zstage(part, way, room)
        remote(ref, ref, self.zs.at[part, way, room], self.zr.at[part, way, room], p.twin()).wait_recv()

    def send_line(self, chip):
        copies, behind, _, _ = self.hop(chip)

        @pl.when((chip != self.p.z) & jnp.logical_not(behind))
        def _():
            for c in copies:
                c.start()

    def forward_line(self, chip):
        copies, behind, way, room = self.hop(chip)

        @pl.when(behind)
        def _():
            for part, c in enumerate(copies):
                self.arrive(part, way, room)
                mine = self.stage(part, self.m - 1, chip, 0)
                got = self.zstage(part, way, room)
                mine[...] = (mine[...].astype(f32) + got[...].astype(f32)).astype(bf16)
                c.start()

    def pass_on(self, level, chip):
        self.add_plane(level, chip)
        if level + 1 < self.m:
            self.send_plane(level + 1, chip)
        else:
            self.send_line(chip)

    def end_line(self):
        p = self.p
        puts = []
        for way, there in ((0, p.z > 0), (1, p.z < p.nz - 1)):

            @pl.when(there)
            def _():
                for part in range(2):
                    self.arrive(part, way, 0)
                    mine = self.stage(part, self.m - 1, p.z, 0)
                    got = self.zstage(part, way, 0)
                    mine[...] = (mine[...].astype(f32) + got[...].astype(f32)).astype(bf16)

        for part in range(2):
            puts.append(
                pltpu.make_async_copy(
                    self.stage(part, self.m - 1, p.z, 0), self.out(part, p.dp), self.fs.at[part]
                )
            )
            puts[-1].start()
        for c in puts:
            c.wait()
        self.back.begin()

    def end(self):
        for level in range(self.m):
            for chip in range(self.p.nz):
                for c in self.plane(level, chip):
                    c.wait_send()
        for chip in range(self.p.nz):
            copies, _, _, _ = self.hop(chip)

            @pl.when(chip != self.p.z)
            def _():
                for c in copies:
                    c.wait_send()

        self.back.end()


def backward_body(
    n, nd, steps, width, len_ref, mine_ref, theirs_ref, x_ref, g_ref, gm_ref, branch_ref, mod_ref,
    db_ref, dbias_ref, code_ref, extra_ref, l_ref, ehs_ref, dm_ref, n_hbm, q_hbm, k_hbm, v_hbm,
    o_hbm, wa_hbm,
    out_ref, ym_ref, ya_ref, tg_ref, small_ref,
    got, awide, spare, normed, wp, qs_, ks_, vs_, os_, ku, kut, dk, dv, gqs, gkv, masks,
    dmk, mstage, mz, da, astage, az, gmine, ghalo, pay, part, held,
    xs, xr, load, wl, ld, mks,
    mps, mpr, mzs, mzr, mos, mor, mfs, aps, apr, azs, azr, aos, aor, afs,
    gs, gr, hs, hr, s1, r1, s2, r2, s3, r3, s4, r4,
):
    p = Place(n, nd)
    nz, tok = p.nz, x_ref.shape[0]
    rounds = len(steps)
    blocks = 2 * rounds + 2
    pairs = l_ref.shape[0]
    merge = LANES // width
    arows = 4 * width // nd
    units = dbias_ref.shape[0] * dbias_ref.shape[2] // nz
    t = CORES * tok
    half = D // 2
    m = bits_of(nd)
    chunk = 6 * D // n
    owners = owners_of(p, steps)
    table = lambda which: mod_ref[:, which * D : (which + 1) * D]

    def base(level):
        return sum(nd >> (i + 1) for i in range(level))

    def kept_slot(q, d):
        bit = p.orders[q][0]
        return ((d >> (bit + 1)) << bit) | (d & ((1 << bit) - 1))

    cut = lambda q: pl.ds(q * half, half)
    rm = Reduce(
        p,
        lambda q, chip, d: dm_ref.at[chip, q, d],
        lambda q, chip, d: dmk.at[q, chip, kept_slot(q, d)],
        lambda q, level, chip, slot: mstage.at[q, base(level) + slot, chip],
        lambda q, way, room: mz.at[q, way, room],
        lambda q, d: ym_ref.at[q, d],
        (mps, mpr, mzs, mzr, mos, mor, mfs),
    )
    a_own = lambda q, chip, d: da.at[chip, pl.ds(d * arows, arows), cut(q)]
    ra = Reduce(
        p,
        a_own,
        a_own,
        lambda q, level, chip, slot: astage.at[q, base(level) + slot, chip],
        lambda q, way, room: az.at[q, way, room],
        lambda q, d: ya_ref.at[pl.ds(d * arows, arows), cut(q)],
        (aps, apr, azs, azr, aos, aor, afs),
    )
    p.greet_all()
    far = [p.turn(k) for k in range(nz)]
    swaps = [remote(theirs_ref.at[i], got.at[i], xs.at[i], xr.at[i], p.twin()) for i in range(2)]
    swaps.append(remote(awide.at[0], awide.at[1], xs.at[2], xr.at[2], p.twin()))
    swaps[0].start()
    swaps[1].start()
    early = far[: nz // 2]
    for o in early:
        rm.send_plane(0, o)
    loads = [
        pltpu.make_async_copy(wa_hbm.at[:, pl.ds(3 * width, width)], wp, load.at[0]),
        pltpu.make_async_copy(n_hbm, normed.at[pl.ds(0, blocks * tok)], load.at[1]),
    ]
    for c in loads:
        c.start()

    def fetch(s, slot):
        return [
            pltpu.make_async_copy(src.at[s], dst.at[slot], ld.at[i, slot])
            for i, (src, dst) in enumerate(
                ((q_hbm, qs_), (k_hbm, ks_), (v_hbm, vs_), (o_hbm, os_))
            )
        ]

    for c in fetch(0, 0):
        c.start()
    keeps = []
    for q in range(2):
        for rel in rm.held(q, 1):
            d = p.dp ^ rel
            keeps.append(
                pltpu.make_async_copy(
                    dm_ref.at[:, q, d], dmk.at[q, :, kept_slot(q, d)], mks.at[q, rel]
                )
            )
            keeps[-1].start()

    item, _ = ranks_at(len_ref, owners[0], tok, (tok, 8), 0)
    picks = (item == lax.broadcasted_iota(jnp.int32, (tok, 8), 1)).astype(bf16)
    gamma_one = per_token(picks, table(GAMMA_ONE))
    resid = x_ref[...].astype(f32) + gamma_one * branch_ref[...]
    normal, rstd = norm_parts(resid)
    scale = per_token(picks, table(SCALE_TWO))
    grad_final = g_ref[...].astype(f32)
    swaps[0].wait()
    second = mine_ref[0] + got[0].astype(f32)
    mid = grad_final + norm_back(normal, rstd, second * (1.0 + scale))
    tg_ref[...] = mid
    attn = (gamma_one * mid).astype(bf16)
    awide[0] = attn
    swaps[2].start()
    pay[...] = jnp.zeros_like(pay)

    def put_items(which, values):
        pay[:, which * D : (which + 1) * D] = per_item(picks, values)

    put_items(SCALE_TWO, second * normal)
    put_items(SHIFT_TWO, second)
    put_items(GAMMA_ONE, mid * branch_ref[...])
    swaps[1].wait()
    mlp_branch = mine_ref[1] + got[1].astype(f32) + db_ref[...]
    out_ref[...] = (resid + per_token(picks, table(GAMMA_TWO)) * mlp_branch).astype(bf16)
    put_items(GAMMA_TWO, grad_final * mlp_branch)
    row_six = SEGS
    pay[row_six : row_six + 1, :D] = jnp.sum(attn.astype(f32), axis=0, keepdims=True)
    pay[row_six : row_six + 1, D : 2 * D] = gm_ref[...]
    codes = code_ref[...]
    bins = NBINS // LANES
    high = lax.broadcasted_iota(jnp.int32, (bins, tok), 0) == codes // LANES
    low = lax.broadcasted_iota(jnp.int32, (LANES, tok), 0) == lax.rem(codes, LANES)
    counts = dot(high.astype(f32).astype(bf16), low.astype(f32).astype(bf16), 1, 1)
    for i in range(bins):
        at = 2 * D + i * LANES
        pay[row_six : row_six + 1, at : at + LANES] = counts[i : i + 1, :]
    row = pl.ds(SEGS + 1, 1)
    for z in range(nz):
        per = dbias_ref.shape[0] // nz
        for i in range(per):
            at = pl.multiple_of((p.core * nz + z) * units + i * (units // per), LANES)
            pay[row, pl.ds(at, units // per)] = dbias_ref[z * per + i]
    part[:, :, chunk:] = jnp.zeros((n, 8, LANES), f32)

    lists = seen_lists(steps, tok)
    for qi in range(CORES):
        item, rank = ranks_at(len_ref, owners[qi], tok, (8, tok), 1)
        lo, hi = item[:1] * 16, rank[:1]
        for j, b in enumerate(lists[qi]):
            _, e = ranks_at(len_ref, owners[b], tok, (tok, LANES), 0)
            e = e[:, :1]
            masks[qi, j] = jnp.where((e >= lo) & (e <= hi), 0.0, -1e30).astype(bf16)

    def proj_rows(s):
        if merge == 1:
            return wp[s]
        return jnp.concatenate([wp[s * merge + i] for i in range(merge)], axis=0)

    def weight(s, k, count=1):
        at = lambda i, j: normed[((s * merge + i) * 3 + j) * width : ((s * merge + i) * 3 + j + 1) * width, :]
        if merge == 1:
            return normed[(s * 3 + k) * width : (s * 3 + k + count) * width, :]
        rows_of = [at(i, k + j) for j in range(count) for i in range(merge)]
        return jnp.concatenate(rows_of, axis=0)

    def put_grad(s, k, value):
        for i in range(merge):
            da[s * merge + i, k * width : (k + 1) * width, :] = value[
                i * width : (i + 1) * width
            ].astype(bf16)

    for c in loads + keeps:
        c.wait()
    swaps[2].wait()

    trips = pairs * CORES
    agenda = {}

    def at_trip(it, do):
        agenda.setdefault(min(it, trips - 1), []).append(do)

    per_trip = max(1, nz // 4)
    for k, o in enumerate(early):
        at_trip(1 + k // per_trip, functools.partial(rm.pass_on, 0, o))
        if k + len(early) < nz:
            at_trip(
                1 + k // per_trip,
                functools.partial(rm.send_plane, 0, far[k + len(early)]),
            )
    if m > 1:
        for k, o in enumerate(early):
            at_trip(4 + k // per_trip, functools.partial(rm.pass_on, 1, o))
    late = far[len(early) :]
    at_trip(5, functools.partial(rm.pass_on, 0, late[0]))
    if nz == 4 and m == 2:
        at_trip(7, functools.partial(rm.pass_on, 0, late[1]))
        at_trip(6, functools.partial(rm.forward_line, early[0]))

    @pl.loop(0, pairs * CORES)
    def _(it):
        s, qi = it // CORES, lax.rem(it, CORES)
        slot = lax.rem(s, 2)

        @pl.when(qi == 0)
        def _():
            for c in fetch(s, slot):
                c.wait()

            @pl.when(s + 1 < pairs)
            def _():
                for c in fetch(s + 1, 1 - slot):
                    c.start()

            k = ks_[slot]
            unit = k * lax.rsqrt(half_sums(k * k) + epsilon)
            ku[...] = unit.astype(bf16)
            kut[...] = unit.T.astype(bf16)
            dk[...] = jnp.zeros_like(dk)
            dv[...] = jnp.zeros_like(dv)

        at = pl.ds(pl.multiple_of(qi * tok, tok), tok)
        ehs = ehs_ref[s]
        q = qs_[slot, at, :]
        rq = lax.rsqrt(half_sums(q * q) + epsilon)
        qhat = q * rq
        qu = (qhat * ehs).astype(bf16)
        qs = [one_half(qu, h) for h in range(2)]
        g = dot(awide[qi], proj_rows(s), 1, 1).astype(bf16)
        gs_h = [one_half(g, h) for h in range(2)]
        turned = (g.astype(f32) * os_[slot, at, :].astype(f32)).T
        deltas = [
            jnp.sum(turned[:HEAD], axis=0, keepdims=True),
            jnp.sum(turned[HEAD:], axis=0, keepdims=True),
        ]
        invs = [1.0 / l_ref[s, h : h + 1, at] for h in range(2)]
        dqt = [None, None]
        for j in range(len(lists[0])):
            b = block_at(lists, qi, j)
            cols = pl.ds(pl.multiple_of(b * tok, tok), tok)
            mask = masks[qi, j].astype(f32)
            kb, vb = ku[cols, :], vs_[slot, cols, :]
            dvs, dks = None, None
            for h in range(2):
                w = jnp.exp(dot(kb, qs[h], 1, 1) + mask) * invs[h]
                dp = dot(vb, gs_h[h], 1, 1)
                ds = (w * (dp - deltas[h])).astype(bf16)
                a = dot(w.astype(bf16), gs_h[h])
                c = dot(ds, qs[h])
                dvs = a if h == 0 else dvs + a
                dks = c if h == 0 else dks + c
                r = dot(kut[h * HEAD : (h + 1) * HEAD, cols], ds)
                dqt[h] = r if dqt[h] is None else dqt[h] + r
            dv[cols, :] += dvs
            dk[cols, :] += dks
        d = jnp.concatenate(dqt, axis=0).T
        hsum = jnp.sum(d * qhat * ehs, axis=0, keepdims=True)
        gq = (ehs * rq * (d - qhat * half_sums(qhat * d))).astype(bf16)
        gqs[s, at, :] = gq
        qsum = jnp.sum(gq.astype(f32), axis=0, keepdims=True)
        qcol = pl.ds(pl.multiple_of(nz * CORES * units + p.core * nz * width + s * LANES, LANES), LANES)
        vcol = pl.ds(
            pl.multiple_of(
                nz * CORES * (units + width) + p.core * nz * width + s * LANES, LANES
            ),
            LANES,
        )
        pay[row, qcol] += qsum
        for i in range(merge):
            chip = (s * merge + i) * CORES + p.core
            part[chip, SEGS + 1 : SEGS + 2, chunk : chunk + width] += hsum[
                :, i * width : (i + 1) * width
            ]

        @pl.when(qi == CORES - 1)
        def _():
            k = ks_[slot]
            rk = lax.rsqrt(half_sums(k * k) + epsilon)
            khat = k * rk
            d = dk[...]
            gkv[s, :, :LANES] = (rk * (d - khat * half_sums(khat * d))).astype(bf16)
            gv = dv[...].astype(bf16)
            gkv[s, :, LANES:] = gv
            pay[row, vcol] = jnp.sum(gv.astype(f32), axis=0, keepdims=True)
            put_grad(s, 0, dot(gqs[s], normed[:t, :], 0, 0))
            kvg = dot(gkv[s], normed[: blocks * tok, :], 0, 0)
            put_grad(s, 1, kvg[:LANES])
            put_grad(s, 2, kvg[LANES:])
            both = dot(os_[slot, :tok, :], awide[0], 0, 0)
            both = both + dot(os_[slot, tok:, :], awide[1], 0, 0)
            put_grad(s, 3, both)

        for when, todo in agenda.items():

            @pl.when(it == when)
            def _():
                for do in todo:
                    do()

    def norm_grad(b):
        at = pl.ds(b * tok, tok)
        total = None
        for s in range(pairs):
            r = dot(gkv[s, at, :], weight(s, 1, 2))
            if b < CORES:
                r = r + dot(gqs[s, at, :], weight(s, 0))
            total = r if total is None else total + r
        return total

    wloads = [
        pltpu.make_async_copy(
            wa_hbm.at[c, pl.ds(0, 3 * width)],
            normed.at[pl.ds(c * 3 * width, 3 * width)],
            wl.at[c],
        )
        for c in range(nz)
    ]
    for c in wloads:
        c.start()
    rooms = [awide.at[0], awide.at[1], got.at[0], got.at[1]]
    rooms += [spare.at[i] for i in range(spare.shape[0])]
    swap_at = lambda i: rooms[i]
    for c in wloads:
        c.wait()
    gcopies = [
        remote(swap_at(i), gmine.at[i], gs.at[i], gr.at[i], p.twin()) for i in range(rounds + 1)
    ]
    for i in range(rounds, -1, -1):
        swap_at(i)[...] = norm_grad(2 * i + 1).astype(bf16)
        gcopies[i].start()
    for o in late[1:]:
        if not (nz == 4 and m == 2):
            rm.pass_on(0, o)
    for o in far[: nz // 2]:
        ra.send_plane(0, o)
    if m == 2 and nz != 4:
        rm.forward_line(early[0])
    moves = []
    for i, per_core in enumerate(steps):
        own = norm_grad(2 * i + 2)
        gcopies[i + 1].wait()
        gmine[i + 1] = (own + gmine[i + 1].astype(f32)).astype(bf16)
        for c, step in enumerate(per_core):
            if step is None:
                continue
            go = (p.core == c) & (p.z - step >= 0) & (p.z - step < nz)
            have = (p.core == c) & (p.z + step >= 0) & (p.z + step < nz)
            to = (p.dp, jnp.clip(p.z - step, 0, nz - 1) * CORES + p.core)
            copy = remote(gmine.at[i + 1], ghalo.at[i], hs.at[i, c], hr.at[i, c], to)
            pl.when(go)(copy.start)
            moves.append((i, go, have, copy))
    own = norm_grad(0)
    gcopies[0].wait()
    own = own + gmine[0].astype(f32)
    if m > 1:
        for o in late:
            rm.pass_on(1, o)
    for level in range(2, m):
        for o in far:
            rm.pass_on(level, o)
    for o in far[nz // 2 :]:
        ra.send_plane(0, o)
    for k, o in enumerate(far):
        if k or m != 2:
            rm.forward_line(o)
    for o in far[: nz // 2]:
        ra.pass_on(0, o)
    for i, go, have, copy in moves:
        pl.when(have)(copy.wait_recv)
    for i in range(rounds):
        any_have = p.core < 0
        for j, go, have, copy in moves:
            if j == i:
                any_have = any_have | have

        @pl.when(jnp.logical_not(any_have))
        def _():
            ghalo[i] = jnp.zeros((tok, D), bf16)

    first = own
    for i in range(rounds):
        first = first + ghalo[i].astype(f32)
    normal, rstd = norm_parts(x_ref[...].astype(f32))
    scale = per_token(picks, table(SCALE_ONE))
    tg_ref[...] += norm_back(normal, rstd, first * (1.0 + scale))
    for which, values in ((SCALE_ONE, first * normal), (SHIFT_ONE, first)):
        pay[:SEGS, which * D : (which + 1) * D] = per_item(picks, values)[:SEGS]
    for j in range(n):
        part[j, :, :chunk] = pay[:, j * chunk : (j + 1) * chunk]
    line = p.line()
    sums = [remote(part.at[q[1]], held.at[o], s1.at[o], r1.at[o], q) for o, q in enumerate(line)]
    for c in sums:
        c.start()
    for o in far[nz // 2 :]:
        ra.pass_on(0, o)
    for c in sums:
        c.wait()
    total = part[p.me] + extra_ref[...]
    for o in range(n - 1):
        total = total + held[o]
    small_ref[p.core, p.dp, p.z] = total
    mine = small_ref.at[p.core, p.dp, p.z]
    sums = [remote(mine, mine, s3.at[o], r3.at[o], p.on_chip(o)) for o in p.far]
    for c in sums:
        c.start()
    for level in range(1, m):
        for o in far:
            ra.pass_on(level, o)
    for c in sums:
        c.wait()
    mine = small_ref.at[p.core, p.dp]
    plane = [(lax.rem(p.dp + o, nd), p.me) for o in range(1, nd)]
    sums = [remote(mine, mine, s2.at[o], r2.at[o], q) for o, q in enumerate(plane)]
    for c in sums:
        c.start()
    rm.end_line()
    for o in far:
        ra.forward_line(o)
    rm.back.step(0)
    ra.end_line()
    for c in sums:
        c.wait()
    mine = small_ref.at[p.core]
    last = remote(mine, mine, s4, r4, p.twin())
    last.start()
    for level in range(m):
        if level:
            rm.back.step(level)
        ra.back.step(level)
    last.wait()
    rm.end()
    ra.end()
    for i, go, have, copy in moves:
        pl.when(go)(copy.wait_send)


def backward(
    lengths, mine, theirs, tokens, out_grad, gmlp, branch, mod, down_bias, dbias, codes, extra, l,
    ehs, dm, normed, q, k, v, o, wa, steps, nd, width,
):
    n = wa.shape[0] * CORES
    nz = n // CORES
    tok = tokens.shape[0]
    rounds = len(steps)
    t, w = CORES * tok, k.shape[1]
    pairs = k.shape[0]
    piece, arows = dm.shape[3], 4 * width // nd
    rows, cols = extra.shape
    seen = len(seen_lists(steps, tok)[0])
    dma = pltpu.SemaphoreType.DMA
    vmem = pl.BlockSpec(memory_space=pltpu.VMEM)
    anywhere = pl.BlockSpec(memory_space=pl.ANY)
    m = bits_of(nd)
    scr = pltpu.VMEM
    plane = (2, m, nz, max(1, nd // 2))
    sems = lambda: [
        dma(plane),
        dma(plane),
        dma((2, 2, nz)),
        dma((2, 2, nz)),
        dma((2, nd)),
        dma((2, nd)),
        dma((2,)),
    ]
    return pl.pallas_call(
        functools.partial(backward_body, n, nd, steps, width),
        out_shape=[
            jax.ShapeDtypeStruct((tok, D), bf16),
            jax.ShapeDtypeStruct(dm.shape[1:], bf16),
            jax.ShapeDtypeStruct((4 * width, D), bf16),
            jax.ShapeDtypeStruct((tok, D), f32),
            jax.ShapeDtypeStruct((CORES, nd, nz, rows, cols), f32),
        ],
        in_specs=[pl.BlockSpec(memory_space=pltpu.SMEM)]
        + [vmem] * 13
        + [anywhere] * 7,
        out_specs=[vmem, anywhere, anywhere, vmem, vmem],
        scratch_shapes=[
            scr((2, tok, D), bf16),
            scr((CORES, tok, D), bf16),
            scr((max(1, rounds - 3), tok if rounds > 3 else 16, D), bf16),
            scr((max(w, pairs * 3 * LANES), D), bf16),
            scr((nz, width, D), bf16),
            scr((2, t, LANES), f32),
            scr((2, w, LANES), f32),
            scr((2, w, LANES), bf16),
            scr((2, t, LANES), bf16),
            scr((w, LANES), bf16),
            scr((LANES, w), bf16),
            scr((w, LANES), f32),
            scr((w, LANES), f32),
            scr((pairs, t, LANES), bf16),
            scr((pairs, w, 2 * LANES), bf16),
            scr((CORES, seen, tok, tok), bf16),
            scr((2, nz, max(1, nd // 2), piece, D), bf16),
            scr((2, nd - 1, nz, piece, D), bf16),
            scr((2, 2, nz - 1, piece, D), bf16),
            scr((nz, 4 * width, D), bf16),
            scr((2, nd - 1, nz, arows, D // 2), bf16),
            scr((2, 2, nz - 1, arows, D // 2), bf16),
            scr((rounds + 1, tok, D), bf16),
            scr((rounds, tok, D), bf16),
            scr((8, 6 * D), f32),
            scr((n, rows, cols), f32),
            scr((n - 1, rows, cols), f32),
            dma((3,)),
            dma((3,)),
            dma((2,)),
            dma((nz,)),
            dma((4, 2)),
            dma((2, nd)),
        ]
        + sems()
        + sems()
        + [
            dma((rounds + 1,)),
            dma((rounds + 1,)),
            dma((rounds, CORES)),
            dma((rounds, CORES)),
            dma((n - 1,)),
            dma((n - 1,)),
            dma((nd - 1,)),
            dma((nd - 1,)),
            dma((nz,)),
            dma((nz,)),
            dma,
            dma,
        ],
        compiler_params=pltpu.CompilerParams(
            collective_id=1, has_side_effects=True, vmem_limit_bytes=60 << 20
        ),
        name="backward",
    )(
        lengths, mine, theirs, tokens, out_grad, gmlp, branch, mod, down_bias, dbias, codes, extra,
        l, ehs, dm, normed, q, k, v, o, wa,
    )


def local(
    nd,
    nt,
    tokens,
    class_embed,
    item_lengths,
    token_codes,
    ada_weight,
    ada_bias,
    qkv_weight,
    query_bias,
    value_bias,
    head_scale,
    proj_weight,
    proj_bias,
    up_weight,
    up_bias,
    down_weight,
    down_bias,
    out_grad,
):
    d, t = lax.axis_index("dp"), lax.axis_index("tensor")
    nz = nt // CORES
    z, core = t // CORES, t % CORES
    tok = tokens.shape[0]
    heads = head_scale.shape[0]
    width = heads * HEAD
    wide = nz * width
    pairs = wide // LANES
    units = up_weight.shape[1]
    feat = class_embed.shape[2]

    per_chip = CORES * tok
    seen = [[], []]
    for c in range(CORES):
        for step in range(1, nz):
            if step * per_chip - c * tok - tok < BEHIND:
                seen[c].append(step)
        for step in range(1, nz):
            if (step - 1) * per_chip + c * tok < AHEAD:
                seen[c].append(-step)
    rounds = max(len(s) for s in seen)
    steps = [
        tuple(s[len(s) - 1 - i] if i < len(s) else None for s in seen) for i in range(rounds)
    ]

    chunk = ada_weight.shape[1] // nt
    cond_act = jax.nn.silu(class_embed[0]).astype(bf16)
    apack = jnp.concatenate(
        [qkv_weight.transpose(1, 2, 0).reshape(3 * width, D), proj_weight], axis=0
    )
    up_pack = up_weight.T.reshape(nd, units // nd, D)
    down_pack = down_weight.reshape(nd, units // nd, D)
    (
        normed, q_raw, k_raw, v_in, heads_out, weight_sums, wattn, wmlp, branch, resid, nwide,
        gwide, mod_wide, ehs,
    ) = forward(
        item_lengths[0], head_scale, tokens, out_grad, class_embed[0], ada_weight, ada_bias[None],
        query_bias[None], value_bias[None], proj_bias[None], apack, up_pack, down_pack, steps,
        nt, nd, width,
    )
    up_own = lax.dynamic_index_in_dim(
        up_bias.reshape(nz, CORES, units), core, 1, keepdims=False
    )
    mine, theirs, dmlp, dbias, gsum = mlp(
        nwide.reshape(CORES * tok, D), gwide.reshape(CORES * tok, D), wmlp, up_own
    )
    own_tail = jnp.pad(cond_act.astype(f32), ((0, 8 - SEGS), (chunk, LANES - feat)))
    layer_out, ymlp, yattn, tokens_grad, small = backward(
        item_lengths[0], mine, theirs, tokens, out_grad, gsum, branch, mod_wide,
        down_bias[None], dbias, token_codes.reshape(1, tok), own_tail, weight_sums, ehs, dmlp,
        normed, q_raw, k_raw, v_in, heads_out, wattn, steps, nd, width,
    )

    rows_all = small[..., :chunk].transpose(1, 3, 2, 0, 4).reshape(nd, 8, 6 * D)
    mod_all = rows_all[:, :SEGS].reshape(nd * SEGS, 6 * D)
    mod_own = lax.dynamic_index_in_dim(rows_all, d, 0, keepdims=False)[:SEGS]
    bias_sums = jnp.sum(rows_all[:, SEGS:], axis=0)
    own_small = lax.dynamic_index_in_dim(small, core, 0, keepdims=False)
    own_small = lax.dynamic_index_in_dim(own_small, z, 1, keepdims=False)
    cond_all = own_small[:, :SEGS, chunk : chunk + feat].reshape(nd * SEGS, feat)
    hscale_grad = jnp.sum(own_small[:, 7, chunk : chunk + width].reshape(nd, heads, HEAD), axis=(0, 2))
    adaw_grad = dot(cond_all, mod_all, 0, 0, lax.Precision.HIGH)
    adab_grad = jnp.sum(mod_all, axis=0)
    cond_grad = dot(mod_own, ada_weight.astype(f32), 1, 1, lax.Precision.HIGH)
    embed_grad = jax.vjp(jax.nn.silu, class_embed)[1](cond_grad[None])[0]
    projb_grad, downb_grad = bias_sums[0, :D], bias_sums[0, D : 2 * D]
    code_hist = bias_sums[0, 2 * D :]
    at = lambda base, k: lax.dynamic_slice_in_dim(bias_sums[1], base + (core * nz + z) * k, k, 0)
    upb_grad = at(0, units)
    qbias_grad = at(nt * units, width)
    vbias_grad = at(nt * (units + width), width)
    qkvw_grad = yattn[: 3 * width].astype(f32).reshape(3, width, D).transpose(2, 0, 1)
    projw_grad = yattn[3 * width :].astype(f32)
    upw_grad = ymlp[0].reshape(units, D).astype(f32).T
    downw_grad = ymlp[1].reshape(units, D).astype(f32)
    return (
        layer_out,
        tokens_grad,
        embed_grad,
        adaw_grad,
        adab_grad,
        qkvw_grad,
        qbias_grad,
        vbias_grad,
        hscale_grad,
        projw_grad,
        projb_grad,
        upw_grad,
        upb_grad,
        downw_grad,
        downb_grad,
        code_hist,
    )


def solution(mesh):
    placed = (
        P(("dp", "tensor"), None),
        P("dp", None, "tensor"),
        P("dp", None),
        P(("dp", "tensor")),
        P("tensor", None),
        P(),
        P(None, None, "tensor"),
        P("tensor"),
        P("tensor"),
        P("tensor"),
        P("tensor", None),
        P(),
        P(None, "tensor"),
        P(),
        P("tensor", None),
        P(),
        P(("dp", "tensor"), None),
    )
    return jax.shard_map(
        functools.partial(local, mesh.shape["dp"], mesh.shape["tensor"]),
        mesh=mesh,
        in_specs=placed,
        out_specs=(
            P(("dp", "tensor"), None),
            P(("dp", "tensor"), None),
            P("dp", None, "tensor"),
            P("tensor", None),
            P(),
            P(None, None, "tensor"),
            P("tensor"),
            P("tensor"),
            P("tensor"),
            P("tensor", None),
            P(),
            P(None, "tensor"),
            P("tensor"),
            P("tensor", None),
            P(),
            P(),
        ),
        check_vma=False,
    )
```
